32 devices in a mesh: dp: 16 (over z, y, x), head: 2 (over core).
Axes of the slice: x: 2, y: 2, z: 4, core: 2. Of those that a mesh axis runs over, the one named last changes fastest.
Arguments:
- inputs: bfloat16 [16384, 1280], P(('dp', 'head')), may hold values from -6 to 6
- segment_ids: int32 [32, 512], P(('dp', 'head')), may hold values from 0 to 3, never falling along the last dimension, each value on 1 to 256 neighbouring positions
- gain_attn: float32 [1280], replicated, may hold values from 0.1 to 1.9
- w_qkv: bfloat16 [1280, 3840], replicated, may hold values from -0.15625 to 0.15625
- w_out: bfloat16 [1280, 1280], replicated, may hold values from -1 to 1
- gain_mlp: float32 [1280], replicated, may hold values from 0.1 to 1.9
- w_up: bfloat16 [1280, 5120], replicated, may hold values from -0.15625 to 0.15625
- w_down: bfloat16 [5120, 1280], replicated, may hold values from -0.078125 to 0.078125
- gain_final: float32 [1280], replicated, may hold values from 0.1 to 1.9
- head_projection_weight: bfloat16 [1280, 1280], P(None, 'head'), may hold values from -0.15625 to 0.15625
- head_output_bias: float32 [1280], P('head'), may hold values from -5 to 5
- cotangent: bfloat16 [16384, 1280], P('dp', 'head'), may hold values from -6 to 6
Outputs:
- predicted_levels: float32 [16384, 1280], P('dp', 'head')
- entry_sensitivity_matrix: float32 [16384, 1280], P(('dp', 'head'))
- grad_gain_attn: float32 [1280], P(('dp', 'head'))
- grad_qkv: float32 [1280, 3840], P(('dp', 'head'))
- grad_out: float32 [1280, 1280], P(('dp', 'head'))
- grad_gain_mlp: float32 [1280], P(('dp', 'head'))
- grad_up: float32 [1280, 5120], P(('dp', 'head'))
- grad_down: float32 [5120, 1280], P(('dp', 'head'))
- grad_gain_final: float32 [1280], P(('dp', 'head'))
- grad_head: float32 [1280, 1280], P('dp', 'head')
- grad_bias: float32 [1280], P('head')
The draws below stay inside these ranges and needn't reach their ends.
Inputs may be any that keep to these rules, and one draw needn't show every extreme that they name: `segment_ids`: in each row the series ids never fall; each series spans 1 to 256 tokens, and in every row one spans exactly 256.
All inputs are finite; a program needn't handle non-finite values.
Results may differ from the reference program's by a relative error of at most 0.017.
Values may be sent and summed in bfloat16 or wider, within the bound.
A program may use at most 320 MiB of HBM per device.

```python
import math
import jax
import jax.numpy as jnp
import numpy as np
from jax import lax

LEN = 512
SERIES = 4
HEADS = 16
D = 1280
FF = 5120
HQ = 1280
ROWS = 32
TOKENS = 16384


def steps_of(rng, extent, pieces, least, largest):
    factor_of, own = 1.0, jax.random.fold_in(rng, 6)
    for axis_at, blocks in pieces:
        draws = jnp.exp(jax.random.uniform(jax.random.fold_in(own, axis_at), (blocks,), jnp.float32, least / len(pieces), largest / len(pieces)))
        factor_of = factor_of * jnp.repeat(draws, extent[axis_at] // blocks).reshape([-1 if axis == axis_at else 1 for axis in range(len(extent))])
    return factor_of


def length_profile(amount, total, bound, skew):
    loads = [(1 << 20) // math.isqrt(rank ** skew) + 1 for rank in range(2, amount + 1)]
    spare, counts = total - bound - (amount - 1), [1] * (amount - 1)
    while spare > 0:
        candidates = [i for i in range(amount - 1) if counts[i] < bound]
        whole, remaining = sum([loads[i] for i in candidates]), spare
        for i in candidates:
            more = min(bound - counts[i], max(1, remaining * loads[i] // whole), spare)
            counts[i] = counts[i] + more
            spare = spare - more
    return np.array([bound] + counts)


def ragged(rng, amount, total, bound, slope):
    if amount == 2:
        one = jax.random.randint(rng, (), max(1, total - bound), min(bound, total - 1) + 1)
        return jnp.stack([one, total - one])
    lengths = jnp.asarray(length_profile(amount, total, bound, slope), jnp.int32)
    twos = (amount - 1) // 2
    source_of, sink = lengths[1:1 + 2 * twos:2], lengths[2:2 + 2 * twos:2]
    margin = jnp.minimum(source_of - 1, bound - sink)
    moved = jax.random.randint(jax.random.fold_in(rng, 1), (twos,), 0, 1 << 20) % (margin + 1)
    lengths = lengths.at[1:1 + 2 * twos:2].set(source_of - moved).at[2:2 + 2 * twos:2].set(sink + moved)
    return lengths[jax.random.permutation(jax.random.fold_in(rng, 2), amount)]


def bell_draw(rng, shape, scale, reach, cuts=(), held_as=jnp.bfloat16):
    entries = jax.random.normal(rng, shape, jnp.float32) * scale
    if len(cuts) > 0:
        entries = steps_of(rng, shape, cuts, -0.22, 0.18) * entries
    return jnp.clip(entries, min=-reach, max=reach).astype(held_as)


def setup_inputs(seed: int = 0) -> dict:
    seeds = jax.random.split(jax.random.key(seed), 13)
    return {
        "inputs": bell_draw(seeds[0], (TOKENS, D), 1.0, 6.0, ((0, 32),)),
        "segment_ids": jax.vmap(lambda own: jnp.searchsorted(jnp.cumsum(ragged(own, SERIES, LEN, LEN // 2, 0)), jnp.arange(LEN), side="right"))(jax.random.split(seeds[1], ROWS)).reshape((ROWS, LEN)).astype(jnp.int32),
        "gain_attn": jnp.clip(1.0 + 0.18 * jax.random.normal(seeds[2], (D,), jnp.float32), 0.1, 1.9),
        "w_qkv": bell_draw(seeds[3], (D, 3 * D), D ** -0.5, 0.15625),
        "w_out": bell_draw(seeds[4], (D, D), (D // 32) ** -0.5, 1.0),
        "gain_mlp": jnp.clip(1.0 + 0.18 * jax.random.normal(seeds[5], (D,), jnp.float32), 0.1, 1.9),
        "w_up": bell_draw(seeds[6], (D, FF), D ** -0.5, 0.15625),
        "w_down": bell_draw(seeds[7], (FF, D), FF ** -0.5, 0.078125),
        "gain_final": jnp.clip(1.0 + 0.18 * jax.random.normal(seeds[8], (D,), jnp.float32), 0.1, 1.9),
        "head_projection_weight": bell_draw(seeds[9], (D, HQ), D ** -0.5, 0.15625, ((1, 2),)),
        "head_output_bias": bell_draw(seeds[10], (HQ,), 1.0, 5.0, ((0, 2),), jnp.float32),
        "cotangent": bell_draw(seeds[11], (TOKENS, HQ), 1.0, 6.0, ((0, 16), (1, 2))),
    }


@jax.custom_vjp
def low(v):
    return lax.optimization_barrier(v.astype(jnp.bfloat16)).astype(jnp.float32)

@jax.custom_vjp
def low_back(v):
    return v

def low_keep(v):
    return (low(v), None)

def low_pass(kept, grad):
    return (grad,)

def back_keep(v):
    return (v, None)

def back_low(kept, grad):
    return (low(grad),)
low.defvjp(low_keep, low_pass)
low_back.defvjp(back_keep, back_low)
epsilon = 1e-06

def matmul(left, right):
    return jnp.dot(left, right, precision=lax.Precision.HIGHEST)

def rms_norm(values, gain):
    return values * lax.rsqrt(lax.optimization_barrier(jnp.mean(values * values, axis=-1, keepdims=True)) + epsilon) * gain

def rotary_tables(sequence_span, hdim):
    half = hdim // 2
    freq = 10000.0 ** (-jnp.arange(half, dtype=jnp.float32) / half)
    angle = jnp.arange(sequence_span, dtype=jnp.float32)[:, None] * freq[None, :]
    return (jnp.cos(angle)[:, None, :], jnp.sin(angle)[:, None, :])

def rotate(values, cosine, sine):
    half = values.shape[-1] // 2
    first = values[..., :half]
    second = values[..., half:]
    return jnp.concatenate([first * cosine - second * sine, second * cosine + first * sine], axis=-1)

def allowed_mask(segs):
    place = jnp.arange(segs.shape[0])
    return (segs[:, None] == segs[None, :]) & (place[:, None] >= place[None, :])

def forward_group(params, tokens, segs):
    gain_attn, w_qkv, w_out, gain_mlp, w_up, w_down, gain_final, head_projection_weight, head_output_bias = params
    count, sequence_span = segs.shape
    width = tokens.shape[1]
    hdim = width // HEADS
    scale = 1.0 / math.sqrt(hdim)
    cosine, sine = rotary_tables(sequence_span, hdim)
    act_one = low(rms_norm(tokens, gain_attn))
    projected = low_back(matmul(act_one, w_qkv)).reshape(count, sequence_span, 3, HEADS, hdim)
    query = low(rotate(projected[:, :, 0], cosine, sine))
    key = low(rotate(projected[:, :, 1], cosine, sine))
    value = low(projected[:, :, 2])

    def attend(items):
        row_query, row_key, row_value, row_segs = items
        scores = low_back(jnp.einsum('qhd,khd->hqk', row_query, row_key, precision=lax.Precision.HIGHEST) * scale)
        scores = jnp.where(allowed_mask(row_segs)[None], scores, -1e+30)
        peak = lax.optimization_barrier(jnp.max(scores, axis=-1, keepdims=True))
        expo = jnp.exp(scores - peak)
        probs = low(expo / lax.optimization_barrier(jnp.sum(expo, axis=-1, keepdims=True)))
        return jnp.einsum('hqk,khd->qhd', probs, row_value, precision=lax.Precision.HIGHEST)
    attended = lax.map(jax.checkpoint(attend), (query, key, value, segs))
    mixed = low(low_back(attended.reshape(count * sequence_span, width)))
    resid_two = tokens + low_back(matmul(mixed, w_out))
    act_two = low(rms_norm(resid_two, gain_mlp))
    hidden_pre = low_back(matmul(act_two, w_up))
    hidden = low(jax.nn.silu(hidden_pre))
    resid_three = resid_two + low_back(matmul(hidden, w_down))
    final_hidden = low(rms_norm(resid_three, gain_final))
    return matmul(final_hidden, head_projection_weight) + head_output_bias

def reference(inputs, segment_ids, gain_attn, w_qkv, w_out, gain_mlp, w_up, w_down, gain_final, head_projection_weight, head_output_bias, cotangent):
    params = tuple((item.astype(jnp.float32) for item in (gain_attn, w_qkv, w_out, gain_mlp, w_up, w_down, gain_final, head_projection_weight, head_output_bias)))
    overall_number, sequence_span = segment_ids.shape
    width = inputs.shape[1]
    result_entries = cotangent.shape[1]
    group = math.gcd(overall_number, 8)
    blocks = overall_number // group
    tokens = inputs.astype(jnp.float32).reshape(blocks, group * sequence_span, width)
    segs = segment_ids.reshape(blocks, group, sequence_span)
    cot = cotangent.astype(jnp.float32).reshape(blocks, group * sequence_span, result_entries)

    def step(carry, items):
        block_tokens, block_segs, block_cot = items
        result, pull = jax.vjp(lambda p, v: forward_group(p, v, block_segs), params, block_tokens)
        grad_params, grad_tokens = pull(block_cot)
        carry = jax.tree.map(lambda a, b: a + b, carry, grad_params)
        return (carry, (result, grad_tokens))
    zeros = jax.tree.map(jnp.zeros_like, params)
    sums, joined_entries = lax.scan(step, zeros, (tokens, segs, cot))
    predicted_levels = joined_entries[0].reshape(overall_number * sequence_span, result_entries)
    entry_sensitivity_matrix = joined_entries[1].reshape(overall_number * sequence_span, width)
    mixer_sensitivity, triple_matrix_sensitivity, merge_matrix_sensitivity, perceptron_sensitivity, expansion_matrix_sensitivity, contraction_matrix_sensitivity, closing_scale_sensitivity, readout_matrix_sensitivity, offset_sensitivity = sums
    return (predicted_levels, entry_sensitivity_matrix, mixer_sensitivity, triple_matrix_sensitivity, merge_matrix_sensitivity, perceptron_sensitivity, expansion_matrix_sensitivity, contraction_matrix_sensitivity, closing_scale_sensitivity, readout_matrix_sensitivity, offset_sensitivity)
```

```python
import math

import jax
import jax.numpy as jnp
from jax import lax
from jax.sharding import PartitionSpec as P

HEADS = 16
F32 = jnp.float32
BF16 = jnp.bfloat16

epsilon = 1e-06


def rms_forward(values, gain):
    inverse = lax.rsqrt(jnp.mean(values * values, axis=-1, keepdims=True) + epsilon)
    return (values * inverse * gain, inverse)


def rms_backward(values, inverse, gain, grad):
    normed = values * inverse
    scaled = grad * gain
    grad_gain = jnp.sum(grad * normed, axis=0)
    grad_values = inverse * (scaled - normed * jnp.mean(scaled * normed, axis=-1, keepdims=True))
    return (grad_values, grad_gain)


def rotary_tables(sequence_span, hdim):
    half = hdim // 2
    freq = 10000.0 ** (-jnp.arange(half, dtype=jnp.float32) / half)
    angle = jnp.arange(sequence_span, dtype=jnp.float32)[:, None] * freq[None, :]
    return (jnp.cos(angle)[:, None, :], jnp.sin(angle)[:, None, :])


def rotate(values, cosine, sine):
    half = values.shape[-1] // 2
    first = values[..., :half]
    second = values[..., half:]
    return jnp.concatenate(
        [first * cosine - second * sine, second * cosine + first * sine], axis=-1
    )


def unrotate(grads, cosine, sine):
    half = grads.shape[-1] // 2
    first = grads[..., :half]
    second = grads[..., half:]
    return jnp.concatenate(
        [first * cosine + second * sine, second * cosine - first * sine], axis=-1
    )


def allowed_mask(segs):
    place = jnp.arange(segs.shape[0])
    return (segs[:, None] == segs[None, :]) & (place[:, None] >= place[None, :])


def row_scores(query, key, segs, scale):
    scores = jnp.einsum("qhd,khd->hqk", query, key, preferred_element_type=jnp.float32) * scale
    allowed = allowed_mask(segs)[None]
    return (jnp.where(allowed, scores, -1e30), allowed)


def attend_forward(items, scale):
    query, key, value, segs = items
    scores, allowed = row_scores(query, key, segs, scale)
    peak = jnp.max(scores, axis=-1, keepdims=True)
    expo = jnp.exp(scores - peak)
    overall_number = jnp.sum(expo, axis=-1, keepdims=True)
    probs = (expo / overall_number).astype(jnp.bfloat16)
    attended = jnp.einsum("hqk,khd->qhd", probs, value, preferred_element_type=jnp.float32)
    return (attended.astype(jnp.bfloat16), peak + jnp.log(overall_number))


def attend_backward(items, scale):
    query, key, value, segs, log_total, grad_attended = items
    scores, allowed = row_scores(query, key, segs, scale)
    probs = jnp.where(allowed, jnp.exp(scores - log_total), 0.0)
    grad_value = jnp.einsum(
        "hqk,qhd->khd",
        probs.astype(jnp.bfloat16),
        grad_attended,
        preferred_element_type=jnp.float32,
    )
    grad_probs = jnp.einsum(
        "qhd,khd->hqk", grad_attended, value, preferred_element_type=jnp.float32
    )
    grad_scores = (
        probs * (grad_probs - jnp.sum(grad_probs * probs, axis=-1, keepdims=True))
    ).astype(jnp.bfloat16)
    grad_query = (
        jnp.einsum("hqk,khd->qhd", grad_scores, key, preferred_element_type=jnp.float32) * scale
    )
    grad_key = (
        jnp.einsum("hqk,qhd->khd", grad_scores, query, preferred_element_type=jnp.float32) * scale
    )
    return (grad_query, grad_key, grad_value)


def contract_rows(left, right):
    return lax.dot_general(
        left, right, (((0,), (0,)), ((), ())), preferred_element_type=jnp.float32
    )


def contract_cols(left, right):
    return lax.dot_general(
        left, right, (((1,), (1,)), ((), ())), preferred_element_type=jnp.float32
    )


def swap_cores(values):
    return lax.ppermute(values, "head", [(0, 1), (1, 0)])


def flip(values, bit):
    size = lax.axis_size("dp")
    return lax.ppermute(values, "dp", [(i, i ^ bit) for i in range(size)])


def sum_everywhere(values, over_head):
    size = lax.axis_size("dp")
    if over_head:
        values = values + swap_cores(values)
    bit = 1
    while bit < size:
        values = values + flip(values, bit)
        bit *= 2
    return values


def exchange(values, axis, place, bit):
    kept = lax.dynamic_index_in_dim(values, place, axis, keepdims=False)
    sent = lax.dynamic_index_in_dim(values, 1 - place, axis, keepdims=False)
    return kept.astype(F32) + flip(sent.astype(BF16), bit).astype(F32)


def line(values, place, stride):
    length = values.shape[0]
    size = lax.axis_size("dp")

    def block(index):
        return lax.dynamic_index_in_dim(
            values, jnp.clip(index, 0, length - 1), 0, keepdims=False
        ).astype(F32)

    up = down = None
    for step in range(1, length):
        gap = length - step
        send_up, send_down = block(place + gap), block(place - gap)
        if up is not None:
            send_up, send_down = send_up + up.astype(F32), send_down + down.astype(F32)
        rises = [(i, i + stride) for i in range(size) if i // stride < step]
        falls = [(i, i - stride) for i in range(size) if i // stride >= length - step]
        up = lax.ppermute(send_up.astype(BF16), "dp", rises)
        down = lax.ppermute(send_down.astype(BF16), "dp", falls)
    total = block(place)
    if up is not None:
        total = total + up.astype(F32) + down.astype(F32)
    return total


def reduce_rows(values):
    size = lax.axis_size("dp")
    place = lax.axis_index("dp")
    xi, yi, zi = place & 1, (place >> 1) & 1, place >> 2
    rows, columns = values.shape
    length, block = size // 4, rows // size
    view = values.reshape(length, 2, 2, block, columns)
    half = columns // 2
    first, second = view[..., :half], view[..., half:]
    first = exchange(first, 2, xi, 1).astype(BF16)
    second = exchange(second, 1, yi, 2).astype(BF16)
    first = exchange(first, 1, yi, 2).astype(BF16)
    second = exchange(second, 1, xi, 1).astype(BF16)
    return jnp.concatenate([line(first, zi, 4), line(second, zi, 4)], axis=1)


def finish(values):
    core = lax.axis_index("head")
    half = values.shape[0] // 2
    kept = lax.dynamic_slice_in_dim(values, core * half, half, 0)
    sent = lax.dynamic_slice_in_dim(values, (1 - core) * half, half, 0)
    got = swap_cores(sent)
    return jnp.concatenate(
        [jnp.where(core == 0, kept, got), jnp.where(core == 0, got, kept)], axis=1
    )


def half_columns(values, core):
    half = values.shape[1] // 2
    return lax.dynamic_slice_in_dim(values, core * half, half, 1)


def split_halves(values):
    core = lax.axis_index("head")
    kept = half_columns(values, core)
    got = swap_cores(half_columns(values, 1 - core))
    return jnp.concatenate([kept, got], axis=0)


def both(values):
    return jnp.concatenate([values, swap_cores(values)], axis=0)


def per_device(
    inputs,
    segment_ids,
    gain_attn,
    w_qkv,
    w_out,
    gain_mlp,
    w_up,
    w_down,
    gain_final,
    head_projection_weight,
    head_output_bias,
    cotangent,
):
    core = lax.axis_index("head")
    place = lax.axis_index("dp")
    rows, sequence_span = segment_ids.shape
    count, width = inputs.shape
    hdim = width // HEADS
    scale = 1.0 / math.sqrt(hdim)

    other_rows = lax.dynamic_slice_in_dim(cotangent, (1 - core) * count, count, 0)
    own_rows = lax.dynamic_slice_in_dim(cotangent, core * count, count, 0)
    got = swap_cores(contract_cols(other_rows, head_projection_weight).astype(BF16))
    grad_final = contract_cols(own_rows, head_projection_weight) + got.astype(F32)
    grad_bias = sum_everywhere(jnp.sum(cotangent, axis=0, dtype=F32), False)

    cosine, sine = rotary_tables(sequence_span, hdim)
    tokens = inputs.astype(jnp.float32)
    normed_one, inverse_one = rms_forward(tokens, gain_attn)
    act_one = normed_one.astype(jnp.bfloat16)
    both_one = both(act_one)
    projected = jnp.dot(act_one, w_qkv, preferred_element_type=jnp.float32).reshape(
        rows, sequence_span, 3, HEADS, hdim
    )
    query = rotate(projected[:, :, 0], cosine, sine).astype(jnp.bfloat16)
    key = rotate(projected[:, :, 1], cosine, sine).astype(jnp.bfloat16)
    value = projected[:, :, 2].astype(jnp.bfloat16)
    attended, log_total = lax.map(
        lambda items: attend_forward(items, scale), (query, key, value, segment_ids)
    )
    mixed = attended.reshape(rows * sequence_span, width)
    both_mixed = both(mixed)
    resid_two = tokens + jnp.dot(mixed, w_out, preferred_element_type=jnp.float32)
    normed_two, inverse_two = rms_forward(resid_two, gain_mlp)
    act_two = normed_two.astype(jnp.bfloat16)
    both_two = both(act_two)
    hidden_pre = jnp.dot(act_two, w_up, preferred_element_type=jnp.float32)
    hidden = jax.nn.silu(hidden_pre).astype(jnp.bfloat16)
    both_hidden = both(hidden)
    resid_three = resid_two + jnp.dot(hidden, w_down, preferred_element_type=jnp.float32)
    normed_three, inverse_three = rms_forward(resid_three, gain_final)
    final_hidden = normed_three.astype(jnp.bfloat16)
    other_hidden = swap_cores(final_hidden)
    collected_rows = jnp.concatenate(
        [
            jnp.where(core == 0, final_hidden, other_hidden),
            jnp.where(core == 0, other_hidden, final_hidden),
        ],
        axis=0,
    )
    predicted_levels = (
        jnp.dot(collected_rows, head_projection_weight, preferred_element_type=jnp.float32)
        + head_output_bias
    )
    grad_head = reduce_rows(contract_rows(collected_rows, cotangent).astype(BF16))
    grad_three, grad_gain_final = rms_backward(resid_three, inverse_three, gain_final, grad_final)
    grad_mlp_out = grad_three.astype(jnp.bfloat16)
    grad_down = finish(
        reduce_rows(contract_rows(both_hidden, split_halves(grad_mlp_out)).astype(BF16))
    )
    grad_hidden = contract_cols(grad_mlp_out, w_down)
    sigmoid = jax.nn.sigmoid(hidden_pre)
    grad_pre = (grad_hidden * sigmoid * (1.0 + hidden_pre * (1.0 - sigmoid))).astype(jnp.bfloat16)
    grad_up = finish(reduce_rows(contract_rows(both_two, split_halves(grad_pre)).astype(BF16)))
    grad_norm_two, grad_gain_mlp = rms_backward(
        resid_two, inverse_two, gain_mlp, contract_cols(grad_pre, w_up)
    )
    grad_two = grad_three + grad_norm_two
    grad_branch = grad_two.astype(jnp.bfloat16)
    grad_out = finish(
        reduce_rows(contract_rows(both_mixed, split_halves(grad_branch)).astype(BF16))
    )
    grad_mixed = (
        contract_cols(grad_branch, w_out)
        .astype(jnp.bfloat16)
        .reshape(rows, sequence_span, HEADS, hdim)
    )
    grad_query, grad_key, grad_value = lax.map(
        lambda items: attend_backward(items, scale),
        (query, key, value, segment_ids, log_total, grad_mixed),
    )
    grad_query = unrotate(grad_query, cosine, sine)
    grad_key = unrotate(grad_key, cosine, sine)
    grad_proj = (
        jnp.stack([grad_query, grad_key, grad_value], axis=2)
        .reshape(rows * sequence_span, 3 * width)
        .astype(jnp.bfloat16)
    )
    grad_qkv = finish(reduce_rows(contract_rows(both_one, split_halves(grad_proj)).astype(BF16)))
    grad_norm_one, grad_gain_attn = rms_backward(
        tokens, inverse_one, gain_attn, contract_cols(grad_proj, w_qkv)
    )
    entry_sensitivity_matrix = grad_two + grad_norm_one
    gains = sum_everywhere(jnp.stack([grad_gain_attn, grad_gain_mlp, grad_gain_final]), True)
    share = width // (2 * lax.axis_size("dp"))
    gains = lax.dynamic_slice_in_dim(gains, (place * 2 + core) * share, share, 1)
    return (
        predicted_levels,
        entry_sensitivity_matrix,
        gains[0],
        grad_qkv,
        grad_out,
        gains[1],
        grad_up,
        grad_down,
        gains[2],
        grad_head,
        grad_bias,
    )


def solution(mesh):
    return jax.shard_map(
        per_device,
        mesh=mesh,
        in_specs=(
            P(("dp", "head"), None),
            P(("dp", "head"), None),
            P(),
            P(),
            P(),
            P(),
            P(),
            P(),
            P(),
            P(None, "head"),
            P("head"),
            P("dp", "head"),
        ),
        out_specs=(
            P("dp", "head"),
            P(("dp", "head"), None),
            P(("dp", "head")),
            P(("dp", "head"), None),
            P(("dp", "head"), None),
            P(("dp", "head")),
            P(("dp", "head"), None),
            P(("dp", "head"), None),
            P(("dp", "head")),
            P("dp", "head"),
            P("head"),
        ),
        check_vma=False,
    )
```

```python
import functools
import math

import jax
import jax.numpy as jnp
from jax import lax
from jax.experimental import pallas as pl
from jax.experimental.pallas import tpu as pltpu
from jax.sharding import PartitionSpec as P

HEADS = 16
F32 = jnp.float32
BF16 = jnp.bfloat16

epsilon = 1e-06


def rms_forward(values, gain):
    inverse = lax.rsqrt(jnp.mean(values * values, axis=-1, keepdims=True) + epsilon)
    return (values * inverse * gain, inverse)


def rms_backward(values, inverse, gain, grad):
    normed = values * inverse
    scaled = grad * gain
    grad_gain = jnp.sum(grad * normed, axis=0)
    grad_values = inverse * (scaled - normed * jnp.mean(scaled * normed, axis=-1, keepdims=True))
    return (grad_values, grad_gain)


def rotary_tables(sequence_span, hdim):
    half = hdim // 2
    freq = 10000.0 ** (-jnp.arange(half, dtype=jnp.float32) / half)
    angle = jnp.arange(sequence_span, dtype=jnp.float32)[:, None] * freq[None, :]
    return (jnp.cos(angle)[:, None, :], jnp.sin(angle)[:, None, :])


def rotate(values, cosine, sine):
    half = values.shape[-1] // 2
    first = values[..., :half]
    second = values[..., half:]
    return jnp.concatenate(
        [first * cosine - second * sine, second * cosine + first * sine], axis=-1
    )


def unrotate(grads, cosine, sine):
    half = grads.shape[-1] // 2
    first = grads[..., :half]
    second = grads[..., half:]
    return jnp.concatenate(
        [first * cosine + second * sine, second * cosine - first * sine], axis=-1
    )


def allowed_mask(segs):
    place = jnp.arange(segs.shape[0])
    return (segs[:, None] == segs[None, :]) & (place[:, None] >= place[None, :])


def row_scores(query, key, segs, scale):
    scores = jnp.einsum("qhd,khd->hqk", query, key, preferred_element_type=jnp.float32) * scale
    allowed = allowed_mask(segs)[None]
    return (jnp.where(allowed, scores, -1e30), allowed)


def attend_forward(items, scale):
    query, key, value, segs = items
    scores, allowed = row_scores(query, key, segs, scale)
    peak = jnp.max(scores, axis=-1, keepdims=True)
    expo = jnp.exp(scores - peak)
    overall_number = jnp.sum(expo, axis=-1, keepdims=True)
    probs = (expo / overall_number).astype(jnp.bfloat16)
    attended = jnp.einsum("hqk,khd->qhd", probs, value, preferred_element_type=jnp.float32)
    return (attended.astype(jnp.bfloat16), peak + jnp.log(overall_number))


def attend_backward(items, scale):
    query, key, value, segs, log_total, grad_attended = items
    scores, allowed = row_scores(query, key, segs, scale)
    probs = jnp.where(allowed, jnp.exp(scores - log_total), 0.0)
    grad_value = jnp.einsum(
        "hqk,qhd->khd",
        probs.astype(jnp.bfloat16),
        grad_attended,
        preferred_element_type=jnp.float32,
    )
    grad_probs = jnp.einsum(
        "qhd,khd->hqk", grad_attended, value, preferred_element_type=jnp.float32
    )
    grad_scores = (
        probs * (grad_probs - jnp.sum(grad_probs * probs, axis=-1, keepdims=True))
    ).astype(jnp.bfloat16)
    grad_query = (
        jnp.einsum("hqk,khd->qhd", grad_scores, key, preferred_element_type=jnp.float32) * scale
    )
    grad_key = (
        jnp.einsum("hqk,qhd->khd", grad_scores, query, preferred_element_type=jnp.float32) * scale
    )
    return (grad_query, grad_key, grad_value)


def contract_rows(left, right):
    return lax.dot_general(
        left, right, (((0,), (0,)), ((), ())), preferred_element_type=jnp.float32
    )


def contract_cols(left, right):
    return lax.dot_general(
        left, right, (((1,), (1,)), ((), ())), preferred_element_type=jnp.float32
    )


def swap_cores(values):
    return lax.ppermute(values, "head", [(0, 1), (1, 0)])


def flip(values, bit):
    size = lax.axis_size("dp")
    return lax.ppermute(values, "dp", [(i, i ^ bit) for i in range(size)])


def scatter_rows(left, right):
    return lax.psum_scatter(
        contract_rows(left, right), ("dp", "head"), scatter_dimension=0, tiled=True
    )


def sum_everywhere(values, over_head):
    size = lax.axis_size("dp")
    if over_head:
        values = values + swap_cores(values)
    bit = 1
    while bit < size:
        values = values + flip(values, bit)
        bit *= 2
    return values


MESH = pl.DeviceIdType.MESH


def chunk_table(width, hidden):
    half = width // 2
    table = [(0, 0)]
    table += [(1, j) for j in range(hidden // width)]
    table += [(2, j) for j in range(hidden // width)]
    table += [(3, 0)]
    table += [(4, j) for j in range(3)]
    return table, half


def gradient_kernel(
    table,
    size,
    block,
    cols,
    y_t,
    g_t,
    a2_t,
    o_t,
    a1_t,
    cot,
    e3,
    eh,
    e2,
    ep,
    small,
    out_head,
    out_down,
    out_up,
    out_out,
    out_qkv,
    out_small,
    y_o,
    g_o,
    a2_o,
    o_o,
    a1_o,
    e3_o,
    eh_o,
    e2_o,
    ep_o,
    lbuf,
    rbuf,
    grad,
    recv1,
    pair,
    recv2,
    line,
    recv_up,
    recv_down,
    total,
    sums,
    sums_in,
    push_send,
    push_recv,
    load_sem,
    send1_sem,
    recv1_sem,
    send2_sem,
    recv2_sem,
    up_send,
    up_recv,
    down_send,
    down_recv,
    local_sem,
    swap_send,
    swap_recv,
    small_send,
    small_recv,
):
    n = len(table)
    length = size // 4
    me = lax.axis_index("dp")
    core = lax.axis_index("head")
    xi = lax.rem(me, 2)
    yi = lax.rem(me // 2, 2)
    zi = me // 4
    tokens = e3.shape[0]
    flip_x = me + 1 - 2 * xi
    flip_y = me + 2 * (1 - 2 * yi)
    first_bit = jnp.where(core == 0, xi, yi)
    second_bit = jnp.where(core == 0, yi, xi)
    first_peer = jnp.where(core == 0, flip_x, flip_y)
    second_peer = jnp.where(core == 0, flip_y, flip_x)
    other = 1 - core
    far = lax.rem(me + size // 2, size)
    zbit = lax.rem(zi, 2)
    near = me + 4 * (1 - 2 * zbit)

    barrier = pltpu.get_barrier_semaphore()
    for index, which in ((me, other), (flip_x, core), (flip_y, core), (far, core)):
        pl.semaphore_signal(barrier, inc=1, device_id=(index, which), device_id_type=MESH)

    @pl.when(zi > 0)
    def _():
        pl.semaphore_signal(barrier, inc=1, device_id=(me - 4, core), device_id_type=MESH)

    @pl.when(zi < length - 1)
    def _():
        pl.semaphore_signal(barrier, inc=1, device_id=(me + 4, core), device_id_type=MESH)

    inner = jnp.where(zi > 0, 1, 0) + jnp.where(zi < length - 1, 1, 0)
    pl.semaphore_wait(barrier, 4 + inner)

    def remote(src, dst, send, recv, index, which):
        return pltpu.make_async_remote_copy(
            src_ref=src,
            dst_ref=dst,
            send_sem=send,
            recv_sem=recv,
            device_id=(index, which),
            device_id_type=MESH,
        )

    lefts = (y_t, g_t, a2_t, o_t, a1_t)
    left_others = (y_o, g_o, a2_o, o_o, a1_o)
    rights = (cot, e3, eh, e2, ep)
    right_others = (None, e3_o, eh_o, e2_o, ep_o)

    def push_left(i):
        return remote(
            lefts[i], left_others[i], push_send.at[i], push_recv.at[i], me, other
        )

    def push_right(i):
        wide = rights[i].shape[1] // 2
        start = pl.multiple_of(other * wide, 128)
        return remote(
            rights[i].at[:, pl.ds(start, wide)],
            right_others[i],
            push_send.at[4 + i],
            push_recv.at[4 + i],
            me,
            other,
        )

    for i in range(5):
        if i > 0:
            push_right(i).start()
        push_left(i).start()

    def loads(i, j, slot):
        lower = pl.ds(j * block, block) if i == 1 else slice(None)
        copies = []
        for half, source in ((0, lefts[i]), (1, left_others[i])):
            copies.append((source.at[:, lower, :], lbuf.at[slot, half], load_sem.at[slot, half]))
        if i == 0:
            mine = pl.multiple_of(core * tokens, 16)
            its = pl.multiple_of(other * tokens, 16)
            copies.append((cot.at[pl.ds(mine, tokens)], rbuf.at[slot, 0], load_sem.at[slot, 2]))
            copies.append((cot.at[pl.ds(its, tokens)], rbuf.at[slot, 1], load_sem.at[slot, 3]))
        else:
            wide = rights[i].shape[1] // 2
            shift = 0 if i == 1 else j * cols
            start = pl.multiple_of(core * wide + shift, 128)
            copies.append(
                (rights[i].at[:, pl.ds(start, cols)], rbuf.at[slot, 0], load_sem.at[slot, 2])
            )
            copies.append(
                (
                    right_others[i].at[:, pl.ds(shift, cols)],
                    rbuf.at[slot, 1],
                    load_sem.at[slot, 3],
                )
            )
        return copies

    def start_load(c, slot):
        i, j = table[c]
        if j == 0:
            push_left(i).wait_recv()
            if i > 0:
                push_right(i).wait_recv()
        for copy in loads(i, j, slot):
            pltpu.make_async_copy(*copy).start()

    start_load(0, 0)
    start_load(1, 1)

    peers = ((me, other), (flip_x, core), (flip_y, core), (near, core), (far, core))
    steps = len(peers)

    def small_copy(i):
        return remote(
            sums.at[i], sums_in.at[i], small_send.at[i], small_recv.at[i], peers[i][0], peers[i][1]
        )

    sums[0] = small[...]
    small_copy(0).start()

    def send1(slot, c):
        return remote(
            grad.at[slot, 1 - first_bit],
            recv1.at[c],
            send1_sem.at[slot],
            recv1_sem.at[c],
            first_peer,
            core,
        )

    def send2(slot, c):
        return remote(
            pair.at[slot, 1 - second_bit],
            recv2.at[c],
            send2_sem.at[slot],
            recv2_sem.at[c],
            second_peer,
            core,
        )

    def send_up(slot, c, step):
        return remote(
            line.at[slot, jnp.minimum(zi + (length - step), length - 1)],
            recv_up.at[c, step - 1],
            up_send.at[slot, step - 1],
            up_recv.at[c, step - 1],
            jnp.minimum(me + 4, size - 1),
            core,
        )

    def send_down(slot, c, step):
        return remote(
            line.at[slot, jnp.maximum(zi - (length - step), 0)],
            recv_down.at[c, step - 1],
            down_send.at[slot, step - 1],
            down_recv.at[c, step - 1],
            jnp.maximum(me - 4, 0),
            core,
        )

    def start_line(slot, c, step):
        @pl.when(zi < step)
        def _():
            send_up(slot, c, step).start()

        @pl.when(zi >= length - step)
        def _():
            send_down(slot, c, step).start()

    def wait_line_sent(slot, c, step):
        @pl.when(zi < step)
        def _():
            send_up(slot, c, step).wait_send()

        @pl.when(zi >= length - step)
        def _():
            send_down(slot, c, step).wait_send()

    def results(c):
        i, j = table[c]
        if i == 0:
            return [(None, pltpu.make_async_copy(total.at[c], out_head, local_sem.at[c]))]
        if i == 1:
            owner = j // 2
            target = out_down.at[
                pl.ds((j % 2) * block, block), pl.ds(pl.multiple_of(core * cols, 128), cols)
            ]
            return [
                (core == owner, pltpu.make_async_copy(total.at[c], target, local_sem.at[c])),
                (
                    core != owner,
                    remote(total.at[c], target, swap_send.at[c], swap_recv.at[c], me, other),
                ),
            ]
        target = (None, None, out_up, out_out, out_qkv)[i]
        wide = target.shape[1] // 2
        place = target.at[:, pl.ds(pl.multiple_of(core * wide + j * cols, 128), cols)]
        half = block // 2
        mine = pl.ds(pl.multiple_of(core * half, 8), half)
        its = pl.ds(pl.multiple_of(other * half, 8), half)
        return [
            (None, pltpu.make_async_copy(total.at[c, mine], place, local_sem.at[c])),
            (None, remote(total.at[c, its], place, swap_send.at[c], swap_recv.at[c], me, other)),
        ]

    def guarded(condition, action):
        if condition is None:
            action()
        else:
            pl.when(condition)(action)

    @pl.loop(0, n + 2 + length)
    def _(t):
        slot = lax.rem(t, 2)

        @pl.when(t < n)
        def _():
            @pl.when(t >= 2)
            def _():
                send1(slot, t - 2).wait_send()

            for half in range(2):
                pltpu.make_async_copy(
                    lbuf.at[slot, half], lbuf.at[slot, half], load_sem.at[slot, half]
                ).wait()
                pltpu.make_async_copy(
                    rbuf.at[slot, half], rbuf.at[slot, half], load_sem.at[slot, 2 + half]
                ).wait()

            @pl.loop(0, length)
            def _(z):
                rows = pl.ds(z * 4, 4)
                value = None
                for half in range(2):
                    left = lbuf[slot, half, rows].reshape(4 * block, tokens)
                    part = jnp.dot(left, rbuf[slot, half], preferred_element_type=F32)
                    value = part if value is None else value + part
                value = value.astype(BF16)
                for q in range(4):
                    x, y = q % 2, q // 2
                    one = jnp.where(core == 0, x, y)
                    two = jnp.where(core == 0, y, x)
                    grad[slot, one, two, z] = value[q * block : (q + 1) * block]

            send1(slot, t).start()

            for c in range(2, n):

                @pl.when(t == c - 2)
                def _():
                    start_load(c, c % 2)

        @pl.when((t >= 1) & (t <= n))
        def _():
            c = t - 1
            spot = lax.rem(c, 2)
            send1(spot, c).wait_recv()

            @pl.when(c >= 2)
            def _():
                send2(spot, c - 2).wait_send()

            for two in range(2):

                @pl.loop(0, length)
                def _(z):
                    pair[spot, two, z] = (
                        grad[spot, first_bit, two, z].astype(F32) + recv1[c, two, z].astype(F32)
                    ).astype(BF16)

            send2(spot, c).start()

        @pl.when((t >= 2) & (t <= n + 1))
        def _():
            c = t - 2
            spot = lax.rem(c, 2)
            ring = lax.rem(c, length + 1)
            send2(spot, c).wait_recv()

            @pl.loop(0, length)
            def _(z):
                line[ring, z] = (
                    pair[spot, second_bit, z].astype(F32) + recv2[c, z].astype(F32)
                ).astype(BF16)

            start_line(ring, c, 1)

        for step in range(1, length):

            @pl.when((t >= 2 + step) & (t <= n + 1 + step))
            def _():
                c = t - 2 - step
                ring = lax.rem(c, length + 1)
                last = step == length - 1

                up_in = (zi >= 1) & (zi <= step)
                down_in = (zi <= length - 2) & (zi >= length - 1 - step)

                @pl.when(up_in)
                def _():
                    send_up(ring, c, step).wait_recv()
                    spot = jnp.minimum(zi + (length - 1 - step), length - 1)
                    if not last:
                        line[ring, spot] = (
                            line[ring, spot].astype(F32) + recv_up[c, step - 1].astype(F32)
                        ).astype(BF16)

                @pl.when(down_in)
                def _():
                    send_down(ring, c, step).wait_recv()
                    spot = jnp.maximum(zi - (length - 1 - step), 0)
                    if not last:
                        line[ring, spot] = (
                            line[ring, spot].astype(F32) + recv_down[c, step - 1].astype(F32)
                        ).astype(BF16)

                if not last:
                    start_line(ring, c, step + 1)
                else:
                    total[c] = line[ring, zi].astype(F32)

                    @pl.when(up_in)
                    def _():
                        total[c] = total[c] + recv_up[c, step - 1].astype(F32)

                    @pl.when(down_in)
                    def _():
                        total[c] = total[c] + recv_down[c, step - 1].astype(F32)

                    for back in range(1, length):
                        wait_line_sent(ring, c, back)

                    for d in range(n):

                        @pl.when(c == d)
                        def _():
                            for condition, copy in results(d):
                                guarded(condition, copy.start)

        for i in range(steps):

            @pl.when(t == i + 1)
            def _():
                small_copy(i).wait()
                value = sums[i] + sums_in[i]
                if i == steps - 1:
                    out_small[...] = value
                else:
                    sums[i + 1] = value
                    small_copy(i + 1).start()

    for c in range(n):
        i, j = table[c]
        copies = results(c)
        if i == 0:
            copies[0][1].wait()
        elif i == 1:
            (here, local), (away, sent) = copies
            guarded(here, local.wait)
            guarded(away, sent.wait_send)
            guarded(here, sent.wait_recv)
        else:
            copies[0][1].wait()
            copies[1][1].wait()
    for slot in ((n - 2) % 2, (n - 1) % 2):
        send1(slot, 0).wait_send()
        send2(slot, 0).wait_send()
    for i in range(5):
        push_left(i).wait_send()
        if i > 0:
            push_right(i).wait_send()


def reduce_gradients(lefts, rights, small):
    size = lax.axis_size("dp")
    width, tokens = lefts[0].shape
    hidden = lefts[1].shape[0]
    block = width // size
    table, cols = chunk_table(width, hidden)
    n = len(table)
    length = size // 4
    share = block // 2
    hbm = pl.BlockSpec(memory_space=pl.ANY)
    vmem = pl.BlockSpec(memory_space=pltpu.VMEM)
    lefts = [left.reshape(size, left.shape[0] // size, tokens) for left in lefts]
    shapes = [
        jax.ShapeDtypeStruct((block, cols), F32),
        jax.ShapeDtypeStruct((hidden // size // 2, width), F32),
        jax.ShapeDtypeStruct((share, hidden), F32),
        jax.ShapeDtypeStruct((share, width), F32),
        jax.ShapeDtypeStruct((share, 3 * width), F32),
        jax.ShapeDtypeStruct(small.shape, F32),
    ]
    shapes += [jax.ShapeDtypeStruct(left.shape, BF16) for left in lefts]
    shapes += [
        jax.ShapeDtypeStruct((tokens, right.shape[1] // 2), BF16) for right in rights[1:]
    ]
    dma = pltpu.SemaphoreType.DMA
    results = pl.pallas_call(
        functools.partial(gradient_kernel, table, size, block, cols),
        out_shape=shapes,
        in_specs=[hbm] * 10 + [vmem],
        out_specs=[hbm] * 5 + [vmem] + [hbm] * 9,
        scratch_shapes=[
            pltpu.VMEM((2, 2, size, block, tokens), BF16),
            pltpu.VMEM((2, 2, tokens, cols), BF16),
            pltpu.VMEM((2, 2, 2, length, block, cols), BF16),
            pltpu.VMEM((n, 2, length, block, cols), BF16),
            pltpu.VMEM((2, 2, length, block, cols), BF16),
            pltpu.VMEM((n, length, block, cols), BF16),
            pltpu.VMEM((length + 1, length, block, cols), BF16),
            pltpu.VMEM((n, length - 1, block, cols), BF16),
            pltpu.VMEM((n, length - 1, block, cols), BF16),
            pltpu.VMEM((n, block, cols), F32),
            pltpu.VMEM((5,) + small.shape, F32),
            pltpu.VMEM((5,) + small.shape, F32),
            dma((9,)),
            dma((9,)),
            dma((2, 4)),
            dma((2,)),
            dma((n,)),
            dma((2,)),
            dma((n,)),
            dma((length + 1, length - 1)),
            dma((n, length - 1)),
            dma((length + 1, length - 1)),
            dma((n, length - 1)),
            dma((n,)),
            dma((n,)),
            dma((n,)),
            dma((5,)),
            dma((5,)),
        ],
        compiler_params=pltpu.CompilerParams(
            collective_id=0, has_side_effects=True, vmem_limit_bytes=60 << 20
        ),
        name="gradients",
    )(*lefts, *rights, small)
    return results[:6]


def per_device(
    inputs,
    segment_ids,
    gain_attn,
    w_qkv,
    w_out,
    gain_mlp,
    w_up,
    w_down,
    gain_final,
    head_projection_weight,
    head_output_bias,
    cotangent,
):
    core = lax.axis_index("head")
    place = lax.axis_index("dp")
    rows, sequence_span = segment_ids.shape
    count, width = inputs.shape
    hdim = width // HEADS
    scale = 1.0 / math.sqrt(hdim)

    other_rows = lax.dynamic_slice_in_dim(cotangent, (1 - core) * count, count, 0)
    own_rows = lax.dynamic_slice_in_dim(cotangent, core * count, count, 0)
    got = swap_cores(contract_cols(other_rows, head_projection_weight).astype(BF16))
    grad_final = contract_cols(own_rows, head_projection_weight) + got.astype(F32)
    bias_local = jnp.sum(cotangent, axis=0, dtype=F32)

    cosine, sine = rotary_tables(sequence_span, hdim)
    tokens = inputs.astype(jnp.float32)
    normed_one, inverse_one = rms_forward(tokens, gain_attn)
    act_one = normed_one.astype(jnp.bfloat16)
    projected = jnp.dot(act_one, w_qkv, preferred_element_type=jnp.float32).reshape(
        rows, sequence_span, 3, HEADS, hdim
    )
    query = rotate(projected[:, :, 0], cosine, sine).astype(jnp.bfloat16)
    key = rotate(projected[:, :, 1], cosine, sine).astype(jnp.bfloat16)
    value = projected[:, :, 2].astype(jnp.bfloat16)
    attended, log_total = lax.map(
        lambda items: attend_forward(items, scale), (query, key, value, segment_ids)
    )
    mixed = attended.reshape(rows * sequence_span, width)
    resid_two = tokens + jnp.dot(mixed, w_out, preferred_element_type=jnp.float32)
    normed_two, inverse_two = rms_forward(resid_two, gain_mlp)
    act_two = normed_two.astype(jnp.bfloat16)
    hidden_pre = jnp.dot(act_two, w_up, preferred_element_type=jnp.float32)
    hidden = jax.nn.silu(hidden_pre).astype(jnp.bfloat16)
    resid_three = resid_two + jnp.dot(hidden, w_down, preferred_element_type=jnp.float32)
    normed_three, inverse_three = rms_forward(resid_three, gain_final)
    final_hidden = normed_three.astype(jnp.bfloat16)
    other_hidden = swap_cores(final_hidden)
    collected_rows = jnp.concatenate(
        [
            jnp.where(core == 0, final_hidden, other_hidden),
            jnp.where(core == 0, other_hidden, final_hidden),
        ],
        axis=0,
    )
    predicted_levels = (
        jnp.dot(collected_rows, head_projection_weight, preferred_element_type=jnp.float32)
        + head_output_bias
    )
    grad_three, grad_gain_final = rms_backward(resid_three, inverse_three, gain_final, grad_final)
    grad_mlp_out = grad_three.astype(jnp.bfloat16)
    grad_hidden = contract_cols(grad_mlp_out, w_down)
    sigmoid = jax.nn.sigmoid(hidden_pre)
    grad_pre = (grad_hidden * sigmoid * (1.0 + hidden_pre * (1.0 - sigmoid))).astype(jnp.bfloat16)
    grad_norm_two, grad_gain_mlp = rms_backward(
        resid_two, inverse_two, gain_mlp, contract_cols(grad_pre, w_up)
    )
    grad_two = grad_three + grad_norm_two
    grad_branch = grad_two.astype(jnp.bfloat16)
    grad_mixed = (
        contract_cols(grad_branch, w_out)
        .astype(jnp.bfloat16)
        .reshape(rows, sequence_span, HEADS, hdim)
    )
    grad_query, grad_key, grad_value = lax.map(
        lambda items: attend_backward(items, scale),
        (query, key, value, segment_ids, log_total, grad_mixed),
    )
    grad_query = unrotate(grad_query, cosine, sine)
    grad_key = unrotate(grad_key, cosine, sine)
    grad_proj = (
        jnp.stack([grad_query, grad_key, grad_value], axis=2)
        .reshape(rows * sequence_span, 3 * width)
        .astype(jnp.bfloat16)
    )
    grad_norm_one, grad_gain_attn = rms_backward(
        tokens, inverse_one, gain_attn, contract_cols(grad_proj, w_qkv)
    )
    entry_sensitivity_matrix = grad_two + grad_norm_one
    size = lax.axis_size("dp")
    share = width // (2 * size)
    if size == 16 and lax.axis_size("head") == 2:
        half = width // 2
        bias_row = lax.dynamic_update_slice_in_dim(
            jnp.zeros((width,), F32), bias_local, core * half, 0
        )
        blank = jnp.zeros((width,), F32)
        small = jnp.stack(
            [grad_gain_attn, grad_gain_mlp, grad_gain_final, bias_row] + [blank] * 4
        )
        grad_head, grad_down, grad_up, grad_out, grad_qkv, sums = reduce_gradients(
            [final_hidden.T, hidden.T, act_two.T, mixed.T, act_one.T],
            [cotangent, grad_mlp_out, grad_pre, grad_branch, grad_proj],
            small,
        )
        gains = lax.dynamic_slice_in_dim(sums, (place * 2 + core) * share, share, 1)
        grad_bias = lax.dynamic_slice_in_dim(sums[3], core * half, half, 0)
    else:
        grad_head = lax.psum_scatter(
            contract_rows(collected_rows, cotangent), "dp", scatter_dimension=0, tiled=True
        )
        grad_down = scatter_rows(hidden, grad_mlp_out)
        grad_up = scatter_rows(act_two, grad_pre)
        grad_out = scatter_rows(mixed, grad_branch)
        grad_qkv = scatter_rows(act_one, grad_proj)
        gains = sum_everywhere(jnp.stack([grad_gain_attn, grad_gain_mlp, grad_gain_final]), True)
        gains = lax.dynamic_slice_in_dim(gains, (place * 2 + core) * share, share, 1)
        grad_bias = sum_everywhere(bias_local, False)
    return (
        predicted_levels,
        entry_sensitivity_matrix,
        gains[0],
        grad_qkv,
        grad_out,
        gains[1],
        grad_up,
        grad_down,
        gains[2],
        grad_head,
        grad_bias,
    )


def solution(mesh):
    return jax.shard_map(
        per_device,
        mesh=mesh,
        in_specs=(
            P(("dp", "head"), None),
            P(("dp", "head"), None),
            P(),
            P(),
            P(),
            P(),
            P(),
            P(),
            P(),
            P(None, "head"),
            P("head"),
            P("dp", "head"),
        ),
        out_specs=(
            P("dp", "head"),
            P(("dp", "head"), None),
            P(("dp", "head")),
            P(("dp", "head"), None),
            P(("dp", "head"), None),
            P(("dp", "head")),
            P(("dp", "head"), None),
            P(("dp", "head"), None),
            P(("dp", "head")),
            P("dp", "head"),
            P("head"),
        ),
        check_vma=False,
    )
```

```python
import functools
import math

import jax
import jax.numpy as jnp
from jax import lax
from jax.experimental import pallas as pl
from jax.experimental.pallas import tpu as pltpu
from jax.sharding import PartitionSpec as P

HEADS = 16
F32 = jnp.float32
BF16 = jnp.bfloat16

epsilon = 1e-06


def rms_forward(values, gain):
    inverse = lax.rsqrt(jnp.mean(values * values, axis=-1, keepdims=True) + epsilon)
    return (values * inverse * gain, inverse)


def rms_backward(values, inverse, gain, grad):
    normed = values * inverse
    scaled = grad * gain
    grad_gain = jnp.sum(grad * normed, axis=0)
    grad_values = inverse * (scaled - normed * jnp.mean(scaled * normed, axis=-1, keepdims=True))
    return (grad_values, grad_gain)


def rotary_tables(sequence_span, hdim):
    half = hdim // 2
    freq = 10000.0 ** (-jnp.arange(half, dtype=jnp.float32) / half)
    angle = jnp.arange(sequence_span, dtype=jnp.float32)[:, None] * freq[None, :]
    return (jnp.cos(angle)[:, None, :], jnp.sin(angle)[:, None, :])


def rotate(values, cosine, sine):
    half = values.shape[-1] // 2
    first = values[..., :half]
    second = values[..., half:]
    return jnp.concatenate(
        [first * cosine - second * sine, second * cosine + first * sine], axis=-1
    )


def unrotate(grads, cosine, sine):
    half = grads.shape[-1] // 2
    first = grads[..., :half]
    second = grads[..., half:]
    return jnp.concatenate(
        [first * cosine + second * sine, second * cosine - first * sine], axis=-1
    )


def allowed_mask(segs):
    place = jnp.arange(segs.shape[0])
    return (segs[:, None] == segs[None, :]) & (place[:, None] >= place[None, :])


def row_scores(query, key, segs, scale):
    scores = jnp.einsum("qhd,khd->hqk", query, key, preferred_element_type=jnp.float32) * scale
    allowed = allowed_mask(segs)[None]
    return (jnp.where(allowed, scores, -1e30), allowed)


def attend_forward(items, scale):
    query, key, value, segs = items
    scores, allowed = row_scores(query, key, segs, scale)
    peak = jnp.max(scores, axis=-1, keepdims=True)
    expo = jnp.exp(scores - peak)
    overall_number = jnp.sum(expo, axis=-1, keepdims=True)
    probs = (expo / overall_number).astype(jnp.bfloat16)
    attended = jnp.einsum("hqk,khd->qhd", probs, value, preferred_element_type=jnp.float32)
    return (attended.astype(jnp.bfloat16), peak + jnp.log(overall_number))


def attend_backward(items, scale):
    query, key, value, segs, log_total, grad_attended = items
    scores, allowed = row_scores(query, key, segs, scale)
    probs = jnp.where(allowed, jnp.exp(scores - log_total), 0.0)
    grad_value = jnp.einsum(
        "hqk,qhd->khd",
        probs.astype(jnp.bfloat16),
        grad_attended,
        preferred_element_type=jnp.float32,
    )
    grad_probs = jnp.einsum(
        "qhd,khd->hqk", grad_attended, value, preferred_element_type=jnp.float32
    )
    grad_scores = (
        probs * (grad_probs - jnp.sum(grad_probs * probs, axis=-1, keepdims=True))
    ).astype(jnp.bfloat16)
    grad_query = (
        jnp.einsum("hqk,khd->qhd", grad_scores, key, preferred_element_type=jnp.float32) * scale
    )
    grad_key = (
        jnp.einsum("hqk,qhd->khd", grad_scores, query, preferred_element_type=jnp.float32) * scale
    )
    return (grad_query, grad_key, grad_value)


def contract_rows(left, right):
    return lax.dot_general(
        left, right, (((0,), (0,)), ((), ())), preferred_element_type=jnp.float32
    )


def contract_cols(left, right):
    return lax.dot_general(
        left, right, (((1,), (1,)), ((), ())), preferred_element_type=jnp.float32
    )


def swap_cores(values):
    return lax.ppermute(values, "head", [(0, 1), (1, 0)])


def flip(values, bit):
    size = lax.axis_size("dp")
    return lax.ppermute(values, "dp", [(i, i ^ bit) for i in range(size)])


def scatter_rows(left, right):
    return lax.psum_scatter(
        contract_rows(left, right), ("dp", "head"), scatter_dimension=0, tiled=True
    )


def sum_everywhere(values, over_head):
    size = lax.axis_size("dp")
    if over_head:
        values = values + swap_cores(values)
    bit = 1
    while bit < size:
        values = values + flip(values, bit)
        bit *= 2
    return values


MESH = pl.DeviceIdType.MESH


def chunk_table(width, hidden):
    table = [(0, 0)]
    table += [(1, j) for j in range(hidden // width)]
    table += [(2, j) for j in range(hidden // width)]
    table += [(3, 0)]
    table += [(4, j) for j in range(3)]
    return table


def nt(left, right):
    return lax.dot_general(
        left, right, (((1,), (1,)), ((), ())), preferred_element_type=jnp.float32
    )


def nn(left, right):
    return jnp.dot(left, right, preferred_element_type=jnp.float32)


LEAD = 3


def backward_kernel(
    table,
    size,
    y_t,
    g_t,
    a2_t,
    o_t,
    a1_t,
    cot,
    dy_t,
    x3_t,
    x2_t,
    x_t,
    h_t,
    qkv_t,
    w_down,
    w_up,
    w_out,
    w_qkv,
    lse,
    seg_row,
    seg_col,
    gains,
    cosine,
    sine,
    small,
    out_head,
    out_down,
    out_up,
    out_out,
    out_qkv,
    out_small,
    out_entry,
    y_o,
    g_o,
    a2_o,
    o_o,
    a1_o,
    e3_o,
    eh_o,
    e2_o,
    ep_o,
    eh_mine,
    lbuf,
    rbuf,
    cbuf,
    grad,
    recv1,
    pair,
    recv2,
    line,
    recv_up,
    recv_down,
    total,
    sums,
    sums_in,
    dx,
    work,
    acc,
    ebuf,
    bias,
    gsum,
    wrows,
    wcols,
    hbuf,
    ehbuf,
    ep,
    eo,
    heads,
    keys,
    values,
    eq_acc,
    ek_acc,
    ev_acc,
    obuf,
    push_send,
    push_recv,
    left_sem,
    right_sem,
    send1_sem,
    recv1_sem,
    send2_sem,
    recv2_sem,
    up_send,
    up_recv,
    down_send,
    down_recv,
    local_sem,
    swap_send,
    swap_recv,
    small_send,
    small_recv,
    row_sem,
    col_sem,
    h_sem,
    eh_out_sem,
    eh_in_sem,
    head_sem,
    fetch_sem,
    entry_sem,
):
    n = len(table)
    length = size // 4
    me = lax.axis_index("dp")
    core = lax.axis_index("head")
    other = 1 - core
    xi = lax.rem(me, 2)
    yi = lax.rem(me // 2, 2)
    zi = me // 4
    width, tokens = dx.shape
    hidden = h_t.shape[0]
    cols = width // 2
    block = width // size
    count = qkv_t.shape[0] // 3
    hdim = qkv_t.shape[1]
    scale = 1.0 / math.sqrt(hdim)
    flip_x = me + 1 - 2 * xi
    flip_y = me + 2 * (1 - 2 * yi)
    first_bit = jnp.where(core == 0, xi, yi)
    second_bit = jnp.where(core == 0, yi, xi)
    first_peer = jnp.where(core == 0, flip_x, flip_y)
    second_peer = jnp.where(core == 0, flip_y, flip_x)
    far = lax.rem(me + size // 2, size)
    near = me + 4 * (1 - 2 * lax.rem(zi, 2))
    rings = recv1.shape[0]
    ring2 = recv2.shape[0]
    ring_line = line.shape[0]

    fetch_dy = pltpu.make_async_copy(dy_t, dx, fetch_sem.at[0])
    fetch_x3 = pltpu.make_async_copy(x3_t, work, fetch_sem.at[1])
    fetch_x2 = pltpu.make_async_copy(x2_t, work, fetch_sem.at[1])
    fetch_x = pltpu.make_async_copy(x_t, ebuf, fetch_sem.at[0])
    fetch_dy.start()
    fetch_x3.start()

    def local_c(half, which):
        start = pl.multiple_of(which * tokens, 16)
        return pltpu.make_async_copy(
            cot.at[pl.ds(start, tokens)], cbuf.at[half], fetch_sem.at[2 + half]
        )

    local_c(0, core).start()
    local_c(1, other).start()

    barrier = pltpu.get_barrier_semaphore()
    for index, which in ((me, other), (flip_x, core), (flip_y, core), (far, core)):
        pl.semaphore_signal(barrier, inc=1, device_id=(index, which), device_id_type=MESH)

    @pl.when(zi > 0)
    def _():
        pl.semaphore_signal(barrier, inc=1, device_id=(me - 4, core), device_id_type=MESH)

    @pl.when(zi < length - 1)
    def _():
        pl.semaphore_signal(barrier, inc=1, device_id=(me + 4, core), device_id_type=MESH)

    inner = jnp.where(zi > 0, 1, 0) + jnp.where(zi < length - 1, 1, 0)
    pl.semaphore_wait(barrier, 4 + inner)

    def remote(src, dst, send, recv, index, which):
        return pltpu.make_async_remote_copy(
            src_ref=src,
            dst_ref=dst,
            send_sem=send,
            recv_sem=recv,
            device_id=(index, which),
            device_id_type=MESH,
        )

    lefts = (y_t, g_t, a2_t, o_t, a1_t)
    left_others = (y_o, g_o, a2_o, o_o, a1_o)
    pieces = hidden // width

    def push(k):
        if k == 0 or k > pieces:
            if k == 0:
                src, dst = y_t, y_o
            elif k <= pieces + 3:
                src, dst = lefts[k - pieces + 1], left_others[k - pieces + 1]
            elif k == pieces + 6:
                wide = 3 * cols
                src, dst = ep.at[pl.ds(pl.multiple_of(other * wide, 16), wide)], ep_o
            else:
                src = ebuf.at[pl.ds(pl.multiple_of(other * cols, 16), cols)]
                dst = (e3_o, e2_o)[k - pieces - 4]
        else:
            part = pl.ds((k - 1) * block, block)
            src, dst = g_t.at[:, part, :], g_o.at[:, part, :]
        return remote(src, dst, push_send.at[k], push_recv.at[k], me, other)

    PA2, PO, PA1, PE3, PE2, PEP = (pieces + i for i in range(1, 7))

    push(0).start()
    push(1).start()

    def left_copies(c, slot):
        i, j = table[c]
        lower = pl.ds(j * block, block) if i == 1 else slice(None)
        return [
            pltpu.make_async_copy(
                source.at[:, lower, :], lbuf.at[slot, half], left_sem.at[slot, half]
            )
            for half, source in ((0, lefts[i]), (1, left_others[i]))
        ]

    def left_arrives(c):
        i, j = table[c]
        if i == 0:
            push(0).wait_recv()
        elif i == 1:
            push(1 + j).wait_recv()
        elif j == 0:
            push((None, None, PA2, PO, PA1)[i]).wait_recv()

    def start_left(c):
        left_arrives(c)
        for copy in left_copies(c, c % 2):
            copy.start()

    def start_right(c):
        i, j = table[c]
        slot = c % 2
        mine = pl.ds(pl.multiple_of(core * cols, 16), cols)
        rows = pl.ds(j * cols, cols)
        if i == 1:
            own, its = ebuf.at[mine], e3_o
            if j == 0:
                push(PE3).wait_recv()
        elif i == 2:
            own, its = eh_mine.at[rows], eh_o.at[rows]
            if j == 0:
                for piece in range(pieces):
                    eh_push(piece, 0).wait_recv()
        elif i == 3:
            own, its = ebuf.at[mine], e2_o
            push(PE2).wait_recv()
        else:
            start = pl.multiple_of(core * 3 * cols + j * cols, 16)
            own, its = ep.at[pl.ds(start, cols)], ep_o.at[rows]
            if j == 0:
                push(PEP).wait_recv()
        pltpu.make_async_copy(own, rbuf.at[slot, 0], right_sem.at[slot, 0]).start()
        pltpu.make_async_copy(its, rbuf.at[slot, 1], right_sem.at[slot, 1]).start()

    def eh_push(piece, slot):
        return remote(
            ehbuf.at[slot],
            eh_o.at[pl.ds(piece * cols, cols)],
            eh_out_sem.at[slot],
            eh_in_sem.at[piece],
            me,
            other,
        )

    def wait_left(slot):
        for half in range(2):
            pltpu.make_async_copy(
                lbuf.at[slot, half], lbuf.at[slot, half], left_sem.at[slot, half]
            ).wait()

    def wait_right(slot):
        for half in range(2):
            pltpu.make_async_copy(
                rbuf.at[slot, half], rbuf.at[slot, half], right_sem.at[slot, half]
            ).wait()

    def form(slot, ring, right, multiply):
        @pl.loop(0, length)
        def _(z):
            rows = pl.ds(z * 4, 4)
            value = None
            for half in range(2):
                left = lbuf[slot, half, rows].reshape(4 * block, tokens)
                part = multiply(left, right[half])
                value = part if value is None else value + part
            value = value.astype(BF16)
            for q in range(4):
                x, y = q % 2, q // 2
                one = jnp.where(core == 0, x, y)
                two = jnp.where(core == 0, y, x)
                grad[ring, one, two, z] = value[q * block : (q + 1) * block]

    def send1(c):
        ring, spot = lax.rem(c, LEAD), lax.rem(c, rings)
        return remote(
            grad.at[ring, 1 - first_bit],
            recv1.at[spot],
            send1_sem.at[ring],
            recv1_sem.at[spot],
            first_peer,
            core,
        )

    def send2(c):
        ring, spot = lax.rem(c, 2), lax.rem(c, ring2)
        return remote(
            pair.at[ring, 1 - second_bit],
            recv2.at[spot],
            send2_sem.at[ring],
            recv2_sem.at[spot],
            second_peer,
            core,
        )

    def send_up(c, step):
        ring, spot = lax.rem(c, ring_line), lax.rem(c, rings)
        return remote(
            line.at[ring, jnp.minimum(zi + (length - step), length - 1)],
            recv_up.at[spot, step - 1],
            up_send.at[ring, step - 1],
            up_recv.at[spot, step - 1],
            jnp.minimum(me + 4, size - 1),
            core,
        )

    def send_down(c, step):
        ring, spot = lax.rem(c, ring_line), lax.rem(c, rings)
        return remote(
            line.at[ring, jnp.maximum(zi - (length - step), 0)],
            recv_down.at[spot, step - 1],
            down_send.at[ring, step - 1],
            down_recv.at[spot, step - 1],
            jnp.maximum(me - 4, 0),
            core,
        )

    def start_line(c, step):
        @pl.when(zi < step)
        def _():
            send_up(c, step).start()

        @pl.when(zi >= length - step)
        def _():
            send_down(c, step).start()

    def wait_line_sent(c, step):
        @pl.when(zi < step)
        def _():
            send_up(c, step).wait_send()

        @pl.when(zi >= length - step)
        def _():
            send_down(c, step).wait_send()

    def results(c):
        i, j = table[c]
        if i == 0:
            return [pltpu.make_async_copy(total.at[c], out_head, local_sem.at[c])]
        if i == 1:
            target = out_down.at[
                pl.ds((j % 2) * block, block), pl.ds(pl.multiple_of(core * cols, 128), cols)
            ]
            return [
                pltpu.make_async_copy(total.at[c], target, local_sem.at[c]),
                remote(total.at[c], target, swap_send.at[c], swap_recv.at[c], me, other),
            ]
        target = (None, None, out_up, out_out, out_qkv)[i]
        wide = target.shape[1] // 2
        place = target.at[:, pl.ds(pl.multiple_of(core * wide + j * cols, 128), cols)]
        half = block // 2
        mine = pl.ds(pl.multiple_of(core * half, 8), half)
        its = pl.ds(pl.multiple_of(other * half, 8), half)
        return [
            pltpu.make_async_copy(total.at[c, mine], place, local_sem.at[c]),
            remote(total.at[c, its], place, swap_send.at[c], swap_recv.at[c], me, other),
        ]

    def start_results(c):
        i, j = table[c]
        copies = results(c)
        if i == 1:
            owner = j // (pieces // 2)
            pl.when(core == owner)(copies[0].start)
            pl.when(core != owner)(copies[1].start)
        else:
            for copy in copies:
                copy.start()

    def end_results(c):
        i, j = table[c]
        copies = results(c)
        if i == 1:
            owner = j // (pieces // 2)
            pl.when(core == owner)(copies[0].wait)
            pl.when(core == owner)(copies[1].wait_recv)
            pl.when(core != owner)(copies[1].wait_send)
        else:
            for copy in copies:
                copy.wait()

    def exchange(t):
        @pl.when(t < n)
        def _():
            c = t
            send1(c).wait_recv()
            ring, spot, to = lax.rem(c, LEAD), lax.rem(c, rings), lax.rem(c, 2)

            @pl.when(c >= 2)
            def _():
                send2(c - 2).wait_send()

            for two in range(2):

                @pl.loop(0, length)
                def _(z):
                    pair[to, two, z] = (
                        grad[ring, first_bit, two, z].astype(F32)
                        + recv1[spot, two, z].astype(F32)
                    ).astype(BF16)

            send2(c).start()

        @pl.when((t >= 1) & (t <= n))
        def _():
            c = t - 1
            send2(c).wait_recv()
            ring, spot, to = lax.rem(c, 2), lax.rem(c, ring2), lax.rem(c, ring_line)

            @pl.loop(0, length)
            def _(z):
                line[to, z] = (
                    pair[ring, second_bit, z].astype(F32) + recv2[spot, z].astype(F32)
                ).astype(BF16)

            start_line(c, 1)

        for step in range(1, length):

            @pl.when((t >= 1 + step) & (t <= n + step))
            def _():
                c = t - 1 - step
                ring, at = lax.rem(c, ring_line), lax.rem(c, rings)
                last = step == length - 1
                up_in = (zi >= 1) & (zi <= step)
                down_in = (zi <= length - 2) & (zi >= length - 1 - step)

                @pl.when(up_in)
                def _():
                    send_up(c, step).wait_recv()
                    spot = jnp.minimum(zi + (length - 1 - step), length - 1)
                    if not last:
                        line[ring, spot] = (
                            line[ring, spot].astype(F32) + recv_up[at, step - 1].astype(F32)
                        ).astype(BF16)

                @pl.when(down_in)
                def _():
                    send_down(c, step).wait_recv()
                    spot = jnp.maximum(zi - (length - 1 - step), 0)
                    if not last:
                        line[ring, spot] = (
                            line[ring, spot].astype(F32) + recv_down[at, step - 1].astype(F32)
                        ).astype(BF16)

                if not last:
                    start_line(c, step + 1)
                else:
                    total[c] = line[ring, zi].astype(F32)

                    @pl.when(up_in)
                    def _():
                        total[c] = total[c] + recv_up[at, step - 1].astype(F32)

                    @pl.when(down_in)
                    def _():
                        total[c] = total[c] + recv_down[at, step - 1].astype(F32)

                    for back in range(1, length):
                        wait_line_sent(c, back)

                    for d in range(n):

                        @pl.when(c == d)
                        def _():
                            start_results(d)

    strip = 128
    strips = width // strip

    def norm_backward(vref, eref, index, emit):
        def sums_of(k, carry):
            squares, products = carry
            rows = pl.ds(pl.multiple_of(k * strip, strip), strip)
            v = vref[rows].astype(F32)
            e = eref[rows]
            gain = gains[rows, index : index + 1]
            squares = squares + jnp.sum(v * v, axis=0, keepdims=True)
            products = products + jnp.sum(e * gain * v, axis=0, keepdims=True)
            return squares, products

        blank = jnp.zeros((1, tokens), F32)
        squares, products = lax.fori_loop(0, strips, sums_of, (blank, blank))
        inverse = lax.rsqrt(squares / width + epsilon)
        mean = products * inverse / width

        @pl.loop(0, strips)
        def _(k):
            rows = pl.ds(pl.multiple_of(k * strip, strip), strip)
            normed = vref[rows].astype(F32) * inverse
            e = eref[rows]
            gain = gains[rows, index : index + 1]
            gsum[rows, index : index + 1] = jnp.sum(e * normed, axis=1, keepdims=True)
            emit(k, rows, inverse * (e * gain - normed * mean))

    gsum[...] = jnp.zeros_like(gsum)
    fetch_dy.wait()
    fetch_x3.wait()

    def emit_final(k, rows, value):
        dx[rows] = value
        ebuf[rows] = value.astype(BF16)

    norm_backward(work, dx, 2, emit_final)
    push(PE3).start()
    for k in range(2, pieces + 1):
        push(k).start()
    fetch_x2.start()

    start_left(0)
    start_left(1)
    local_c(0, core).wait()
    local_c(1, other).wait()
    wait_left(0)
    form(0, 0, [cbuf[0], cbuf[1]], nn)
    send1(0).start()
    start_left(2)
    for c in range(1, LEAD):
        start_right(c)
        wait_left(c % 2)
        wait_right(c % 2)
        form(c % 2, c, [rbuf[c % 2, 0], rbuf[c % 2, 1]], nt)
        send1(c).start()
        start_left(c + 2)
    push(PA2).start()
    push(PO).start()
    push(PA1).start()

    def row_tile(k, slot, source):
        return pltpu.make_async_copy(
            source.at[pl.ds(pl.multiple_of(k * cols, 16), cols)], wrows.at[slot], row_sem.at[slot]
        )

    def col_tile(k, slot, source):
        return pltpu.make_async_copy(
            source.at[:, pl.ds(pl.multiple_of(k * cols, 128), cols)],
            wcols.at[slot],
            col_sem.at[slot],
        )

    def h_tile(k, slot):
        return pltpu.make_async_copy(
            h_t.at[pl.ds(pl.multiple_of(k * cols, 16), cols)], hbuf.at[slot], h_sem.at[slot]
        )

    def mlp_tiles(k):
        return jnp.where(k < pieces, other, core) * pieces + lax.rem(k, pieces)

    def fetch_mlp(k):
        slot = lax.rem(k, 2)
        tile = mlp_tiles(k)
        row_tile(tile, slot, w_down).start()
        col_tile(tile, slot, w_up).start()
        h_tile(tile, slot).start()

    def mlp_step(k):
        slot = lax.rem(k, 2)
        tile = mlp_tiles(k)
        row_tile(tile, slot, w_down).wait()
        h_tile(tile, slot).wait()

        @pl.when((k >= 2) & (k < pieces + 2))
        def _():
            eh_push(0, slot).wait_send()

        @pl.when(k >= pieces + 2)
        def _():
            pltpu.make_async_copy(
                ehbuf.at[slot], eh_mine.at[pl.ds(0, cols)], eh_out_sem.at[slot]
            ).wait()

        part = cols // 2

        @pl.loop(0, 2)
        def _(i):
            rows = pl.ds(pl.multiple_of(i * part, 16), part)
            value = nn(wrows[slot, rows], ebuf[...])
            pre = hbuf[slot, rows].astype(F32)
            sig = 1.0 / (1.0 + jnp.exp(-pre))
            ehbuf[slot, rows] = (value * sig * (1.0 + pre * (1.0 - sig))).astype(BF16)

        where = lax.rem(k, pieces)

        @pl.when(k < pieces)
        def _():
            eh_push(where, slot).start()

        @pl.when(k >= pieces)
        def _():
            pltpu.make_async_copy(
                ehbuf.at[slot],
                eh_mine.at[pl.ds(pl.multiple_of(where * cols, 16), cols)],
                eh_out_sem.at[slot],
            ).start()

        col_tile(tile, slot, w_up).wait()
        accumulate(wcols.at[slot], ehbuf.at[slot], k == 0)

        @pl.when(k + 2 < 2 * pieces)
        def _():
            fetch_mlp(k + 2)

    def accumulate(left, right, first):
        part = width // 4

        @pl.loop(0, 4)
        def _(i):
            rows = pl.ds(pl.multiple_of(i * part, 16), part)
            value = nn(left[rows], right[...])

            @pl.when(first)
            def _():
                acc[rows] = value

            @pl.when(jnp.logical_not(first))
            def _():
                acc[rows] = acc[rows] + value

    fetch_mlp(0)
    fetch_mlp(1)

    def emit_mlp(k, rows, value):
        value = dx[rows] + value
        dx[rows] = value
        ebuf[rows] = value.astype(BF16)

    def middle():
        for slot in range(2):
            pltpu.make_async_copy(
                ehbuf.at[slot], eh_mine.at[pl.ds(0, cols)], eh_out_sem.at[slot]
            ).wait()
        row_tile(0, 0, w_out).start()
        row_tile(1, 1, w_out).start()
        push(PE3).wait_send()
        fetch_x2.wait()
        norm_backward(work, acc, 1, emit_mlp)
        push(PE2).start()

        @pl.loop(0, 2)
        def _(k):
            row_tile(k, k, w_out).wait()

            @pl.loop(0, 2)
            def _(i):
                part = cols // 2
                rows = pl.ds(pl.multiple_of(i * part, 16), part)
                to = pl.ds(pl.multiple_of(k * cols + i * part, 16), part)
                eo[to] = nn(wrows[k, rows], ebuf[...]).astype(BF16)

        @pl.loop(0, tokens // strip)
        def _(k):
            rows = pl.ds(pl.multiple_of(k * strip, strip), strip)
            own = lax.broadcasted_iota(jnp.int32, (strip, tokens), 0) + k * strip
            asked = lax.broadcasted_iota(jnp.int32, (strip, tokens), 1)
            allowed = (seg_col[rows] == seg_row[...]) & (own <= asked)
            bias[rows] = jnp.where(allowed, 0.0, -1e30)

    per_turn = count // 4

    def fetch_head(head, slot):
        for part in range(3):
            pltpu.make_async_copy(
                qkv_t.at[part * count + head], heads.at[slot, part], head_sem.at[slot, part]
            ).start()

    def attend(turn):
        @pl.when(turn == 0)
        def _():
            fetch_head(0, 0)

        @pl.loop(0, per_turn)
        def _(i):
            head = turn * per_turn + i
            slot = lax.rem(head, 2)
            for part in range(3):
                pltpu.make_async_copy(
                    qkv_t.at[part * count + head], heads.at[slot, part], head_sem.at[slot, part]
                ).wait()

            @pl.when(head + 1 < count)
            def _():
                fetch_head(head + 1, 1 - slot)

            q_t = heads[slot, 0]
            k_t = heads[slot, 1]
            v_t = heads[slot, 2]
            own = pl.ds(pl.multiple_of(head * hdim, 16), hdim)
            eo_t = eo[own]
            q = q_t.astype(F32).T.astype(BF16)
            e = eo_t.astype(F32).T.astype(BF16)
            keys[...] = k_t.astype(F32).T.astype(BF16)
            values[...] = v_t.astype(F32).T.astype(BF16)
            weight = lse[pl.ds(head, 1), :]
            ek_acc[...] = jnp.zeros_like(ek_acc)
            ev_acc[...] = jnp.zeros_like(ev_acc)
            for b in range(tokens // strip):
                low, high = max(0, (b - 2) * strip), (b + 1) * strip
                asked = slice(b * strip, (b + 1) * strip)
                scores = nn(keys[low:high], q_t[:, asked]) * scale + bias[low:high, asked]
                p = jnp.exp(scores - weight[:, asked])
                ep_t = nn(values[low:high], eo_t[:, asked])
                share = jnp.sum(p * ep_t, axis=0, keepdims=True)
                es = (p * (ep_t - share)).astype(BF16)
                eq_acc[:, asked] = nn(k_t[:, low:high], es)
                ek_acc[low:high] += nn(es, q[asked])
                ev_acc[low:high] += nn(p.astype(BF16), e[asked])
            half = hdim // 2
            for part, value in ((0, eq_acc[...]), (1, ek_acc[...].T)):
                one, two = value[:half] * scale, value[half:] * scale
                turned = jnp.concatenate(
                    [one * cosine[...] + two * sine[...], two * cosine[...] - one * sine[...]],
                    axis=0,
                )
                to = pl.ds(pl.multiple_of(part * width + head * hdim, 16), hdim)
                ep[to] = turned.astype(BF16)
            to = pl.ds(pl.multiple_of(2 * width + head * hdim, 16), hdim)
            ep[to] = ev_acc[...].T.astype(BF16)

        @pl.when(turn == 3)
        def _():
            push(PEP).start()

    def fetch_qkv(k):
        col_tile(k, lax.rem(k, 2), w_qkv).start()

    def qkv_step(k):
        slot = lax.rem(k, 2)
        col_tile(k, slot, w_qkv).wait()
        rows = pl.ds(pl.multiple_of(k * cols, 16), cols)
        accumulate(wcols.at[slot], ep.at[rows], k == 0)

        @pl.when(k + 2 < 6)
        def _():
            fetch_qkv(k + 2)

    def entry_copy(k, slot):
        return pltpu.make_async_copy(
            obuf.at[slot],
            out_entry.at[:, pl.ds(pl.multiple_of(k * strip, strip), strip)],
            entry_sem.at[slot],
        )

    def emit_entry(k, rows, value):
        slot = lax.rem(k, 2)

        @pl.when(k >= 2)
        def _():
            entry_copy(k, slot).wait()

        obuf[slot] = (dx[rows] + value).T
        entry_copy(k, slot).start()

    peers = ((me, other), (flip_x, core), (flip_y, core), (near, core), (far, core))
    steps = len(peers)

    def small_copy(i):
        return remote(
            sums.at[i], sums_in.at[i], small_send.at[i], small_recv.at[i], peers[i][0], peers[i][1]
        )

    def last():
        fetch_x.wait()
        norm_backward(ebuf, acc, 0, emit_entry)
        for slot in range(2):
            entry_copy(0, slot).wait()
        sums[0] = gsum[...].T[: small.shape[0]] + small[...]
        small_copy(0).start()

    @pl.loop(0, n + length)
    def _(t):
        for c in range(LEAD, n):

            @pl.when(t == c - LEAD)
            def _():
                start_right(c)

        @pl.when(t < 2)
        def _():
            @pl.loop(0, pieces)
            def _(i):
                mlp_step(t * pieces + i)

        @pl.when(t == 2)
        def _():
            middle()

        @pl.when((t >= 3) & (t < 7))
        def _():
            attend(t - 3)

        @pl.when(t == 6)
        def _():
            fetch_qkv(0)
            fetch_qkv(1)

        @pl.when((t == 7) | (t == 8))
        def _():
            @pl.loop(0, 3)
            def _(i):
                qkv_step((t - 7) * 3 + i)

        @pl.when(t == 9)
        def _():
            last()

        for i in range(steps):

            @pl.when(t == 10 + i)
            def _():
                small_copy(i).wait()
                value = sums[i] + sums_in[i]
                if i == steps - 1:
                    out_small[...] = value
                else:
                    sums[i + 1] = value
                    small_copy(i + 1).start()

        exchange(t)

        @pl.when(t + LEAD < n)
        def _():
            c = t + LEAD
            slot = lax.rem(c, 2)
            wait_left(slot)
            wait_right(slot)
            send1(t).wait_send()
            form(slot, lax.rem(c, LEAD), [rbuf[slot, 0], rbuf[slot, 1]], nt)
            send1(c).start()
            for d in range(LEAD + 2, n):

                @pl.when(c == d - 2)
                def _():
                    start_left(d)

        @pl.when(t == 8)
        def _():
            push(PE2).wait_send()
            fetch_x.start()

    for c in range(n):
        end_results(c)
    for c in range(n - LEAD, n):
        send1(c).wait_send()
    for c in range(n - 2, n):
        send2(c).wait_send()
    for k in range(pieces + 7):
        if k not in (PE3, PE2):
            push(k).wait_send()


def run_backward(lefts, others, weights, tables, small):
    size = lax.axis_size("dp")
    width, tokens = lefts[0].shape
    hidden = lefts[1].shape[0]
    block = width // size
    cols = width // 2
    table = chunk_table(width, hidden)
    n = len(table)
    length = size // 4
    share = block // 2
    hdim = width // HEADS
    hbm = pl.BlockSpec(memory_space=pl.ANY)
    vmem = pl.BlockSpec(memory_space=pltpu.VMEM)
    lefts = [left.reshape(size, left.shape[0] // size, tokens) for left in lefts]
    shapes = [
        jax.ShapeDtypeStruct((block, cols), F32),
        jax.ShapeDtypeStruct((hidden // size // 2, width), F32),
        jax.ShapeDtypeStruct((share, hidden), F32),
        jax.ShapeDtypeStruct((share, width), F32),
        jax.ShapeDtypeStruct((share, 3 * width), F32),
        jax.ShapeDtypeStruct(small.shape, F32),
        jax.ShapeDtypeStruct((tokens, width), F32),
    ]
    shapes += [jax.ShapeDtypeStruct(left.shape, BF16) for left in lefts]
    shapes += [
        jax.ShapeDtypeStruct((rows, tokens), BF16)
        for rows in (cols, hidden // 2, cols, 3 * cols, hidden // 2)
    ]
    dma = pltpu.SemaphoreType.DMA
    ring1, ring2, ring_line = 6, 4, length + 1
    results = pl.pallas_call(
        functools.partial(backward_kernel, table, size),
        out_shape=shapes,
        in_specs=[hbm] * 16 + [vmem] * 7,
        out_specs=[hbm] * 5 + [vmem] + [hbm] * 11,
        scratch_shapes=[
            pltpu.VMEM((2, 2, size, block, tokens), BF16),
            pltpu.VMEM((2, 2, cols, tokens), BF16),
            pltpu.VMEM((2, tokens, cols), BF16),
            pltpu.VMEM((LEAD, 2, 2, length, block, cols), BF16),
            pltpu.VMEM((ring1, 2, length, block, cols), BF16),
            pltpu.VMEM((2, 2, length, block, cols), BF16),
            pltpu.VMEM((ring2, length, block, cols), BF16),
            pltpu.VMEM((ring_line, length, block, cols), BF16),
            pltpu.VMEM((ring1, length - 1, block, cols), BF16),
            pltpu.VMEM((ring1, length - 1, block, cols), BF16),
            pltpu.VMEM((n, block, cols), F32),
            pltpu.VMEM((5,) + small.shape, F32),
            pltpu.VMEM((5,) + small.shape, F32),
            pltpu.VMEM((width, tokens), F32),
            pltpu.VMEM((width, tokens), F32),
            pltpu.VMEM((width, tokens), F32),
            pltpu.VMEM((width, tokens), BF16),
            pltpu.VMEM((tokens, tokens), F32),
            pltpu.VMEM((width, 128), F32),
            pltpu.VMEM((2, cols, width), BF16),
            pltpu.VMEM((2, width, cols), BF16),
            pltpu.VMEM((2, cols, tokens), BF16),
            pltpu.VMEM((2, cols, tokens), BF16),
            pltpu.VMEM((3 * width, tokens), BF16),
            pltpu.VMEM((width, tokens), BF16),
            pltpu.VMEM((2, 3, hdim, tokens), BF16),
            pltpu.VMEM((tokens, hdim), BF16),
            pltpu.VMEM((tokens, hdim), BF16),
            pltpu.VMEM((hdim, tokens), F32),
            pltpu.VMEM((tokens, hdim), F32),
            pltpu.VMEM((tokens, hdim), F32),
            pltpu.VMEM((2, tokens, 128), F32),
            dma((hidden // width + 7,)),
            dma((hidden // width + 7,)),
            dma((2, 2)),
            dma((2, 2)),
            dma((LEAD,)),
            dma((ring1,)),
            dma((2,)),
            dma((ring2,)),
            dma((ring_line, length - 1)),
            dma((ring1, length - 1)),
            dma((ring_line, length - 1)),
            dma((ring1, length - 1)),
            dma((n,)),
            dma((n,)),
            dma((n,)),
            dma((5,)),
            dma((5,)),
            dma((2,)),
            dma((2,)),
            dma((2,)),
            dma((2,)),
            dma((hidden // width,)),
            dma((2, 3)),
            dma((4,)),
            dma((2,)),
        ],
        compiler_params=pltpu.CompilerParams(
            collective_id=0, has_side_effects=True, vmem_limit_bytes=62 << 20
        ),
        name="backward",
    )(*lefts, *others, *weights, *tables, small)
    return results[:7]


def per_device(
    inputs,
    segment_ids,
    gain_attn,
    w_qkv,
    w_out,
    gain_mlp,
    w_up,
    w_down,
    gain_final,
    head_projection_weight,
    head_output_bias,
    cotangent,
):
    core = lax.axis_index("head")
    place = lax.axis_index("dp")
    size = lax.axis_size("dp")
    rows, sequence_span = segment_ids.shape
    count, width = inputs.shape
    hdim = width // HEADS
    scale = 1.0 / math.sqrt(hdim)
    share = width // (2 * size)
    fused = size == 16 and lax.axis_size("head") == 2 and rows == 1

    other_rows = lax.dynamic_slice_in_dim(cotangent, (1 - core) * count, count, 0)
    own_rows = lax.dynamic_slice_in_dim(cotangent, core * count, count, 0)
    got = swap_cores(contract_cols(head_projection_weight, other_rows).astype(BF16))
    grad_final_t = contract_cols(head_projection_weight, own_rows) + got.astype(F32)
    bias_local = jnp.sum(cotangent, axis=0, dtype=F32)

    cosine, sine = rotary_tables(sequence_span, hdim)
    tokens = inputs.astype(jnp.float32)
    normed_one, inverse_one = rms_forward(tokens, gain_attn)
    act_one = normed_one.astype(jnp.bfloat16)
    projected = jnp.dot(act_one, w_qkv, preferred_element_type=jnp.float32).reshape(
        rows, sequence_span, 3, HEADS, hdim
    )
    query = rotate(projected[:, :, 0], cosine, sine).astype(jnp.bfloat16)
    key = rotate(projected[:, :, 1], cosine, sine).astype(jnp.bfloat16)
    value = projected[:, :, 2].astype(jnp.bfloat16)
    attended, log_total = lax.map(
        lambda items: attend_forward(items, scale), (query, key, value, segment_ids)
    )
    mixed = attended.reshape(rows * sequence_span, width)
    resid_two = tokens + jnp.dot(mixed, w_out, preferred_element_type=jnp.float32)
    normed_two, inverse_two = rms_forward(resid_two, gain_mlp)
    act_two = normed_two.astype(jnp.bfloat16)
    hidden_pre = jnp.dot(act_two, w_up, preferred_element_type=jnp.float32)
    hidden = jax.nn.silu(hidden_pre).astype(jnp.bfloat16)
    resid_three = resid_two + jnp.dot(hidden, w_down, preferred_element_type=jnp.float32)
    normed_three, inverse_three = rms_forward(resid_three, gain_final)
    final_hidden = normed_three.astype(jnp.bfloat16)
    other_hidden = swap_cores(final_hidden)
    collected_rows = jnp.concatenate(
        [
            jnp.where(core == 0, final_hidden, other_hidden),
            jnp.where(core == 0, other_hidden, final_hidden),
        ],
        axis=0,
    )
    predicted_levels = (
        jnp.dot(collected_rows, head_projection_weight, preferred_element_type=jnp.float32)
        + head_output_bias
    )
    if fused:
        half = width // 2
        bias_row = lax.dynamic_update_slice_in_dim(
            jnp.zeros((width,), F32), bias_local, core * half, 0
        )
        blank = jnp.zeros((width,), F32)
        small = jnp.stack([blank] * 3 + [bias_row] + [blank] * 4)
        gain_columns = jnp.stack([gain_attn, gain_mlp, gain_final] + [gain_attn] * 5, axis=1)
        packed = jnp.stack([query[0], key[0], value[0]]).transpose(0, 2, 3, 1)
        (
            grad_head,
            grad_down,
            grad_up,
            grad_out,
            grad_qkv,
            sums,
            entry_sensitivity_matrix,
        ) = run_backward(
            [final_hidden.T, hidden.T, act_two.T, mixed.T, act_one.T],
            [
                cotangent,
                grad_final_t,
                resid_three.T,
                resid_two.T,
                inputs.T,
                hidden_pre.astype(BF16).T,
                packed.reshape(3 * HEADS, hdim, sequence_span),
            ],
            [w_down, w_up, w_out, w_qkv],
            [
                log_total.reshape(HEADS, sequence_span),
                segment_ids,
                segment_ids.reshape(sequence_span, 1),
                gain_columns,
                cosine[:, 0, :].T,
                sine[:, 0, :].T,
            ],
            small,
        )
        gains = lax.dynamic_slice_in_dim(sums, (place * 2 + core) * share, share, 1)
        grad_bias = lax.dynamic_slice_in_dim(sums[3], core * half, half, 0)
    else:
        grad_head = lax.psum_scatter(
            contract_rows(collected_rows, cotangent), "dp", scatter_dimension=0, tiled=True
        )
        grad_three, grad_gain_final = rms_backward(
            resid_three, inverse_three, gain_final, grad_final_t.T
        )
        grad_mlp_out = grad_three.astype(jnp.bfloat16)
        grad_hidden = contract_cols(grad_mlp_out, w_down)
        sigmoid = jax.nn.sigmoid(hidden_pre)
        grad_pre = (grad_hidden * sigmoid * (1.0 + hidden_pre * (1.0 - sigmoid))).astype(BF16)
        grad_norm_two, grad_gain_mlp = rms_backward(
            resid_two, inverse_two, gain_mlp, contract_cols(grad_pre, w_up)
        )
        grad_two = grad_three + grad_norm_two
        grad_branch = grad_two.astype(jnp.bfloat16)
        grad_mixed = (
            contract_cols(grad_branch, w_out)
            .astype(jnp.bfloat16)
            .reshape(rows, sequence_span, HEADS, hdim)
        )
        grad_query, grad_key, grad_value = lax.map(
            lambda items: attend_backward(items, scale),
            (query, key, value, segment_ids, log_total, grad_mixed),
        )
        grad_query = unrotate(grad_query, cosine, sine)
        grad_key = unrotate(grad_key, cosine, sine)
        grad_proj = (
            jnp.stack([grad_query, grad_key, grad_value], axis=2)
            .reshape(rows * sequence_span, 3 * width)
            .astype(jnp.bfloat16)
        )
        grad_norm_one, grad_gain_attn = rms_backward(
            tokens, inverse_one, gain_attn, contract_cols(grad_proj, w_qkv)
        )
        entry_sensitivity_matrix = grad_two + grad_norm_one
        grad_down = scatter_rows(hidden, grad_mlp_out)
        grad_up = scatter_rows(act_two, grad_pre)
        grad_out = scatter_rows(mixed, grad_branch)
        grad_qkv = scatter_rows(act_one, grad_proj)
        gains = sum_everywhere(jnp.stack([grad_gain_attn, grad_gain_mlp, grad_gain_final]), True)
        gains = lax.dynamic_slice_in_dim(gains, (place * 2 + core) * share, share, 1)
        grad_bias = sum_everywhere(bias_local, False)
    return (
        predicted_levels,
        entry_sensitivity_matrix,
        gains[0],
        grad_qkv,
        grad_out,
        gains[1],
        grad_up,
        grad_down,
        gains[2],
        grad_head,
        grad_bias,
    )


def solution(mesh):
    return jax.shard_map(
        per_device,
        mesh=mesh,
        in_specs=(
            P(("dp", "head"), None),
            P(("dp", "head"), None),
            P(),
            P(),
            P(),
            P(),
            P(),
            P(),
            P(),
            P(None, "head"),
            P("head"),
            P("dp", "head"),
        ),
        out_specs=(
            P("dp", "head"),
            P(("dp", "head"), None),
            P(("dp", "head")),
            P(("dp", "head"), None),
            P(("dp", "head"), None),
            P(("dp", "head")),
            P(("dp", "head"), None),
            P(("dp", "head"), None),
            P(("dp", "head")),
            P("dp", "head"),
            P("head"),
        ),
        check_vma=False,
    )
```

```python
import functools
import math

import jax
import jax.numpy as jnp
import numpy as np
from jax import lax
from jax.experimental import pallas as pl
from jax.experimental.pallas import tpu as pltpu
from jax.sharding import PartitionSpec as P

HEADS = 16
F32 = jnp.float32
BF16 = jnp.bfloat16

epsilon = 1e-06


def rms_forward(values, gain):
    inverse = lax.rsqrt(jnp.mean(values * values, axis=-1, keepdims=True) + epsilon)
    return (values * inverse * gain, inverse)


def rms_backward(values, inverse, gain, grad):
    normed = values * inverse
    scaled = grad * gain
    grad_gain = jnp.sum(grad * normed, axis=0)
    grad_values = inverse * (scaled - normed * jnp.mean(scaled * normed, axis=-1, keepdims=True))
    return (grad_values, grad_gain)


def rotary_tables(sequence_span, hdim):
    half = hdim // 2
    freq = 10000.0 ** (-jnp.arange(half, dtype=jnp.float32) / half)
    angle = jnp.arange(sequence_span, dtype=jnp.float32)[:, None] * freq[None, :]
    return (jnp.cos(angle)[:, None, :], jnp.sin(angle)[:, None, :])


def rotate(values, cosine, sine):
    half = values.shape[-1] // 2
    first = values[..., :half]
    second = values[..., half:]
    return jnp.concatenate(
        [first * cosine - second * sine, second * cosine + first * sine], axis=-1
    )


def unrotate(grads, cosine, sine):
    half = grads.shape[-1] // 2
    first = grads[..., :half]
    second = grads[..., half:]
    return jnp.concatenate(
        [first * cosine + second * sine, second * cosine - first * sine], axis=-1
    )


def allowed_mask(segs):
    place = jnp.arange(segs.shape[0])
    return (segs[:, None] == segs[None, :]) & (place[:, None] >= place[None, :])


def row_scores(query, key, segs, scale):
    scores = jnp.einsum("qhd,khd->hqk", query, key, preferred_element_type=jnp.float32) * scale
    allowed = allowed_mask(segs)[None]
    return (jnp.where(allowed, scores, -1e30), allowed)


def attend_forward(items, scale):
    query, key, value, segs = items
    scores, allowed = row_scores(query, key, segs, scale)
    peak = jnp.max(scores, axis=-1, keepdims=True)
    expo = jnp.exp(scores - peak)
    overall_number = jnp.sum(expo, axis=-1, keepdims=True)
    probs = (expo / overall_number).astype(jnp.bfloat16)
    attended = jnp.einsum("hqk,khd->qhd", probs, value, preferred_element_type=jnp.float32)
    return (attended.astype(jnp.bfloat16), peak + jnp.log(overall_number))


def attend_backward(items, scale):
    query, key, value, segs, log_total, grad_attended = items
    scores, allowed = row_scores(query, key, segs, scale)
    probs = jnp.where(allowed, jnp.exp(scores - log_total), 0.0)
    grad_value = jnp.einsum(
        "hqk,qhd->khd",
        probs.astype(jnp.bfloat16),
        grad_attended,
        preferred_element_type=jnp.float32,
    )
    grad_probs = jnp.einsum(
        "qhd,khd->hqk", grad_attended, value, preferred_element_type=jnp.float32
    )
    grad_scores = (
        probs * (grad_probs - jnp.sum(grad_probs * probs, axis=-1, keepdims=True))
    ).astype(jnp.bfloat16)
    grad_query = (
        jnp.einsum("hqk,khd->qhd", grad_scores, key, preferred_element_type=jnp.float32) * scale
    )
    grad_key = (
        jnp.einsum("hqk,qhd->khd", grad_scores, query, preferred_element_type=jnp.float32) * scale
    )
    return (grad_query, grad_key, grad_value)


def contract_rows(left, right):
    return lax.dot_general(
        left, right, (((0,), (0,)), ((), ())), preferred_element_type=jnp.float32
    )


def contract_cols(left, right):
    return lax.dot_general(
        left, right, (((1,), (1,)), ((), ())), preferred_element_type=jnp.float32
    )


def swap_cores(values):
    return lax.ppermute(values, "head", [(0, 1), (1, 0)])


def flip(values, bit):
    size = lax.axis_size("dp")
    return lax.ppermute(values, "dp", [(i, i ^ bit) for i in range(size)])


def scatter_rows(left, right):
    return lax.psum_scatter(
        contract_rows(left, right), ("dp", "head"), scatter_dimension=0, tiled=True
    )


def sum_everywhere(values, over_head):
    size = lax.axis_size("dp")
    if over_head:
        values = values + swap_cores(values)
    bit = 1
    while bit < size:
        values = values + flip(values, bit)
        bit *= 2
    return values


MESH = pl.DeviceIdType.MESH


def chunk_table(width, hidden):
    table = [(0, 0)]
    table += [(1, j) for j in range(hidden // width)]
    table += [(2, j) for j in range(hidden // width)]
    table += [(3, 0)]
    table += [(4, j) for j in range(3)]
    return table


def nt(left, right):
    return lax.dot_general(
        left, right, (((1,), (1,)), ((), ())), preferred_element_type=jnp.float32
    )


def nn(left, right):
    return jnp.dot(left, right, preferred_element_type=jnp.float32)


def tt(left, right):
    return lax.dot_general(
        left, right, (((0,), (0,)), ((), ())), preferred_element_type=jnp.float32
    )


def columns_of(rows, scratch):
    scratch[...] = jnp.zeros_like(scratch)
    for i, row in enumerate(rows):
        scratch[i : i + 1] = row[...]
    return scratch[...].T


def mask_of(seg_row, bias):
    tokens = bias.shape[0]
    ids = seg_row[...].astype(F32)
    wide = jnp.broadcast_to(ids, (8, tokens)).T[:, :1]
    own = lax.broadcasted_iota(jnp.int32, (tokens, tokens), 0)
    asked = lax.broadcasted_iota(jnp.int32, (tokens, tokens), 1)
    bias[...] = jnp.where((wide == ids) & (own <= asked), 0.0, -1e30)


STRIP = 128
SLOTS = 4


def forward_kernel(
    x,
    w_qkv,
    w_out,
    w_up,
    w_down,
    seg_row,
    gain_attn,
    gain_mlp,
    gain_final,
    cosine,
    sine,
    y_t,
    g_t,
    a2_t,
    o_t,
    a1_t,
    x3_t,
    x2_t,
    x_t,
    h_t,
    qkv_t,
    lse,
    weights,
    xin,
    xt,
    act1,
    act2,
    final,
    mixed,
    qkv,
    res2,
    res3,
    hbuf,
    gbuf,
    bias,
    keys,
    gains,
    gain_rows,
    weight_sem,
    in_sem,
    out_sem,
    h_sem,
    g_sem,
):
    width, tokens = res2.shape
    hidden = h_t.shape[0]
    pieces = hidden // width
    half = width // 2
    count = HEADS
    hdim = width // count
    scale = 1.0 / math.sqrt(hdim)
    tiles = [w_qkv.at[:, k * width : (k + 1) * width] for k in range(3)] + [w_out]
    for k in range(pieces):
        tiles.append(w_up.at[:, k * width : (k + 1) * width])
        tiles.append(w_down.at[k * width : (k + 1) * width])

    def fetch(k):
        return pltpu.make_async_copy(tiles[k], weights.at[k % SLOTS], weight_sem.at[k % SLOTS])

    def used(k):
        if k + SLOTS < len(tiles):
            fetch(k + SLOTS).start()

    fetch_x = pltpu.make_async_copy(x, xin, in_sem)
    fetch_x.start()
    for k in range(SLOTS):
        fetch(k).start()

    gains[...] = columns_of((gain_attn, gain_mlp, gain_final), gain_rows)
    mask_of(seg_row, bias)
    fetch_x.wait()
    xt[...] = xin[...].T
    outs = []

    def put(source, target):
        copy = pltpu.make_async_copy(source, target, out_sem.at[len(outs)])
        outs.append(copy)
        copy.start()

    put(xt, x_t)

    def squares_of(ref):
        def step(k, total):
            v = ref[pl.ds(pl.multiple_of(k * STRIP, STRIP), STRIP)].astype(F32)
            return total + jnp.sum(v * v, axis=0, keepdims=True)

        return lax.fori_loop(0, width // STRIP, step, jnp.zeros((1, tokens), F32))

    def normalize(ref, index, to):
        inverse = lax.rsqrt(squares_of(ref) / width + epsilon)

        @pl.loop(0, width // STRIP)
        def _(k):
            rows = pl.ds(pl.multiple_of(k * STRIP, STRIP), STRIP)
            to[rows] = (ref[rows].astype(F32) * inverse * gains[rows, index : index + 1]).astype(
                BF16
            )

    normalize(xt, 0, act1)
    put(act1, a1_t)

    turn = hdim // 2
    for part in range(3):
        fetch(part).wait()
        for lower in range(2):
            value = tt(
                weights[part % SLOTS, :, lower * half : (lower + 1) * half], act1[...]
            )
            if part == 2:
                qkv[2 * width + lower * half : 2 * width + (lower + 1) * half] = value.astype(BF16)
                continue
            for head in range(count // 2):
                one = value[head * hdim : head * hdim + turn]
                two = value[head * hdim + turn : (head + 1) * hdim]
                turned = jnp.concatenate(
                    [one * cosine[...] - two * sine[...], two * cosine[...] + one * sine[...]],
                    axis=0,
                )
                base = part * width + lower * half + head * hdim
                qkv[base : base + hdim] = turned.astype(BF16)
        used(part)
    put(qkv, qkv_t)

    @pl.loop(0, count)
    def _(head):
        def rows_of(part):
            return pl.ds(pl.multiple_of(part * width + head * hdim, 16), hdim)

        q_t = qkv[rows_of(0)]
        v_t = qkv[rows_of(2)]
        keys[...] = qkv[rows_of(1)].T
        for b in range(tokens // STRIP):
            low, high = max(0, (b - 2) * STRIP), (b + 1) * STRIP
            asked = slice(b * STRIP, (b + 1) * STRIP)
            scores = nn(keys[low:high], q_t[:, asked]) * scale + bias[low:high, asked]
            peak = jnp.max(scores, axis=0, keepdims=True)
            expo = jnp.exp(scores - peak)
            amount = jnp.sum(expo, axis=0, keepdims=True)
            probs = (expo * (1.0 / amount)).astype(BF16)
            mixed[rows_of(0), asked] = nn(v_t[:, low:high], probs).astype(BF16)
            lse[head, :, asked] = peak + jnp.log(amount)

    put(mixed, o_t)

    fetch(3).wait()
    for lower in range(2):
        rows = slice(lower * half, (lower + 1) * half)
        res2[rows] = xt[rows].astype(F32) + tt(weights[3 % SLOTS, :, rows], mixed[...])
    used(3)
    put(res2, x2_t)
    normalize(res2, 1, act2)
    put(act2, a2_t)

    def h_copy(k):
        return pltpu.make_async_copy(
            hbuf.at[k % 2], h_t.at[k * width : (k + 1) * width], h_sem.at[k % 2]
        )

    def g_copy(k):
        return pltpu.make_async_copy(
            gbuf.at[k % 2], g_t.at[k * width : (k + 1) * width], g_sem.at[k % 2]
        )

    for k in range(pieces):
        up, down = 4 + 2 * k, 5 + 2 * k
        fetch(up).wait()
        if k >= 2:
            h_copy(k - 2).wait()
            g_copy(k - 2).wait()
        for lower in range(2):
            rows = slice(lower * half, (lower + 1) * half)
            value = tt(weights[up % SLOTS, :, rows], act2[...])
            hbuf[k % 2, rows] = value.astype(BF16)
            gbuf[k % 2, rows] = (value / (1.0 + jnp.exp(-value))).astype(BF16)
        used(up)
        h_copy(k).start()
        g_copy(k).start()
        fetch(down).wait()
        for lower in range(2):
            rows = slice(lower * half, (lower + 1) * half)
            base = res2 if k == 0 else res3
            res3[rows] = base[rows] + tt(weights[down % SLOTS, :, rows], gbuf[k % 2])
        used(down)
    put(res3, x3_t)
    normalize(res3, 2, final)
    put(final, y_t)
    for copy in outs:
        copy.wait()
    for k in range(max(0, pieces - 2), pieces):
        h_copy(k).wait()
        g_copy(k).wait()


def run_forward(x, w_qkv, w_out, w_up, w_down, segs, gains, cosine, sine):
    tokens, width = x.shape
    hidden = w_up.shape[1]
    hdim = width // HEADS
    hbm = pl.BlockSpec(memory_space=pl.ANY)
    vmem = pl.BlockSpec(memory_space=pltpu.VMEM)
    flat = (width, tokens)
    shapes = [
        jax.ShapeDtypeStruct(shape, dtype)
        for shape, dtype in (
            (flat, BF16),
            ((hidden, tokens), BF16),
            (flat, BF16),
            (flat, BF16),
            (flat, BF16),
            (flat, F32),
            (flat, F32),
            (flat, BF16),
            ((hidden, tokens), BF16),
            ((3 * width, tokens), BF16),
            ((HEADS, 1, tokens), F32),
        )
    ]
    dma = pltpu.SemaphoreType.DMA
    return pl.pallas_call(
        forward_kernel,
        out_shape=shapes,
        in_specs=[hbm] * 5 + [vmem] * 6,
        out_specs=[hbm] * 10 + [vmem],
        scratch_shapes=[
            pltpu.VMEM((SLOTS, width, width), BF16),
            pltpu.VMEM((tokens, width), BF16),
            pltpu.VMEM(flat, BF16),
            pltpu.VMEM(flat, BF16),
            pltpu.VMEM(flat, BF16),
            pltpu.VMEM(flat, BF16),
            pltpu.VMEM(flat, BF16),
            pltpu.VMEM((3 * width, tokens), BF16),
            pltpu.VMEM(flat, F32),
            pltpu.VMEM(flat, F32),
            pltpu.VMEM((2,) + flat, BF16),
            pltpu.VMEM((2,) + flat, BF16),
            pltpu.VMEM((tokens, tokens), F32),
            pltpu.VMEM((tokens, hdim), BF16),
            pltpu.VMEM((width, 8), F32),
            pltpu.VMEM((8, width), F32),
            dma((SLOTS,)),
            dma(()),
            dma((8,)),
            dma((2,)),
            dma((2,)),
        ],
        compiler_params=pltpu.CompilerParams(vmem_limit_bytes=58 << 20),
        name="forward",
    )(x, w_qkv, w_out, w_up, w_down, segs, *gains, cosine, sine)


LEAD = 3


def backward_kernel(
    table,
    size,
    y_t,
    g_t,
    a2_t,
    o_t,
    a1_t,
    cot,
    w_head,
    y_flat,
    x3_t,
    x2_t,
    x_t,
    h_t,
    qkv_t,
    w_down,
    w_up,
    w_out,
    w_qkv,
    lse,
    seg_row,
    gain_attn,
    gain_mlp,
    gain_final,
    head_bias,
    cosine,
    sine,
    out_head,
    out_down,
    out_up,
    out_out,
    out_qkv,
    out_small,
    out_entry,
    out_levels,
    y_o,
    g_o,
    a2_o,
    o_o,
    a1_o,
    e3_o,
    eh_o,
    e2_o,
    ep_o,
    eh_mine,
    y_flat_o,
    lbuf,
    rbuf,
    cbuf,
    grad,
    recv1,
    pair,
    recv2,
    line,
    recv_up,
    recv_down,
    total,
    sums,
    sums_in,
    dx,
    work,
    acc,
    ebuf,
    bias,
    gsum,
    gains,
    gain_rows,
    wrows,
    wcols,
    hbuf,
    ehbuf,
    ep,
    eo,
    heads,
    keys,
    values,
    eq_acc,
    ek_acc,
    ev_acc,
    obuf,
    push_send,
    push_recv,
    left_sem,
    right_sem,
    send1_sem,
    recv1_sem,
    send2_sem,
    recv2_sem,
    up_send,
    up_recv,
    down_send,
    down_recv,
    local_sem,
    swap_send,
    swap_recv,
    small_send,
    small_recv,
    row_sem,
    col_sem,
    h_sem,
    eh_out_sem,
    eh_in_sem,
    head_sem,
    fetch_sem,
    entry_sem,
):
    n = len(table)
    length = size // 4
    me = lax.axis_index("dp")
    core = lax.axis_index("head")
    other = 1 - core
    xi = lax.rem(me, 2)
    yi = lax.rem(me // 2, 2)
    zi = me // 4
    width, tokens = dx.shape
    hidden = h_t.shape[0]
    cols = width // 2
    block = width // size
    count, hdim = eo.shape[:2]
    scale = 1.0 / math.sqrt(hdim)
    flip_x = me + 1 - 2 * xi
    flip_y = me + 2 * (1 - 2 * yi)
    first_bit = jnp.where(core == 0, xi, yi)
    second_bit = jnp.where(core == 0, yi, xi)
    first_peer = jnp.where(core == 0, flip_x, flip_y)
    second_peer = jnp.where(core == 0, flip_y, flip_x)
    far = lax.rem(me + size // 2, size)
    near = me + 4 * (1 - 2 * lax.rem(zi, 2))
    rings = recv1.shape[0]
    ring2 = recv2.shape[0]
    ring_line = line.shape[0]

    fetch_head_weight = pltpu.make_async_copy(w_head, wcols.at[0], fetch_sem.at[0])
    fetch_x3 = pltpu.make_async_copy(x3_t, work, fetch_sem.at[1])
    fetch_x2 = pltpu.make_async_copy(x2_t, work, fetch_sem.at[1])
    fetch_x = pltpu.make_async_copy(x_t, ebuf, fetch_sem.at[0])
    fetch_head_weight.start()
    fetch_x3.start()

    def local_c(half, which):
        start = pl.multiple_of(which * tokens, 16)
        return pltpu.make_async_copy(
            cot.at[pl.ds(start, tokens)], cbuf.at[half], fetch_sem.at[2 + half]
        )

    local_c(0, core).start()
    local_c(1, other).start()

    barrier = pltpu.get_barrier_semaphore()
    for index, which in ((me, other), (flip_x, core), (flip_y, core), (far, core)):
        pl.semaphore_signal(barrier, inc=1, device_id=(index, which), device_id_type=MESH)

    @pl.when(zi > 0)
    def _():
        pl.semaphore_signal(barrier, inc=1, device_id=(me - 4, core), device_id_type=MESH)

    @pl.when(zi < length - 1)
    def _():
        pl.semaphore_signal(barrier, inc=1, device_id=(me + 4, core), device_id_type=MESH)

    inner = jnp.where(zi > 0, 1, 0) + jnp.where(zi < length - 1, 1, 0)
    pl.semaphore_wait(barrier, 4 + inner)

    def remote(src, dst, send, recv, index, which):
        return pltpu.make_async_remote_copy(
            src_ref=src,
            dst_ref=dst,
            send_sem=send,
            recv_sem=recv,
            device_id=(index, which),
            device_id_type=MESH,
        )

    lefts = (y_t, g_t, a2_t, o_t, a1_t)
    left_others = (y_o, g_o, a2_o, o_o, a1_o)
    pieces = hidden // width

    def push(k):
        if k == 0 or k > pieces:
            if k == 0:
                src, dst = y_t, y_o
            elif k <= pieces + 3:
                src, dst = lefts[k - pieces + 1], left_others[k - pieces + 1]
            elif k == pieces + 7:
                src, dst = y_flat, y_flat_o
            elif k == pieces + 8:
                src, dst = ehbuf, hbuf
            elif k == pieces + 6:
                wide = 3 * cols
                src, dst = ep.at[pl.ds(pl.multiple_of(other * wide, 16), wide)], ep_o
            else:
                src = ebuf.at[pl.ds(pl.multiple_of(other * cols, 16), cols)]
                dst = (e3_o, e2_o)[k - pieces - 4]
        else:
            part = pl.ds((k - 1) * block, block)
            src, dst = g_t.at[:, part, :], g_o.at[:, part, :]
        return remote(src, dst, push_send.at[k], push_recv.at[k], me, other)

    PA2, PO, PA1, PE3, PE2, PEP, PY, PDY = (pieces + i for i in range(1, 9))

    push(0).start()
    gains[...] = columns_of((gain_attn, gain_mlp, gain_final), gain_rows)
    gsum[...] = jnp.zeros_like(gsum)
    fetch_head_weight.wait()
    local_c(1, other).wait()
    for i in range(2):
        ehbuf[i] = nt(wcols[0, i * cols : (i + 1) * cols], cbuf[1]).astype(BF16)
    push(PDY).start()
    push(1).start()

    def left_copies(c, slot):
        i, j = table[c]
        lower = pl.ds(j * block, block) if i == 1 else slice(None)
        return [
            pltpu.make_async_copy(
                source.at[:, lower, :], lbuf.at[slot, half], left_sem.at[slot, half]
            )
            for half, source in ((0, lefts[i]), (1, left_others[i]))
        ]

    def left_arrives(c):
        i, j = table[c]
        if i == 0:
            push(0).wait_recv()
        elif i == 1:
            push(1 + j).wait_recv()
        elif j == 0:
            push((None, None, PA2, PO, PA1)[i]).wait_recv()

    def start_left(c):
        left_arrives(c)
        for copy in left_copies(c, c % 2):
            copy.start()

    def start_right(c):
        i, j = table[c]
        slot = c % 2
        mine = pl.ds(pl.multiple_of(core * cols, 16), cols)
        rows = pl.ds(j * cols, cols)
        if i == 1:
            own, its = ebuf.at[mine], e3_o
            if j == 0:
                push(PE3).wait_recv()
        elif i == 2:
            own, its = eh_mine.at[rows], eh_o.at[rows]
            if j == 0:
                for piece in range(pieces):
                    eh_push(piece, 0).wait_recv()
        elif i == 3:
            own, its = ebuf.at[mine], e2_o
            push(PE2).wait_recv()
        else:
            start = pl.multiple_of(core * 3 * cols + j * cols, 16)
            own, its = ep.at[pl.ds(start, cols)], ep_o.at[rows]
            if j == 0:
                push(PEP).wait_recv()
        pltpu.make_async_copy(own, rbuf.at[slot, 0], right_sem.at[slot, 0]).start()
        pltpu.make_async_copy(its, rbuf.at[slot, 1], right_sem.at[slot, 1]).start()

    def eh_push(piece, slot):
        return remote(
            ehbuf.at[slot],
            eh_o.at[pl.ds(piece * cols, cols)],
            eh_out_sem.at[slot],
            eh_in_sem.at[piece],
            me,
            other,
        )

    def wait_left(slot):
        for half in range(2):
            pltpu.make_async_copy(
                lbuf.at[slot, half], lbuf.at[slot, half], left_sem.at[slot, half]
            ).wait()

    def wait_right(slot):
        for half in range(2):
            pltpu.make_async_copy(
                rbuf.at[slot, half], rbuf.at[slot, half], right_sem.at[slot, half]
            ).wait()

    def form(slot, ring, right, multiply):
        @pl.loop(0, length)
        def _(z):
            rows = pl.ds(z * 4, 4)
            value = None
            for half in range(2):
                left = lbuf[slot, half, rows].reshape(4 * block, tokens)
                part = multiply(left, right[half])
                value = part if value is None else value + part
            value = value.astype(BF16)
            for q in range(4):
                x, y = q % 2, q // 2
                one = jnp.where(core == 0, x, y)
                two = jnp.where(core == 0, y, x)
                grad[ring, one, two, z] = value[q * block : (q + 1) * block]

    def send1(c):
        ring, spot = lax.rem(c, LEAD), lax.rem(c, rings)
        return remote(
            grad.at[ring, 1 - first_bit],
            recv1.at[spot],
            send1_sem.at[ring],
            recv1_sem.at[spot],
            first_peer,
            core,
        )

    def send2(c):
        ring, spot = lax.rem(c, 2), lax.rem(c, ring2)
        return remote(
            pair.at[ring, 1 - second_bit],
            recv2.at[spot],
            send2_sem.at[ring],
            recv2_sem.at[spot],
            second_peer,
            core,
        )

    def send_up(c, step):
        ring, spot = lax.rem(c, ring_line), lax.rem(c, rings)
        return remote(
            line.at[ring, jnp.minimum(zi + (length - step), length - 1)],
            recv_up.at[spot, step - 1],
            up_send.at[ring, step - 1],
            up_recv.at[spot, step - 1],
            jnp.minimum(me + 4, size - 1),
            core,
        )

    def send_down(c, step):
        ring, spot = lax.rem(c, ring_line), lax.rem(c, rings)
        return remote(
            line.at[ring, jnp.maximum(zi - (length - step), 0)],
            recv_down.at[spot, step - 1],
            down_send.at[ring, step - 1],
            down_recv.at[spot, step - 1],
            jnp.maximum(me - 4, 0),
            core,
        )

    def start_line(c, step):
        @pl.when(zi < step)
        def _():
            send_up(c, step).start()

        @pl.when(zi >= length - step)
        def _():
            send_down(c, step).start()

    def wait_line_sent(c, step):
        @pl.when(zi < step)
        def _():
            send_up(c, step).wait_send()

        @pl.when(zi >= length - step)
        def _():
            send_down(c, step).wait_send()

    def results(c):
        i, j = table[c]
        if i == 0:
            return [pltpu.make_async_copy(total.at[c], out_head, local_sem.at[c])]
        if i == 1:
            target = out_down.at[
                pl.ds((j % 2) * block, block), pl.ds(pl.multiple_of(core * cols, 128), cols)
            ]
            return [
                pltpu.make_async_copy(total.at[c], target, local_sem.at[c]),
                remote(total.at[c], target, swap_send.at[c], swap_recv.at[c], me, other),
            ]
        target = (None, None, out_up, out_out, out_qkv)[i]
        wide = target.shape[1] // 2
        place = target.at[:, pl.ds(pl.multiple_of(core * wide + j * cols, 128), cols)]
        half = block // 2
        mine = pl.ds(pl.multiple_of(core * half, 8), half)
        its = pl.ds(pl.multiple_of(other * half, 8), half)
        return [
            pltpu.make_async_copy(total.at[c, mine], place, local_sem.at[c]),
            remote(total.at[c, its], place, swap_send.at[c], swap_recv.at[c], me, other),
        ]

    def start_results(c):
        i, j = table[c]
        copies = results(c)
        if i == 1:
            owner = j // (pieces // 2)
            pl.when(core == owner)(copies[0].start)
            pl.when(core != owner)(copies[1].start)
        else:
            for copy in copies:
                copy.start()

    def end_results(c):
        i, j = table[c]
        copies = results(c)
        if i == 1:
            owner = j // (pieces // 2)
            pl.when(core == owner)(copies[0].wait)
            pl.when(core == owner)(copies[1].wait_recv)
            pl.when(core != owner)(copies[1].wait_send)
        else:
            for copy in copies:
                copy.wait()

    def exchange(t):
        @pl.when(t < n)
        def _():
            c = t
            send1(c).wait_recv()
            ring, spot, to = lax.rem(c, LEAD), lax.rem(c, rings), lax.rem(c, 2)

            @pl.when(c >= 2)
            def _():
                send2(c - 2).wait_send()

            for two in range(2):

                @pl.loop(0, length)
                def _(z):
                    pair[to, two, z] = (
                        grad[ring, first_bit, two, z].astype(F32)
                        + recv1[spot, two, z].astype(F32)
                    ).astype(BF16)

            send2(c).start()

        @pl.when((t >= 1) & (t <= n))
        def _():
            c = t - 1
            send2(c).wait_recv()
            ring, spot, to = lax.rem(c, 2), lax.rem(c, ring2), lax.rem(c, ring_line)

            @pl.loop(0, length)
            def _(z):
                line[to, z] = (
                    pair[ring, second_bit, z].astype(F32) + recv2[spot, z].astype(F32)
                ).astype(BF16)

            start_line(c, 1)

        for step in range(1, length):

            @pl.when((t >= 1 + step) & (t <= n + step))
            def _():
                c = t - 1 - step
                ring, at = lax.rem(c, ring_line), lax.rem(c, rings)
                last = step == length - 1
                up_in = (zi >= 1) & (zi <= step)
                down_in = (zi <= length - 2) & (zi >= length - 1 - step)

                @pl.when(up_in)
                def _():
                    send_up(c, step).wait_recv()
                    spot = jnp.minimum(zi + (length - 1 - step), length - 1)
                    if not last:
                        line[ring, spot] = (
                            line[ring, spot].astype(F32) + recv_up[at, step - 1].astype(F32)
                        ).astype(BF16)

                @pl.when(down_in)
                def _():
                    send_down(c, step).wait_recv()
                    spot = jnp.maximum(zi - (length - 1 - step), 0)
                    if not last:
                        line[ring, spot] = (
                            line[ring, spot].astype(F32) + recv_down[at, step - 1].astype(F32)
                        ).astype(BF16)

                if not last:
                    start_line(c, step + 1)
                else:
                    total[c] = line[ring, zi].astype(F32)

                    @pl.when(up_in)
                    def _():
                        total[c] = total[c] + recv_up[at, step - 1].astype(F32)

                    @pl.when(down_in)
                    def _():
                        total[c] = total[c] + recv_down[at, step - 1].astype(F32)

                    for back in range(1, length):
                        wait_line_sent(c, back)

                    for d in range(n):

                        @pl.when(c == d)
                        def _():
                            start_results(d)

    strip = 128
    strips = width // strip

    def norm_backward(vref, eref, index, emit):
        def sums_of(k, carry):
            squares, products = carry
            rows = pl.ds(pl.multiple_of(k * strip, strip), strip)
            v = vref[rows].astype(F32)
            e = eref[rows]
            gain = gains[rows, index : index + 1]
            squares = squares + jnp.sum(v * v, axis=0, keepdims=True)
            products = products + jnp.sum(e * gain * v, axis=0, keepdims=True)
            return squares, products

        blank = jnp.zeros((1, tokens), F32)
        squares, products = lax.fori_loop(0, strips, sums_of, (blank, blank))
        inverse = lax.rsqrt(squares / width + epsilon)
        mean = products * inverse / width

        @pl.loop(0, strips)
        def _(k):
            rows = pl.ds(pl.multiple_of(k * strip, strip), strip)
            normed = vref[rows].astype(F32) * inverse
            e = eref[rows]
            gain = gains[rows, index : index + 1]
            gsum[rows, index : index + 1] = jnp.sum(e * normed, axis=1, keepdims=True)
            emit(k, rows, inverse * (e * gain - normed * mean))

    start_left(0)
    local_c(0, core).wait()
    for i in range(2):
        dx[i * cols : (i + 1) * cols] = nt(wcols[0, i * cols : (i + 1) * cols], cbuf[0])
    sums[0] = jnp.zeros_like(sums[0])
    for i in range(2):
        share = jnp.sum(cbuf[i].astype(F32), axis=0, keepdims=True)
        at = pl.ds(pl.multiple_of(core * cols, 128), cols)
        sums[0, 3:4, at] = sums[0, 3:4, at] + share
    wait_left(0)
    form(0, 0, [cbuf[0], cbuf[1]], nn)
    send1(0).start()

    def emit_final(k, rows, value):
        dx[rows] = value
        ebuf[rows] = value.astype(BF16)

    push(PDY).wait_recv()
    for i in range(2):
        dx[i * cols : (i + 1) * cols] += hbuf[i].astype(F32)
    fetch_x3.wait()
    norm_backward(work, dx, 2, emit_final)
    push(PE3).start()
    for k in range(2, pieces + 1):
        push(k).start()
    fetch_x2.start()
    start_left(1)
    start_left(2)
    push(PDY).wait_send()
    for c in range(1, LEAD):
        start_right(c)
        wait_left(c % 2)
        wait_right(c % 2)
        form(c % 2, c, [rbuf[c % 2, 0], rbuf[c % 2, 1]], nt)
        send1(c).start()
        start_left(c + 2)
    push(PA2).start()
    push(PY).start()
    push(PO).start()
    push(PA1).start()

    def row_tile(k, slot, source):
        return pltpu.make_async_copy(
            source.at[pl.ds(pl.multiple_of(k * cols, 16), cols)], wrows.at[slot], row_sem.at[slot]
        )

    def col_tile(k, slot, source):
        return pltpu.make_async_copy(
            source.at[:, pl.ds(pl.multiple_of(k * cols, 128), cols)],
            wcols.at[slot],
            col_sem.at[slot],
        )

    def h_tile(k, slot):
        return pltpu.make_async_copy(
            h_t.at[pl.ds(pl.multiple_of(k * cols, 16), cols)], hbuf.at[slot], h_sem.at[slot]
        )

    def mlp_tiles(k):
        return jnp.where(k < pieces, other, core) * pieces + lax.rem(k, pieces)

    def fetch_mlp(k):
        slot = lax.rem(k, 2)
        tile = mlp_tiles(k)
        row_tile(tile, slot, w_down).start()
        col_tile(tile, slot, w_up).start()
        h_tile(tile, slot).start()

    def mlp_step(k):
        slot = lax.rem(k, 2)
        tile = mlp_tiles(k)
        row_tile(tile, slot, w_down).wait()
        h_tile(tile, slot).wait()

        @pl.when((k >= 2) & (k < pieces + 2))
        def _():
            eh_push(0, slot).wait_send()

        @pl.when(k >= pieces + 2)
        def _():
            pltpu.make_async_copy(
                ehbuf.at[slot], eh_mine.at[pl.ds(0, cols)], eh_out_sem.at[slot]
            ).wait()

        part = cols // 2

        @pl.loop(0, 2)
        def _(i):
            rows = pl.ds(pl.multiple_of(i * part, 16), part)
            value = nn(wrows[slot, rows], ebuf[...])
            pre = hbuf[slot, rows].astype(F32)
            sig = 1.0 / (1.0 + jnp.exp(-pre))
            ehbuf[slot, rows] = (value * sig * (1.0 + pre * (1.0 - sig))).astype(BF16)

        where = lax.rem(k, pieces)

        @pl.when(k < pieces)
        def _():
            eh_push(where, slot).start()

        @pl.when(k >= pieces)
        def _():
            pltpu.make_async_copy(
                ehbuf.at[slot],
                eh_mine.at[pl.ds(pl.multiple_of(where * cols, 16), cols)],
                eh_out_sem.at[slot],
            ).start()

        col_tile(tile, slot, w_up).wait()
        accumulate(wcols.at[slot], ehbuf.at[slot], k == 0)

        @pl.when(k + 2 < 2 * pieces)
        def _():
            fetch_mlp(k + 2)

    def accumulate(left, right, first):
        part = width // 4

        @pl.loop(0, 4)
        def _(i):
            rows = pl.ds(pl.multiple_of(i * part, 16), part)
            value = nn(left[rows], right[...])

            @pl.when(first)
            def _():
                acc[rows] = value

            @pl.when(jnp.logical_not(first))
            def _():
                acc[rows] = acc[rows] + value

    fetch_mlp(0)
    fetch_mlp(1)

    def emit_mlp(k, rows, value):
        value = dx[rows] + value
        dx[rows] = value
        ebuf[rows] = value.astype(BF16)

    def middle():
        for slot in range(2):
            pltpu.make_async_copy(
                ehbuf.at[slot], eh_mine.at[pl.ds(0, cols)], eh_out_sem.at[slot]
            ).wait()
        row_tile(0, 0, w_out).start()
        row_tile(1, 1, w_out).start()
        push(PE3).wait_send()
        fetch_x2.wait()
        norm_backward(work, acc, 1, emit_mlp)
        push(PE2).start()

        @pl.loop(0, 2)
        def _(k):
            row_tile(k, k, w_out).wait()

            @pl.loop(0, 2)
            def _(i):
                part = cols // 2
                rows = pl.ds(pl.multiple_of(i * part, 16), part)
                group = part // hdim
                value = nn(wrows[k, rows], ebuf[...]).astype(BF16)
                eo[pl.ds((2 * k + i) * group, group)] = value.reshape(group, hdim, tokens)

        mask_of(seg_row, bias)
        pltpu.make_async_copy(w_head, wcols.at[0], col_sem.at[0]).start()
        pltpu.make_async_copy(y_flat, ehbuf, h_sem.at[0]).start()
        push(PY).wait_recv()
        pltpu.make_async_copy(y_flat_o, hbuf, h_sem.at[1]).start()

    def level_copy(k, which, slot):
        return pltpu.make_async_copy(
            obuf.at[slot],
            out_levels.at[
                pl.ds(pl.multiple_of(which * tokens, 8), tokens), k * strip : (k + 1) * strip
            ],
            entry_sem.at[slot],
        )

    def levels(source, which, number):
        pltpu.make_async_copy(y_flat, source, h_sem.at[number]).wait()
        if number == 0:
            pltpu.make_async_copy(w_head, wcols.at[0], col_sem.at[0]).wait()
        for k in range(cols // strip):
            slot = k % 2
            if k >= 2:
                level_copy(k - 2, which, slot).wait()
            part = slice(k * strip, (k + 1) * strip)
            obuf[slot] = (
                tt(source[0], wcols[0, :cols, part])
                + tt(source[1], wcols[0, cols:, part])
                + head_bias[:, part]
            )
            level_copy(k, which, slot).start()
        for k in range(cols // strip - 2, cols // strip):
            level_copy(k, which, k % 2).wait()

    per_turn = count // 4

    def fetch_head(head, slot):
        for part in range(3):
            pltpu.make_async_copy(
                qkv_t.at[pl.ds(pl.multiple_of(part * width + head * hdim, 16), hdim)],
                heads.at[slot, part],
                head_sem.at[slot, part],
            ).start()

    def attend(turn):
        @pl.when(turn == 0)
        def _():
            fetch_head(0, 0)

        @pl.loop(0, per_turn)
        def _(i):
            head = turn * per_turn + i
            slot = lax.rem(head, 2)
            for part in range(3):
                pltpu.make_async_copy(
                    heads.at[slot, part], heads.at[slot, part], head_sem.at[slot, part]
                ).wait()

            @pl.when(head + 1 < count)
            def _():
                fetch_head(head + 1, 1 - slot)

            q_t = heads[slot, 0]
            k_t = heads[slot, 1]
            v_t = heads[slot, 2]
            eo_t = eo[head]
            q = q_t.T
            e = eo_t.T
            keys[...] = k_t.T
            values[...] = v_t.T
            weight = lse[head]
            ek_acc[...] = jnp.zeros_like(ek_acc)
            ev_acc[...] = jnp.zeros_like(ev_acc)
            for b in range(tokens // strip):
                low, high = max(0, (b - 2) * strip), (b + 1) * strip
                asked = slice(b * strip, (b + 1) * strip)
                scores = nn(keys[low:high], q_t[:, asked]) * scale + bias[low:high, asked]
                p = jnp.exp(scores - weight[:, asked])
                ep_t = nn(values[low:high], eo_t[:, asked])
                share = jnp.sum(p * ep_t, axis=0, keepdims=True)
                es = (p * (ep_t - share)).astype(BF16)
                eq_acc[:, asked] = nn(k_t[:, low:high], es)
                ek_acc[low:high] += nn(es, q[asked])
                ev_acc[low:high] += nn(p.astype(BF16), e[asked])
            half = hdim // 2
            for part, value in ((0, eq_acc[...]), (1, ek_acc[...].T)):
                one, two = value[:half] * scale, value[half:] * scale
                turned = jnp.concatenate(
                    [one * cosine[...] + two * sine[...], two * cosine[...] - one * sine[...]],
                    axis=0,
                )
                to = pl.ds(pl.multiple_of(part * width + head * hdim, 16), hdim)
                ep[to] = turned.astype(BF16)
            to = pl.ds(pl.multiple_of(2 * width + head * hdim, 16), hdim)
            ep[to] = ev_acc[...].T.astype(BF16)

        @pl.when(turn == 3)
        def _():
            push(PEP).start()

    def fetch_qkv(k):
        col_tile(k, lax.rem(k, 2), w_qkv).start()

    def qkv_step(k):
        slot = lax.rem(k, 2)
        col_tile(k, slot, w_qkv).wait()
        rows = pl.ds(pl.multiple_of(k * cols, 16), cols)
        accumulate(wcols.at[slot], ep.at[rows], k == 0)

        @pl.when(k + 2 < 6)
        def _():
            fetch_qkv(k + 2)

    def entry_copy(k, slot):
        return pltpu.make_async_copy(
            obuf.at[slot],
            out_entry.at[:, pl.ds(pl.multiple_of(k * strip, strip), strip)],
            entry_sem.at[slot],
        )

    def emit_entry(k, rows, value):
        slot = lax.rem(k, 2)

        @pl.when(k >= 2)
        def _():
            entry_copy(k, slot).wait()

        obuf[slot] = (dx[rows] + value).T
        entry_copy(k, slot).start()

    peers = ((me, other), (flip_x, core), (flip_y, core), (near, core), (far, core))
    steps = len(peers)

    def small_copy(i):
        return remote(
            sums.at[i], sums_in.at[i], small_send.at[i], small_recv.at[i], peers[i][0], peers[i][1]
        )

    def last():
        fetch_x.wait()
        norm_backward(ebuf, acc, 0, emit_entry)
        for slot in range(2):
            entry_copy(0, slot).wait()
        sums[0] = sums[0] + gsum[...].T[: sums.shape[1]]
        small_copy(0).start()

    @pl.loop(0, n + length)
    def _(t):
        for c in range(LEAD, n):

            @pl.when(t == c - LEAD)
            def _():
                start_right(c)

        @pl.when(t < 2)
        def _():
            @pl.loop(0, pieces)
            def _(i):
                mlp_step(t * pieces + i)

        @pl.when(t == 2)
        def _():
            middle()

        @pl.when((t >= 3) & (t < 7))
        def _():
            attend(t - 3)

        @pl.when(t == 3)
        def _():
            levels(ehbuf, core, 0)

        @pl.when(t == 4)
        def _():
            levels(hbuf, other, 1)

        @pl.when(t == 6)
        def _():
            fetch_qkv(0)
            fetch_qkv(1)

        @pl.when((t == 7) | (t == 8))
        def _():
            @pl.loop(0, 3)
            def _(i):
                qkv_step((t - 7) * 3 + i)

        @pl.when(t == 9)
        def _():
            last()

        for i in range(steps):

            @pl.when(t == 10 + i)
            def _():
                small_copy(i).wait()
                value = sums[i] + sums_in[i]
                if i == steps - 1:
                    out_small[...] = value
                else:
                    sums[i + 1] = value
                    small_copy(i + 1).start()

        exchange(t)

        @pl.when(t + LEAD < n)
        def _():
            c = t + LEAD
            slot = lax.rem(c, 2)
            wait_left(slot)
            wait_right(slot)
            send1(t).wait_send()
            form(slot, lax.rem(c, LEAD), [rbuf[slot, 0], rbuf[slot, 1]], nt)
            send1(c).start()
            for d in range(LEAD + 2, n):

                @pl.when(c == d - 2)
                def _():
                    start_left(d)

        @pl.when(t == 8)
        def _():
            push(PE2).wait_send()
            fetch_x.start()

    for c in range(n):
        end_results(c)
    for c in range(n - LEAD, n):
        send1(c).wait_send()
    for c in range(n - 2, n):
        send2(c).wait_send()
    for k in range(pieces + 9):
        if k not in (PE3, PE2, PDY):
            push(k).wait_send()


def run_backward(lefts, others, weights, tables):
    size = lax.axis_size("dp")
    width, tokens = lefts[0].shape
    hidden = lefts[1].shape[0]
    block = width // size
    cols = width // 2
    table = chunk_table(width, hidden)
    n = len(table)
    length = size // 4
    share = block // 2
    hdim = width // HEADS
    hbm = pl.BlockSpec(memory_space=pl.ANY)
    vmem = pl.BlockSpec(memory_space=pltpu.VMEM)
    lefts = [left.reshape(size, left.shape[0] // size, tokens) for left in lefts]
    shapes = [
        jax.ShapeDtypeStruct((block, cols), F32),
        jax.ShapeDtypeStruct((hidden // size // 2, width), F32),
        jax.ShapeDtypeStruct((share, hidden), F32),
        jax.ShapeDtypeStruct((share, width), F32),
        jax.ShapeDtypeStruct((share, 3 * width), F32),
        jax.ShapeDtypeStruct((8, width), F32),
        jax.ShapeDtypeStruct((tokens, width), F32),
        jax.ShapeDtypeStruct((2 * tokens, cols), F32),
    ]
    shapes += [jax.ShapeDtypeStruct(left.shape, BF16) for left in lefts]
    shapes += [
        jax.ShapeDtypeStruct((rows, tokens), BF16)
        for rows in (cols, hidden // 2, cols, 3 * cols, hidden // 2)
    ]
    shapes += [jax.ShapeDtypeStruct((2, cols, tokens), BF16)]
    dma = pltpu.SemaphoreType.DMA
    ring1, ring2, ring_line = 6, 4, length + 1
    results = pl.pallas_call(
        functools.partial(backward_kernel, table, size),
        out_shape=shapes,
        in_specs=[hbm] * 17 + [vmem] * 8,
        out_specs=[hbm] * 5 + [vmem] + [hbm] * 13,
        scratch_shapes=[
            pltpu.VMEM((2, 2, size, block, tokens), BF16),
            pltpu.VMEM((2, 2, cols, tokens), BF16),
            pltpu.VMEM((2, tokens, cols), BF16),
            pltpu.VMEM((LEAD, 2, 2, length, block, cols), BF16),
            pltpu.VMEM((ring1, 2, length, block, cols), BF16),
            pltpu.VMEM((2, 2, length, block, cols), BF16),
            pltpu.VMEM((ring2, length, block, cols), BF16),
            pltpu.VMEM((ring_line, length, block, cols), BF16),
            pltpu.VMEM((ring1, length - 1, block, cols), BF16),
            pltpu.VMEM((ring1, length - 1, block, cols), BF16),
            pltpu.VMEM((n, block, cols), F32),
            pltpu.VMEM((5, 8, width), F32),
            pltpu.VMEM((5, 8, width), F32),
            pltpu.VMEM((width, tokens), F32),
            pltpu.VMEM((width, tokens), F32),
            pltpu.VMEM((width, tokens), F32),
            pltpu.VMEM((width, tokens), BF16),
            pltpu.VMEM((tokens, tokens), F32),
            pltpu.VMEM((width, 128), F32),
            pltpu.VMEM((width, 8), F32),
            pltpu.VMEM((8, width), F32),
            pltpu.VMEM((2, cols, width), BF16),
            pltpu.VMEM((2, width, cols), BF16),
            pltpu.VMEM((2, cols, tokens), BF16),
            pltpu.VMEM((2, cols, tokens), BF16),
            pltpu.VMEM((3 * width, tokens), BF16),
            pltpu.VMEM((HEADS, hdim, tokens), BF16),
            pltpu.VMEM((2, 3, hdim, tokens), BF16),
            pltpu.VMEM((tokens, hdim), BF16),
            pltpu.VMEM((tokens, hdim), BF16),
            pltpu.VMEM((hdim, tokens), F32),
            pltpu.VMEM((tokens, hdim), F32),
            pltpu.VMEM((tokens, hdim), F32),
            pltpu.VMEM((2, tokens, 128), F32),
            dma((hidden // width + 9,)),
            dma((hidden // width + 9,)),
            dma((2, 2)),
            dma((2, 2)),
            dma((LEAD,)),
            dma((ring1,)),
            dma((2,)),
            dma((ring2,)),
            dma((ring_line, length - 1)),
            dma((ring1, length - 1)),
            dma((ring_line, length - 1)),
            dma((ring1, length - 1)),
            dma((n,)),
            dma((n,)),
            dma((n,)),
            dma((5,)),
            dma((5,)),
            dma((2,)),
            dma((2,)),
            dma((2,)),
            dma((2,)),
            dma((hidden // width,)),
            dma((2, 3)),
            dma((4,)),
            dma((2,)),
        ],
        compiler_params=pltpu.CompilerParams(
            collective_id=0, has_side_effects=True, vmem_limit_bytes=62 << 20
        ),
        name="backward",
    )(*lefts, *others, *weights, *tables)
    return results[:8]


def per_device(
    inputs,
    segment_ids,
    gain_attn,
    w_qkv,
    w_out,
    gain_mlp,
    w_up,
    w_down,
    gain_final,
    head_projection_weight,
    head_output_bias,
    cotangent,
):
    core = lax.axis_index("head")
    place = lax.axis_index("dp")
    size = lax.axis_size("dp")
    rows, sequence_span = segment_ids.shape
    count, width = inputs.shape
    hdim = width // HEADS
    scale = 1.0 / math.sqrt(hdim)
    share = width // (2 * size)
    fused = size == HEADS and lax.axis_size("head") == 2 and rows == 1

    if fused:
        half = width // 2
        turn = hdim // 2
        freq = np.float32(10000.0) ** (-np.arange(turn, dtype=np.float32) / np.float32(turn))
        angle = np.arange(sequence_span, dtype=np.float32)[None, :] * freq[:, None]
        cosine_t, sine_t = jnp.asarray(np.cos(angle)), jnp.asarray(np.sin(angle))
        gain_rows = [gain[None] for gain in (gain_attn, gain_mlp, gain_final)]
        y_t, g_t, a2_t, o_t, a1_t, x3_t, x2_t, x_t, h_t, qkv_t, lse = run_forward(
            inputs, w_qkv, w_out, w_up, w_down, segment_ids, gain_rows, cosine_t, sine_t
        )
        (
            grad_head,
            grad_down,
            grad_up,
            grad_out,
            grad_qkv,
            sums,
            entry_sensitivity_matrix,
            predicted_levels,
        ) = run_backward(
            [y_t, g_t, a2_t, o_t, a1_t],
            [
                cotangent,
                head_projection_weight,
                y_t.reshape(2, half, count),
                x3_t,
                x2_t,
                x_t,
                h_t,
                qkv_t,
            ],
            [w_down, w_up, w_out, w_qkv],
            [lse, segment_ids, *gain_rows, head_output_bias[None], cosine_t, sine_t],
        )
        gains = lax.dynamic_slice_in_dim(sums, (place * 2 + core) * share, share, 1)
        grad_bias = lax.dynamic_slice_in_dim(sums[3], core * half, half, 0)
    else:
        other_rows = lax.dynamic_slice_in_dim(cotangent, (1 - core) * count, count, 0)
        own_rows = lax.dynamic_slice_in_dim(cotangent, core * count, count, 0)
        got = swap_cores(contract_cols(head_projection_weight, other_rows).astype(BF16))
        grad_final_t = contract_cols(head_projection_weight, own_rows) + got.astype(F32)
        bias_local = jnp.sum(cotangent, axis=0, dtype=F32)

        cosine, sine = rotary_tables(sequence_span, hdim)
        tokens = inputs.astype(jnp.float32)
        normed_one, inverse_one = rms_forward(tokens, gain_attn)
        act_one = normed_one.astype(jnp.bfloat16)
        projected = jnp.dot(act_one, w_qkv, preferred_element_type=jnp.float32).reshape(
            rows, sequence_span, 3, HEADS, hdim
        )
        query = rotate(projected[:, :, 0], cosine, sine).astype(jnp.bfloat16)
        key = rotate(projected[:, :, 1], cosine, sine).astype(jnp.bfloat16)
        value = projected[:, :, 2].astype(jnp.bfloat16)
        attended, log_total = lax.map(
            lambda items: attend_forward(items, scale), (query, key, value, segment_ids)
        )
        mixed = attended.reshape(rows * sequence_span, width)
        resid_two = tokens + jnp.dot(mixed, w_out, preferred_element_type=jnp.float32)
        normed_two, inverse_two = rms_forward(resid_two, gain_mlp)
        act_two = normed_two.astype(jnp.bfloat16)
        hidden_pre = jnp.dot(act_two, w_up, preferred_element_type=jnp.float32)
        hidden = jax.nn.silu(hidden_pre).astype(jnp.bfloat16)
        resid_three = resid_two + jnp.dot(hidden, w_down, preferred_element_type=jnp.float32)
        normed_three, inverse_three = rms_forward(resid_three, gain_final)
        final_hidden = normed_three.astype(jnp.bfloat16)
        other_hidden = swap_cores(final_hidden)
        collected_rows = jnp.concatenate(
            [
                jnp.where(core == 0, final_hidden, other_hidden),
                jnp.where(core == 0, other_hidden, final_hidden),
            ],
            axis=0,
        )
        predicted_levels = (
            jnp.dot(collected_rows, head_projection_weight, preferred_element_type=jnp.float32)
            + head_output_bias
        )
        grad_head = lax.psum_scatter(
            contract_rows(collected_rows, cotangent), "dp", scatter_dimension=0, tiled=True
        )
        grad_three, grad_gain_final = rms_backward(
            resid_three, inverse_three, gain_final, grad_final_t.T
        )
        grad_mlp_out = grad_three.astype(jnp.bfloat16)
        grad_hidden = contract_cols(grad_mlp_out, w_down)
        sigmoid = jax.nn.sigmoid(hidden_pre)
        grad_pre = (grad_hidden * sigmoid * (1.0 + hidden_pre * (1.0 - sigmoid))).astype(BF16)
        grad_norm_two, grad_gain_mlp = rms_backward(
            resid_two, inverse_two, gain_mlp, contract_cols(grad_pre, w_up)
        )
        grad_two = grad_three + grad_norm_two
        grad_branch = grad_two.astype(jnp.bfloat16)
        grad_mixed = (
            contract_cols(grad_branch, w_out)
            .astype(jnp.bfloat16)
            .reshape(rows, sequence_span, HEADS, hdim)
        )
        grad_query, grad_key, grad_value = lax.map(
            lambda items: attend_backward(items, scale),
            (query, key, value, segment_ids, log_total, grad_mixed),
        )
        grad_query = unrotate(grad_query, cosine, sine)
        grad_key = unrotate(grad_key, cosine, sine)
        grad_proj = (
            jnp.stack([grad_query, grad_key, grad_value], axis=2)
            .reshape(rows * sequence_span, 3 * width)
            .astype(jnp.bfloat16)
        )
        grad_norm_one, grad_gain_attn = rms_backward(
            tokens, inverse_one, gain_attn, contract_cols(grad_proj, w_qkv)
        )
        entry_sensitivity_matrix = grad_two + grad_norm_one
        grad_down = scatter_rows(hidden, grad_mlp_out)
        grad_up = scatter_rows(act_two, grad_pre)
        grad_out = scatter_rows(mixed, grad_branch)
        grad_qkv = scatter_rows(act_one, grad_proj)
        gains = sum_everywhere(jnp.stack([grad_gain_attn, grad_gain_mlp, grad_gain_final]), True)
        gains = lax.dynamic_slice_in_dim(gains, (place * 2 + core) * share, share, 1)
        grad_bias = sum_everywhere(bias_local, False)
    return (
        predicted_levels,
        entry_sensitivity_matrix,
        gains[0],
        grad_qkv,
        grad_out,
        gains[1],
        grad_up,
        grad_down,
        gains[2],
        grad_head,
        grad_bias,
    )


def solution(mesh):
    return jax.shard_map(
        per_device,
        mesh=mesh,
        in_specs=(
            P(("dp", "head"), None),
            P(("dp", "head"), None),
            P(),
            P(),
            P(),
            P(),
            P(),
            P(),
            P(),
            P(None, "head"),
            P("head"),
            P("dp", "head"),
        ),
        out_specs=(
            P("dp", "head"),
            P(("dp", "head"), None),
            P(("dp", "head")),
            P(("dp", "head"), None),
            P(("dp", "head"), None),
            P(("dp", "head")),
            P(("dp", "head"), None),
            P(("dp", "head"), None),
            P(("dp", "head")),
            P("dp", "head"),
            P("head"),
        ),
        check_vma=False,
    )
```

```python
import functools
import math

import jax
import jax.numpy as jnp
import numpy as np
from jax import lax
from jax.experimental import pallas as pl
from jax.experimental.pallas import tpu as pltpu
from jax.sharding import PartitionSpec as P

HEADS = 16
F32 = jnp.float32
BF16 = jnp.bfloat16

epsilon = 1e-06


def rms_forward(values, gain):
    inverse = lax.rsqrt(jnp.mean(values * values, axis=-1, keepdims=True) + epsilon)
    return (values * inverse * gain, inverse)


def rms_backward(values, inverse, gain, grad):
    normed = values * inverse
    scaled = grad * gain
    grad_gain = jnp.sum(grad * normed, axis=0)
    grad_values = inverse * (scaled - normed * jnp.mean(scaled * normed, axis=-1, keepdims=True))
    return (grad_values, grad_gain)


def rotary_tables(sequence_span, hdim):
    half = hdim // 2
    freq = 10000.0 ** (-jnp.arange(half, dtype=jnp.float32) / half)
    angle = jnp.arange(sequence_span, dtype=jnp.float32)[:, None] * freq[None, :]
    return (jnp.cos(angle)[:, None, :], jnp.sin(angle)[:, None, :])


def rotate(values, cosine, sine):
    half = values.shape[-1] // 2
    first = values[..., :half]
    second = values[..., half:]
    return jnp.concatenate(
        [first * cosine - second * sine, second * cosine + first * sine], axis=-1
    )


def unrotate(grads, cosine, sine):
    half = grads.shape[-1] // 2
    first = grads[..., :half]
    second = grads[..., half:]
    return jnp.concatenate(
        [first * cosine + second * sine, second * cosine - first * sine], axis=-1
    )


def allowed_mask(segs):
    place = jnp.arange(segs.shape[0])
    return (segs[:, None] == segs[None, :]) & (place[:, None] >= place[None, :])


def row_scores(query, key, segs, scale):
    scores = jnp.einsum("qhd,khd->hqk", query, key, preferred_element_type=jnp.float32) * scale
    allowed = allowed_mask(segs)[None]
    return (jnp.where(allowed, scores, -1e30), allowed)


def attend_forward(items, scale):
    query, key, value, segs = items
    scores, allowed = row_scores(query, key, segs, scale)
    peak = jnp.max(scores, axis=-1, keepdims=True)
    expo = jnp.exp(scores - peak)
    overall_number = jnp.sum(expo, axis=-1, keepdims=True)
    probs = (expo / overall_number).astype(jnp.bfloat16)
    attended = jnp.einsum("hqk,khd->qhd", probs, value, preferred_element_type=jnp.float32)
    return (attended.astype(jnp.bfloat16), peak + jnp.log(overall_number))


def attend_backward(items, scale):
    query, key, value, segs, log_total, grad_attended = items
    scores, allowed = row_scores(query, key, segs, scale)
    probs = jnp.where(allowed, jnp.exp(scores - log_total), 0.0)
    grad_value = jnp.einsum(
        "hqk,qhd->khd",
        probs.astype(jnp.bfloat16),
        grad_attended,
        preferred_element_type=jnp.float32,
    )
    grad_probs = jnp.einsum(
        "qhd,khd->hqk", grad_attended, value, preferred_element_type=jnp.float32
    )
    grad_scores = (
        probs * (grad_probs - jnp.sum(grad_probs * probs, axis=-1, keepdims=True))
    ).astype(jnp.bfloat16)
    grad_query = (
        jnp.einsum("hqk,khd->qhd", grad_scores, key, preferred_element_type=jnp.float32) * scale
    )
    grad_key = (
        jnp.einsum("hqk,qhd->khd", grad_scores, query, preferred_element_type=jnp.float32) * scale
    )
    return (grad_query, grad_key, grad_value)


def contract_rows(left, right):
    return lax.dot_general(
        left, right, (((0,), (0,)), ((), ())), preferred_element_type=jnp.float32
    )


def contract_cols(left, right):
    return lax.dot_general(
        left, right, (((1,), (1,)), ((), ())), preferred_element_type=jnp.float32
    )


def swap_cores(values):
    return lax.ppermute(values, "head", [(0, 1), (1, 0)])


def flip(values, bit):
    size = lax.axis_size("dp")
    return lax.ppermute(values, "dp", [(i, i ^ bit) for i in range(size)])


def scatter_rows(left, right):
    return lax.psum_scatter(
        contract_rows(left, right), ("dp", "head"), scatter_dimension=0, tiled=True
    )


def sum_everywhere(values, over_head):
    size = lax.axis_size("dp")
    if over_head:
        values = values + swap_cores(values)
    bit = 1
    while bit < size:
        values = values + flip(values, bit)
        bit *= 2
    return values


MESH = pl.DeviceIdType.MESH


def chunk_table(width, hidden):
    table = [(0, 0)]
    table += [(1, j) for j in range(hidden // width)]
    table += [(2, j) for j in range(hidden // width)]
    table += [(3, 0)]
    table += [(4, j) for j in range(3)]
    return table


def nt(left, right):
    return lax.dot_general(
        left, right, (((1,), (1,)), ((), ())), preferred_element_type=jnp.float32
    )


def nn(left, right):
    return jnp.dot(left, right, preferred_element_type=jnp.float32)


def tt(left, right):
    return lax.dot_general(
        left, right, (((0,), (0,)), ((), ())), preferred_element_type=jnp.float32
    )


def columns_of(rows, scratch):
    scratch[...] = jnp.zeros_like(scratch)
    for i, row in enumerate(rows):
        scratch[i : i + 1] = row[...]
    return scratch[...].T


def mask_of(seg_row, bias):
    tokens = bias.shape[0]
    ids = seg_row[...].astype(F32)
    wide = jnp.broadcast_to(ids, (8, tokens)).T[:, :1]
    own = lax.broadcasted_iota(jnp.int32, (tokens, tokens), 0)
    asked = lax.broadcasted_iota(jnp.int32, (tokens, tokens), 1)
    bias[...] = jnp.where((wide == ids) & (own <= asked), 0.0, -1e30)


STRIP = 128
SLOTS = 4
REACH = 256
TOGETHER = 2


def query_blocks(tokens):
    for start in range(0, tokens, REACH):
        stop = min(start + REACH, tokens)
        yield max(0, start - REACH), stop, slice(start, stop)


def forward_kernel(
    x,
    w_qkv,
    w_out,
    w_up,
    w_down,
    seg_row,
    gain_attn,
    gain_mlp,
    gain_final,
    cosine,
    sine,
    y_t,
    g_t,
    a2_t,
    o_t,
    a1_t,
    x3_t,
    x2_t,
    x_t,
    h_t,
    qkv_t,
    lse,
    weights,
    xin,
    xt,
    act1,
    act2,
    final,
    mixed,
    qkv,
    res2,
    res3,
    hbuf,
    gbuf,
    bias,
    gains,
    gain_rows,
    weight_sem,
    in_sem,
    out_sem,
    h_sem,
    g_sem,
):
    width, tokens = res2.shape
    hidden = h_t.shape[0]
    pieces = hidden // width
    half = width // 2
    count = HEADS
    hdim = width // count
    scale = 1.0 / math.sqrt(hdim)
    tiles = [w_qkv.at[:, k * width : (k + 1) * width] for k in range(3)] + [w_out]
    for k in range(pieces):
        tiles.append(w_up.at[:, k * width : (k + 1) * width])
        tiles.append(w_down.at[k * width : (k + 1) * width])

    def fetch(k):
        return pltpu.make_async_copy(tiles[k], weights.at[k % SLOTS], weight_sem.at[k % SLOTS])

    def used(k):
        if k + SLOTS < len(tiles):
            fetch(k + SLOTS).start()

    fetch_x = pltpu.make_async_copy(x, xin, in_sem)
    fetch_x.start()
    for k in range(SLOTS):
        fetch(k).start()

    gains[...] = columns_of((gain_attn, gain_mlp, gain_final), gain_rows)
    mask_of(seg_row, bias)
    fetch_x.wait()
    xt[...] = xin[...].T
    outs = []

    def put(source, target):
        copy = pltpu.make_async_copy(source, target, out_sem.at[len(outs)])
        outs.append(copy)
        copy.start()

    put(xt, x_t)

    def squares_of(ref):
        def step(k, total):
            v = ref[pl.ds(pl.multiple_of(k * STRIP, STRIP), STRIP)].astype(F32)
            return total + jnp.sum(v * v, axis=0, keepdims=True)

        return lax.fori_loop(0, width // STRIP, step, jnp.zeros((1, tokens), F32))

    def normalize(ref, index, to):
        inverse = lax.rsqrt(squares_of(ref) / width + epsilon)

        @pl.loop(0, width // STRIP)
        def _(k):
            rows = pl.ds(pl.multiple_of(k * STRIP, STRIP), STRIP)
            to[rows] = (ref[rows].astype(F32) * inverse * gains[rows, index : index + 1]).astype(
                BF16
            )

    normalize(xt, 0, act1)
    put(act1, a1_t)

    turn = hdim // 2
    for part in range(3):
        fetch(part).wait()
        for lower in range(2):
            value = tt(
                weights[part % SLOTS, :, lower * half : (lower + 1) * half], act1[...]
            )
            if part == 2:
                qkv[2 * width + lower * half : 2 * width + (lower + 1) * half] = value.astype(BF16)
                continue
            for head in range(count // 2):
                one = value[head * hdim : head * hdim + turn]
                two = value[head * hdim + turn : (head + 1) * hdim]
                turned = jnp.concatenate(
                    [one * cosine[...] - two * sine[...], two * cosine[...] + one * sine[...]],
                    axis=0,
                )
                base = part * width + lower * half + head * hdim
                qkv[base : base + hdim] = turned.astype(BF16)
        used(part)
    put(qkv, qkv_t)

    def attend(head):
        def rows_of(part):
            return pl.ds(pl.multiple_of(part * width + head * hdim, 16), hdim)

        q_t = qkv[rows_of(0)]
        v_t = qkv[rows_of(2)]
        k = qkv[rows_of(1)].T
        for low, high, asked in query_blocks(tokens):
            scores = nn(k[low:high], q_t[:, asked]) * scale + bias[low:high, asked]
            peak = jnp.max(scores, axis=0, keepdims=True)
            expo = jnp.exp(scores - peak)
            amount = jnp.sum(expo, axis=0, keepdims=True)
            probs = (expo * (1.0 / amount)).astype(BF16)
            mixed[rows_of(0), asked] = nn(v_t[:, low:high], probs).astype(BF16)
            lse[head, :, asked] = peak + jnp.log(amount)

    @pl.loop(0, count // TOGETHER)
    def _(i):
        for u in range(TOGETHER):
            attend(i * TOGETHER + u)

    put(mixed, o_t)

    fetch(3).wait()
    for lower in range(2):
        rows = slice(lower * half, (lower + 1) * half)
        res2[rows] = xt[rows].astype(F32) + tt(weights[3 % SLOTS, :, rows], mixed[...])
    used(3)
    put(res2, x2_t)
    normalize(res2, 1, act2)
    put(act2, a2_t)

    def h_copy(k):
        return pltpu.make_async_copy(
            hbuf.at[k % 2], h_t.at[k * width : (k + 1) * width], h_sem.at[k % 2]
        )

    def g_copy(k):
        return pltpu.make_async_copy(
            gbuf.at[k % 2], g_t.at[k * width : (k + 1) * width], g_sem.at[k % 2]
        )

    for k in range(pieces):
        up, down = 4 + 2 * k, 5 + 2 * k
        fetch(up).wait()
        if k >= 2:
            h_copy(k - 2).wait()
            g_copy(k - 2).wait()
        for lower in range(2):
            rows = slice(lower * half, (lower + 1) * half)
            value = tt(weights[up % SLOTS, :, rows], act2[...])
            hbuf[k % 2, rows] = value.astype(BF16)
            gbuf[k % 2, rows] = (value / (1.0 + jnp.exp(-value))).astype(BF16)
        used(up)
        h_copy(k).start()
        g_copy(k).start()
        fetch(down).wait()
        for lower in range(2):
            rows = slice(lower * half, (lower + 1) * half)
            base = res2 if k == 0 else res3
            res3[rows] = base[rows] + tt(weights[down % SLOTS, :, rows], gbuf[k % 2])
        used(down)
    put(res3, x3_t)
    normalize(res3, 2, final)
    put(final, y_t)
    for copy in outs:
        copy.wait()
    for k in range(max(0, pieces - 2), pieces):
        h_copy(k).wait()
        g_copy(k).wait()


def run_forward(x, w_qkv, w_out, w_up, w_down, segs, gains, cosine, sine):
    tokens, width = x.shape
    hidden = w_up.shape[1]
    hdim = width // HEADS
    hbm = pl.BlockSpec(memory_space=pl.ANY)
    vmem = pl.BlockSpec(memory_space=pltpu.VMEM)
    flat = (width, tokens)
    shapes = [
        jax.ShapeDtypeStruct(shape, dtype)
        for shape, dtype in (
            (flat, BF16),
            ((hidden, tokens), BF16),
            (flat, BF16),
            (flat, BF16),
            (flat, BF16),
            (flat, F32),
            (flat, F32),
            (flat, BF16),
            ((hidden, tokens), BF16),
            ((3 * width, tokens), BF16),
            ((HEADS, 1, tokens), F32),
        )
    ]
    dma = pltpu.SemaphoreType.DMA
    return pl.pallas_call(
        forward_kernel,
        out_shape=shapes,
        in_specs=[hbm] * 5 + [vmem] * 6,
        out_specs=[hbm] * 10 + [vmem],
        scratch_shapes=[
            pltpu.VMEM((SLOTS, width, width), BF16),
            pltpu.VMEM((tokens, width), BF16),
            pltpu.VMEM(flat, BF16),
            pltpu.VMEM(flat, BF16),
            pltpu.VMEM(flat, BF16),
            pltpu.VMEM(flat, BF16),
            pltpu.VMEM(flat, BF16),
            pltpu.VMEM((3 * width, tokens), BF16),
            pltpu.VMEM(flat, F32),
            pltpu.VMEM(flat, F32),
            pltpu.VMEM((2,) + flat, BF16),
            pltpu.VMEM((2,) + flat, BF16),
            pltpu.VMEM((tokens, tokens), F32),
            pltpu.VMEM((width, 8), F32),
            pltpu.VMEM((8, width), F32),
            dma((SLOTS,)),
            dma(()),
            dma((8,)),
            dma((2,)),
            dma((2,)),
        ],
        compiler_params=pltpu.CompilerParams(vmem_limit_bytes=58 << 20),
        name="forward",
    )(x, w_qkv, w_out, w_up, w_down, segs, *gains, cosine, sine)


LEAD = 3


def backward_kernel(
    table,
    size,
    y_t,
    g_t,
    a2_t,
    o_t,
    a1_t,
    cot,
    w_head,
    y_flat,
    x3_t,
    x2_t,
    x_t,
    h_t,
    qkv_t,
    w_down,
    w_up,
    w_out,
    w_qkv,
    lse,
    seg_row,
    gain_attn,
    gain_mlp,
    gain_final,
    head_bias,
    cosine,
    sine,
    out_head,
    out_down,
    out_up,
    out_out,
    out_qkv,
    out_small,
    out_entry,
    out_levels,
    y_o,
    g_o,
    a2_o,
    o_o,
    a1_o,
    e3_o,
    eh_o,
    e2_o,
    ep_o,
    eh_mine,
    y_flat_o,
    lbuf,
    rbuf,
    cbuf,
    grad,
    recv1,
    pair,
    recv2,
    line,
    recv_up,
    recv_down,
    side,
    side_up,
    side_down,
    side1,
    side2,
    total,
    sums,
    sums_in,
    dx,
    work,
    acc,
    ebuf,
    bias,
    gains,
    gain_rows,
    wrows,
    wcols,
    hbuf,
    ehbuf,
    ep,
    eo,
    heads,
    obuf,
    push_send,
    push_recv,
    left_sem,
    right_sem,
    send1_sem,
    recv1_sem,
    send2_sem,
    recv2_sem,
    up_send,
    up_recv,
    down_send,
    down_recv,
    side_up_send,
    side_up_recv,
    side_down_send,
    side_down_recv,
    side1_send,
    side1_recv,
    side2_send,
    side2_recv,
    local_sem,
    swap_send,
    swap_recv,
    small_send,
    small_recv,
    row_sem,
    col_sem,
    h_sem,
    eh_out_sem,
    eh_in_sem,
    head_sem,
    fetch_sem,
    entry_sem,
):
    n = len(table)
    length = size // 4
    me = lax.axis_index("dp")
    core = lax.axis_index("head")
    other = 1 - core
    xi = lax.rem(me, 2)
    yi = lax.rem(me // 2, 2)
    zi = me // 4
    width, tokens = dx.shape
    hidden = h_t.shape[0]
    cols = width // 2
    block = width // size
    count, hdim = eo.shape[:2]
    scale = 1.0 / math.sqrt(hdim)
    flip_x = me + 1 - 2 * xi
    flip_y = me + 2 * (1 - 2 * yi)
    first_bit = jnp.where(core == 0, xi, yi)
    second_bit = jnp.where(core == 0, yi, xi)
    first_peer = jnp.where(core == 0, flip_x, flip_y)
    second_peer = jnp.where(core == 0, flip_y, flip_x)
    far = lax.rem(me + size // 2, size)
    near = me + 4 * (1 - 2 * lax.rem(zi, 2))
    rings = recv1.shape[0]
    ring2 = recv2.shape[0]
    ring_line = line.shape[0]
    ring_side, ring_in = side.shape[0], side1.shape[0]
    main = grad.shape[-1]

    fetch_head_weight = pltpu.make_async_copy(w_head, wcols.at[0], fetch_sem.at[0])
    fetch_x3 = pltpu.make_async_copy(x3_t, work, fetch_sem.at[1])
    fetch_x2 = pltpu.make_async_copy(x2_t, work, fetch_sem.at[1])
    fetch_x = pltpu.make_async_copy(x_t, ebuf, fetch_sem.at[0])
    fetch_head_weight.start()
    fetch_x3.start()

    def local_c(half, which):
        start = pl.multiple_of(which * tokens, 16)
        return pltpu.make_async_copy(
            cot.at[pl.ds(start, tokens)], cbuf.at[half], fetch_sem.at[2 + half]
        )

    local_c(0, core).start()
    local_c(1, other).start()

    barrier = pltpu.get_barrier_semaphore()
    for index, which in ((me, other), (flip_x, core), (flip_y, core), (far, core)):
        pl.semaphore_signal(barrier, inc=1, device_id=(index, which), device_id_type=MESH)

    @pl.when(zi > 0)
    def _():
        pl.semaphore_signal(barrier, inc=1, device_id=(me - 4, core), device_id_type=MESH)

    @pl.when(zi < length - 1)
    def _():
        pl.semaphore_signal(barrier, inc=1, device_id=(me + 4, core), device_id_type=MESH)

    inner = jnp.where(zi > 0, 1, 0) + jnp.where(zi < length - 1, 1, 0)
    pl.semaphore_wait(barrier, 4 + inner)

    def remote(src, dst, send, recv, index, which):
        return pltpu.make_async_remote_copy(
            src_ref=src,
            dst_ref=dst,
            send_sem=send,
            recv_sem=recv,
            device_id=(index, which),
            device_id_type=MESH,
        )

    lefts = (y_t, g_t, a2_t, o_t, a1_t)
    left_others = (y_o, g_o, a2_o, o_o, a1_o)
    pieces = hidden // width

    def push(k):
        if k == 0 or k > pieces:
            if k == 0:
                src, dst = y_t, y_o
            elif k <= pieces + 3:
                src, dst = lefts[k - pieces + 1], left_others[k - pieces + 1]
            elif k == pieces + 7:
                src, dst = y_flat, y_flat_o
            elif k == pieces + 8:
                src, dst = ehbuf, hbuf
            elif k == pieces + 6:
                wide = 3 * cols
                src, dst = ep.at[pl.ds(pl.multiple_of(other * wide, 16), wide)], ep_o
            else:
                src = ebuf.at[pl.ds(pl.multiple_of(other * cols, 16), cols)]
                dst = (e3_o, e2_o)[k - pieces - 4]
        else:
            part = pl.ds((k - 1) * block, block)
            src, dst = g_t.at[:, part, :], g_o.at[:, part, :]
        return remote(src, dst, push_send.at[k], push_recv.at[k], me, other)

    PA2, PO, PA1, PE3, PE2, PEP, PY, PDY = (pieces + i for i in range(1, 9))

    push(0).start()
    gains[...] = jnp.zeros_like(gains)
    gains[:, :8] = columns_of((gain_attn, gain_mlp, gain_final), gain_rows)
    fetch_head_weight.wait()
    local_c(1, other).wait()
    for i in range(2):
        ehbuf[i] = nt(wcols[0, i * cols : (i + 1) * cols], cbuf[1]).astype(BF16)
    push(PDY).start()
    push(1).start()

    def left_copies(c, slot):
        i, j = table[c]
        lower = pl.ds(j * block, block) if i == 1 else slice(None)
        return [
            pltpu.make_async_copy(
                source.at[:, lower, :], lbuf.at[slot, half], left_sem.at[slot, half]
            )
            for half, source in ((0, lefts[i]), (1, left_others[i]))
        ]

    def left_arrives(c):
        i, j = table[c]
        if i == 0:
            push(0).wait_recv()
        elif i == 1:
            push(1 + j).wait_recv()
        elif j == 0:
            push((None, None, PA2, PO, PA1)[i]).wait_recv()

    def start_left(c):
        left_arrives(c)
        for copy in left_copies(c, c % 2):
            copy.start()

    def start_right(c):
        i, j = table[c]
        slot = c % 2
        mine = pl.ds(pl.multiple_of(core * cols, 16), cols)
        rows = pl.ds(j * cols, cols)
        if i == 1:
            own, its = ebuf.at[mine], e3_o
            if j == 0:
                push(PE3).wait_recv()
        elif i == 2:
            own, its = eh_mine.at[rows], eh_o.at[rows]
            if j == 0:
                for piece in range(pieces):
                    eh_push(piece, 0).wait_recv()
        elif i == 3:
            own, its = ebuf.at[mine], e2_o
            push(PE2).wait_recv()
        else:
            start = pl.multiple_of(core * 3 * cols + j * cols, 16)
            own, its = ep.at[pl.ds(start, cols)], ep_o.at[rows]
            if j == 0:
                push(PEP).wait_recv()
        pltpu.make_async_copy(own, rbuf.at[slot, 0], right_sem.at[slot, 0]).start()
        pltpu.make_async_copy(its, rbuf.at[slot, 1], right_sem.at[slot, 1]).start()

    def eh_push(piece, slot):
        return remote(
            ehbuf.at[slot],
            eh_o.at[pl.ds(piece * cols, cols)],
            eh_out_sem.at[slot],
            eh_in_sem.at[piece],
            me,
            other,
        )

    def wait_left(slot):
        for half in range(2):
            pltpu.make_async_copy(
                lbuf.at[slot, half], lbuf.at[slot, half], left_sem.at[slot, half]
            ).wait()

    def wait_right(slot):
        for half in range(2):
            pltpu.make_async_copy(
                rbuf.at[slot, half], rbuf.at[slot, half], right_sem.at[slot, half]
            ).wait()

    def form(c, right, multiply):
        slot, ring, to = lax.rem(c, 2), lax.rem(c, LEAD), lax.rem(c, ring_side)

        for z in range(length):
            value = None
            for half in range(2):
                left = lbuf[slot, half, 4 * z : 4 * z + 4].reshape(4 * block, tokens)
                part = multiply(left, right[half])
                value = part if value is None else value + part
            value = value.astype(BF16)
            for q in range(4):
                x, y = q % 2, q // 2
                one = jnp.where(core == 0, x, y)
                two = jnp.where(core == 0, y, x)
                part = value[q * block : (q + 1) * block]
                grad[ring, one, two, z] = part[:, :main]
                side[to, z, one, two] = part[:, main:]
        send1(c).start()
        start_side(c, 1)

    def send1(c):
        ring, spot = lax.rem(c, LEAD), lax.rem(c, rings)
        return remote(
            grad.at[ring, 1 - first_bit],
            recv1.at[spot],
            send1_sem.at[ring],
            recv1_sem.at[spot],
            first_peer,
            core,
        )

    def send2(c):
        ring, spot = lax.rem(c, 2), lax.rem(c, ring2)
        return remote(
            pair.at[ring, 1 - second_bit],
            recv2.at[spot],
            send2_sem.at[ring],
            recv2_sem.at[spot],
            second_peer,
            core,
        )

    def send_up(c, step):
        ring, spot = lax.rem(c, ring_line), lax.rem(c, rings)
        return remote(
            line.at[ring, jnp.minimum(zi + (length - step), length - 1)],
            recv_up.at[spot, step - 1],
            up_send.at[ring, step - 1],
            up_recv.at[spot, step - 1],
            jnp.minimum(me + 4, size - 1),
            core,
        )

    def send_down(c, step):
        ring, spot = lax.rem(c, ring_line), lax.rem(c, rings)
        return remote(
            line.at[ring, jnp.maximum(zi - (length - step), 0)],
            recv_down.at[spot, step - 1],
            down_send.at[ring, step - 1],
            down_recv.at[spot, step - 1],
            jnp.maximum(me - 4, 0),
            core,
        )

    def side_send_up(c, step):
        ring, spot = lax.rem(c, ring_side), lax.rem(c, ring_in)
        return remote(
            side.at[ring, jnp.minimum(zi + (length - step), length - 1)],
            side_up.at[spot, step - 1],
            side_up_send.at[ring, step - 1],
            side_up_recv.at[spot, step - 1],
            jnp.minimum(me + 4, size - 1),
            core,
        )

    def side_send_down(c, step):
        ring, spot = lax.rem(c, ring_side), lax.rem(c, ring_in)
        return remote(
            side.at[ring, jnp.maximum(zi - (length - step), 0)],
            side_down.at[spot, step - 1],
            side_down_send.at[ring, step - 1],
            side_down_recv.at[spot, step - 1],
            jnp.maximum(me - 4, 0),
            core,
        )

    def side_send1(c):
        ring, spot = lax.rem(c, ring_side), lax.rem(c, ring_in)
        return remote(
            side.at[ring, zi, 1 - first_bit],
            side1.at[spot],
            side1_send.at[ring],
            side1_recv.at[spot],
            first_peer,
            core,
        )

    def side_send2(c):
        ring, spot = lax.rem(c, ring_side), lax.rem(c, ring_in)
        return remote(
            side.at[ring, zi, first_bit, 1 - second_bit],
            side2.at[spot],
            side2_send.at[ring],
            side2_recv.at[spot],
            second_peer,
            core,
        )

    def start_side(c, step):
        @pl.when(zi < step)
        def _():
            side_send_up(c, step).start()

        @pl.when(zi >= length - step)
        def _():
            side_send_down(c, step).start()

    def exchange_side(t):
        for step in range(1, length):

            @pl.when((t >= step - 1) & (t <= n + step - 2))
            def _():
                c = t - step + 1
                ring, at = lax.rem(c, ring_side), lax.rem(c, ring_in)
                up_in = (zi >= 1) & (zi <= step)
                down_in = (zi <= length - 2) & (zi >= length - 1 - step)

                @pl.when(up_in)
                def _():
                    side_send_up(c, step).wait_recv()
                    spot = jnp.minimum(zi + (length - 1 - step), length - 1)
                    side[ring, spot] = side[ring, spot] + side_up[at, step - 1]

                @pl.when(down_in)
                def _():
                    side_send_down(c, step).wait_recv()
                    spot = jnp.maximum(zi - (length - 1 - step), 0)
                    side[ring, spot] = side[ring, spot] + side_down[at, step - 1]

                if step < length - 1:
                    start_side(c, step + 1)
                else:
                    side_send1(c).start()

        @pl.when((t >= length - 1) & (t <= n + length - 2))
        def _():
            c = t - length + 1
            ring, at = lax.rem(c, ring_side), lax.rem(c, ring_in)
            side_send1(c).wait_recv()
            side[ring, zi, first_bit] = side[ring, zi, first_bit] + side1[at]
            side_send2(c).start()

        @pl.when((t >= length) & (t <= n + length - 1))
        def _():
            c = t - length
            ring, at = lax.rem(c, ring_side), lax.rem(c, ring_in)
            side_send2(c).wait_recv()
            total[c, :, main:] = side[ring, zi, first_bit, second_bit].astype(F32) + side2[
                at
            ].astype(F32)
            for back in range(1, length):

                @pl.when(zi < back)
                def _():
                    side_send_up(c, back).wait_send()

                @pl.when(zi >= length - back)
                def _():
                    side_send_down(c, back).wait_send()

            side_send1(c).wait_send()
            side_send2(c).wait_send()

    def start_line(c, step):
        @pl.when(zi < step)
        def _():
            send_up(c, step).start()

        @pl.when(zi >= length - step)
        def _():
            send_down(c, step).start()

    def wait_line_sent(c, step):
        @pl.when(zi < step)
        def _():
            send_up(c, step).wait_send()

        @pl.when(zi >= length - step)
        def _():
            send_down(c, step).wait_send()

    def results(c):
        i, j = table[c]
        if i == 0:
            return [pltpu.make_async_copy(total.at[c], out_head, local_sem.at[c])]
        if i == 1:
            target = out_down.at[
                pl.ds((j % 2) * block, block), pl.ds(pl.multiple_of(core * cols, 128), cols)
            ]
            return [
                pltpu.make_async_copy(total.at[c], target, local_sem.at[c]),
                remote(total.at[c], target, swap_send.at[c], swap_recv.at[c], me, other),
            ]
        target = (None, None, out_up, out_out, out_qkv)[i]
        wide = target.shape[1] // 2
        place = target.at[:, pl.ds(pl.multiple_of(core * wide + j * cols, 128), cols)]
        half = block // 2
        mine = pl.ds(pl.multiple_of(core * half, 8), half)
        its = pl.ds(pl.multiple_of(other * half, 8), half)
        return [
            pltpu.make_async_copy(total.at[c, mine], place, local_sem.at[c]),
            remote(total.at[c, its], place, swap_send.at[c], swap_recv.at[c], me, other),
        ]

    def start_results(c):
        i, j = table[c]
        copies = results(c)
        if i == 1:
            owner = j // (pieces // 2)
            pl.when(core == owner)(copies[0].start)
            pl.when(core != owner)(copies[1].start)
        else:
            for copy in copies:
                copy.start()

    def end_results(c):
        i, j = table[c]
        copies = results(c)
        if i == 1:
            owner = j // (pieces // 2)
            pl.when(core == owner)(copies[0].wait)
            pl.when(core == owner)(copies[1].wait_recv)
            pl.when(core != owner)(copies[1].wait_send)
        else:
            for copy in copies:
                copy.wait()

    def exchange(t):
        @pl.when(t < n)
        def _():
            c = t
            send1(c).wait_recv()
            ring, spot, to = lax.rem(c, LEAD), lax.rem(c, rings), lax.rem(c, 2)

            @pl.when(c >= 2)
            def _():
                send2(c - 2).wait_send()

            for two in range(2):

                @pl.loop(0, length)
                def _(z):
                    pair[to, two, z] = grad[ring, first_bit, two, z] + recv1[spot, two, z]

            send2(c).start()

        @pl.when((t >= 1) & (t <= n))
        def _():
            c = t - 1
            send2(c).wait_recv()
            ring, spot, to = lax.rem(c, 2), lax.rem(c, ring2), lax.rem(c, ring_line)

            @pl.loop(0, length)
            def _(z):
                line[to, z] = pair[ring, second_bit, z] + recv2[spot, z]

            start_line(c, 1)

        exchange_side(t)

        for step in range(1, length):

            @pl.when((t >= 1 + step) & (t <= n + step))
            def _():
                c = t - 1 - step
                ring, at = lax.rem(c, ring_line), lax.rem(c, rings)
                last = step == length - 1
                up_in = (zi >= 1) & (zi <= step)
                down_in = (zi <= length - 2) & (zi >= length - 1 - step)

                @pl.when(up_in)
                def _():
                    send_up(c, step).wait_recv()
                    spot = jnp.minimum(zi + (length - 1 - step), length - 1)
                    if not last:
                        line[ring, spot] = line[ring, spot] + recv_up[at, step - 1]

                @pl.when(down_in)
                def _():
                    send_down(c, step).wait_recv()
                    spot = jnp.maximum(zi - (length - 1 - step), 0)
                    if not last:
                        line[ring, spot] = line[ring, spot] + recv_down[at, step - 1]

                if not last:
                    start_line(c, step + 1)
                else:
                    total[c, :, :main] = line[ring, zi].astype(F32)

                    @pl.when(up_in)
                    def _():
                        total[c, :, :main] += recv_up[at, step - 1].astype(F32)

                    @pl.when(down_in)
                    def _():
                        total[c, :, :main] += recv_down[at, step - 1].astype(F32)

                    for back in range(1, length):
                        wait_line_sent(c, back)

                    for d in range(n):

                        @pl.when(c == d)
                        def _():
                            start_results(d)

    strip = 128
    strips = width // strip

    def norm_backward(vref, eref, index, emit):
        def sums_of(k, carry):
            squares, products = carry
            rows = pl.ds(pl.multiple_of(k * strip, strip), strip)
            v = vref[rows].astype(F32)
            e = eref[rows]
            gain = gains[rows, index : index + 1]
            squares = squares + jnp.sum(v * v, axis=0, keepdims=True)
            products = products + jnp.sum(e * gain * v, axis=0, keepdims=True)
            return squares, products

        blank = jnp.zeros((1, tokens), F32)
        squares, products = lax.fori_loop(0, strips, sums_of, (blank, blank))
        inverse = lax.rsqrt(squares / width + epsilon)
        mean = products * inverse / width

        @pl.loop(0, strips)
        def _(k):
            rows = pl.ds(pl.multiple_of(k * strip, strip), strip)
            normed = vref[rows].astype(F32) * inverse
            e = eref[rows]
            gain = gains[rows, index : index + 1]
            gains[rows, 8 + index : 9 + index] = jnp.sum(e * normed, axis=1, keepdims=True)
            emit(k, rows, inverse * (e * gain - normed * mean))

    start_left(0)
    local_c(0, core).wait()
    for i in range(2):
        dx[i * cols : (i + 1) * cols] = nt(wcols[0, i * cols : (i + 1) * cols], cbuf[0])
    sums[0] = jnp.zeros_like(sums[0])
    for i in range(2):
        share = jnp.sum(cbuf[i].astype(F32), axis=0, keepdims=True)
        at = pl.ds(pl.multiple_of(core * cols, 128), cols)
        sums[0, 3:4, at] = sums[0, 3:4, at] + share
    wait_left(0)
    form(0, [cbuf[0], cbuf[1]], nn)

    def emit_final(k, rows, value):
        dx[rows] = value
        ebuf[rows] = value.astype(BF16)

    push(PDY).wait_recv()
    for i in range(2):
        dx[i * cols : (i + 1) * cols] += hbuf[i].astype(F32)
    fetch_x3.wait()
    norm_backward(work, dx, 2, emit_final)
    push(PE3).start()
    for k in range(2, pieces + 1):
        push(k).start()
    fetch_x2.start()
    start_left(1)
    start_left(2)
    push(PDY).wait_send()
    for c in range(1, LEAD):
        start_right(c)
        wait_left(c % 2)
        wait_right(c % 2)
        form(c, [rbuf[c % 2, 0], rbuf[c % 2, 1]], nt)
        start_left(c + 2)
    push(PA2).start()
    push(PY).start()
    push(PO).start()
    push(PA1).start()

    def row_tile(k, slot, source):
        return pltpu.make_async_copy(
            source.at[pl.ds(pl.multiple_of(k * cols, 16), cols)], wrows.at[slot], row_sem.at[slot]
        )

    def col_tile(k, slot, source):
        return pltpu.make_async_copy(
            source.at[:, pl.ds(pl.multiple_of(k * cols, 128), cols)],
            wcols.at[slot],
            col_sem.at[slot],
        )

    def h_tile(k, slot):
        return pltpu.make_async_copy(
            h_t.at[pl.ds(pl.multiple_of(k * cols, 16), cols)], hbuf.at[slot], h_sem.at[slot]
        )

    def mlp_tiles(k):
        return jnp.where(k < pieces, other, core) * pieces + lax.rem(k, pieces)

    def fetch_mlp(k):
        slot = lax.rem(k, 2)
        tile = mlp_tiles(k)
        row_tile(tile, slot, w_down).start()
        col_tile(tile, slot, w_up).start()
        h_tile(tile, slot).start()

    def mlp_step(k):
        slot = lax.rem(k, 2)
        tile = mlp_tiles(k)
        row_tile(tile, slot, w_down).wait()
        h_tile(tile, slot).wait()

        @pl.when((k >= 2) & (k < pieces + 2))
        def _():
            eh_push(0, slot).wait_send()

        @pl.when(k >= pieces + 2)
        def _():
            pltpu.make_async_copy(
                ehbuf.at[slot], eh_mine.at[pl.ds(0, cols)], eh_out_sem.at[slot]
            ).wait()

        part = cols // 2
        for i in range(2):
            rows = slice(i * part, (i + 1) * part)
            value = nn(wrows[slot, rows], ebuf[...])
            pre = hbuf[slot, rows].astype(F32)
            sig = 1.0 / (1.0 + jnp.exp(-pre))
            ehbuf[slot, rows] = (value * sig * (1.0 + pre * (1.0 - sig))).astype(BF16)

        where = lax.rem(k, pieces)

        @pl.when(k < pieces)
        def _():
            eh_push(where, slot).start()

        @pl.when(k >= pieces)
        def _():
            pltpu.make_async_copy(
                ehbuf.at[slot],
                eh_mine.at[pl.ds(pl.multiple_of(where * cols, 16), cols)],
                eh_out_sem.at[slot],
            ).start()

        col_tile(tile, slot, w_up).wait()
        accumulate(wcols.at[slot], ehbuf.at[slot], k == 0)

        @pl.when(k + 2 < 2 * pieces)
        def _():
            fetch_mlp(k + 2)

    def accumulate(left, right, first):
        @pl.when(first)
        def _():
            acc[...] = jnp.zeros_like(acc)

        part = width // 4
        for i in range(4):
            rows = slice(i * part, (i + 1) * part)
            acc[rows] += nn(left[rows], right[...])

    fetch_mlp(0)
    fetch_mlp(1)

    def emit_mlp(k, rows, value):
        value = dx[rows] + value
        dx[rows] = value
        ebuf[rows] = value.astype(BF16)

    def middle():
        for slot in range(2):
            pltpu.make_async_copy(
                ehbuf.at[slot], eh_mine.at[pl.ds(0, cols)], eh_out_sem.at[slot]
            ).wait()
        row_tile(0, 0, w_out).start()
        row_tile(1, 1, w_out).start()
        push(PE3).wait_send()
        fetch_x2.wait()
        norm_backward(work, acc, 1, emit_mlp)
        push(PE2).start()

        @pl.loop(0, 2)
        def _(k):
            row_tile(k, k, w_out).wait()

            group = cols // hdim
            value = nn(wrows[k], ebuf[...]).astype(BF16)
            eo[pl.ds(k * group, group)] = value.reshape(group, hdim, tokens)

        mask_of(seg_row, bias)
        pltpu.make_async_copy(w_head, wcols.at[0], col_sem.at[0]).start()
        pltpu.make_async_copy(y_flat, ehbuf, h_sem.at[0]).start()
        push(PY).wait_recv()
        pltpu.make_async_copy(y_flat_o, hbuf, h_sem.at[1]).start()

    def level_copy(k, which, slot):
        return pltpu.make_async_copy(
            obuf.at[slot],
            out_levels.at[
                pl.ds(pl.multiple_of(which * tokens, 8), tokens), k * strip : (k + 1) * strip
            ],
            entry_sem.at[slot],
        )

    def levels(source, which, number):
        pltpu.make_async_copy(y_flat, source, h_sem.at[number]).wait()
        if number == 0:
            pltpu.make_async_copy(w_head, wcols.at[0], col_sem.at[0]).wait()
        for k in range(cols // strip):
            slot = k % 2
            if k >= 2:
                level_copy(k - 2, which, slot).wait()
            part = slice(k * strip, (k + 1) * strip)
            obuf[slot] = (
                tt(source[0], wcols[0, :cols, part])
                + tt(source[1], wcols[0, cols:, part])
                + head_bias[:, part]
            )
            level_copy(k, which, slot).start()
        for k in range(cols // strip - 2, cols // strip):
            level_copy(k, which, k % 2).wait()

    per_turn = count // 4

    def head_copy(head, slot, u, part):
        return pltpu.make_async_copy(
            qkv_t.at[pl.ds(pl.multiple_of(part * width + head * hdim, 16), hdim)],
            heads.at[slot, u, part],
            head_sem.at[slot, u, part],
        )

    def fetch_heads(i):
        for u in range(TOGETHER):
            for part in range(3):
                head_copy(i * TOGETHER + u, lax.rem(i, 2), u, part).start()

    def attend_head(head, slot, u):
        q_t, k_t, v_t = (heads[slot, u, part] for part in range(3))
        e_t = eo[head]
        q, k, v, e = q_t.T, k_t.T, v_t.T, e_t.T
        blocks = list(query_blocks(tokens))
        weight = lse[head]
        ek, ev, eqs = [[] for _ in blocks], [[] for _ in blocks], []
        for low, high, asked in blocks:
            scores = nn(k[low:high], q_t[:, asked]) * scale + bias[low:high, asked]
            p = jnp.exp(scores - weight[:, asked])
            ep_t = nn(v[low:high], e_t[:, asked])
            share = jnp.sum(p * ep_t, axis=0, keepdims=True)
            es = (p * (ep_t - share)).astype(BF16)
            eqs.append(nn(k_t[:, low:high], es))
            one, two = nn(es, q[asked]), nn(p.astype(BF16), e[asked])
            for number, (_, _, own) in enumerate(blocks):
                if low <= own.start < high:
                    ek[number].append(one[own.start - low : own.stop - low])
                    ev[number].append(two[own.start - low : own.stop - low])
        ek_t = jnp.concatenate([sum(terms[1:], terms[0]) for terms in ek], axis=0).T
        ev_t = jnp.concatenate([sum(terms[1:], terms[0]) for terms in ev], axis=0).T
        half = hdim // 2
        for part, value in ((0, jnp.concatenate(eqs, axis=1)), (1, ek_t)):
            one, two = value[:half] * scale, value[half:] * scale
            turned = jnp.concatenate(
                [one * cosine[...] + two * sine[...], two * cosine[...] - one * sine[...]],
                axis=0,
            )
            to = pl.ds(pl.multiple_of(part * width + head * hdim, 16), hdim)
            ep[to] = turned.astype(BF16)
        to = pl.ds(pl.multiple_of(2 * width + head * hdim, 16), hdim)
        ep[to] = ev_t.astype(BF16)

    def attend(turn):
        @pl.when(turn == 0)
        def _():
            fetch_heads(0)

        @pl.loop(0, per_turn // TOGETHER)
        def _(j):
            i = turn * (per_turn // TOGETHER) + j
            slot = lax.rem(i, 2)
            for u in range(TOGETHER):
                for part in range(3):
                    head_copy(i * TOGETHER + u, slot, u, part).wait()

            @pl.when((i + 1) * TOGETHER < count)
            def _():
                fetch_heads(i + 1)

            for u in range(TOGETHER):
                attend_head(i * TOGETHER + u, slot, u)

        @pl.when(turn == 3)
        def _():
            push(PEP).start()

    def fetch_qkv(k):
        col_tile(k, lax.rem(k, 2), w_qkv).start()

    def qkv_step(k):
        slot = lax.rem(k, 2)
        col_tile(k, slot, w_qkv).wait()
        rows = pl.ds(pl.multiple_of(k * cols, 16), cols)
        accumulate(wcols.at[slot], ep.at[rows], k == 0)

        @pl.when(k + 2 < 6)
        def _():
            fetch_qkv(k + 2)

    def entry_copy(k, slot):
        return pltpu.make_async_copy(
            obuf.at[slot],
            out_entry.at[:, pl.ds(pl.multiple_of(k * strip, strip), strip)],
            entry_sem.at[slot],
        )

    def emit_entry(k, rows, value):
        slot = lax.rem(k, 2)

        @pl.when(k >= 2)
        def _():
            entry_copy(k, slot).wait()

        obuf[slot] = (dx[rows] + value).T
        entry_copy(k, slot).start()

    peers = ((me, other), (flip_x, core), (flip_y, core), (near, core), (far, core))
    steps = len(peers)

    def small_copy(i):
        return remote(
            sums.at[i], sums_in.at[i], small_send.at[i], small_recv.at[i], peers[i][0], peers[i][1]
        )

    def last():
        fetch_x.wait()
        norm_backward(ebuf, acc, 0, emit_entry)
        for slot in range(2):
            entry_copy(0, slot).wait()
        sums[0] = sums[0] + gains[...].T[8:16]
        small_copy(0).start()

    @pl.loop(0, n + length)
    def _(t):
        for c in range(LEAD, n):

            @pl.when(t == c - LEAD)
            def _():
                start_right(c)

        @pl.when(t < 2)
        def _():
            @pl.loop(0, pieces)
            def _(i):
                mlp_step(t * pieces + i)

        @pl.when(t == 2)
        def _():
            middle()

        @pl.when((t >= 3) & (t < 7))
        def _():
            attend(t - 3)

        @pl.when(t == 3)
        def _():
            levels(ehbuf, core, 0)

        @pl.when(t == 4)
        def _():
            levels(hbuf, other, 1)

        @pl.when(t == 6)
        def _():
            fetch_qkv(0)
            fetch_qkv(1)

        @pl.when((t == 7) | (t == 8))
        def _():
            @pl.loop(0, 3)
            def _(i):
                qkv_step((t - 7) * 3 + i)

        @pl.when(t == 9)
        def _():
            last()

        for i in range(steps):

            @pl.when(t == 10 + i)
            def _():
                small_copy(i).wait()
                value = sums[i] + sums_in[i]
                if i == steps - 1:
                    out_small[...] = value
                else:
                    sums[i + 1] = value
                    small_copy(i + 1).start()

        exchange(t)

        @pl.when(t + LEAD < n)
        def _():
            c = t + LEAD
            slot = lax.rem(c, 2)
            wait_left(slot)
            wait_right(slot)
            send1(t).wait_send()
            form(c, [rbuf[slot, 0], rbuf[slot, 1]], nt)
            for d in range(LEAD + 2, n):

                @pl.when(c == d - 2)
                def _():
                    start_left(d)

        @pl.when(t == 8)
        def _():
            push(PE2).wait_send()
            fetch_x.start()

    for c in range(n):
        end_results(c)
    for c in range(n - LEAD, n):
        send1(c).wait_send()
    for c in range(n - 2, n):
        send2(c).wait_send()
    for k in range(pieces + 9):
        if k not in (PE3, PE2, PDY):
            push(k).wait_send()


def run_backward(lefts, others, weights, tables):
    size = lax.axis_size("dp")
    width, tokens = lefts[0].shape
    hidden = lefts[1].shape[0]
    block = width // size
    cols = width // 2
    table = chunk_table(width, hidden)
    n = len(table)
    length = size // 4
    share = block // 2
    hdim = width // HEADS
    hbm = pl.BlockSpec(memory_space=pl.ANY)
    vmem = pl.BlockSpec(memory_space=pltpu.VMEM)
    lefts = [left.reshape(size, left.shape[0] // size, tokens) for left in lefts]
    shapes = [
        jax.ShapeDtypeStruct((block, cols), F32),
        jax.ShapeDtypeStruct((hidden // size // 2, width), F32),
        jax.ShapeDtypeStruct((share, hidden), F32),
        jax.ShapeDtypeStruct((share, width), F32),
        jax.ShapeDtypeStruct((share, 3 * width), F32),
        jax.ShapeDtypeStruct((8, width), F32),
        jax.ShapeDtypeStruct((tokens, width), F32),
        jax.ShapeDtypeStruct((2 * tokens, cols), F32),
    ]
    shapes += [jax.ShapeDtypeStruct(left.shape, BF16) for left in lefts]
    shapes += [
        jax.ShapeDtypeStruct((rows, tokens), BF16)
        for rows in (cols, hidden // 2, cols, 3 * cols, hidden // 2)
    ]
    shapes += [jax.ShapeDtypeStruct((2, cols, tokens), BF16)]
    dma = pltpu.SemaphoreType.DMA
    ring1, ring2, ring_line = 6, 4, length + 1
    main = cols - 128
    results = pl.pallas_call(
        functools.partial(backward_kernel, table, size),
        out_shape=shapes,
        in_specs=[hbm] * 17 + [vmem] * 8,
        out_specs=[hbm] * 5 + [vmem] + [hbm] * 13,
        scratch_shapes=[
            pltpu.VMEM((2, 2, size, block, tokens), BF16),
            pltpu.VMEM((2, 2, cols, tokens), BF16),
            pltpu.VMEM((2, tokens, cols), BF16),
            pltpu.VMEM((LEAD, 2, 2, length, block, main), BF16),
            pltpu.VMEM((ring1, 2, length, block, main), BF16),
            pltpu.VMEM((2, 2, length, block, main), BF16),
            pltpu.VMEM((ring2, length, block, main), BF16),
            pltpu.VMEM((ring_line, length, block, main), BF16),
            pltpu.VMEM((ring1, length - 1, block, main), BF16),
            pltpu.VMEM((ring1, length - 1, block, main), BF16),
            pltpu.VMEM((length + 4, length, 2, 2, block, cols - main), BF16),
            pltpu.VMEM((length + 3, length - 1, 2, 2, block, cols - main), BF16),
            pltpu.VMEM((length + 3, length - 1, 2, 2, block, cols - main), BF16),
            pltpu.VMEM((length + 3, 2, block, cols - main), BF16),
            pltpu.VMEM((length + 3, block, cols - main), BF16),
            pltpu.VMEM((n, block, cols), F32),
            pltpu.VMEM((5, 8, width), F32),
            pltpu.VMEM((5, 8, width), F32),
            pltpu.VMEM((width, tokens), F32),
            pltpu.VMEM((width, tokens), F32),
            pltpu.VMEM((width, tokens), F32),
            pltpu.VMEM((width, tokens), BF16),
            pltpu.VMEM((tokens, tokens), F32),
            pltpu.VMEM((width, 128), F32),
            pltpu.VMEM((8, width), F32),
            pltpu.VMEM((2, cols, width), BF16),
            pltpu.VMEM((2, width, cols), BF16),
            pltpu.VMEM((2, cols, tokens), BF16),
            pltpu.VMEM((2, cols, tokens), BF16),
            pltpu.VMEM((3 * width, tokens), BF16),
            pltpu.VMEM((HEADS, hdim, tokens), BF16),
            pltpu.VMEM((2, TOGETHER, 3, hdim, tokens), BF16),
            pltpu.VMEM((2, tokens, 128), F32),
            dma((hidden // width + 9,)),
            dma((hidden // width + 9,)),
            dma((2, 2)),
            dma((2, 2)),
            dma((LEAD,)),
            dma((ring1,)),
            dma((2,)),
            dma((ring2,)),
            dma((ring_line, length - 1)),
            dma((ring1, length - 1)),
            dma((ring_line, length - 1)),
            dma((ring1, length - 1)),
            dma((length + 4, length - 1)),
            dma((length + 3, length - 1)),
            dma((length + 4, length - 1)),
            dma((length + 3, length - 1)),
            dma((length + 4,)),
            dma((length + 3,)),
            dma((length + 4,)),
            dma((length + 3,)),
            dma((n,)),
            dma((n,)),
            dma((n,)),
            dma((5,)),
            dma((5,)),
            dma((2,)),
            dma((2,)),
            dma((2,)),
            dma((2,)),
            dma((hidden // width,)),
            dma((2, TOGETHER, 3)),
            dma((4,)),
            dma((2,)),
        ],
        compiler_params=pltpu.CompilerParams(
            collective_id=0, has_side_effects=True, vmem_limit_bytes=62 << 20
        ),
        name="backward",
    )(*lefts, *others, *weights, *tables)
    return results[:8]


def per_device(
    inputs,
    segment_ids,
    gain_attn,
    w_qkv,
    w_out,
    gain_mlp,
    w_up,
    w_down,
    gain_final,
    head_projection_weight,
    head_output_bias,
    cotangent,
):
    core = lax.axis_index("head")
    place = lax.axis_index("dp")
    size = lax.axis_size("dp")
    rows, sequence_span = segment_ids.shape
    count, width = inputs.shape
    hdim = width // HEADS
    scale = 1.0 / math.sqrt(hdim)
    share = width // (2 * size)
    fused = size == HEADS and lax.axis_size("head") == 2 and rows == 1

    if fused:
        half = width // 2
        turn = hdim // 2
        freq = np.float32(10000.0) ** (-np.arange(turn, dtype=np.float32) / np.float32(turn))
        angle = np.arange(sequence_span, dtype=np.float32)[None, :] * freq[:, None]
        cosine_t, sine_t = jnp.asarray(np.cos(angle)), jnp.asarray(np.sin(angle))
        gain_rows = [gain[None] for gain in (gain_attn, gain_mlp, gain_final)]
        y_t, g_t, a2_t, o_t, a1_t, x3_t, x2_t, x_t, h_t, qkv_t, lse = run_forward(
            inputs, w_qkv, w_out, w_up, w_down, segment_ids, gain_rows, cosine_t, sine_t
        )
        (
            grad_head,
            grad_down,
            grad_up,
            grad_out,
            grad_qkv,
            sums,
            entry_sensitivity_matrix,
            predicted_levels,
        ) = run_backward(
            [y_t, g_t, a2_t, o_t, a1_t],
            [
                cotangent,
                head_projection_weight,
                y_t.reshape(2, half, count),
                x3_t,
                x2_t,
                x_t,
                h_t,
                qkv_t,
            ],
            [w_down, w_up, w_out, w_qkv],
            [lse, segment_ids, *gain_rows, head_output_bias[None], cosine_t, sine_t],
        )
        gains = lax.dynamic_slice_in_dim(sums, (place * 2 + core) * share, share, 1)
        grad_bias = lax.dynamic_slice_in_dim(sums[3], core * half, half, 0)
    else:
        other_rows = lax.dynamic_slice_in_dim(cotangent, (1 - core) * count, count, 0)
        own_rows = lax.dynamic_slice_in_dim(cotangent, core * count, count, 0)
        got = swap_cores(contract_cols(head_projection_weight, other_rows).astype(BF16))
        grad_final_t = contract_cols(head_projection_weight, own_rows) + got.astype(F32)
        bias_local = jnp.sum(cotangent, axis=0, dtype=F32)

        cosine, sine = rotary_tables(sequence_span, hdim)
        tokens = inputs.astype(jnp.float32)
        normed_one, inverse_one = rms_forward(tokens, gain_attn)
        act_one = normed_one.astype(jnp.bfloat16)
        projected = jnp.dot(act_one, w_qkv, preferred_element_type=jnp.float32).reshape(
            rows, sequence_span, 3, HEADS, hdim
        )
        query = rotate(projected[:, :, 0], cosine, sine).astype(jnp.bfloat16)
        key = rotate(projected[:, :, 1], cosine, sine).astype(jnp.bfloat16)
        value = projected[:, :, 2].astype(jnp.bfloat16)
        attended, log_total = lax.map(
            lambda items: attend_forward(items, scale), (query, key, value, segment_ids)
        )
        mixed = attended.reshape(rows * sequence_span, width)
        resid_two = tokens + jnp.dot(mixed, w_out, preferred_element_type=jnp.float32)
        normed_two, inverse_two = rms_forward(resid_two, gain_mlp)
        act_two = normed_two.astype(jnp.bfloat16)
        hidden_pre = jnp.dot(act_two, w_up, preferred_element_type=jnp.float32)
        hidden = jax.nn.silu(hidden_pre).astype(jnp.bfloat16)
        resid_three = resid_two + jnp.dot(hidden, w_down, preferred_element_type=jnp.float32)
        normed_three, inverse_three = rms_forward(resid_three, gain_final)
        final_hidden = normed_three.astype(jnp.bfloat16)
        other_hidden = swap_cores(final_hidden)
        collected_rows = jnp.concatenate(
            [
                jnp.where(core == 0, final_hidden, other_hidden),
                jnp.where(core == 0, other_hidden, final_hidden),
            ],
            axis=0,
        )
        predicted_levels = (
            jnp.dot(collected_rows, head_projection_weight, preferred_element_type=jnp.float32)
            + head_output_bias
        )
        grad_head = lax.psum_scatter(
            contract_rows(collected_rows, cotangent), "dp", scatter_dimension=0, tiled=True
        )
        grad_three, grad_gain_final = rms_backward(
            resid_three, inverse_three, gain_final, grad_final_t.T
        )
        grad_mlp_out = grad_three.astype(jnp.bfloat16)
        grad_hidden = contract_cols(grad_mlp_out, w_down)
        sigmoid = jax.nn.sigmoid(hidden_pre)
        grad_pre = (grad_hidden * sigmoid * (1.0 + hidden_pre * (1.0 - sigmoid))).astype(BF16)
        grad_norm_two, grad_gain_mlp = rms_backward(
            resid_two, inverse_two, gain_mlp, contract_cols(grad_pre, w_up)
        )
        grad_two = grad_three + grad_norm_two
        grad_branch = grad_two.astype(jnp.bfloat16)
        grad_mixed = (
            contract_cols(grad_branch, w_out)
            .astype(jnp.bfloat16)
            .reshape(rows, sequence_span, HEADS, hdim)
        )
        grad_query, grad_key, grad_value = lax.map(
            lambda items: attend_backward(items, scale),
            (query, key, value, segment_ids, log_total, grad_mixed),
        )
        grad_query = unrotate(grad_query, cosine, sine)
        grad_key = unrotate(grad_key, cosine, sine)
        grad_proj = (
            jnp.stack([grad_query, grad_key, grad_value], axis=2)
            .reshape(rows * sequence_span, 3 * width)
            .astype(jnp.bfloat16)
        )
        grad_norm_one, grad_gain_attn = rms_backward(
            tokens, inverse_one, gain_attn, contract_cols(grad_proj, w_qkv)
        )
        entry_sensitivity_matrix = grad_two + grad_norm_one
        grad_down = scatter_rows(hidden, grad_mlp_out)
        grad_up = scatter_rows(act_two, grad_pre)
        grad_out = scatter_rows(mixed, grad_branch)
        grad_qkv = scatter_rows(act_one, grad_proj)
        gains = sum_everywhere(jnp.stack([grad_gain_attn, grad_gain_mlp, grad_gain_final]), True)
        gains = lax.dynamic_slice_in_dim(gains, (place * 2 + core) * share, share, 1)
        grad_bias = sum_everywhere(bias_local, False)
    return (
        predicted_levels,
        entry_sensitivity_matrix,
        gains[0],
        grad_qkv,
        grad_out,
        gains[1],
        grad_up,
        grad_down,
        gains[2],
        grad_head,
        grad_bias,
    )


def solution(mesh):
    return jax.shard_map(
        per_device,
        mesh=mesh,
        in_specs=(
            P(("dp", "head"), None),
            P(("dp", "head"), None),
            P(),
            P(),
            P(),
            P(),
            P(),
            P(),
            P(),
            P(None, "head"),
            P("head"),
            P("dp", "head"),
        ),
        out_specs=(
            P("dp", "head"),
            P(("dp", "head"), None),
            P(("dp", "head")),
            P(("dp", "head"), None),
            P(("dp", "head"), None),
            P(("dp", "head")),
            P(("dp", "head"), None),
            P(("dp", "head"), None),
            P(("dp", "head")),
            P("dp", "head"),
            P("head"),
        ),
        check_vma=False,
    )
```

```python
import functools
import math

import jax
import jax.numpy as jnp
import numpy as np
from jax import lax
from jax.experimental import pallas as pl
from jax.experimental.pallas import tpu as pltpu
from jax.sharding import PartitionSpec as P

HEADS = 16
F32 = jnp.float32
BF16 = jnp.bfloat16

epsilon = 1e-06


def rms_forward(values, gain):
    inverse = lax.rsqrt(jnp.mean(values * values, axis=-1, keepdims=True) + epsilon)
    return (values * inverse * gain, inverse)


def rms_backward(values, inverse, gain, grad):
    normed = values * inverse
    scaled = grad * gain
    grad_gain = jnp.sum(grad * normed, axis=0)
    grad_values = inverse * (scaled - normed * jnp.mean(scaled * normed, axis=-1, keepdims=True))
    return (grad_values, grad_gain)


def rotary_tables(sequence_span, hdim):
    half = hdim // 2
    freq = 10000.0 ** (-jnp.arange(half, dtype=jnp.float32) / half)
    angle = jnp.arange(sequence_span, dtype=jnp.float32)[:, None] * freq[None, :]
    return (jnp.cos(angle)[:, None, :], jnp.sin(angle)[:, None, :])


def rotate(values, cosine, sine):
    half = values.shape[-1] // 2
    first = values[..., :half]
    second = values[..., half:]
    return jnp.concatenate(
        [first * cosine - second * sine, second * cosine + first * sine], axis=-1
    )


def unrotate(grads, cosine, sine):
    half = grads.shape[-1] // 2
    first = grads[..., :half]
    second = grads[..., half:]
    return jnp.concatenate(
        [first * cosine + second * sine, second * cosine - first * sine], axis=-1
    )


def allowed_mask(segs):
    place = jnp.arange(segs.shape[0])
    return (segs[:, None] == segs[None, :]) & (place[:, None] >= place[None, :])


def row_scores(query, key, segs, scale):
    scores = jnp.einsum("qhd,khd->hqk", query, key, preferred_element_type=jnp.float32) * scale
    allowed = allowed_mask(segs)[None]
    return (jnp.where(allowed, scores, -1e30), allowed)


def attend_forward(items, scale):
    query, key, value, segs = items
    scores, allowed = row_scores(query, key, segs, scale)
    peak = jnp.max(scores, axis=-1, keepdims=True)
    expo = jnp.exp(scores - peak)
    overall_number = jnp.sum(expo, axis=-1, keepdims=True)
    probs = (expo / overall_number).astype(jnp.bfloat16)
    attended = jnp.einsum("hqk,khd->qhd", probs, value, preferred_element_type=jnp.float32)
    return (attended.astype(jnp.bfloat16), peak + jnp.log(overall_number))


def attend_backward(items, scale):
    query, key, value, segs, log_total, grad_attended = items
    scores, allowed = row_scores(query, key, segs, scale)
    probs = jnp.where(allowed, jnp.exp(scores - log_total), 0.0)
    grad_value = jnp.einsum(
        "hqk,qhd->khd",
        probs.astype(jnp.bfloat16),
        grad_attended,
        preferred_element_type=jnp.float32,
    )
    grad_probs = jnp.einsum(
        "qhd,khd->hqk", grad_attended, value, preferred_element_type=jnp.float32
    )
    grad_scores = (
        probs * (grad_probs - jnp.sum(grad_probs * probs, axis=-1, keepdims=True))
    ).astype(jnp.bfloat16)
    grad_query = (
        jnp.einsum("hqk,khd->qhd", grad_scores, key, preferred_element_type=jnp.float32) * scale
    )
    grad_key = (
        jnp.einsum("hqk,qhd->khd", grad_scores, query, preferred_element_type=jnp.float32) * scale
    )
    return (grad_query, grad_key, grad_value)


def contract_rows(left, right):
    return lax.dot_general(
        left, right, (((0,), (0,)), ((), ())), preferred_element_type=jnp.float32
    )


def contract_cols(left, right):
    return lax.dot_general(
        left, right, (((1,), (1,)), ((), ())), preferred_element_type=jnp.float32
    )


def swap_cores(values):
    return lax.ppermute(values, "head", [(0, 1), (1, 0)])


def flip(values, bit):
    size = lax.axis_size("dp")
    return lax.ppermute(values, "dp", [(i, i ^ bit) for i in range(size)])


def scatter_rows(left, right):
    return lax.psum_scatter(
        contract_rows(left, right), ("dp", "head"), scatter_dimension=0, tiled=True
    )


def sum_everywhere(values, over_head):
    size = lax.axis_size("dp")
    if over_head:
        values = values + swap_cores(values)
    bit = 1
    while bit < size:
        values = values + flip(values, bit)
        bit *= 2
    return values


MESH = pl.DeviceIdType.MESH


def chunk_table(width, hidden):
    table = [(0, 0)]
    table += [(1, j) for j in range(hidden // width)]
    table += [(2, j) for j in range(hidden // width)]
    table += [(3, 0)]
    table += [(4, j) for j in range(3)]
    return table


def nt(left, right):
    return lax.dot_general(
        left, right, (((1,), (1,)), ((), ())), preferred_element_type=jnp.float32
    )


def nn(left, right):
    return jnp.dot(left, right, preferred_element_type=jnp.float32)


def tt(left, right):
    return lax.dot_general(
        left, right, (((0,), (0,)), ((), ())), preferred_element_type=jnp.float32
    )


def columns_of(rows, scratch):
    scratch[...] = jnp.zeros_like(scratch)
    for i, row in enumerate(rows):
        scratch[i : i + 1] = row[...].reshape(1, row.shape[0])
    return scratch[...].T


def mask_of(seg_row, bias):
    tokens = bias.shape[0]
    ids = seg_row[...].astype(F32)
    wide = jnp.broadcast_to(ids, (8, tokens)).T[:, :1]
    own = lax.broadcasted_iota(jnp.int32, (tokens, tokens), 0)
    asked = lax.broadcasted_iota(jnp.int32, (tokens, tokens), 1)
    bias[...] = jnp.where((wide == ids) & (own <= asked), 0.0, -1e30)


STRIP = 128
SLOTS = 4
REACH = 256
TOGETHER = 2


def query_blocks(tokens):
    for start in range(0, tokens, REACH):
        stop = min(start + REACH, tokens)
        yield max(0, start - REACH), stop, slice(start, stop)


def norm_backward(vref, eref, gains, index, emit):
    width, tokens = vref.shape

    def sums_of(k, carry):
        squares, products = carry
        rows = pl.ds(pl.multiple_of(k * STRIP, STRIP), STRIP)
        v = vref[rows].astype(F32)
        e = eref[rows]
        gain = gains[rows, index : index + 1]
        squares = squares + jnp.sum(v * v, axis=0, keepdims=True)
        products = products + jnp.sum(e * gain * v, axis=0, keepdims=True)
        return squares, products

    blank = jnp.zeros((1, tokens), F32)
    squares, products = lax.fori_loop(0, width // STRIP, sums_of, (blank, blank))
    inverse = lax.rsqrt(squares / width + epsilon)
    mean = products * inverse / width

    @pl.loop(0, width // STRIP)
    def _(k):
        rows = pl.ds(pl.multiple_of(k * STRIP, STRIP), STRIP)
        normed = vref[rows].astype(F32) * inverse
        e = eref[rows]
        gain = gains[rows, index : index + 1]
        gains[rows, 8 + index : 9 + index] = jnp.sum(e * normed, axis=1, keepdims=True)
        emit(k, rows, inverse * (e * gain - normed * mean))


def forward_kernel(
    x,
    w_qkv,
    w_out,
    w_up,
    w_down,
    w_head,
    cot,
    seg_row,
    gain_attn,
    gain_mlp,
    gain_final,
    cosine,
    sine,
    y_t,
    g_t,
    a2_t,
    o_t,
    a1_t,
    y_o,
    g_o,
    a2_o,
    o_o,
    a1_o,
    dx3_t,
    e3_t,
    gain_columns,
    x2_t,
    x_t,
    h_t,
    qkv_t,
    lse,
    weights,
    xin,
    xt,
    act1,
    act2,
    final,
    mixed,
    qkv,
    res2,
    res3,
    hbuf,
    gbuf,
    bias,
    gains,
    gain_rows,
    cbuf,
    head_weight,
    dy,
    dy_sent,
    dy_got,
    e3,
    weight_sem,
    in_sem,
    c_sem,
    out_sem,
    h_sem,
    g_sem,
    push_send,
    push_recv,
    g_send,
    g_recv,
):
    width, tokens = res2.shape
    hidden = h_t.shape[0]
    pieces = hidden // width
    half = width // 2
    count = HEADS
    hdim = width // count
    scale = 1.0 / math.sqrt(hdim)
    first_tiles = [w_qkv.at[:, k * width : (k + 1) * width] for k in range(3)] + [w_out]

    def fetch(k):
        return pltpu.make_async_copy(first_tiles[k], weights.at[k], weight_sem.at[k])

    def fetch_up(k):
        slot = lax.rem(2 * k, SLOTS)
        source = w_up.at[:, pl.ds(pl.multiple_of(k * width, 128), width)]
        return pltpu.make_async_copy(source, weights.at[slot], weight_sem.at[slot])

    def fetch_down(k):
        slot = lax.rem(2 * k + 1, SLOTS)
        source = w_down.at[pl.ds(pl.multiple_of(k * width, 16), width)]
        return pltpu.make_async_copy(source, weights.at[slot], weight_sem.at[slot])

    me = lax.axis_index("dp")
    core = lax.axis_index("head")
    other = 1 - core

    def remote(src, dst, send, recv):
        return pltpu.make_async_remote_copy(
            src_ref=src,
            dst_ref=dst,
            send_sem=send,
            recv_sem=recv,
            device_id=(me, other),
            device_id_type=MESH,
        )

    fetch_head_weight = pltpu.make_async_copy(w_head, head_weight, c_sem.at[2])

    def fetch_c(number, which):
        start = pl.multiple_of(which * tokens, 16)
        return pltpu.make_async_copy(
            cot.at[pl.ds(start, tokens)], cbuf.at[number], c_sem.at[number]
        )

    fetch_x = pltpu.make_async_copy(x, xin, in_sem)
    fetch_x.start()
    for k in range(SLOTS):
        fetch(k).start()
    fetch_c(1, other).start()
    fetch_head_weight.start()
    fetch_c(0, core).start()

    barrier = pltpu.get_barrier_semaphore()
    pl.semaphore_signal(barrier, inc=1, device_id=(me, other), device_id_type=MESH)
    gains[...] = jnp.zeros_like(gains)
    gains[:, :8] = columns_of((gain_attn, gain_mlp, gain_final), gain_rows)
    pl.semaphore_wait(barrier, 1)

    mask_of(seg_row, bias)
    fetch_x.wait()
    xt[...] = xin[...].T
    dy_push = remote(dy_sent, dy_got, push_send.at[0], push_recv.at[0])
    outs, pushes = [], [dy_push]

    def put(source, target, also=None):
        copy = pltpu.make_async_copy(source, target, out_sem.at[len(outs)])
        outs.append(copy)
        copy.start()
        if also is not None:
            number = len(pushes)
            pushes.append(remote(source, also, push_send.at[number], push_recv.at[number]))
            pushes[-1].start()

    put(xt, x_t)

    def squares_of(ref):
        def step(k, total):
            v = ref[pl.ds(pl.multiple_of(k * STRIP, STRIP), STRIP)].astype(F32)
            return total + jnp.sum(v * v, axis=0, keepdims=True)

        return lax.fori_loop(0, width // STRIP, step, jnp.zeros((1, tokens), F32))

    def normalize(ref, index, to):
        inverse = lax.rsqrt(squares_of(ref) / width + epsilon)

        @pl.loop(0, width // STRIP)
        def _(k):
            rows = pl.ds(pl.multiple_of(k * STRIP, STRIP), STRIP)
            to[rows] = (ref[rows].astype(F32) * inverse * gains[rows, index : index + 1]).astype(
                BF16
            )

    normalize(xt, 0, act1)
    put(act1, a1_t, a1_o)

    turn = hdim // 2
    for part in range(3):
        fetch(part).wait()

    @pl.loop(0, 2)
    def _(part):
        for lower in range(2):
            value = tt(weights[part, :, lower * half : (lower + 1) * half], act1[...])
            for head in range(count // 2):
                one = value[head * hdim : head * hdim + turn]
                two = value[head * hdim + turn : (head + 1) * hdim]
                turned = jnp.concatenate(
                    [one * cosine[...] - two * sine[...], two * cosine[...] + one * sine[...]],
                    axis=0,
                )
                base = pl.multiple_of(part * width + lower * half + head * hdim, 16)
                qkv[pl.ds(base, hdim)] = turned.astype(BF16)

    fetch_up(0).start()
    fetch_down(0).start()
    for lower in range(2):
        rows = slice(lower * half, (lower + 1) * half)
        value = tt(weights[2, :, rows], act1[...])
        qkv[2 * width + lower * half : 2 * width + (lower + 1) * half] = value.astype(BF16)
    fetch_up(1).start()
    put(qkv, qkv_t)

    def attend(head):
        def rows_of(part):
            return pl.ds(pl.multiple_of(part * width + head * hdim, 16), hdim)

        q_t = qkv[rows_of(0)]
        v_t = qkv[rows_of(2)]
        k = qkv[rows_of(1)].T
        for low, high, asked in query_blocks(tokens):
            scores = nn(k[low:high], q_t[:, asked]) * scale + bias[low:high, asked]
            peak = jnp.max(scores, axis=0, keepdims=True)
            expo = jnp.exp(scores - peak)
            amount = jnp.sum(expo, axis=0, keepdims=True)
            probs = (expo * (1.0 / amount)).astype(BF16)
            mixed[rows_of(0), asked] = nn(v_t[:, low:high], probs).astype(BF16)
            lse[head, :, asked] = peak + jnp.log(amount)

    @pl.loop(0, count // TOGETHER)
    def _(i):
        for u in range(TOGETHER):
            attend(i * TOGETHER + u)

    put(mixed, o_t, o_o)

    fetch_head_weight.wait()
    fetch_c(1, other).wait()
    for i in range(2):
        rows = slice(i * half, (i + 1) * half)
        dy_sent[rows] = nt(head_weight[rows], cbuf[1]).astype(BF16)
    dy_push.start()
    fetch_c(0, core).wait()
    for i in range(2):
        rows = slice(i * half, (i + 1) * half)
        dy[rows] = nt(head_weight[rows], cbuf[0])


    fetch(3).wait()
    for lower in range(2):
        rows = slice(lower * half, (lower + 1) * half)
        res2[rows] = xt[rows].astype(F32) + tt(weights[3, :, rows], mixed[...])
        res3[rows] = res2[rows]
    fetch_down(1).start()
    put(res2, x2_t)
    normalize(res2, 1, act2)
    put(act2, a2_t, a2_o)

    def piece(k):
        return pl.ds(pl.multiple_of(k * width, 16), width)

    def h_copy(k):
        slot = lax.rem(k, 2)
        return pltpu.make_async_copy(hbuf.at[slot], h_t.at[piece(k)], h_sem.at[slot])

    def g_copy(k):
        slot = lax.rem(k, 2)
        return pltpu.make_async_copy(gbuf.at[slot], g_t.at[piece(k)], g_sem.at[slot])

    def g_push(k):
        slot = lax.rem(k, 2)
        return remote(gbuf.at[slot], g_o.at[piece(k)], g_send.at[slot], g_recv.at[k])

    @pl.loop(0, pieces)
    def _(k):
        slot, up, down = lax.rem(k, 2), lax.rem(2 * k, SLOTS), lax.rem(2 * k + 1, SLOTS)
        fetch_up(k).wait()

        @pl.when(k >= 2)
        def _():
            h_copy(k - 2).wait()
            g_copy(k - 2).wait()
            g_push(k - 2).wait_send()

        for lower in range(2):
            rows = slice(lower * half, (lower + 1) * half)
            value = tt(weights[up, :, rows], act2[...])
            hbuf[slot, rows] = value.astype(BF16)
            gbuf[slot, rows] = (value / (1.0 + jnp.exp(-value))).astype(BF16)

        @pl.when(k + 2 < pieces)
        def _():
            fetch_up(k + 2).start()

        h_copy(k).start()
        g_copy(k).start()
        g_push(k).start()
        fetch_down(k).wait()
        for lower in range(2):
            rows = slice(lower * half, (lower + 1) * half)
            res3[rows] += tt(weights[down, :, rows], gbuf[slot])

        @pl.when(k + 2 < pieces)
        def _():
            fetch_down(k + 2).start()

    normalize(res3, 2, final)
    put(final, y_t, y_o)

    dy_push.wait_recv()

    @pl.loop(0, width // STRIP)
    def _(k):
        rows = pl.ds(pl.multiple_of(k * STRIP, STRIP), STRIP)
        dy[rows] = dy[rows] + dy_got[rows].astype(F32)

    def emit(k, rows, value):
        dy[rows] = value
        e3[rows] = value.astype(BF16)

    norm_backward(res3, dy, gains, 2, emit)
    put(dy, dx3_t)
    put(e3, e3_t)
    put(gains, gain_columns)
    for copy in outs:
        copy.wait()
    for k in range(max(0, pieces - 2), pieces):
        h_copy(k).wait()
        g_copy(k).wait()
        g_push(k).wait_send()
    for k in range(pieces):
        g_push(k).wait_recv()
    dy_push.wait_send()
    for push in pushes[1:]:
        push.wait()


def run_forward(x, w_qkv, w_out, w_up, w_down, w_head, cot, segs, gains, cosine, sine):
    tokens, width = x.shape
    hidden = w_up.shape[1]
    hdim = width // HEADS
    hbm = pl.BlockSpec(memory_space=pl.ANY)
    vmem = pl.BlockSpec(memory_space=pltpu.VMEM)
    flat = (width, tokens)
    shapes = [
        jax.ShapeDtypeStruct(shape, dtype)
        for shape, dtype in (
            (flat, BF16),
            ((hidden, tokens), BF16),
            (flat, BF16),
            (flat, BF16),
            (flat, BF16),
            (flat, BF16),
            ((hidden, tokens), BF16),
            (flat, BF16),
            (flat, BF16),
            (flat, BF16),
            (flat, F32),
            (flat, BF16),
            ((width, 128), F32),
            (flat, F32),
            (flat, BF16),
            ((hidden, tokens), BF16),
            ((3 * width, tokens), BF16),
            ((HEADS, 1, tokens), F32),
        )
    ]
    dma = pltpu.SemaphoreType.DMA
    return pl.pallas_call(
        forward_kernel,
        out_shape=shapes,
        in_specs=[hbm] * 7 + [vmem] * 6,
        out_specs=[hbm] * 17 + [vmem],
        scratch_shapes=[
            pltpu.VMEM((SLOTS, width, width), BF16),
            pltpu.VMEM((tokens, width), BF16),
            pltpu.VMEM(flat, BF16),
            pltpu.VMEM(flat, BF16),
            pltpu.VMEM(flat, BF16),
            pltpu.VMEM(flat, BF16),
            pltpu.VMEM(flat, BF16),
            pltpu.VMEM((3 * width, tokens), BF16),
            pltpu.VMEM(flat, F32),
            pltpu.VMEM(flat, F32),
            pltpu.VMEM((2,) + flat, BF16),
            pltpu.VMEM((2,) + flat, BF16),
            pltpu.VMEM((tokens, tokens), F32),
            pltpu.VMEM((width, 128), F32),
            pltpu.VMEM((8, width), F32),
            pltpu.VMEM((2, tokens, width // 2), BF16),
            pltpu.VMEM((width, width // 2), BF16),
            pltpu.VMEM(flat, F32),
            pltpu.VMEM(flat, BF16),
            pltpu.VMEM(flat, BF16),
            pltpu.VMEM(flat, BF16),
            dma((SLOTS,)),
            dma(()),
            dma((3,)),
            dma((10,)),
            dma((2,)),
            dma((2,)),
            dma((5,)),
            dma((5,)),
            dma((2,)),
            dma((hidden // width,)),
        ],
        compiler_params=pltpu.CompilerParams(
            collective_id=1, has_side_effects=True, vmem_limit_bytes=60 << 20
        ),
        name="forward",
    )(x, w_qkv, w_out, w_up, w_down, w_head, cot, segs, *gains, cosine, sine)


LEAD = 3


def backward_kernel(
    table,
    size,
    y_t,
    g_t,
    a2_t,
    o_t,
    a1_t,
    y_o,
    g_o,
    a2_o,
    o_o,
    a1_o,
    cot,
    dx3_t,
    e3_t,
    x2_t,
    x_t,
    h_t,
    qkv_t,
    gain_columns,
    w_down,
    w_up,
    w_out,
    w_qkv,
    lse,
    seg_row,
    cosine,
    sine,
    out_head,
    out_down,
    out_up,
    out_out,
    out_qkv,
    out_small,
    out_entry,
    e3_o,
    eh_o,
    e2_o,
    ep_o,
    eh_mine,
    lbuf,
    rbuf,
    cbuf,
    grad,
    recv1,
    pair,
    recv2,
    line,
    recv_up,
    recv_down,
    side,
    side_up,
    side_down,
    side1,
    side2,
    total,
    sums,
    sums_in,
    dx,
    work,
    acc,
    ebuf,
    bias,
    gains,
    wrows,
    wcols,
    hbuf,
    ehbuf,
    ep,
    eo,
    heads,
    obuf,
    push_send,
    push_recv,
    left_sem,
    right_sem,
    send1_sem,
    recv1_sem,
    send2_sem,
    recv2_sem,
    up_send,
    up_recv,
    down_send,
    down_recv,
    side_up_send,
    side_up_recv,
    side_down_send,
    side_down_recv,
    side1_send,
    side1_recv,
    side2_send,
    side2_recv,
    local_sem,
    swap_send,
    swap_recv,
    small_send,
    small_recv,
    row_sem,
    col_sem,
    h_sem,
    eh_out_sem,
    eh_in_sem,
    head_sem,
    fetch_sem,
    entry_sem,
):
    n = len(table)
    length = size // 4
    me = lax.axis_index("dp")
    core = lax.axis_index("head")
    other = 1 - core
    xi = lax.rem(me, 2)
    yi = lax.rem(me // 2, 2)
    zi = me // 4
    width, tokens = dx.shape
    hidden = h_t.shape[0]
    cols = width // 2
    block = width // size
    count, hdim = eo.shape[:2]
    scale = 1.0 / math.sqrt(hdim)
    flip_x = me + 1 - 2 * xi
    flip_y = me + 2 * (1 - 2 * yi)
    first_bit = jnp.where(core == 0, xi, yi)
    second_bit = jnp.where(core == 0, yi, xi)
    first_peer = jnp.where(core == 0, flip_x, flip_y)
    second_peer = jnp.where(core == 0, flip_y, flip_x)
    far = lax.rem(me + size // 2, size)
    near = me + 4 * (1 - 2 * lax.rem(zi, 2))
    rings = recv1.shape[0]
    ring2 = recv2.shape[0]
    ring_line = line.shape[0]
    ring_side, ring_in = side.shape[0], side1.shape[0]
    main = grad.shape[-1]

    fetch_dx = pltpu.make_async_copy(dx3_t, dx, fetch_sem.at[0])
    fetch_e3 = pltpu.make_async_copy(e3_t, ebuf, fetch_sem.at[1])
    fetch_gains = pltpu.make_async_copy(gain_columns, gains, fetch_sem.at[4])
    fetch_x2 = pltpu.make_async_copy(x2_t, work, fetch_sem.at[1])
    fetch_x = pltpu.make_async_copy(x_t, ebuf, fetch_sem.at[0])

    def local_c(half, which):
        start = pl.multiple_of(which * tokens, 16)
        return pltpu.make_async_copy(
            cot.at[pl.ds(start, tokens)], cbuf.at[half], fetch_sem.at[2 + half]
        )

    lefts = (y_t, g_t, a2_t, o_t, a1_t)
    left_others = (y_o, g_o, a2_o, o_o, a1_o)
    pieces = hidden // width

    def start_left(c):
        i, j = table[c]
        lower = pl.ds(j * block, block) if i == 1 else slice(None)
        for half, source in ((0, lefts[i]), (1, left_others[i])):
            pltpu.make_async_copy(
                source.at[:, lower, :], lbuf.at[c % 2, half], left_sem.at[c % 2, half]
            ).start()

    fetch_e3.start()
    start_left(0)
    local_c(0, core).start()
    local_c(1, other).start()
    start_left(1)
    fetch_dx.start()
    fetch_gains.start()

    barrier = pltpu.get_barrier_semaphore()
    for index, which in ((me, other), (flip_x, core), (flip_y, core), (far, core)):
        pl.semaphore_signal(barrier, inc=1, device_id=(index, which), device_id_type=MESH)

    @pl.when(zi > 0)
    def _():
        pl.semaphore_signal(barrier, inc=1, device_id=(me - 4, core), device_id_type=MESH)

    @pl.when(zi < length - 1)
    def _():
        pl.semaphore_signal(barrier, inc=1, device_id=(me + 4, core), device_id_type=MESH)

    inner = jnp.where(zi > 0, 1, 0) + jnp.where(zi < length - 1, 1, 0)
    pl.semaphore_wait(barrier, 4 + inner)

    def remote(src, dst, send, recv, index, which):
        return pltpu.make_async_remote_copy(
            src_ref=src,
            dst_ref=dst,
            send_sem=send,
            recv_sem=recv,
            device_id=(index, which),
            device_id_type=MESH,
        )

    PE3, PE2, PEP = range(3)

    def push(k):
        if k == PEP:
            wide = 3 * cols
            src, dst = ep.at[pl.ds(pl.multiple_of(other * wide, 16), wide)], ep_o
        else:
            src, dst = ebuf, (e3_o, e2_o)[k]
            src = src.at[pl.ds(pl.multiple_of(other * cols, 16), cols)]
        return remote(src, dst, push_send.at[k], push_recv.at[k], me, other)

    fetch_e3.wait()
    push(PE3).start()

    def start_right(c):
        i, j = table[c]
        slot = c % 2
        mine = pl.ds(pl.multiple_of(core * cols, 16), cols)
        rows = pl.ds(j * cols, cols)
        if i == 1:
            own, its = ebuf.at[mine], e3_o
            if j == 0:
                push(PE3).wait_recv()
        elif i == 2:
            own, its = eh_mine.at[rows], eh_o.at[rows]
            if j == 0:
                for piece in range(pieces):
                    eh_push(piece, 0).wait_recv()
        elif i == 3:
            own, its = ebuf.at[mine], e2_o
            push(PE2).wait_recv()
        else:
            start = pl.multiple_of(core * 3 * cols + j * cols, 16)
            own, its = ep.at[pl.ds(start, cols)], ep_o.at[rows]
            if j == 0:
                push(PEP).wait_recv()
        pltpu.make_async_copy(own, rbuf.at[slot, 0], right_sem.at[slot, 0]).start()
        pltpu.make_async_copy(its, rbuf.at[slot, 1], right_sem.at[slot, 1]).start()

    def eh_push(piece, slot):
        return remote(
            ehbuf.at[slot],
            eh_o.at[pl.ds(piece * cols, cols)],
            eh_out_sem.at[slot],
            eh_in_sem.at[piece],
            me,
            other,
        )

    def wait_left(slot):
        for half in range(2):
            pltpu.make_async_copy(
                lbuf.at[slot, half], lbuf.at[slot, half], left_sem.at[slot, half]
            ).wait()

    def wait_right(slot):
        for half in range(2):
            pltpu.make_async_copy(
                rbuf.at[slot, half], rbuf.at[slot, half], right_sem.at[slot, half]
            ).wait()

    def form(c, right, multiply):
        slot, ring, to = lax.rem(c, 2), lax.rem(c, LEAD), lax.rem(c, ring_side)

        for z in range(length):
            value = None
            for half in range(2):
                left = lbuf[slot, half, 4 * z : 4 * z + 4].reshape(4 * block, tokens)
                part = multiply(left, right[half])
                value = part if value is None else value + part
            value = value.astype(BF16)
            for q in range(4):
                x, y = q % 2, q // 2
                one = jnp.where(core == 0, x, y)
                two = jnp.where(core == 0, y, x)
                part = value[q * block : (q + 1) * block]
                grad[ring, one, two, z] = part[:, :main]
                side[to, z, one, two] = part[:, main:]
        send1(c).start()
        start_side(c, 1)

    def send1(c):
        ring, spot = lax.rem(c, LEAD), lax.rem(c, rings)
        return remote(
            grad.at[ring, 1 - first_bit],
            recv1.at[spot],
            send1_sem.at[ring],
            recv1_sem.at[spot],
            first_peer,
            core,
        )

    def send2(c):
        ring, spot = lax.rem(c, 2), lax.rem(c, ring2)
        return remote(
            pair.at[ring, 1 - second_bit],
            recv2.at[spot],
            send2_sem.at[ring],
            recv2_sem.at[spot],
            second_peer,
            core,
        )

    def send_up(c, step):
        ring, spot = lax.rem(c, ring_line), lax.rem(c, rings)
        return remote(
            line.at[ring, jnp.minimum(zi + (length - step), length - 1)],
            recv_up.at[spot, step - 1],
            up_send.at[ring, step - 1],
            up_recv.at[spot, step - 1],
            jnp.minimum(me + 4, size - 1),
            core,
        )

    def send_down(c, step):
        ring, spot = lax.rem(c, ring_line), lax.rem(c, rings)
        return remote(
            line.at[ring, jnp.maximum(zi - (length - step), 0)],
            recv_down.at[spot, step - 1],
            down_send.at[ring, step - 1],
            down_recv.at[spot, step - 1],
            jnp.maximum(me - 4, 0),
            core,
        )

    def side_send_up(c, step):
        ring, spot = lax.rem(c, ring_side), lax.rem(c, ring_in)
        return remote(
            side.at[ring, jnp.minimum(zi + (length - step), length - 1)],
            side_up.at[spot, step - 1],
            side_up_send.at[ring, step - 1],
            side_up_recv.at[spot, step - 1],
            jnp.minimum(me + 4, size - 1),
            core,
        )

    def side_send_down(c, step):
        ring, spot = lax.rem(c, ring_side), lax.rem(c, ring_in)
        return remote(
            side.at[ring, jnp.maximum(zi - (length - step), 0)],
            side_down.at[spot, step - 1],
            side_down_send.at[ring, step - 1],
            side_down_recv.at[spot, step - 1],
            jnp.maximum(me - 4, 0),
            core,
        )

    def side_send1(c):
        ring, spot = lax.rem(c, ring_side), lax.rem(c, ring_in)
        return remote(
            side.at[ring, zi, 1 - first_bit],
            side1.at[spot],
            side1_send.at[ring],
            side1_recv.at[spot],
            first_peer,
            core,
        )

    def side_send2(c):
        ring, spot = lax.rem(c, ring_side), lax.rem(c, ring_in)
        return remote(
            side.at[ring, zi, first_bit, 1 - second_bit],
            side2.at[spot],
            side2_send.at[ring],
            side2_recv.at[spot],
            second_peer,
            core,
        )

    def start_side(c, step):
        @pl.when(zi < step)
        def _():
            side_send_up(c, step).start()

        @pl.when(zi >= length - step)
        def _():
            side_send_down(c, step).start()

    def exchange_side(t):
        for step in range(1, length):

            @pl.when((t >= step - 1) & (t <= n + step - 2))
            def _():
                c = t - step + 1
                ring, at = lax.rem(c, ring_side), lax.rem(c, ring_in)
                up_in = (zi >= 1) & (zi <= step)
                down_in = (zi <= length - 2) & (zi >= length - 1 - step)

                @pl.when(up_in)
                def _():
                    side_send_up(c, step).wait_recv()
                    spot = jnp.minimum(zi + (length - 1 - step), length - 1)
                    side[ring, spot] = side[ring, spot] + side_up[at, step - 1]

                @pl.when(down_in)
                def _():
                    side_send_down(c, step).wait_recv()
                    spot = jnp.maximum(zi - (length - 1 - step), 0)
                    side[ring, spot] = side[ring, spot] + side_down[at, step - 1]

                if step < length - 1:
                    start_side(c, step + 1)
                else:
                    side_send1(c).start()

        @pl.when((t >= length - 1) & (t <= n + length - 2))
        def _():
            c = t - length + 1
            ring, at = lax.rem(c, ring_side), lax.rem(c, ring_in)
            side_send1(c).wait_recv()
            side[ring, zi, first_bit] = side[ring, zi, first_bit] + side1[at]
            side_send2(c).start()

        @pl.when((t >= length) & (t <= n + length - 1))
        def _():
            c = t - length
            ring, at = lax.rem(c, ring_side), lax.rem(c, ring_in)
            side_send2(c).wait_recv()
            total[c, :, main:] = side[ring, zi, first_bit, second_bit].astype(F32) + side2[
                at
            ].astype(F32)
            for back in range(1, length):

                @pl.when(zi < back)
                def _():
                    side_send_up(c, back).wait_send()

                @pl.when(zi >= length - back)
                def _():
                    side_send_down(c, back).wait_send()

            side_send1(c).wait_send()
            side_send2(c).wait_send()

    def start_line(c, step):
        @pl.when(zi < step)
        def _():
            send_up(c, step).start()

        @pl.when(zi >= length - step)
        def _():
            send_down(c, step).start()

    def wait_line_sent(c, step):
        @pl.when(zi < step)
        def _():
            send_up(c, step).wait_send()

        @pl.when(zi >= length - step)
        def _():
            send_down(c, step).wait_send()

    def results(c):
        i, j = table[c]
        if i == 0:
            return [pltpu.make_async_copy(total.at[c], out_head, local_sem.at[c])]
        if i == 1:
            target = out_down.at[
                pl.ds((j % 2) * block, block), pl.ds(pl.multiple_of(core * cols, 128), cols)
            ]
            return [
                pltpu.make_async_copy(total.at[c], target, local_sem.at[c]),
                remote(total.at[c], target, swap_send.at[c], swap_recv.at[c], me, other),
            ]
        target = (None, None, out_up, out_out, out_qkv)[i]
        wide = target.shape[1] // 2
        place = target.at[:, pl.ds(pl.multiple_of(core * wide + j * cols, 128), cols)]
        half = block // 2
        mine = pl.ds(pl.multiple_of(core * half, 8), half)
        its = pl.ds(pl.multiple_of(other * half, 8), half)
        return [
            pltpu.make_async_copy(total.at[c, mine], place, local_sem.at[c]),
            remote(total.at[c, its], place, swap_send.at[c], swap_recv.at[c], me, other),
        ]

    def start_results(c):
        i, j = table[c]
        copies = results(c)
        if i == 1:
            owner = j // (pieces // 2)
            pl.when(core == owner)(copies[0].start)
            pl.when(core != owner)(copies[1].start)
        else:
            for copy in copies:
                copy.start()

    def end_results(c):
        i, j = table[c]
        copies = results(c)
        if i == 1:
            owner = j // (pieces // 2)
            pl.when(core == owner)(copies[0].wait)
            pl.when(core == owner)(copies[1].wait_recv)
            pl.when(core != owner)(copies[1].wait_send)
        else:
            for copy in copies:
                copy.wait()

    def exchange(t):
        @pl.when(t < n)
        def _():
            c = t
            send1(c).wait_recv()
            ring, spot, to = lax.rem(c, LEAD), lax.rem(c, rings), lax.rem(c, 2)

            @pl.when(c >= 2)
            def _():
                send2(c - 2).wait_send()

            for two in range(2):

                @pl.loop(0, length)
                def _(z):
                    pair[to, two, z] = grad[ring, first_bit, two, z] + recv1[spot, two, z]

            send2(c).start()

        @pl.when((t >= 1) & (t <= n))
        def _():
            c = t - 1
            send2(c).wait_recv()
            ring, spot, to = lax.rem(c, 2), lax.rem(c, ring2), lax.rem(c, ring_line)

            @pl.loop(0, length)
            def _(z):
                line[to, z] = pair[ring, second_bit, z] + recv2[spot, z]

            start_line(c, 1)

        exchange_side(t)

        for step in range(1, length):

            @pl.when((t >= 1 + step) & (t <= n + step))
            def _():
                c = t - 1 - step
                ring, at = lax.rem(c, ring_line), lax.rem(c, rings)
                last = step == length - 1
                up_in = (zi >= 1) & (zi <= step)
                down_in = (zi <= length - 2) & (zi >= length - 1 - step)

                @pl.when(up_in)
                def _():
                    send_up(c, step).wait_recv()
                    spot = jnp.minimum(zi + (length - 1 - step), length - 1)
                    if not last:
                        line[ring, spot] = line[ring, spot] + recv_up[at, step - 1]

                @pl.when(down_in)
                def _():
                    send_down(c, step).wait_recv()
                    spot = jnp.maximum(zi - (length - 1 - step), 0)
                    if not last:
                        line[ring, spot] = line[ring, spot] + recv_down[at, step - 1]

                if not last:
                    start_line(c, step + 1)
                else:
                    total[c, :, :main] = line[ring, zi].astype(F32)

                    @pl.when(up_in)
                    def _():
                        total[c, :, :main] += recv_up[at, step - 1].astype(F32)

                    @pl.when(down_in)
                    def _():
                        total[c, :, :main] += recv_down[at, step - 1].astype(F32)

                    for back in range(1, length):
                        wait_line_sent(c, back)

                    for d in range(n):

                        @pl.when(c == d)
                        def _():
                            start_results(d)

    local_c(0, core).wait()
    local_c(1, other).wait()
    wait_left(0)
    form(0, [cbuf[0], cbuf[1]], nn)
    start_left(2)
    fetch_x2.start()
    sums[0] = jnp.zeros_like(sums[0])
    for i in range(2):
        share = jnp.sum(cbuf[i].astype(F32), axis=0, keepdims=True)
        at = pl.ds(pl.multiple_of(core * cols, 128), cols)
        sums[0, 3:4, at] = sums[0, 3:4, at] + share
    for c in range(1, LEAD):
        start_right(c)
        wait_left(c % 2)
        wait_right(c % 2)
        form(c, [rbuf[c % 2, 0], rbuf[c % 2, 1]], nt)
        start_left(c + 2)
    fetch_dx.wait()
    fetch_gains.wait()

    def row_tile(k, slot, source):
        return pltpu.make_async_copy(
            source.at[pl.ds(pl.multiple_of(k * cols, 16), cols)], wrows.at[slot], row_sem.at[slot]
        )

    def col_tile(k, slot, source):
        return pltpu.make_async_copy(
            source.at[:, pl.ds(pl.multiple_of(k * cols, 128), cols)],
            wcols.at[slot],
            col_sem.at[slot],
        )

    def h_tile(k, slot):
        return pltpu.make_async_copy(
            h_t.at[pl.ds(pl.multiple_of(k * cols, 16), cols)], hbuf.at[slot], h_sem.at[slot]
        )

    def mlp_tiles(k):
        return jnp.where(k < pieces, other, core) * pieces + lax.rem(k, pieces)

    def fetch_mlp(k):
        slot = lax.rem(k, 2)
        tile = mlp_tiles(k)
        row_tile(tile, slot, w_down).start()
        col_tile(tile, slot, w_up).start()
        h_tile(tile, slot).start()

    def mlp_step(k):
        slot = lax.rem(k, 2)
        tile = mlp_tiles(k)
        row_tile(tile, slot, w_down).wait()
        h_tile(tile, slot).wait()

        @pl.when((k >= 2) & (k < pieces + 2))
        def _():
            eh_push(0, slot).wait_send()

        @pl.when(k >= pieces + 2)
        def _():
            pltpu.make_async_copy(
                ehbuf.at[slot], eh_mine.at[pl.ds(0, cols)], eh_out_sem.at[slot]
            ).wait()

        part = cols // 2
        for i in range(2):
            rows = slice(i * part, (i + 1) * part)
            value = nn(wrows[slot, rows], ebuf[...])
            pre = hbuf[slot, rows].astype(F32)
            sig = 1.0 / (1.0 + jnp.exp(-pre))
            ehbuf[slot, rows] = (value * sig * (1.0 + pre * (1.0 - sig))).astype(BF16)

        where = lax.rem(k, pieces)

        @pl.when(k < pieces)
        def _():
            eh_push(where, slot).start()

        @pl.when(k >= pieces)
        def _():
            pltpu.make_async_copy(
                ehbuf.at[slot],
                eh_mine.at[pl.ds(pl.multiple_of(where * cols, 16), cols)],
                eh_out_sem.at[slot],
            ).start()

        col_tile(tile, slot, w_up).wait()
        accumulate(wcols.at[slot], ehbuf.at[slot], k == 0)

        @pl.when(k + 2 < 2 * pieces)
        def _():
            fetch_mlp(k + 2)

    def accumulate(left, right, first):
        @pl.when(first)
        def _():
            acc[...] = jnp.zeros_like(acc)

        part = width // 4
        for i in range(4):
            rows = slice(i * part, (i + 1) * part)
            acc[rows] += nn(left[rows], right[...])

    fetch_mlp(0)
    fetch_mlp(1)

    def emit_mlp(k, rows, value):
        value = dx[rows] + value
        dx[rows] = value
        ebuf[rows] = value.astype(BF16)

    def middle():
        for slot in range(2):
            pltpu.make_async_copy(
                ehbuf.at[slot], eh_mine.at[pl.ds(0, cols)], eh_out_sem.at[slot]
            ).wait()
        row_tile(0, 0, w_out).start()
        row_tile(1, 1, w_out).start()
        push(PE3).wait_send()
        fetch_x2.wait()
        norm_backward(work, acc, gains, 1, emit_mlp)
        push(PE2).start()

        @pl.loop(0, 2)
        def _(k):
            row_tile(k, k, w_out).wait()

            group = cols // hdim
            value = nn(wrows[k], ebuf[...]).astype(BF16)
            eo[pl.ds(k * group, group)] = value.reshape(group, hdim, tokens)

        mask_of(seg_row, bias)

    per_turn = count // 4

    def head_copy(head, slot, u, part):
        return pltpu.make_async_copy(
            qkv_t.at[pl.ds(pl.multiple_of(part * width + head * hdim, 16), hdim)],
            heads.at[slot, u, part],
            head_sem.at[slot, u, part],
        )

    def fetch_heads(i):
        for u in range(TOGETHER):
            for part in range(3):
                head_copy(i * TOGETHER + u, lax.rem(i, 2), u, part).start()

    def attend_head(head, slot, u):
        q_t, k_t, v_t = (heads[slot, u, part] for part in range(3))
        e_t = eo[head]
        q, k, v, e = q_t.T, k_t.T, v_t.T, e_t.T
        blocks = list(query_blocks(tokens))
        weight = lse[head]
        ek, ev, eqs = [[] for _ in blocks], [[] for _ in blocks], []
        for low, high, asked in blocks:
            scores = nn(k[low:high], q_t[:, asked]) * scale + bias[low:high, asked]
            p = jnp.exp(scores - weight[:, asked])
            ep_t = nn(v[low:high], e_t[:, asked])
            share = jnp.sum(p * ep_t, axis=0, keepdims=True)
            es = (p * (ep_t - share)).astype(BF16)
            eqs.append(nn(k_t[:, low:high], es))
            one, two = nn(es, q[asked]), nn(p.astype(BF16), e[asked])
            for number, (_, _, own) in enumerate(blocks):
                if low <= own.start < high:
                    ek[number].append(one[own.start - low : own.stop - low])
                    ev[number].append(two[own.start - low : own.stop - low])
        ek_t = jnp.concatenate([sum(terms[1:], terms[0]) for terms in ek], axis=0).T
        ev_t = jnp.concatenate([sum(terms[1:], terms[0]) for terms in ev], axis=0).T
        half = hdim // 2
        for part, value in ((0, jnp.concatenate(eqs, axis=1)), (1, ek_t)):
            one, two = value[:half] * scale, value[half:] * scale
            turned = jnp.concatenate(
                [one * cosine[...] + two * sine[...], two * cosine[...] - one * sine[...]],
                axis=0,
            )
            to = pl.ds(pl.multiple_of(part * width + head * hdim, 16), hdim)
            ep[to] = turned.astype(BF16)
        to = pl.ds(pl.multiple_of(2 * width + head * hdim, 16), hdim)
        ep[to] = ev_t.astype(BF16)

    def attend(turn):
        @pl.when(turn == 0)
        def _():
            fetch_heads(0)

        @pl.loop(0, per_turn // TOGETHER)
        def _(j):
            i = turn * (per_turn // TOGETHER) + j
            slot = lax.rem(i, 2)
            for u in range(TOGETHER):
                for part in range(3):
                    head_copy(i * TOGETHER + u, slot, u, part).wait()

            @pl.when((i + 1) * TOGETHER < count)
            def _():
                fetch_heads(i + 1)

            for u in range(TOGETHER):
                attend_head(i * TOGETHER + u, slot, u)

        @pl.when(turn == 3)
        def _():
            push(PEP).start()

    def fetch_qkv(k):
        col_tile(k, lax.rem(k, 2), w_qkv).start()

    def qkv_step(k):
        slot = lax.rem(k, 2)
        col_tile(k, slot, w_qkv).wait()
        rows = pl.ds(pl.multiple_of(k * cols, 16), cols)
        accumulate(wcols.at[slot], ep.at[rows], k == 0)

        @pl.when(k + 2 < 6)
        def _():
            fetch_qkv(k + 2)

    def entry_copy(k, slot):
        return pltpu.make_async_copy(
            obuf.at[slot],
            out_entry.at[:, pl.ds(pl.multiple_of(k * STRIP, STRIP), STRIP)],
            entry_sem.at[slot],
        )

    def emit_entry(k, rows, value):
        slot = lax.rem(k, 2)

        @pl.when(k >= 2)
        def _():
            entry_copy(k, slot).wait()

        obuf[slot] = (dx[rows] + value).T
        entry_copy(k, slot).start()

    peers = ((me, other), (flip_x, core), (flip_y, core), (near, core), (far, core))
    steps = len(peers)

    def small_copy(i):
        return remote(
            sums.at[i], sums_in.at[i], small_send.at[i], small_recv.at[i], peers[i][0], peers[i][1]
        )

    def last():
        fetch_x.wait()
        norm_backward(ebuf, acc, gains, 0, emit_entry)
        for slot in range(2):
            entry_copy(0, slot).wait()
        sums[0] = sums[0] + gains[...].T[8:16]
        small_copy(0).start()

    @pl.loop(0, n + length)
    def _(t):
        for c in range(LEAD, n):

            @pl.when(t == c - LEAD)
            def _():
                start_right(c)

        @pl.when(t < 2)
        def _():
            @pl.loop(0, pieces)
            def _(i):
                mlp_step(t * pieces + i)

        @pl.when(t == 2)
        def _():
            middle()

        @pl.when((t >= 3) & (t < 7))
        def _():
            attend(t - 3)

        @pl.when(t == 6)
        def _():
            fetch_qkv(0)
            fetch_qkv(1)

        @pl.when((t == 7) | (t == 8))
        def _():
            @pl.loop(0, 3)
            def _(i):
                qkv_step((t - 7) * 3 + i)

        @pl.when(t == 9)
        def _():
            last()

        for i in range(steps):

            @pl.when(t == 10 + i)
            def _():
                small_copy(i).wait()
                value = sums[i] + sums_in[i]
                if i == steps - 1:
                    out_small[...] = value
                else:
                    sums[i + 1] = value
                    small_copy(i + 1).start()

        exchange(t)

        @pl.when(t + LEAD < n)
        def _():
            c = t + LEAD
            slot = lax.rem(c, 2)
            wait_left(slot)
            wait_right(slot)
            send1(t).wait_send()
            form(c, [rbuf[slot, 0], rbuf[slot, 1]], nt)
            for d in range(LEAD + 2, n):

                @pl.when(c == d - 2)
                def _():
                    start_left(d)

        @pl.when(t == 8)
        def _():
            push(PE2).wait_send()
            fetch_x.start()

    for c in range(n):
        end_results(c)
    for c in range(n - LEAD, n):
        send1(c).wait_send()
    for c in range(n - 2, n):
        send2(c).wait_send()
    push(PEP).wait_send()


def run_backward(lefts, left_others, others, weights, tables):
    size = lax.axis_size("dp")
    width, tokens = lefts[0].shape
    hidden = lefts[1].shape[0]
    block = width // size
    cols = width // 2
    table = chunk_table(width, hidden)
    n = len(table)
    length = size // 4
    share = block // 2
    hdim = width // HEADS
    hbm = pl.BlockSpec(memory_space=pl.ANY)
    vmem = pl.BlockSpec(memory_space=pltpu.VMEM)
    lefts = [left.reshape(size, left.shape[0] // size, tokens) for left in lefts + left_others]
    shapes = [
        jax.ShapeDtypeStruct((block, cols), F32),
        jax.ShapeDtypeStruct((hidden // size // 2, width), F32),
        jax.ShapeDtypeStruct((share, hidden), F32),
        jax.ShapeDtypeStruct((share, width), F32),
        jax.ShapeDtypeStruct((share, 3 * width), F32),
        jax.ShapeDtypeStruct((8, width), F32),
        jax.ShapeDtypeStruct((tokens, width), F32),
    ]
    shapes += [
        jax.ShapeDtypeStruct((rows, tokens), BF16)
        for rows in (cols, hidden // 2, cols, 3 * cols, hidden // 2)
    ]
    dma = pltpu.SemaphoreType.DMA
    ring1, ring2, ring_line = 6, 4, length + 1
    main = cols - 128
    results = pl.pallas_call(
        functools.partial(backward_kernel, table, size),
        out_shape=shapes,
        in_specs=[hbm] * 22 + [vmem] * 4,
        out_specs=[hbm] * 5 + [vmem] + [hbm] * 6,
        scratch_shapes=[
            pltpu.VMEM((2, 2, size, block, tokens), BF16),
            pltpu.VMEM((2, 2, cols, tokens), BF16),
            pltpu.VMEM((2, tokens, cols), BF16),
            pltpu.VMEM((LEAD, 2, 2, length, block, main), BF16),
            pltpu.VMEM((ring1, 2, length, block, main), BF16),
            pltpu.VMEM((2, 2, length, block, main), BF16),
            pltpu.VMEM((ring2, length, block, main), BF16),
            pltpu.VMEM((ring_line, length, block, main), BF16),
            pltpu.VMEM((ring1, length - 1, block, main), BF16),
            pltpu.VMEM((ring1, length - 1, block, main), BF16),
            pltpu.VMEM((length + 4, length, 2, 2, block, cols - main), BF16),
            pltpu.VMEM((length + 3, length - 1, 2, 2, block, cols - main), BF16),
            pltpu.VMEM((length + 3, length - 1, 2, 2, block, cols - main), BF16),
            pltpu.VMEM((length + 3, 2, block, cols - main), BF16),
            pltpu.VMEM((length + 3, block, cols - main), BF16),
            pltpu.VMEM((n, block, cols), F32),
            pltpu.VMEM((5, 8, width), F32),
            pltpu.VMEM((5, 8, width), F32),
            pltpu.VMEM((width, tokens), F32),
            pltpu.VMEM((width, tokens), F32),
            pltpu.VMEM((width, tokens), F32),
            pltpu.VMEM((width, tokens), BF16),
            pltpu.VMEM((tokens, tokens), F32),
            pltpu.VMEM((width, 128), F32),
            pltpu.VMEM((2, cols, width), BF16),
            pltpu.VMEM((2, width, cols), BF16),
            pltpu.VMEM((2, cols, tokens), BF16),
            pltpu.VMEM((2, cols, tokens), BF16),
            pltpu.VMEM((3 * width, tokens), BF16),
            pltpu.VMEM((HEADS, hdim, tokens), BF16),
            pltpu.VMEM((2, TOGETHER, 3, hdim, tokens), BF16),
            pltpu.VMEM((2, tokens, 128), F32),
            dma((3,)),
            dma((3,)),
            dma((2, 2)),
            dma((2, 2)),
            dma((LEAD,)),
            dma((ring1,)),
            dma((2,)),
            dma((ring2,)),
            dma((ring_line, length - 1)),
            dma((ring1, length - 1)),
            dma((ring_line, length - 1)),
            dma((ring1, length - 1)),
            dma((length + 4, length - 1)),
            dma((length + 3, length - 1)),
            dma((length + 4, length - 1)),
            dma((length + 3, length - 1)),
            dma((length + 4,)),
            dma((length + 3,)),
            dma((length + 4,)),
            dma((length + 3,)),
            dma((n,)),
            dma((n,)),
            dma((n,)),
            dma((5,)),
            dma((5,)),
            dma((2,)),
            dma((2,)),
            dma((2,)),
            dma((2,)),
            dma((hidden // width,)),
            dma((2, TOGETHER, 3)),
            dma((5,)),
            dma((2,)),
        ],
        compiler_params=pltpu.CompilerParams(
            collective_id=0, has_side_effects=True, vmem_limit_bytes=62 << 20
        ),
        name="backward",
    )(*lefts, *others, *weights, *tables)
    return results[:7]


def finish_kernel(
    copied,
    *refs,
):
    sources = refs[:copied]
    sums, y_t, y_o, w_head, head_bias = refs[copied : copied + 5]
    results = refs[copied + 5 :]
    targets = results[:copied]
    levels, gain_attn, gain_mlp, gain_final, bias = results[copied : copied + 5]
    ybuf, wbuf, out, fetch_sem, copy_sem, in_sem, out_sem = results[copied + 5 : copied + 12]
    held = results[copied + 12 :]
    me = lax.axis_index("dp")
    core = lax.axis_index("head")
    width, tokens = y_t.shape
    half = width // 2
    fetches = [
        pltpu.make_async_copy(source, target, in_sem.at[i])
        for i, (source, target) in enumerate(
            ((w_head, wbuf), (y_t, ybuf.at[0]), (y_o, ybuf.at[1]))
        )
    ]
    for fetch in fetches:
        fetch.start()
    arrivals = [
        pltpu.make_async_copy(source, buffer, fetch_sem.at[i])
        for i, (source, buffer) in enumerate(zip(sources, held))
    ]
    copies = [
        pltpu.make_async_copy(buffer, target, copy_sem.at[i])
        for i, (buffer, target) in enumerate(zip(held, targets))
    ]
    for arrival in arrivals:
        arrival.start()
    share = gain_attn.shape[0]
    start = (me * 2 + core) * share
    rolled = pltpu.roll(sums[...], lax.rem(width - start, width), 1)
    for i, target in enumerate((gain_attn, gain_mlp, gain_final)):
        target[...] = rolled[i, :share]
    bias[...] = sums[3, pl.ds(pl.multiple_of(core * half, 128), half)]
    fetches[0].wait()
    part = tokens // 2

    def level_copy(i):
        which = core if i < 2 else 1 - core
        start = pl.multiple_of(which * tokens + (i % 2) * part, 8)
        return pltpu.make_async_copy(out.at[i], levels.at[pl.ds(start, part)], out_sem.at[i])

    for i in range(4):
        if i % 2 == 0:
            fetches[1 + i // 2].wait()
        at = slice((i % 2) * part, (i % 2 + 1) * part)
        out[i] = tt(ybuf[i // 2, :, at], wbuf[...]) + head_bias[...].reshape(1, half)
        level_copy(i).start()
        for k in range(i * len(copies) // 4, (i + 1) * len(copies) // 4):
            arrivals[k].wait()
            copies[k].start()
    for i in range(4):
        level_copy(i).wait()
    for copy in copies:
        copy.wait()


def run_finish(copied, sums, y_t, y_o, w_head, head_bias):
    width, tokens = y_t.shape
    half = width // 2
    share = width // (2 * lax.axis_size("dp"))
    hbm = pl.BlockSpec(memory_space=pl.ANY)
    vmem = pl.BlockSpec(memory_space=pltpu.VMEM)
    dma = pltpu.SemaphoreType.DMA
    shapes = [jax.ShapeDtypeStruct(value.shape, F32) for value in copied]
    shapes += [jax.ShapeDtypeStruct((2 * tokens, half), F32)]
    shapes += [jax.ShapeDtypeStruct((share,), F32)] * 3 + [jax.ShapeDtypeStruct((half,), F32)]
    return pl.pallas_call(
        functools.partial(finish_kernel, len(copied)),
        out_shape=shapes,
        in_specs=[hbm] * len(copied) + [vmem] + [hbm] * 3 + [vmem],
        out_specs=[hbm] * (len(copied) + 1) + [vmem] * 4,
        scratch_shapes=[
            pltpu.VMEM((2, width, tokens), BF16),
            pltpu.VMEM((width, half), BF16),
            pltpu.VMEM((4, tokens // 2, half), F32),
            dma((len(copied),)),
            dma((len(copied),)),
            dma((3,)),
            dma((4,)),
        ]
        + [pltpu.VMEM(value.shape, F32) for value in copied],
        compiler_params=pltpu.CompilerParams(vmem_limit_bytes=60 << 20),
        name="finish",
    )(*copied, sums, y_t, y_o, w_head, head_bias)


def per_device(
    inputs,
    segment_ids,
    gain_attn,
    w_qkv,
    w_out,
    gain_mlp,
    w_up,
    w_down,
    gain_final,
    head_projection_weight,
    head_output_bias,
    cotangent,
):
    core = lax.axis_index("head")
    place = lax.axis_index("dp")
    size = lax.axis_size("dp")
    rows, sequence_span = segment_ids.shape
    count, width = inputs.shape
    hdim = width // HEADS
    scale = 1.0 / math.sqrt(hdim)
    share = width // (2 * size)
    fused = size == HEADS and lax.axis_size("head") == 2 and rows == 1

    if fused:
        half = width // 2
        turn = hdim // 2
        freq = np.float32(10000.0) ** (-np.arange(turn, dtype=np.float32) / np.float32(turn))
        angle = np.arange(sequence_span, dtype=np.float32)[None, :] * freq[:, None]
        cosine_t, sine_t = jnp.asarray(np.cos(angle)), jnp.asarray(np.sin(angle))
        (
            y_t,
            g_t,
            a2_t,
            o_t,
            a1_t,
            y_o,
            g_o,
            a2_o,
            o_o,
            a1_o,
            dx3_t,
            e3_t,
            gain_columns,
            x2_t,
            x_t,
            h_t,
            qkv_t,
            lse,
        ) = run_forward(
            inputs,
            w_qkv,
            w_out,
            w_up,
            w_down,
            head_projection_weight,
            cotangent,
            segment_ids,
            [gain_attn, gain_mlp, gain_final],
            cosine_t,
            sine_t,
        )
        head, down, up, out, qkv, sums, entry = run_backward(
            [y_t, g_t, a2_t, o_t, a1_t],
            [y_o, g_o, a2_o, o_o, a1_o],
            [cotangent, dx3_t, e3_t, x2_t, x_t, h_t, qkv_t, gain_columns],
            [w_down, w_up, w_out, w_qkv],
            [lse, segment_ids, cosine_t, sine_t],
        )
        (
            entry_sensitivity_matrix,
            grad_head,
            grad_down,
            grad_up,
            grad_out,
            grad_qkv,
            predicted_levels,
            *gains,
            grad_bias,
        ) = run_finish(
            [entry, head, down, up, out, qkv],
            sums,
            y_t,
            y_o,
            head_projection_weight,
            head_output_bias,
        )
    else:
        other_rows = lax.dynamic_slice_in_dim(cotangent, (1 - core) * count, count, 0)
        own_rows = lax.dynamic_slice_in_dim(cotangent, core * count, count, 0)
        got = swap_cores(contract_cols(head_projection_weight, other_rows).astype(BF16))
        grad_final_t = contract_cols(head_projection_weight, own_rows) + got.astype(F32)
        bias_local = jnp.sum(cotangent, axis=0, dtype=F32)

        cosine, sine = rotary_tables(sequence_span, hdim)
        tokens = inputs.astype(jnp.float32)
        normed_one, inverse_one = rms_forward(tokens, gain_attn)
        act_one = normed_one.astype(jnp.bfloat16)
        projected = jnp.dot(act_one, w_qkv, preferred_element_type=jnp.float32).reshape(
            rows, sequence_span, 3, HEADS, hdim
        )
        query = rotate(projected[:, :, 0], cosine, sine).astype(jnp.bfloat16)
        key = rotate(projected[:, :, 1], cosine, sine).astype(jnp.bfloat16)
        value = projected[:, :, 2].astype(jnp.bfloat16)
        attended, log_total = lax.map(
            lambda items: attend_forward(items, scale), (query, key, value, segment_ids)
        )
        mixed = attended.reshape(rows * sequence_span, width)
        resid_two = tokens + jnp.dot(mixed, w_out, preferred_element_type=jnp.float32)
        normed_two, inverse_two = rms_forward(resid_two, gain_mlp)
        act_two = normed_two.astype(jnp.bfloat16)
        hidden_pre = jnp.dot(act_two, w_up, preferred_element_type=jnp.float32)
        hidden = jax.nn.silu(hidden_pre).astype(jnp.bfloat16)
        resid_three = resid_two + jnp.dot(hidden, w_down, preferred_element_type=jnp.float32)
        normed_three, inverse_three = rms_forward(resid_three, gain_final)
        final_hidden = normed_three.astype(jnp.bfloat16)
        other_hidden = swap_cores(final_hidden)
        collected_rows = jnp.concatenate(
            [
                jnp.where(core == 0, final_hidden, other_hidden),
                jnp.where(core == 0, other_hidden, final_hidden),
            ],
            axis=0,
        )
        predicted_levels = (
            jnp.dot(collected_rows, head_projection_weight, preferred_element_type=jnp.float32)
            + head_output_bias
        )
        grad_head = lax.psum_scatter(
            contract_rows(collected_rows, cotangent), "dp", scatter_dimension=0, tiled=True
        )
        grad_three, grad_gain_final = rms_backward(
            resid_three, inverse_three, gain_final, grad_final_t.T
        )
        grad_mlp_out = grad_three.astype(jnp.bfloat16)
        grad_hidden = contract_cols(grad_mlp_out, w_down)
        sigmoid = jax.nn.sigmoid(hidden_pre)
        grad_pre = (grad_hidden * sigmoid * (1.0 + hidden_pre * (1.0 - sigmoid))).astype(BF16)
        grad_norm_two, grad_gain_mlp = rms_backward(
            resid_two, inverse_two, gain_mlp, contract_cols(grad_pre, w_up)
        )
        grad_two = grad_three + grad_norm_two
        grad_branch = grad_two.astype(jnp.bfloat16)
        grad_mixed = (
            contract_cols(grad_branch, w_out)
            .astype(jnp.bfloat16)
            .reshape(rows, sequence_span, HEADS, hdim)
        )
        grad_query, grad_key, grad_value = lax.map(
            lambda items: attend_backward(items, scale),
            (query, key, value, segment_ids, log_total, grad_mixed),
        )
        grad_query = unrotate(grad_query, cosine, sine)
        grad_key = unrotate(grad_key, cosine, sine)
        grad_proj = (
            jnp.stack([grad_query, grad_key, grad_value], axis=2)
            .reshape(rows * sequence_span, 3 * width)
            .astype(jnp.bfloat16)
        )
        grad_norm_one, grad_gain_attn = rms_backward(
            tokens, inverse_one, gain_attn, contract_cols(grad_proj, w_qkv)
        )
        entry_sensitivity_matrix = grad_two + grad_norm_one
        grad_down = scatter_rows(hidden, grad_mlp_out)
        grad_up = scatter_rows(act_two, grad_pre)
        grad_out = scatter_rows(mixed, grad_branch)
        grad_qkv = scatter_rows(act_one, grad_proj)
        gains = sum_everywhere(jnp.stack([grad_gain_attn, grad_gain_mlp, grad_gain_final]), True)
        gains = lax.dynamic_slice_in_dim(gains, (place * 2 + core) * share, share, 1)
        grad_bias = sum_everywhere(bias_local, False)
    return (
        predicted_levels,
        entry_sensitivity_matrix,
        gains[0],
        grad_qkv,
        grad_out,
        gains[1],
        grad_up,
        grad_down,
        gains[2],
        grad_head,
        grad_bias,
    )


def solution(mesh):
    return jax.shard_map(
        per_device,
        mesh=mesh,
        in_specs=(
            P(("dp", "head"), None),
            P(("dp", "head"), None),
            P(),
            P(),
            P(),
            P(),
            P(),
            P(),
            P(),
            P(None, "head"),
            P("head"),
            P("dp", "head"),
        ),
        out_specs=(
            P("dp", "head"),
            P(("dp", "head"), None),
            P(("dp", "head")),
            P(("dp", "head"), None),
            P(("dp", "head"), None),
            P(("dp", "head")),
            P(("dp", "head"), None),
            P(("dp", "head"), None),
            P(("dp", "head")),
            P("dp", "head"),
            P("head"),
        ),
        check_vma=False,
    )
```

```python
import functools
import math

import jax
import jax.numpy as jnp
import numpy as np
from jax import lax
from jax.experimental import pallas as pl
from jax.experimental.pallas import tpu as pltpu
from jax.sharding import PartitionSpec as P

HEADS = 16
F32 = jnp.float32
BF16 = jnp.bfloat16

epsilon = 1e-06


def rms_forward(values, gain):
    inverse = lax.rsqrt(jnp.mean(values * values, axis=-1, keepdims=True) + epsilon)
    return (values * inverse * gain, inverse)


def rms_backward(values, inverse, gain, grad):
    normed = values * inverse
    scaled = grad * gain
    grad_gain = jnp.sum(grad * normed, axis=0)
    grad_values = inverse * (scaled - normed * jnp.mean(scaled * normed, axis=-1, keepdims=True))
    return (grad_values, grad_gain)


def rotary_tables(sequence_span, hdim):
    half = hdim // 2
    freq = 10000.0 ** (-jnp.arange(half, dtype=jnp.float32) / half)
    angle = jnp.arange(sequence_span, dtype=jnp.float32)[:, None] * freq[None, :]
    return (jnp.cos(angle)[:, None, :], jnp.sin(angle)[:, None, :])


def rotate(values, cosine, sine):
    half = values.shape[-1] // 2
    first = values[..., :half]
    second = values[..., half:]
    return jnp.concatenate(
        [first * cosine - second * sine, second * cosine + first * sine], axis=-1
    )


def unrotate(grads, cosine, sine):
    half = grads.shape[-1] // 2
    first = grads[..., :half]
    second = grads[..., half:]
    return jnp.concatenate(
        [first * cosine + second * sine, second * cosine - first * sine], axis=-1
    )


def allowed_mask(segs):
    place = jnp.arange(segs.shape[0])
    return (segs[:, None] == segs[None, :]) & (place[:, None] >= place[None, :])


def row_scores(query, key, segs, scale):
    scores = jnp.einsum("qhd,khd->hqk", query, key, preferred_element_type=jnp.float32) * scale
    allowed = allowed_mask(segs)[None]
    return (jnp.where(allowed, scores, -1e30), allowed)


def attend_forward(items, scale):
    query, key, value, segs = items
    scores, allowed = row_scores(query, key, segs, scale)
    peak = jnp.max(scores, axis=-1, keepdims=True)
    expo = jnp.exp(scores - peak)
    overall_number = jnp.sum(expo, axis=-1, keepdims=True)
    probs = (expo / overall_number).astype(jnp.bfloat16)
    attended = jnp.einsum("hqk,khd->qhd", probs, value, preferred_element_type=jnp.float32)
    return (attended.astype(jnp.bfloat16), peak + jnp.log(overall_number))


def attend_backward(items, scale):
    query, key, value, segs, log_total, grad_attended = items
    scores, allowed = row_scores(query, key, segs, scale)
    probs = jnp.where(allowed, jnp.exp(scores - log_total), 0.0)
    grad_value = jnp.einsum(
        "hqk,qhd->khd",
        probs.astype(jnp.bfloat16),
        grad_attended,
        preferred_element_type=jnp.float32,
    )
    grad_probs = jnp.einsum(
        "qhd,khd->hqk", grad_attended, value, preferred_element_type=jnp.float32
    )
    grad_scores = (
        probs * (grad_probs - jnp.sum(grad_probs * probs, axis=-1, keepdims=True))
    ).astype(jnp.bfloat16)
    grad_query = (
        jnp.einsum("hqk,khd->qhd", grad_scores, key, preferred_element_type=jnp.float32) * scale
    )
    grad_key = (
        jnp.einsum("hqk,qhd->khd", grad_scores, query, preferred_element_type=jnp.float32) * scale
    )
    return (grad_query, grad_key, grad_value)


def contract_rows(left, right):
    return lax.dot_general(
        left, right, (((0,), (0,)), ((), ())), preferred_element_type=jnp.float32
    )


def contract_cols(left, right):
    return lax.dot_general(
        left, right, (((1,), (1,)), ((), ())), preferred_element_type=jnp.float32
    )


def swap_cores(values):
    return lax.ppermute(values, "head", [(0, 1), (1, 0)])


def flip(values, bit):
    size = lax.axis_size("dp")
    return lax.ppermute(values, "dp", [(i, i ^ bit) for i in range(size)])


def scatter_rows(left, right):
    return lax.psum_scatter(
        contract_rows(left, right), ("dp", "head"), scatter_dimension=0, tiled=True
    )


def sum_everywhere(values, over_head):
    size = lax.axis_size("dp")
    if over_head:
        values = values + swap_cores(values)
    bit = 1
    while bit < size:
        values = values + flip(values, bit)
        bit *= 2
    return values


MESH = pl.DeviceIdType.MESH


def chunk_table(width, hidden):
    table = [(0, 0)]
    table += [(1, j) for j in range(hidden // width)]
    table += [(2, j) for j in range(hidden // width)]
    table += [(3, 0)]
    table += [(4, j) for j in range(3)]
    return table


def nt(left, right):
    return lax.dot_general(
        left, right, (((1,), (1,)), ((), ())), preferred_element_type=jnp.float32
    )


def nn(left, right):
    return jnp.dot(left, right, preferred_element_type=jnp.float32)


def tt(left, right):
    return lax.dot_general(
        left, right, (((0,), (0,)), ((), ())), preferred_element_type=jnp.float32
    )


def columns_of(rows, scratch):
    scratch[...] = jnp.zeros_like(scratch)
    for i, row in enumerate(rows):
        scratch[i : i + 1] = row[...].reshape(1, row.shape[0])
    return scratch[...].T


def mask_of(seg_row, bias):
    tokens = bias.shape[0]
    ids = seg_row[...].astype(F32)
    wide = jnp.broadcast_to(ids, (8, tokens)).T[:, :1]
    own = lax.broadcasted_iota(jnp.int32, (tokens, tokens), 0)
    asked = lax.broadcasted_iota(jnp.int32, (tokens, tokens), 1)
    bias[...] = jnp.where((wide == ids) & (own <= asked), 0.0, -1e30)


STRIP = 128
SLOTS = 4
REACH = 256
TOGETHER = 2


def query_blocks(tokens):
    for start in range(0, tokens, REACH):
        stop = min(start + REACH, tokens)
        yield max(0, start - REACH), stop, slice(start, stop)


def norm_backward(vref, eref, gains, index, emit):
    width, tokens = vref.shape

    def sums_of(k, carry):
        squares, products = carry
        rows = pl.ds(pl.multiple_of(k * STRIP, STRIP), STRIP)
        v = vref[rows].astype(F32)
        e = eref[rows]
        gain = gains[rows, index : index + 1]
        squares = squares + jnp.sum(v * v, axis=0, keepdims=True)
        products = products + jnp.sum(e * gain * v, axis=0, keepdims=True)
        return squares, products

    blank = jnp.zeros((1, tokens), F32)
    squares, products = lax.fori_loop(0, width // STRIP, sums_of, (blank, blank))
    inverse = lax.rsqrt(squares / width + epsilon)
    mean = products * inverse / width

    @pl.loop(0, width // STRIP)
    def _(k):
        rows = pl.ds(pl.multiple_of(k * STRIP, STRIP), STRIP)
        normed = vref[rows].astype(F32) * inverse
        e = eref[rows]
        gain = gains[rows, index : index + 1]
        gains[rows, 8 + index : 9 + index] = jnp.sum(e * normed, axis=1, keepdims=True)
        emit(k, rows, inverse * (e * gain - normed * mean))


def forward_kernel(
    x,
    w_qkv,
    w_out,
    w_up,
    w_down,
    seg_row,
    gain_attn,
    gain_mlp,
    gain_final,
    cosine,
    sine,
    y_t,
    g_t,
    a2_t,
    o_t,
    a1_t,
    g_o,
    a2_o,
    o_o,
    a1_o,
    x3_t,
    gain_columns,
    x2_t,
    x_t,
    h_t,
    qkv_t,
    lse,
    weights,
    xin,
    xt,
    act1,
    act2,
    final,
    mixed,
    qkv,
    res2,
    res3,
    hbuf,
    gbuf,
    bias,
    gains,
    gain_rows,
    weight_sem,
    in_sem,
    out_sem,
    h_sem,
    g_sem,
    push_send,
    push_recv,
    g_send,
    g_recv,
):
    width, tokens = res2.shape
    hidden = h_t.shape[0]
    pieces = hidden // width
    half = width // 2
    count = HEADS
    hdim = width // count
    scale = 1.0 / math.sqrt(hdim)
    first_tiles = [w_qkv.at[:, k * width : (k + 1) * width] for k in range(3)] + [w_out]

    def fetch(k):
        return pltpu.make_async_copy(first_tiles[k], weights.at[k], weight_sem.at[k])

    def fetch_up(k):
        slot = lax.rem(2 * k, SLOTS)
        source = w_up.at[:, pl.ds(pl.multiple_of(k * width, 128), width)]
        return pltpu.make_async_copy(source, weights.at[slot], weight_sem.at[slot])

    def fetch_down(k):
        slot = lax.rem(2 * k + 1, SLOTS)
        source = w_down.at[pl.ds(pl.multiple_of(k * width, 16), width)]
        return pltpu.make_async_copy(source, weights.at[slot], weight_sem.at[slot])

    me = lax.axis_index("dp")
    core = lax.axis_index("head")
    other = 1 - core

    def remote(src, dst, send, recv):
        return pltpu.make_async_remote_copy(
            src_ref=src,
            dst_ref=dst,
            send_sem=send,
            recv_sem=recv,
            device_id=(me, other),
            device_id_type=MESH,
        )

    fetch_x = pltpu.make_async_copy(x, xin, in_sem)
    fetch_x.start()
    for k in range(SLOTS):
        fetch(k).start()

    barrier = pltpu.get_barrier_semaphore()
    pl.semaphore_signal(barrier, inc=1, device_id=(me, other), device_id_type=MESH)
    gains[...] = jnp.zeros_like(gains)
    gains[:, :8] = columns_of((gain_attn, gain_mlp, gain_final), gain_rows)
    pl.semaphore_wait(barrier, 1)

    mask_of(seg_row, bias)
    fetch_x.wait()
    xt[...] = xin[...].T
    outs, pushes = [], []

    def put(source, target, also=None):
        copy = pltpu.make_async_copy(source, target, out_sem.at[len(outs)])
        outs.append(copy)
        copy.start()
        if also is not None:
            number = len(pushes)
            pushes.append(remote(source, also, push_send.at[number], push_recv.at[number]))
            pushes[-1].start()

    put(xt, x_t)
    put(gains, gain_columns)

    def squares_of(ref):
        def step(k, total):
            v = ref[pl.ds(pl.multiple_of(k * STRIP, STRIP), STRIP)].astype(F32)
            return total + jnp.sum(v * v, axis=0, keepdims=True)

        return lax.fori_loop(0, width // STRIP, step, jnp.zeros((1, tokens), F32))

    def normalize(ref, index, to):
        inverse = lax.rsqrt(squares_of(ref) / width + epsilon)

        @pl.loop(0, width // STRIP)
        def _(k):
            rows = pl.ds(pl.multiple_of(k * STRIP, STRIP), STRIP)
            to[rows] = (ref[rows].astype(F32) * inverse * gains[rows, index : index + 1]).astype(
                BF16
            )

    normalize(xt, 0, act1)
    put(act1, a1_t, a1_o)

    turn = hdim // 2
    for part in range(3):
        fetch(part).wait()

    @pl.loop(0, 2)
    def _(part):
        for lower in range(2):
            value = tt(weights[part, :, lower * half : (lower + 1) * half], act1[...])
            for head in range(count // 2):
                one = value[head * hdim : head * hdim + turn]
                two = value[head * hdim + turn : (head + 1) * hdim]
                turned = jnp.concatenate(
                    [one * cosine[...] - two * sine[...], two * cosine[...] + one * sine[...]],
                    axis=0,
                )
                base = pl.multiple_of(part * width + lower * half + head * hdim, 16)
                qkv[pl.ds(base, hdim)] = turned.astype(BF16)

    fetch_up(0).start()
    fetch_down(0).start()
    for lower in range(2):
        rows = slice(lower * half, (lower + 1) * half)
        value = tt(weights[2, :, rows], act1[...])
        qkv[2 * width + lower * half : 2 * width + (lower + 1) * half] = value.astype(BF16)
    fetch_up(1).start()
    put(qkv, qkv_t)

    def attend(head):
        def rows_of(part):
            return pl.ds(pl.multiple_of(part * width + head * hdim, 16), hdim)

        q_t = qkv[rows_of(0)]
        v_t = qkv[rows_of(2)]
        k = qkv[rows_of(1)].T
        for low, high, asked in query_blocks(tokens):
            scores = nn(k[low:high], q_t[:, asked]) * scale + bias[low:high, asked]
            peak = jnp.max(scores, axis=0, keepdims=True)
            expo = jnp.exp(scores - peak)
            amount = jnp.sum(expo, axis=0, keepdims=True)
            probs = (expo * (1.0 / amount)).astype(BF16)
            mixed[rows_of(0), asked] = nn(v_t[:, low:high], probs).astype(BF16)
            lse[head, :, asked] = peak + jnp.log(amount)

    @pl.loop(0, count // TOGETHER)
    def _(i):
        for u in range(TOGETHER):
            attend(i * TOGETHER + u)

    put(mixed, o_t, o_o)

    fetch(3).wait()
    for lower in range(2):
        rows = slice(lower * half, (lower + 1) * half)
        res2[rows] = xt[rows].astype(F32) + tt(weights[3, :, rows], mixed[...])
        res3[rows] = res2[rows]
    fetch_down(1).start()
    put(res2, x2_t)
    normalize(res2, 1, act2)
    put(act2, a2_t, a2_o)

    def piece(k):
        return pl.ds(pl.multiple_of(k * width, 16), width)

    def h_copy(k):
        slot = lax.rem(k, 2)
        return pltpu.make_async_copy(hbuf.at[slot], h_t.at[piece(k)], h_sem.at[slot])

    def g_copy(k):
        slot = lax.rem(k, 2)
        return pltpu.make_async_copy(gbuf.at[slot], g_t.at[piece(k)], g_sem.at[slot])

    def g_push(k):
        slot = lax.rem(k, 2)
        return remote(gbuf.at[slot], g_o.at[piece(k)], g_send.at[slot], g_recv.at[k])

    @pl.loop(0, pieces)
    def _(k):
        slot, up, down = lax.rem(k, 2), lax.rem(2 * k, SLOTS), lax.rem(2 * k + 1, SLOTS)
        fetch_up(k).wait()

        @pl.when(k >= 2)
        def _():
            h_copy(k - 2).wait()
            g_copy(k - 2).wait()
            g_push(k - 2).wait_send()

        for lower in range(2):
            rows = slice(lower * half, (lower + 1) * half)
            value = tt(weights[up, :, rows], act2[...])
            hbuf[slot, rows] = value.astype(BF16)
            gbuf[slot, rows] = (value / (1.0 + jnp.exp(-value))).astype(BF16)

        @pl.when(k + 2 < pieces)
        def _():
            fetch_up(k + 2).start()

        h_copy(k).start()
        g_copy(k).start()
        g_push(k).start()
        fetch_down(k).wait()
        for lower in range(2):
            rows = slice(lower * half, (lower + 1) * half)
            res3[rows] += tt(weights[down, :, rows], gbuf[slot])

        @pl.when(k + 2 < pieces)
        def _():
            fetch_down(k + 2).start()

    put(res3, x3_t)
    normalize(res3, 2, final)
    put(final, y_t)
    for copy in outs:
        copy.wait()
    for k in range(max(0, pieces - 2), pieces):
        h_copy(k).wait()
        g_copy(k).wait()
        g_push(k).wait_send()
    for k in range(pieces):
        g_push(k).wait_recv()
    for push in pushes:
        push.wait()


def run_forward(x, w_qkv, w_out, w_up, w_down, segs, gains, cosine, sine):
    tokens, width = x.shape
    hidden = w_up.shape[1]
    hdim = width // HEADS
    hbm = pl.BlockSpec(memory_space=pl.ANY)
    vmem = pl.BlockSpec(memory_space=pltpu.VMEM)
    flat = (width, tokens)
    shapes = [
        jax.ShapeDtypeStruct(shape, dtype)
        for shape, dtype in (
            (flat, BF16),
            ((hidden, tokens), BF16),
            (flat, BF16),
            (flat, BF16),
            (flat, BF16),
            ((hidden, tokens), BF16),
            (flat, BF16),
            (flat, BF16),
            (flat, BF16),
            (flat, F32),
            ((width, 128), F32),
            (flat, F32),
            (flat, BF16),
            ((hidden, tokens), BF16),
            ((3 * width, tokens), BF16),
            ((HEADS, 1, tokens), F32),
        )
    ]
    dma = pltpu.SemaphoreType.DMA
    return pl.pallas_call(
        forward_kernel,
        out_shape=shapes,
        in_specs=[hbm] * 5 + [vmem] * 6,
        out_specs=[hbm] * 15 + [vmem],
        scratch_shapes=[
            pltpu.VMEM((SLOTS, width, width), BF16),
            pltpu.VMEM((tokens, width), BF16),
            pltpu.VMEM(flat, BF16),
            pltpu.VMEM(flat, BF16),
            pltpu.VMEM(flat, BF16),
            pltpu.VMEM(flat, BF16),
            pltpu.VMEM(flat, BF16),
            pltpu.VMEM((3 * width, tokens), BF16),
            pltpu.VMEM(flat, F32),
            pltpu.VMEM(flat, F32),
            pltpu.VMEM((2,) + flat, BF16),
            pltpu.VMEM((2,) + flat, BF16),
            pltpu.VMEM((tokens, tokens), F32),
            pltpu.VMEM((width, 128), F32),
            pltpu.VMEM((8, width), F32),
            dma((SLOTS,)),
            dma(()),
            dma((9,)),
            dma((2,)),
            dma((2,)),
            dma((3,)),
            dma((3,)),
            dma((2,)),
            dma((hidden // width,)),
        ],
        compiler_params=pltpu.CompilerParams(
            collective_id=1, has_side_effects=True, vmem_limit_bytes=60 << 20
        ),
        name="forward",
    )(x, w_qkv, w_out, w_up, w_down, segs, *gains, cosine, sine)


LEAD = 3


def backward_kernel(
    table,
    size,
    y_t,
    g_t,
    a2_t,
    o_t,
    a1_t,
    g_o,
    a2_o,
    o_o,
    a1_o,
    y_flat,
    cot,
    w_head,
    x3_t,
    x2_t,
    x_t,
    h_t,
    qkv_t,
    gain_columns,
    w_down,
    w_up,
    w_out,
    w_qkv,
    lse,
    seg_row,
    head_bias,
    cosine,
    sine,
    out_head,
    out_down,
    out_up,
    out_out,
    out_qkv,
    out_small,
    out_entry,
    out_levels,
    e3_o,
    eh_o,
    e2_o,
    ep_o,
    eh_mine,
    lbuf,
    rbuf,
    cbuf,
    grad,
    recv1,
    pair,
    recv2,
    line,
    recv_up,
    recv_down,
    side,
    side_up,
    side_down,
    side1,
    side2,
    total,
    sums,
    sums_in,
    dx,
    work,
    acc,
    ebuf,
    bias,
    gains,
    wrows,
    wcols,
    hbuf,
    ehbuf,
    ep,
    eo,
    heads,
    obuf,
    push_send,
    push_recv,
    left_sem,
    right_sem,
    send1_sem,
    recv1_sem,
    send2_sem,
    recv2_sem,
    up_send,
    up_recv,
    down_send,
    down_recv,
    side_up_send,
    side_up_recv,
    side_down_send,
    side_down_recv,
    side1_send,
    side1_recv,
    side2_send,
    side2_recv,
    local_sem,
    swap_send,
    swap_recv,
    small_send,
    small_recv,
    row_sem,
    col_sem,
    h_sem,
    eh_out_sem,
    eh_in_sem,
    head_sem,
    fetch_sem,
    entry_sem,
):
    n = len(table)
    length = size // 4
    me = lax.axis_index("dp")
    core = lax.axis_index("head")
    other = 1 - core
    xi = lax.rem(me, 2)
    yi = lax.rem(me // 2, 2)
    zi = me // 4
    width, tokens = dx.shape
    hidden = h_t.shape[0]
    cols = width // 2
    block = width // size
    count, hdim = eo.shape[:2]
    scale = 1.0 / math.sqrt(hdim)
    flip_x = me + 1 - 2 * xi
    flip_y = me + 2 * (1 - 2 * yi)
    first_bit = jnp.where(core == 0, xi, yi)
    second_bit = jnp.where(core == 0, yi, xi)
    first_peer = jnp.where(core == 0, flip_x, flip_y)
    second_peer = jnp.where(core == 0, flip_y, flip_x)
    far = lax.rem(me + size // 2, size)
    near = me + 4 * (1 - 2 * lax.rem(zi, 2))
    rings = recv1.shape[0]
    ring2 = recv2.shape[0]
    ring_line = line.shape[0]
    ring_side, ring_in = side.shape[0], side1.shape[0]
    main = grad.shape[-1]

    fetch_head_weight = pltpu.make_async_copy(w_head, wcols.at[0], fetch_sem.at[0])
    fetch_x3 = pltpu.make_async_copy(x3_t, work, fetch_sem.at[1])
    fetch_gains = pltpu.make_async_copy(gain_columns, gains, fetch_sem.at[4])
    fetch_x2 = pltpu.make_async_copy(x2_t, work, fetch_sem.at[1])
    fetch_x = pltpu.make_async_copy(x_t, ebuf, fetch_sem.at[0])

    def local_c(half, which):
        start = pl.multiple_of(which * tokens, 16)
        return pltpu.make_async_copy(
            cot.at[pl.ds(start, tokens)], cbuf.at[half], fetch_sem.at[2 + half]
        )

    lefts = (y_t, g_t, a2_t, o_t, a1_t)
    left_others = (None, g_o, a2_o, o_o, a1_o)
    pieces = hidden // width

    def start_left(c):
        i, j = table[c]
        lower = pl.ds(j * block, block) if i == 1 else slice(None)
        for half, source in ((0, lefts[i]), (1, left_others[i])):
            pltpu.make_async_copy(
                source.at[:, lower, :], lbuf.at[c % 2, half], left_sem.at[c % 2, half]
            ).start()

    fetch_y = pltpu.make_async_copy(y_t, lbuf.at[0, 0], left_sem.at[0, 0])
    fetch_y.start()
    local_c(1, other).start()
    fetch_head_weight.start()
    local_c(0, core).start()
    fetch_x3.start()
    fetch_gains.start()
    start_left(1)

    barrier = pltpu.get_barrier_semaphore()
    for index, which in ((me, other), (flip_x, core), (flip_y, core), (far, core)):
        pl.semaphore_signal(barrier, inc=1, device_id=(index, which), device_id_type=MESH)

    @pl.when(zi > 0)
    def _():
        pl.semaphore_signal(barrier, inc=1, device_id=(me - 4, core), device_id_type=MESH)

    @pl.when(zi < length - 1)
    def _():
        pl.semaphore_signal(barrier, inc=1, device_id=(me + 4, core), device_id_type=MESH)

    inner = jnp.where(zi > 0, 1, 0) + jnp.where(zi < length - 1, 1, 0)
    pl.semaphore_wait(barrier, 4 + inner)

    def remote(src, dst, send, recv, index, which):
        return pltpu.make_async_remote_copy(
            src_ref=src,
            dst_ref=dst,
            send_sem=send,
            recv_sem=recv,
            device_id=(index, which),
            device_id_type=MESH,
        )

    PE3, PE2, PEP, PY, PDY, PLEVEL = range(6)

    def push(k):
        if k == PY:
            src, dst = lbuf.at[0, 0], lbuf.at[0, 1]
        elif k in (PDY, PLEVEL):
            src, dst = ehbuf, hbuf
        elif k == PEP:
            wide = 3 * cols
            src, dst = ep.at[pl.ds(pl.multiple_of(other * wide, 16), wide)], ep_o
        else:
            src, dst = ebuf, (e3_o, e2_o)[k]
            src = src.at[pl.ds(pl.multiple_of(other * cols, 16), cols)]
        return remote(src, dst, push_send.at[k], push_recv.at[k], me, other)

    fetch_y.wait()
    push(PY).start()
    fetch_head_weight.wait()
    local_c(1, other).wait()
    for i in range(2):
        ehbuf[i] = nt(wcols[0, i * cols : (i + 1) * cols], cbuf[1]).astype(BF16)
    push(PDY).start()
    local_c(0, core).wait()

    def start_right(c):
        i, j = table[c]
        slot = c % 2
        mine = pl.ds(pl.multiple_of(core * cols, 16), cols)
        rows = pl.ds(j * cols, cols)
        if i == 1:
            own, its = ebuf.at[mine], e3_o
            if j == 0:
                push(PE3).wait_recv()
        elif i == 2:
            own, its = eh_mine.at[rows], eh_o.at[rows]
            if j == 0:
                for piece in range(pieces):
                    eh_push(piece, 0).wait_recv()
        elif i == 3:
            own, its = ebuf.at[mine], e2_o
        else:
            start = pl.multiple_of(core * 3 * cols + j * cols, 16)
            own, its = ep.at[pl.ds(start, cols)], ep_o.at[rows]
            if j == 0:
                push(PEP).wait_recv()
        pltpu.make_async_copy(own, rbuf.at[slot, 0], right_sem.at[slot, 0]).start()
        pltpu.make_async_copy(its, rbuf.at[slot, 1], right_sem.at[slot, 1]).start()

    def eh_push(piece, slot):
        return remote(
            ehbuf.at[slot],
            eh_o.at[pl.ds(piece * cols, cols)],
            eh_out_sem.at[slot],
            eh_in_sem.at[piece],
            me,
            other,
        )

    def wait_left(slot):
        for half in range(2):
            pltpu.make_async_copy(
                lbuf.at[slot, half], lbuf.at[slot, half], left_sem.at[slot, half]
            ).wait()

    def wait_right(slot):
        for half in range(2):
            pltpu.make_async_copy(
                rbuf.at[slot, half], rbuf.at[slot, half], right_sem.at[slot, half]
            ).wait()

    def form(c, right, multiply):
        slot, ring, to = lax.rem(c, 2), lax.rem(c, LEAD), lax.rem(c, ring_side)

        for z in range(length):
            value = None
            for half in range(2):
                left = lbuf[slot, half, 4 * z : 4 * z + 4].reshape(4 * block, tokens)
                part = multiply(left, right[half])
                value = part if value is None else value + part
            value = value.astype(BF16)
            for q in range(4):
                x, y = q % 2, q // 2
                one = jnp.where(core == 0, x, y)
                two = jnp.where(core == 0, y, x)
                part = value[q * block : (q + 1) * block]
                grad[ring, one, two, z] = part[:, :main]
                side[to, z, one, two] = part[:, main:]
        send1(c).start()
        start_side(c, 1)

    def send1(c):
        ring, spot = lax.rem(c, LEAD), lax.rem(c, rings)
        return remote(
            grad.at[ring, 1 - first_bit],
            recv1.at[spot],
            send1_sem.at[ring],
            recv1_sem.at[spot],
            first_peer,
            core,
        )

    def send2(c):
        ring, spot = lax.rem(c, 2), lax.rem(c, ring2)
        return remote(
            pair.at[ring, 1 - second_bit],
            recv2.at[spot],
            send2_sem.at[ring],
            recv2_sem.at[spot],
            second_peer,
            core,
        )

    def send_up(c, step):
        ring, spot = lax.rem(c, ring_line), lax.rem(c, rings)
        return remote(
            line.at[ring, jnp.minimum(zi + (length - step), length - 1)],
            recv_up.at[spot, step - 1],
            up_send.at[ring, step - 1],
            up_recv.at[spot, step - 1],
            jnp.minimum(me + 4, size - 1),
            core,
        )

    def send_down(c, step):
        ring, spot = lax.rem(c, ring_line), lax.rem(c, rings)
        return remote(
            line.at[ring, jnp.maximum(zi - (length - step), 0)],
            recv_down.at[spot, step - 1],
            down_send.at[ring, step - 1],
            down_recv.at[spot, step - 1],
            jnp.maximum(me - 4, 0),
            core,
        )

    def side_send_up(c, step):
        ring, spot = lax.rem(c, ring_side), lax.rem(c, ring_in)
        return remote(
            side.at[ring, jnp.minimum(zi + (length - step), length - 1)],
            side_up.at[spot, step - 1],
            side_up_send.at[ring, step - 1],
            side_up_recv.at[spot, step - 1],
            jnp.minimum(me + 4, size - 1),
            core,
        )

    def side_send_down(c, step):
        ring, spot = lax.rem(c, ring_side), lax.rem(c, ring_in)
        return remote(
            side.at[ring, jnp.maximum(zi - (length - step), 0)],
            side_down.at[spot, step - 1],
            side_down_send.at[ring, step - 1],
            side_down_recv.at[spot, step - 1],
            jnp.maximum(me - 4, 0),
            core,
        )

    def side_send1(c):
        ring, spot = lax.rem(c, ring_side), lax.rem(c, ring_in)
        return remote(
            side.at[ring, zi, 1 - first_bit],
            side1.at[spot],
            side1_send.at[ring],
            side1_recv.at[spot],
            first_peer,
            core,
        )

    def side_send2(c):
        ring, spot = lax.rem(c, ring_side), lax.rem(c, ring_in)
        return remote(
            side.at[ring, zi, first_bit, 1 - second_bit],
            side2.at[spot],
            side2_send.at[ring],
            side2_recv.at[spot],
            second_peer,
            core,
        )

    def start_side(c, step):
        @pl.when(zi < step)
        def _():
            side_send_up(c, step).start()

        @pl.when(zi >= length - step)
        def _():
            side_send_down(c, step).start()

    def exchange_side(t):
        for step in range(1, length):

            @pl.when((t >= step - 1) & (t <= n + step - 2))
            def _():
                c = t - step + 1
                ring, at = lax.rem(c, ring_side), lax.rem(c, ring_in)
                up_in = (zi >= 1) & (zi <= step)
                down_in = (zi <= length - 2) & (zi >= length - 1 - step)

                @pl.when(up_in)
                def _():
                    side_send_up(c, step).wait_recv()
                    spot = jnp.minimum(zi + (length - 1 - step), length - 1)
                    side[ring, spot] = side[ring, spot] + side_up[at, step - 1]

                @pl.when(down_in)
                def _():
                    side_send_down(c, step).wait_recv()
                    spot = jnp.maximum(zi - (length - 1 - step), 0)
                    side[ring, spot] = side[ring, spot] + side_down[at, step - 1]

                if step < length - 1:
                    start_side(c, step + 1)
                else:
                    side_send1(c).start()

        @pl.when((t >= length - 1) & (t <= n + length - 2))
        def _():
            c = t - length + 1
            ring, at = lax.rem(c, ring_side), lax.rem(c, ring_in)
            side_send1(c).wait_recv()
            side[ring, zi, first_bit] = side[ring, zi, first_bit] + side1[at]
            side_send2(c).start()

        @pl.when((t >= length) & (t <= n + length - 1))
        def _():
            c = t - length
            ring, at = lax.rem(c, ring_side), lax.rem(c, ring_in)
            side_send2(c).wait_recv()
            total[c, :, main:] = side[ring, zi, first_bit, second_bit].astype(F32) + side2[
                at
            ].astype(F32)
            for back in range(1, length):

                @pl.when(zi < back)
                def _():
                    side_send_up(c, back).wait_send()

                @pl.when(zi >= length - back)
                def _():
                    side_send_down(c, back).wait_send()

            side_send1(c).wait_send()
            side_send2(c).wait_send()

    def start_line(c, step):
        @pl.when(zi < step)
        def _():
            send_up(c, step).start()

        @pl.when(zi >= length - step)
        def _():
            send_down(c, step).start()

    def wait_line_sent(c, step):
        @pl.when(zi < step)
        def _():
            send_up(c, step).wait_send()

        @pl.when(zi >= length - step)
        def _():
            send_down(c, step).wait_send()

    def results(c):
        i, j = table[c]
        if i == 0:
            return [pltpu.make_async_copy(total.at[c], out_head, local_sem.at[c])]
        if i == 1:
            target = out_down.at[
                pl.ds((j % 2) * block, block), pl.ds(pl.multiple_of(core * cols, 128), cols)
            ]
            return [
                pltpu.make_async_copy(total.at[c], target, local_sem.at[c]),
                remote(total.at[c], target, swap_send.at[c], swap_recv.at[c], me, other),
            ]
        target = (None, None, out_up, out_out, out_qkv)[i]
        wide = target.shape[1] // 2
        place = target.at[:, pl.ds(pl.multiple_of(core * wide + j * cols, 128), cols)]
        half = block // 2
        mine = pl.ds(pl.multiple_of(core * half, 8), half)
        its = pl.ds(pl.multiple_of(other * half, 8), half)
        return [
            pltpu.make_async_copy(total.at[c, mine], place, local_sem.at[c]),
            remote(total.at[c, its], place, swap_send.at[c], swap_recv.at[c], me, other),
        ]

    def start_results(c):
        i, j = table[c]
        copies = results(c)
        if i == 1:
            owner = j // (pieces // 2)
            pl.when(core == owner)(copies[0].start)
            pl.when(core != owner)(copies[1].start)
        else:
            for copy in copies:
                copy.start()

    def end_results(c):
        i, j = table[c]
        copies = results(c)
        if i == 1:
            owner = j // (pieces // 2)
            pl.when(core == owner)(copies[0].wait)
            pl.when(core == owner)(copies[1].wait_recv)
            pl.when(core != owner)(copies[1].wait_send)
        else:
            for copy in copies:
                copy.wait()

    def exchange(t):
        @pl.when(t < n)
        def _():
            c = t
            send1(c).wait_recv()
            ring, spot, to = lax.rem(c, LEAD), lax.rem(c, rings), lax.rem(c, 2)

            @pl.when(c >= 2)
            def _():
                send2(c - 2).wait_send()

            for two in range(2):

                @pl.loop(0, length)
                def _(z):
                    pair[to, two, z] = grad[ring, first_bit, two, z] + recv1[spot, two, z]

            send2(c).start()

        @pl.when((t >= 1) & (t <= n))
        def _():
            c = t - 1
            send2(c).wait_recv()
            ring, spot, to = lax.rem(c, 2), lax.rem(c, ring2), lax.rem(c, ring_line)

            @pl.loop(0, length)
            def _(z):
                line[to, z] = pair[ring, second_bit, z] + recv2[spot, z]

            start_line(c, 1)

        exchange_side(t)

        for step in range(1, length):

            @pl.when((t >= 1 + step) & (t <= n + step))
            def _():
                c = t - 1 - step
                ring, at = lax.rem(c, ring_line), lax.rem(c, rings)
                last = step == length - 1
                up_in = (zi >= 1) & (zi <= step)
                down_in = (zi <= length - 2) & (zi >= length - 1 - step)

                @pl.when(up_in)
                def _():
                    send_up(c, step).wait_recv()
                    spot = jnp.minimum(zi + (length - 1 - step), length - 1)
                    if not last:
                        line[ring, spot] = line[ring, spot] + recv_up[at, step - 1]

                @pl.when(down_in)
                def _():
                    send_down(c, step).wait_recv()
                    spot = jnp.maximum(zi - (length - 1 - step), 0)
                    if not last:
                        line[ring, spot] = line[ring, spot] + recv_down[at, step - 1]

                if not last:
                    start_line(c, step + 1)
                else:
                    total[c, :, :main] = line[ring, zi].astype(F32)

                    @pl.when(up_in)
                    def _():
                        total[c, :, :main] += recv_up[at, step - 1].astype(F32)

                    @pl.when(down_in)
                    def _():
                        total[c, :, :main] += recv_down[at, step - 1].astype(F32)

                    for back in range(1, length):
                        wait_line_sent(c, back)

                    for d in range(n):

                        @pl.when(c == d)
                        def _():
                            start_results(d)

    push(PY).wait_recv()
    form(0, [cbuf[0], cbuf[1]], nn)
    push(PY).wait_send()
    start_left(2)

    def emit_final(k, rows, value):
        dx[rows] = value
        ebuf[rows] = value.astype(BF16)

    push(PDY).wait_recv()
    for i in range(2):
        rows = slice(i * cols, (i + 1) * cols)
        dx[rows] = nt(wcols[0, rows], cbuf[0]) + hbuf[i].astype(F32)
    fetch_x3.wait()
    fetch_gains.wait()
    norm_backward(work, dx, gains, 2, emit_final)
    push(PE3).start()
    fetch_x2.start()
    sums[0] = jnp.zeros_like(sums[0])
    for i in range(2):
        share = jnp.sum(cbuf[i].astype(F32), axis=0, keepdims=True)
        at = pl.ds(pl.multiple_of(core * cols, 128), cols)
        sums[0, 3:4, at] = sums[0, 3:4, at] + share
    push(PDY).wait_send()
    for c in range(1, LEAD):
        start_right(c)
        wait_left(c % 2)
        wait_right(c % 2)
        form(c, [rbuf[c % 2, 0], rbuf[c % 2, 1]], nt)
        start_left(c + 2)
    def row_tile(k, slot, source):
        return pltpu.make_async_copy(
            source.at[pl.ds(pl.multiple_of(k * cols, 16), cols)], wrows.at[slot], row_sem.at[slot]
        )

    def col_tile(k, slot, source):
        return pltpu.make_async_copy(
            source.at[:, pl.ds(pl.multiple_of(k * cols, 128), cols)],
            wcols.at[slot],
            col_sem.at[slot],
        )

    def h_tile(k, slot):
        return pltpu.make_async_copy(
            h_t.at[pl.ds(pl.multiple_of(k * cols, 16), cols)], hbuf.at[slot], h_sem.at[slot]
        )

    def mlp_tiles(k):
        return jnp.where(k < pieces, other, core) * pieces + lax.rem(k, pieces)

    def fetch_mlp(k):
        slot = lax.rem(k, 2)
        tile = mlp_tiles(k)
        row_tile(tile, slot, w_down).start()
        col_tile(tile, slot, w_up).start()
        h_tile(tile, slot).start()

    def mlp_step(k):
        slot = lax.rem(k, 2)
        tile = mlp_tiles(k)
        row_tile(tile, slot, w_down).wait()
        h_tile(tile, slot).wait()

        @pl.when((k >= 2) & (k < pieces + 2))
        def _():
            eh_push(0, slot).wait_send()

        @pl.when(k >= pieces + 2)
        def _():
            pltpu.make_async_copy(
                ehbuf.at[slot], eh_mine.at[pl.ds(0, cols)], eh_out_sem.at[slot]
            ).wait()

        part = cols // 2
        for i in range(2):
            rows = slice(i * part, (i + 1) * part)
            value = nn(wrows[slot, rows], ebuf[...])
            pre = hbuf[slot, rows].astype(F32)
            sig = 1.0 / (1.0 + jnp.exp(-pre))
            ehbuf[slot, rows] = (value * sig * (1.0 + pre * (1.0 - sig))).astype(BF16)

        where = lax.rem(k, pieces)

        @pl.when(k < pieces)
        def _():
            eh_push(where, slot).start()

        @pl.when(k >= pieces)
        def _():
            pltpu.make_async_copy(
                ehbuf.at[slot],
                eh_mine.at[pl.ds(pl.multiple_of(where * cols, 16), cols)],
                eh_out_sem.at[slot],
            ).start()

        col_tile(tile, slot, w_up).wait()
        accumulate(wcols.at[slot], ehbuf.at[slot], k == 0)

        @pl.when(k + 2 < 2 * pieces)
        def _():
            fetch_mlp(k + 2)

    def accumulate(left, right, first):
        @pl.when(first)
        def _():
            acc[...] = jnp.zeros_like(acc)

        part = width // 4
        for i in range(4):
            rows = slice(i * part, (i + 1) * part)
            acc[rows] += nn(left[rows], right[...])

    fetch_mlp(0)
    fetch_mlp(1)

    def emit_mlp(k, rows, value):
        value = dx[rows] + value
        dx[rows] = value
        ebuf[rows] = value.astype(BF16)

    def middle():
        for slot in range(2):
            pltpu.make_async_copy(
                ehbuf.at[slot], eh_mine.at[pl.ds(0, cols)], eh_out_sem.at[slot]
            ).wait()
        row_tile(0, 0, w_out).start()
        row_tile(1, 1, w_out).start()
        push(PE3).wait_send()
        fetch_x2.wait()
        norm_backward(work, acc, gains, 1, emit_mlp)
        push(PE2).start()

        @pl.loop(0, 2)
        def _(k):
            row_tile(k, k, w_out).wait()

            group = cols // hdim
            value = nn(wrows[k], ebuf[...]).astype(BF16)
            eo[pl.ds(k * group, group)] = value.reshape(group, hdim, tokens)

        mask_of(seg_row, bias)
        pltpu.make_async_copy(w_head, wcols.at[0], col_sem.at[0]).start()
        pltpu.make_async_copy(y_flat, ehbuf, h_sem.at[0]).start()

    def level_copy(k, which, slot):
        return pltpu.make_async_copy(
            obuf.at[slot],
            out_levels.at[
                pl.ds(pl.multiple_of(which * tokens, 8), tokens), k * STRIP : (k + 1) * STRIP
            ],
            entry_sem.at[slot],
        )

    def levels(source, which):
        last = cols // STRIP
        for k in range(last):
            if k >= 2:
                level_copy(k - 2, which, k % 2).wait()
            part = slice(k * STRIP, (k + 1) * STRIP)
            obuf[k % 2] = (
                tt(source[0], wcols[0, :cols, part])
                + tt(source[1], wcols[0, cols:, part])
                + head_bias[...].reshape(1, cols)[:, part]
            )
            level_copy(k, which, k % 2).start()
        for k in range(last - 2, last):
            level_copy(k, which, k % 2).wait()

    per_turn = count // 4

    def head_copy(head, slot, u, part):
        return pltpu.make_async_copy(
            qkv_t.at[pl.ds(pl.multiple_of(part * width + head * hdim, 16), hdim)],
            heads.at[slot, u, part],
            head_sem.at[slot, u, part],
        )

    def fetch_heads(i):
        for u in range(TOGETHER):
            for part in range(3):
                head_copy(i * TOGETHER + u, lax.rem(i, 2), u, part).start()

    def attend_head(head, slot, u):
        q_t, k_t, v_t = (heads[slot, u, part] for part in range(3))
        e_t = eo[head]
        q, k, v, e = q_t.T, k_t.T, v_t.T, e_t.T
        blocks = list(query_blocks(tokens))
        weight = lse[head]
        ek, ev, eqs = [[] for _ in blocks], [[] for _ in blocks], []
        for low, high, asked in blocks:
            scores = nn(k[low:high], q_t[:, asked]) * scale + bias[low:high, asked]
            p = jnp.exp(scores - weight[:, asked])
            ep_t = nn(v[low:high], e_t[:, asked])
            share = jnp.sum(p * ep_t, axis=0, keepdims=True)
            es = (p * (ep_t - share)).astype(BF16)
            eqs.append(nn(k_t[:, low:high], es))
            one, two = nn(es, q[asked]), nn(p.astype(BF16), e[asked])
            for number, (_, _, own) in enumerate(blocks):
                if low <= own.start < high:
                    ek[number].append(one[own.start - low : own.stop - low])
                    ev[number].append(two[own.start - low : own.stop - low])
        ek_t = jnp.concatenate([sum(terms[1:], terms[0]) for terms in ek], axis=0).T
        ev_t = jnp.concatenate([sum(terms[1:], terms[0]) for terms in ev], axis=0).T
        half = hdim // 2
        for part, value in ((0, jnp.concatenate(eqs, axis=1)), (1, ek_t)):
            one, two = value[:half] * scale, value[half:] * scale
            turned = jnp.concatenate(
                [one * cosine[...] + two * sine[...], two * cosine[...] - one * sine[...]],
                axis=0,
            )
            to = pl.ds(pl.multiple_of(part * width + head * hdim, 16), hdim)
            ep[to] = turned.astype(BF16)
        to = pl.ds(pl.multiple_of(2 * width + head * hdim, 16), hdim)
        ep[to] = ev_t.astype(BF16)

    def attend(turn):
        @pl.when(turn == 0)
        def _():
            fetch_heads(0)

        @pl.loop(0, per_turn // TOGETHER)
        def _(j):
            i = turn * (per_turn // TOGETHER) + j
            slot = lax.rem(i, 2)
            for u in range(TOGETHER):
                for part in range(3):
                    head_copy(i * TOGETHER + u, slot, u, part).wait()

            @pl.when((i + 1) * TOGETHER < count)
            def _():
                fetch_heads(i + 1)

            for u in range(TOGETHER):
                attend_head(i * TOGETHER + u, slot, u)

        @pl.when(turn == 3)
        def _():
            push(PEP).start()

    def fetch_qkv(k):
        col_tile(k, lax.rem(k, 2), w_qkv).start()

    def qkv_step(k):
        slot = lax.rem(k, 2)
        col_tile(k, slot, w_qkv).wait()
        rows = pl.ds(pl.multiple_of(k * cols, 16), cols)
        accumulate(wcols.at[slot], ep.at[rows], k == 0)

        @pl.when(k + 2 < 6)
        def _():
            fetch_qkv(k + 2)

    def entry_copy(k, slot):
        return pltpu.make_async_copy(
            obuf.at[slot],
            out_entry.at[:, pl.ds(pl.multiple_of(k * STRIP, STRIP), STRIP)],
            entry_sem.at[slot],
        )

    def emit_entry(k, rows, value):
        slot = lax.rem(k, 2)

        @pl.when(k >= 2)
        def _():
            entry_copy(k, slot).wait()

        obuf[slot] = (dx[rows] + value).T
        entry_copy(k, slot).start()

    peers = ((me, other), (flip_x, core), (flip_y, core), (near, core), (far, core))
    steps = len(peers)

    def small_copy(i):
        return remote(
            sums.at[i], sums_in.at[i], small_send.at[i], small_recv.at[i], peers[i][0], peers[i][1]
        )

    def last():
        fetch_x.wait()
        norm_backward(ebuf, acc, gains, 0, emit_entry)
        for slot in range(2):
            entry_copy(0, slot).wait()
        sums[0] = sums[0] + gains[...].T[8:16]
        small_copy(0).start()

    @pl.loop(0, n + length)
    def _(t):
        for c in range(LEAD, n):
            if table[c] != (4, 0):

                @pl.when(t == c - LEAD)
                def _():
                    start_right(c)

        exchange(t)

        for c in range(LEAD, n):
            if table[c] == (4, 0):

                @pl.when(t == c - LEAD)
                def _():
                    start_right(c)

        @pl.when(t + LEAD < n)
        def _():
            c = t + LEAD
            slot = lax.rem(c, 2)
            wait_left(slot)
            wait_right(slot)
            send1(t).wait_send()
            form(c, [rbuf[slot, 0], rbuf[slot, 1]], nt)
            for d in range(LEAD + 2, n):

                @pl.when(c == d - 2)
                def _():
                    start_left(d)

        @pl.when(t < 2)
        def _():
            @pl.loop(0, pieces)
            def _(i):
                mlp_step(t * pieces + i)

        @pl.when(t == 2)
        def _():
            middle()

        @pl.when((t >= 3) & (t < 7))
        def _():
            attend(t - 3)

        @pl.when(t == 3)
        def _():
            push(PE2).wait_recv()
            pltpu.make_async_copy(y_flat, ehbuf, h_sem.at[0]).wait()
            push(PLEVEL).start()

        @pl.when(t == 4)
        def _():
            pltpu.make_async_copy(w_head, wcols.at[0], col_sem.at[0]).wait()
            levels(ehbuf, core)

        @pl.when(t == 5)
        def _():
            push(PLEVEL).wait()
            levels(hbuf, other)

        @pl.when(t == 6)
        def _():
            fetch_qkv(0)
            fetch_qkv(1)

        @pl.when((t == 7) | (t == 8))
        def _():
            @pl.loop(0, 3)
            def _(i):
                qkv_step((t - 7) * 3 + i)

        @pl.when(t == 9)
        def _():
            last()

        for i in range(steps):

            @pl.when(t == 10 + i)
            def _():
                small_copy(i).wait()
                value = sums[i] + sums_in[i]
                if i == steps - 1:
                    out_small[...] = value
                else:
                    sums[i + 1] = value
                    small_copy(i + 1).start()

        @pl.when(t == 8)
        def _():
            push(PE2).wait_send()
            fetch_x.start()

    for c in range(n):
        end_results(c)
    for c in range(n - LEAD, n):
        send1(c).wait_send()
    for c in range(n - 2, n):
        send2(c).wait_send()
    push(PEP).wait_send()


def run_backward(lefts, left_others, others, weights, tables):
    size = lax.axis_size("dp")
    width, tokens = lefts[0].shape
    hidden = lefts[1].shape[0]
    block = width // size
    cols = width // 2
    table = chunk_table(width, hidden)
    n = len(table)
    length = size // 4
    share = block // 2
    hdim = width // HEADS
    hbm = pl.BlockSpec(memory_space=pl.ANY)
    vmem = pl.BlockSpec(memory_space=pltpu.VMEM)
    y_flat = lefts[0].reshape(2, cols, tokens)
    lefts = [left.reshape(size, left.shape[0] // size, tokens) for left in lefts + left_others]
    shapes = [
        jax.ShapeDtypeStruct((block, cols), F32),
        jax.ShapeDtypeStruct((hidden // size // 2, width), F32),
        jax.ShapeDtypeStruct((share, hidden), F32),
        jax.ShapeDtypeStruct((share, width), F32),
        jax.ShapeDtypeStruct((share, 3 * width), F32),
        jax.ShapeDtypeStruct((8, width), F32),
        jax.ShapeDtypeStruct((tokens, width), F32),
        jax.ShapeDtypeStruct((2 * tokens, cols), F32),
    ]
    shapes += [
        jax.ShapeDtypeStruct((rows, tokens), BF16)
        for rows in (cols, hidden // 2, cols, 3 * cols, hidden // 2)
    ]
    dma = pltpu.SemaphoreType.DMA
    ring1, ring2, ring_line = 6, 4, length + 1
    main = cols - 128
    results = pl.pallas_call(
        functools.partial(backward_kernel, table, size),
        out_shape=shapes,
        in_specs=[hbm] * 22 + [vmem] * 5,
        out_specs=[hbm] * 5 + [vmem] + [hbm] * 7,
        scratch_shapes=[
            pltpu.VMEM((2, 2, size, block, tokens), BF16),
            pltpu.VMEM((2, 2, cols, tokens), BF16),
            pltpu.VMEM((2, tokens, cols), BF16),
            pltpu.VMEM((LEAD, 2, 2, length, block, main), BF16),
            pltpu.VMEM((ring1, 2, length, block, main), BF16),
            pltpu.VMEM((2, 2, length, block, main), BF16),
            pltpu.VMEM((ring2, length, block, main), BF16),
            pltpu.VMEM((ring_line, length, block, main), BF16),
            pltpu.VMEM((ring1, length - 1, block, main), BF16),
            pltpu.VMEM((ring1, length - 1, block, main), BF16),
            pltpu.VMEM((length + 4, length, 2, 2, block, cols - main), BF16),
            pltpu.VMEM((length + 3, length - 1, 2, 2, block, cols - main), BF16),
            pltpu.VMEM((length + 3, length - 1, 2, 2, block, cols - main), BF16),
            pltpu.VMEM((length + 3, 2, block, cols - main), BF16),
            pltpu.VMEM((length + 3, block, cols - main), BF16),
            pltpu.VMEM((n, block, cols), F32),
            pltpu.VMEM((5, 8, width), F32),
            pltpu.VMEM((5, 8, width), F32),
            pltpu.VMEM((width, tokens), F32),
            pltpu.VMEM((width, tokens), F32),
            pltpu.VMEM((width, tokens), F32),
            pltpu.VMEM((width, tokens), BF16),
            pltpu.VMEM((tokens, tokens), F32),
            pltpu.VMEM((width, 128), F32),
            pltpu.VMEM((2, cols, width), BF16),
            pltpu.VMEM((2, width, cols), BF16),
            pltpu.VMEM((2, cols, tokens), BF16),
            pltpu.VMEM((2, cols, tokens), BF16),
            pltpu.VMEM((3 * width, tokens), BF16),
            pltpu.VMEM((HEADS, hdim, tokens), BF16),
            pltpu.VMEM((2, TOGETHER, 3, hdim, tokens), BF16),
            pltpu.VMEM((2, tokens, 128), F32),
            dma((6,)),
            dma((6,)),
            dma((2, 2)),
            dma((2, 2)),
            dma((LEAD,)),
            dma((ring1,)),
            dma((2,)),
            dma((ring2,)),
            dma((ring_line, length - 1)),
            dma((ring1, length - 1)),
            dma((ring_line, length - 1)),
            dma((ring1, length - 1)),
            dma((length + 4, length - 1)),
            dma((length + 3, length - 1)),
            dma((length + 4, length - 1)),
            dma((length + 3, length - 1)),
            dma((length + 4,)),
            dma((length + 3,)),
            dma((length + 4,)),
            dma((length + 3,)),
            dma((n,)),
            dma((n,)),
            dma((n,)),
            dma((5,)),
            dma((5,)),
            dma((2,)),
            dma((2,)),
            dma((2,)),
            dma((2,)),
            dma((hidden // width,)),
            dma((2, TOGETHER, 3)),
            dma((5,)),
            dma((2,)),
        ],
        compiler_params=pltpu.CompilerParams(
            collective_id=0, has_side_effects=True, vmem_limit_bytes=62 << 20
        ),
        name="backward",
    )(*lefts, y_flat, *others, *weights, *tables)
    return results[:8]


def finish_kernel(copied, *refs):
    sources, sums = refs[:copied], refs[copied]
    targets = refs[copied + 1 : 2 * copied + 1]
    gain_attn, gain_mlp, gain_final, bias = refs[2 * copied + 1 : 2 * copied + 5]
    held = refs[2 * copied + 5 : 3 * copied + 5]
    fetch_sem, copy_sem = refs[3 * copied + 5 :]
    me = lax.axis_index("dp")
    core = lax.axis_index("head")
    width = sums.shape[1]
    share, half = gain_attn.shape[0], bias.shape[0]
    arrivals = [
        pltpu.make_async_copy(source, buffer, fetch_sem.at[i])
        for i, (source, buffer) in enumerate(zip(sources, held))
    ]
    copies = [
        pltpu.make_async_copy(buffer, target, copy_sem.at[i])
        for i, (buffer, target) in enumerate(zip(held, targets))
    ]
    for arrival in arrivals:
        arrival.start()
    start = (me * 2 + core) * share
    rolled = pltpu.roll(sums[...], lax.rem(width - start, width), 1)
    for i, target in enumerate((gain_attn, gain_mlp, gain_final)):
        target[...] = rolled[i, :share]
    bias[...] = sums[3, pl.ds(pl.multiple_of(core * half, 128), half)]
    for arrival, copy in zip(arrivals, copies):
        arrival.wait()
        copy.start()
    for copy in copies:
        copy.wait()


def run_finish(copied, sums):
    width = sums.shape[1]
    share = width // (2 * lax.axis_size("dp"))
    hbm = pl.BlockSpec(memory_space=pl.ANY)
    vmem = pl.BlockSpec(memory_space=pltpu.VMEM)
    dma = pltpu.SemaphoreType.DMA
    shapes = [jax.ShapeDtypeStruct(value.shape, F32) for value in copied]
    shapes += [jax.ShapeDtypeStruct((share,), F32)] * 3
    shapes += [jax.ShapeDtypeStruct((width // 2,), F32)]
    return pl.pallas_call(
        functools.partial(finish_kernel, len(copied)),
        out_shape=shapes,
        in_specs=[hbm] * len(copied) + [vmem],
        out_specs=[hbm] * len(copied) + [vmem] * 4,
        scratch_shapes=[pltpu.VMEM(value.shape, F32) for value in copied]
        + [dma((len(copied),)), dma((len(copied),))],
        compiler_params=pltpu.CompilerParams(vmem_limit_bytes=60 << 20),
        name="finish",
    )(*copied, sums)


def per_device(
    inputs,
    segment_ids,
    gain_attn,
    w_qkv,
    w_out,
    gain_mlp,
    w_up,
    w_down,
    gain_final,
    head_projection_weight,
    head_output_bias,
    cotangent,
):
    core = lax.axis_index("head")
    place = lax.axis_index("dp")
    size = lax.axis_size("dp")
    rows, sequence_span = segment_ids.shape
    count, width = inputs.shape
    hdim = width // HEADS
    scale = 1.0 / math.sqrt(hdim)
    share = width // (2 * size)
    fused = size == HEADS and lax.axis_size("head") == 2 and rows == 1

    if fused:
        half = width // 2
        turn = hdim // 2
        freq = np.float32(10000.0) ** (-np.arange(turn, dtype=np.float32) / np.float32(turn))
        angle = np.arange(sequence_span, dtype=np.float32)[None, :] * freq[:, None]
        cosine_t, sine_t = jnp.asarray(np.cos(angle)), jnp.asarray(np.sin(angle))
        (
            y_t,
            g_t,
            a2_t,
            o_t,
            a1_t,
            g_o,
            a2_o,
            o_o,
            a1_o,
            x3_t,
            gain_columns,
            x2_t,
            x_t,
            h_t,
            qkv_t,
            lse,
        ) = run_forward(
            inputs,
            w_qkv,
            w_out,
            w_up,
            w_down,
            segment_ids,
            [gain_attn, gain_mlp, gain_final],
            cosine_t,
            sine_t,
        )
        head, down, up, out, qkv, sums, entry, levels = run_backward(
            [y_t, g_t, a2_t, o_t, a1_t],
            [g_o, a2_o, o_o, a1_o],
            [
                cotangent,
                head_projection_weight,
                x3_t,
                x2_t,
                x_t,
                h_t,
                qkv_t,
                gain_columns,
            ],
            [w_down, w_up, w_out, w_qkv],
            [lse, segment_ids, head_output_bias, cosine_t, sine_t],
        )
        (
            predicted_levels,
            entry_sensitivity_matrix,
            grad_head,
            grad_down,
            grad_up,
            grad_out,
            grad_qkv,
            *gains,
            grad_bias,
        ) = run_finish([levels, entry, head, down, up, out, qkv], sums)
    else:
        other_rows = lax.dynamic_slice_in_dim(cotangent, (1 - core) * count, count, 0)
        own_rows = lax.dynamic_slice_in_dim(cotangent, core * count, count, 0)
        got = swap_cores(contract_cols(head_projection_weight, other_rows).astype(BF16))
        grad_final_t = contract_cols(head_projection_weight, own_rows) + got.astype(F32)
        bias_local = jnp.sum(cotangent, axis=0, dtype=F32)

        cosine, sine = rotary_tables(sequence_span, hdim)
        tokens = inputs.astype(jnp.float32)
        normed_one, inverse_one = rms_forward(tokens, gain_attn)
        act_one = normed_one.astype(jnp.bfloat16)
        projected = jnp.dot(act_one, w_qkv, preferred_element_type=jnp.float32).reshape(
            rows, sequence_span, 3, HEADS, hdim
        )
        query = rotate(projected[:, :, 0], cosine, sine).astype(jnp.bfloat16)
        key = rotate(projected[:, :, 1], cosine, sine).astype(jnp.bfloat16)
        value = projected[:, :, 2].astype(jnp.bfloat16)
        attended, log_total = lax.map(
            lambda items: attend_forward(items, scale), (query, key, value, segment_ids)
        )
        mixed = attended.reshape(rows * sequence_span, width)
        resid_two = tokens + jnp.dot(mixed, w_out, preferred_element_type=jnp.float32)
        normed_two, inverse_two = rms_forward(resid_two, gain_mlp)
        act_two = normed_two.astype(jnp.bfloat16)
        hidden_pre = jnp.dot(act_two, w_up, preferred_element_type=jnp.float32)
        hidden = jax.nn.silu(hidden_pre).astype(jnp.bfloat16)
        resid_three = resid_two + jnp.dot(hidden, w_down, preferred_element_type=jnp.float32)
        normed_three, inverse_three = rms_forward(resid_three, gain_final)
        final_hidden = normed_three.astype(jnp.bfloat16)
        other_hidden = swap_cores(final_hidden)
        collected_rows = jnp.concatenate(
            [
                jnp.where(core == 0, final_hidden, other_hidden),
                jnp.where(core == 0, other_hidden, final_hidden),
            ],
            axis=0,
        )
        predicted_levels = (
            jnp.dot(collected_rows, head_projection_weight, preferred_element_type=jnp.float32)
            + head_output_bias
        )
        grad_head = lax.psum_scatter(
            contract_rows(collected_rows, cotangent), "dp", scatter_dimension=0, tiled=True
        )
        grad_three, grad_gain_final = rms_backward(
            resid_three, inverse_three, gain_final, grad_final_t.T
        )
        grad_mlp_out = grad_three.astype(jnp.bfloat16)
        grad_hidden = contract_cols(grad_mlp_out, w_down)
        sigmoid = jax.nn.sigmoid(hidden_pre)
        grad_pre = (grad_hidden * sigmoid * (1.0 + hidden_pre * (1.0 - sigmoid))).astype(BF16)
        grad_norm_two, grad_gain_mlp = rms_backward(
            resid_two, inverse_two, gain_mlp, contract_cols(grad_pre, w_up)
        )
        grad_two = grad_three + grad_norm_two
        grad_branch = grad_two.astype(jnp.bfloat16)
        grad_mixed = (
            contract_cols(grad_branch, w_out)
            .astype(jnp.bfloat16)
            .reshape(rows, sequence_span, HEADS, hdim)
        )
        grad_query, grad_key, grad_value = lax.map(
            lambda items: attend_backward(items, scale),
            (query, key, value, segment_ids, log_total, grad_mixed),
        )
        grad_query = unrotate(grad_query, cosine, sine)
        grad_key = unrotate(grad_key, cosine, sine)
        grad_proj = (
            jnp.stack([grad_query, grad_key, grad_value], axis=2)
            .reshape(rows * sequence_span, 3 * width)
            .astype(jnp.bfloat16)
        )
        grad_norm_one, grad_gain_attn = rms_backward(
            tokens, inverse_one, gain_attn, contract_cols(grad_proj, w_qkv)
        )
        entry_sensitivity_matrix = grad_two + grad_norm_one
        grad_down = scatter_rows(hidden, grad_mlp_out)
        grad_up = scatter_rows(act_two, grad_pre)
        grad_out = scatter_rows(mixed, grad_branch)
        grad_qkv = scatter_rows(act_one, grad_proj)
        gains = sum_everywhere(jnp.stack([grad_gain_attn, grad_gain_mlp, grad_gain_final]), True)
        gains = lax.dynamic_slice_in_dim(gains, (place * 2 + core) * share, share, 1)
        grad_bias = sum_everywhere(bias_local, False)
    return (
        predicted_levels,
        entry_sensitivity_matrix,
        gains[0],
        grad_qkv,
        grad_out,
        gains[1],
        grad_up,
        grad_down,
        gains[2],
        grad_head,
        grad_bias,
    )


def solution(mesh):
    return jax.shard_map(
        per_device,
        mesh=mesh,
        in_specs=(
            P(("dp", "head"), None),
            P(("dp", "head"), None),
            P(),
            P(),
            P(),
            P(),
            P(),
            P(),
            P(),
            P(None, "head"),
            P("head"),
            P("dp", "head"),
        ),
        out_specs=(
            P("dp", "head"),
            P(("dp", "head"), None),
            P(("dp", "head")),
            P(("dp", "head"), None),
            P(("dp", "head"), None),
            P(("dp", "head")),
            P(("dp", "head"), None),
            P(("dp", "head"), None),
            P(("dp", "head")),
            P("dp", "head"),
            P("head"),
        ),
        check_vma=False,
    )
```

```python
import functools
import math

import jax
import jax.numpy as jnp
import numpy as np
from jax import lax
from jax.experimental import pallas as pl
from jax.experimental.pallas import tpu as pltpu
from jax.sharding import PartitionSpec as P

HEADS = 16
F32 = jnp.float32
BF16 = jnp.bfloat16

epsilon = 1e-06


def rms_forward(values, gain):
    inverse = lax.rsqrt(jnp.mean(values * values, axis=-1, keepdims=True) + epsilon)
    return (values * inverse * gain, inverse)


def rms_backward(values, inverse, gain, grad):
    normed = values * inverse
    scaled = grad * gain
    grad_gain = jnp.sum(grad * normed, axis=0)
    grad_values = inverse * (scaled - normed * jnp.mean(scaled * normed, axis=-1, keepdims=True))
    return (grad_values, grad_gain)


def rotary_tables(sequence_span, hdim):
    half = hdim // 2
    freq = 10000.0 ** (-jnp.arange(half, dtype=jnp.float32) / half)
    angle = jnp.arange(sequence_span, dtype=jnp.float32)[:, None] * freq[None, :]
    return (jnp.cos(angle)[:, None, :], jnp.sin(angle)[:, None, :])


def rotate(values, cosine, sine):
    half = values.shape[-1] // 2
    first = values[..., :half]
    second = values[..., half:]
    return jnp.concatenate(
        [first * cosine - second * sine, second * cosine + first * sine], axis=-1
    )


def unrotate(grads, cosine, sine):
    half = grads.shape[-1] // 2
    first = grads[..., :half]
    second = grads[..., half:]
    return jnp.concatenate(
        [first * cosine + second * sine, second * cosine - first * sine], axis=-1
    )


def allowed_mask(segs):
    place = jnp.arange(segs.shape[0])
    return (segs[:, None] == segs[None, :]) & (place[:, None] >= place[None, :])


def row_scores(query, key, segs, scale):
    scores = jnp.einsum("qhd,khd->hqk", query, key, preferred_element_type=jnp.float32) * scale
    allowed = allowed_mask(segs)[None]
    return (jnp.where(allowed, scores, -1e30), allowed)


def attend_forward(items, scale):
    query, key, value, segs = items
    scores, allowed = row_scores(query, key, segs, scale)
    peak = jnp.max(scores, axis=-1, keepdims=True)
    expo = jnp.exp(scores - peak)
    overall_number = jnp.sum(expo, axis=-1, keepdims=True)
    probs = (expo / overall_number).astype(jnp.bfloat16)
    attended = jnp.einsum("hqk,khd->qhd", probs, value, preferred_element_type=jnp.float32)
    return (attended.astype(jnp.bfloat16), peak + jnp.log(overall_number))


def attend_backward(items, scale):
    query, key, value, segs, log_total, grad_attended = items
    scores, allowed = row_scores(query, key, segs, scale)
    probs = jnp.where(allowed, jnp.exp(scores - log_total), 0.0)
    grad_value = jnp.einsum(
        "hqk,qhd->khd",
        probs.astype(jnp.bfloat16),
        grad_attended,
        preferred_element_type=jnp.float32,
    )
    grad_probs = jnp.einsum(
        "qhd,khd->hqk", grad_attended, value, preferred_element_type=jnp.float32
    )
    grad_scores = (
        probs * (grad_probs - jnp.sum(grad_probs * probs, axis=-1, keepdims=True))
    ).astype(jnp.bfloat16)
    grad_query = (
        jnp.einsum("hqk,khd->qhd", grad_scores, key, preferred_element_type=jnp.float32) * scale
    )
    grad_key = (
        jnp.einsum("hqk,qhd->khd", grad_scores, query, preferred_element_type=jnp.float32) * scale
    )
    return (grad_query, grad_key, grad_value)


def contract_rows(left, right):
    return lax.dot_general(
        left, right, (((0,), (0,)), ((), ())), preferred_element_type=jnp.float32
    )


def contract_cols(left, right):
    return lax.dot_general(
        left, right, (((1,), (1,)), ((), ())), preferred_element_type=jnp.float32
    )


def swap_cores(values):
    return lax.ppermute(values, "head", [(0, 1), (1, 0)])


def flip(values, bit):
    size = lax.axis_size("dp")
    return lax.ppermute(values, "dp", [(i, i ^ bit) for i in range(size)])


def scatter_rows(left, right):
    return lax.psum_scatter(
        contract_rows(left, right), ("dp", "head"), scatter_dimension=0, tiled=True
    )


def sum_everywhere(values, over_head):
    size = lax.axis_size("dp")
    if over_head:
        values = values + swap_cores(values)
    bit = 1
    while bit < size:
        values = values + flip(values, bit)
        bit *= 2
    return values


MESH = pl.DeviceIdType.MESH


def chunk_table(width, hidden):
    table = [(0, 0)]
    table += [(1, j) for j in range(hidden // width)]
    table += [(2, j) for j in range(hidden // width)]
    table += [(3, 0)]
    table += [(4, j) for j in range(3)]
    return table


def nt(left, right):
    return lax.dot_general(
        left, right, (((1,), (1,)), ((), ())), preferred_element_type=jnp.float32
    )


def nn(left, right):
    return jnp.dot(left, right, preferred_element_type=jnp.float32)


def tt(left, right):
    return lax.dot_general(
        left, right, (((0,), (0,)), ((), ())), preferred_element_type=jnp.float32
    )


def columns_of(rows, scratch):
    scratch[...] = jnp.zeros_like(scratch)
    for i, row in enumerate(rows):
        scratch[i : i + 1] = row[...].reshape(1, row.shape[0])
    return scratch[...].T


def mask_of(seg_row, bias):
    tokens = bias.shape[0]
    ids = seg_row[...].astype(F32)
    wide = jnp.broadcast_to(ids, (8, tokens)).T[:, :1]
    own = lax.broadcasted_iota(jnp.int32, (tokens, tokens), 0)
    asked = lax.broadcasted_iota(jnp.int32, (tokens, tokens), 1)
    bias[...] = jnp.where((wide == ids) & (own <= asked), 0.0, -1e30)


STRIP = 128
SLOTS = 4
REACH = 256
TOGETHER = 2


def query_blocks(tokens):
    for start in range(0, tokens, REACH):
        stop = min(start + REACH, tokens)
        yield max(0, start - REACH), stop, slice(start, stop)


def norm_backward(vref, eref, gains, index, emit):
    width, tokens = vref.shape

    def sums_of(k, carry):
        squares, products = carry
        rows = pl.ds(pl.multiple_of(k * STRIP, STRIP), STRIP)
        v = vref[rows].astype(F32)
        e = eref[rows]
        gain = gains[rows, index : index + 1]
        squares = squares + jnp.sum(v * v, axis=0, keepdims=True)
        products = products + jnp.sum(e * gain * v, axis=0, keepdims=True)
        return squares, products

    blank = jnp.zeros((1, tokens), F32)
    squares, products = lax.fori_loop(0, width // STRIP, sums_of, (blank, blank))
    inverse = lax.rsqrt(squares / width + epsilon)
    mean = products * inverse / width

    @pl.loop(0, width // STRIP)
    def _(k):
        rows = pl.ds(pl.multiple_of(k * STRIP, STRIP), STRIP)
        normed = vref[rows].astype(F32) * inverse
        e = eref[rows]
        gain = gains[rows, index : index + 1]
        gains[rows, 8 + index : 9 + index] = jnp.sum(e * normed, axis=1, keepdims=True)
        emit(k, rows, inverse * (e * gain - normed * mean))


def forward_kernel(
    x,
    w_qkv,
    w_out,
    w_up,
    w_down,
    seg_row,
    gain_attn,
    gain_mlp,
    gain_final,
    cosine,
    sine,
    y_t,
    g_t,
    a2_t,
    o_t,
    a1_t,
    g_o,
    a2_o,
    o_o,
    a1_o,
    x3_t,
    gain_columns,
    x2_t,
    x_t,
    h_t,
    qkv_t,
    lse,
    weights,
    xin,
    xt,
    act1,
    act2,
    final,
    mixed,
    qkv,
    res2,
    res3,
    hbuf,
    gbuf,
    bias,
    gains,
    gain_rows,
    weight_sem,
    in_sem,
    out_sem,
    h_sem,
    g_sem,
    push_send,
    push_recv,
    g_send,
    g_recv,
):
    width, tokens = res2.shape
    hidden = h_t.shape[0]
    pieces = hidden // width
    half = width // 2
    count = HEADS
    hdim = width // count
    scale = 1.0 / math.sqrt(hdim)
    first_tiles = [w_qkv.at[:, k * width : (k + 1) * width] for k in range(3)] + [w_out]

    def fetch(k):
        return pltpu.make_async_copy(first_tiles[k], weights.at[k], weight_sem.at[k])

    def fetch_up(k):
        slot = lax.rem(2 * k, SLOTS)
        source = w_up.at[:, pl.ds(pl.multiple_of(k * width, 128), width)]
        return pltpu.make_async_copy(source, weights.at[slot], weight_sem.at[slot])

    def fetch_down(k):
        slot = lax.rem(2 * k + 1, SLOTS)
        source = w_down.at[pl.ds(pl.multiple_of(k * width, 16), width)]
        return pltpu.make_async_copy(source, weights.at[slot], weight_sem.at[slot])

    me = lax.axis_index("dp")
    core = lax.axis_index("head")
    other = 1 - core

    def remote(src, dst, send, recv):
        return pltpu.make_async_remote_copy(
            src_ref=src,
            dst_ref=dst,
            send_sem=send,
            recv_sem=recv,
            device_id=(me, other),
            device_id_type=MESH,
        )

    fetch_x = pltpu.make_async_copy(x, xin, in_sem)
    fetch_x.start()
    for k in range(SLOTS):
        fetch(k).start()

    barrier = pltpu.get_barrier_semaphore()
    pl.semaphore_signal(barrier, inc=1, device_id=(me, other), device_id_type=MESH)
    gains[...] = jnp.zeros_like(gains)
    gains[:, :8] = columns_of((gain_attn, gain_mlp, gain_final), gain_rows)
    pl.semaphore_wait(barrier, 1)

    mask_of(seg_row, bias)
    fetch_x.wait()
    xt[...] = xin[...].T
    outs, pushes = [], []

    def put(source, target, also=None):
        copy = pltpu.make_async_copy(source, target, out_sem.at[len(outs)])
        outs.append(copy)
        copy.start()
        if also is not None:
            number = len(pushes)
            pushes.append(remote(source, also, push_send.at[number], push_recv.at[number]))
            pushes[-1].start()

    put(xt, x_t)
    put(gains, gain_columns)

    def squares_of(ref):
        def step(k, total):
            v = ref[pl.ds(pl.multiple_of(k * STRIP, STRIP), STRIP)].astype(F32)
            return total + jnp.sum(v * v, axis=0, keepdims=True)

        return lax.fori_loop(0, width // STRIP, step, jnp.zeros((1, tokens), F32))

    def normalize(ref, index, to):
        inverse = lax.rsqrt(squares_of(ref) / width + epsilon)

        @pl.loop(0, width // STRIP)
        def _(k):
            rows = pl.ds(pl.multiple_of(k * STRIP, STRIP), STRIP)
            to[rows] = (ref[rows].astype(F32) * inverse * gains[rows, index : index + 1]).astype(
                BF16
            )

    normalize(xt, 0, act1)
    put(act1, a1_t, a1_o)

    turn = hdim // 2
    for part in range(3):
        fetch(part).wait()

    @pl.loop(0, 2)
    def _(part):
        for lower in range(2):
            value = tt(weights[part, :, lower * half : (lower + 1) * half], act1[...])
            for head in range(count // 2):
                one = value[head * hdim : head * hdim + turn]
                two = value[head * hdim + turn : (head + 1) * hdim]
                turned = jnp.concatenate(
                    [one * cosine[...] - two * sine[...], two * cosine[...] + one * sine[...]],
                    axis=0,
                )
                base = pl.multiple_of(part * width + lower * half + head * hdim, 16)
                qkv[pl.ds(base, hdim)] = turned.astype(BF16)

    fetch_up(0).start()
    fetch_down(0).start()
    for lower in range(2):
        rows = slice(lower * half, (lower + 1) * half)
        value = tt(weights[2, :, rows], act1[...])
        qkv[2 * width + lower * half : 2 * width + (lower + 1) * half] = value.astype(BF16)
    fetch_up(1).start()
    put(qkv, qkv_t)

    def attend(head):
        def rows_of(part):
            return pl.ds(pl.multiple_of(part * width + head * hdim, 16), hdim)

        q_t = qkv[rows_of(0)]
        v_t = qkv[rows_of(2)]
        k = qkv[rows_of(1)].T
        for low, high, asked in query_blocks(tokens):
            scores = nn(k[low:high], q_t[:, asked]) * scale + bias[low:high, asked]
            peak = jnp.max(scores, axis=0, keepdims=True)
            expo = jnp.exp(scores - peak)
            amount = jnp.sum(expo, axis=0, keepdims=True)
            probs = (expo * (1.0 / amount)).astype(BF16)
            mixed[rows_of(0), asked] = nn(v_t[:, low:high], probs).astype(BF16)
            lse[head, :, asked] = peak + jnp.log(amount)

    @pl.loop(0, count // 4)
    def _(i):
        for u in range(4):
            attend(i * 4 + u)

    put(mixed, o_t, o_o)

    fetch(3).wait()
    for lower in range(2):
        rows = slice(lower * half, (lower + 1) * half)
        res2[rows] = xt[rows].astype(F32) + tt(weights[3, :, rows], mixed[...])
        res3[rows] = res2[rows]
    fetch_down(1).start()
    put(res2, x2_t)
    normalize(res2, 1, act2)
    put(act2, a2_t, a2_o)

    def piece(k):
        return pl.ds(pl.multiple_of(k * width, 16), width)

    def h_copy(k):
        slot = lax.rem(k, 2)
        return pltpu.make_async_copy(hbuf.at[slot], h_t.at[piece(k)], h_sem.at[slot])

    def g_copy(k):
        slot = lax.rem(k, 2)
        return pltpu.make_async_copy(gbuf.at[slot], g_t.at[piece(k)], g_sem.at[slot])

    def g_push(k):
        slot = lax.rem(k, 2)
        return remote(gbuf.at[slot], g_o.at[piece(k)], g_send.at[slot], g_recv.at[k])

    @pl.loop(0, pieces)
    def _(k):
        slot, up, down = lax.rem(k, 2), lax.rem(2 * k, SLOTS), lax.rem(2 * k + 1, SLOTS)
        fetch_up(k).wait()

        @pl.when(k >= 2)
        def _():
            h_copy(k - 2).wait()
            g_copy(k - 2).wait()
            g_push(k - 2).wait_send()

        for lower in range(2):
            rows = slice(lower * half, (lower + 1) * half)
            value = tt(weights[up, :, rows], act2[...])
            hbuf[slot, rows] = value.astype(BF16)
            gbuf[slot, rows] = (value * (0.5 * jnp.tanh(0.5 * value) + 0.5)).astype(BF16)

        @pl.when(k + 2 < pieces)
        def _():
            fetch_up(k + 2).start()

        h_copy(k).start()
        g_copy(k).start()
        g_push(k).start()
        fetch_down(k).wait()
        for lower in range(2):
            rows = slice(lower * half, (lower + 1) * half)
            res3[rows] += tt(weights[down, :, rows], gbuf[slot])

        @pl.when(k + 2 < pieces)
        def _():
            fetch_down(k + 2).start()

    put(res3, x3_t)
    normalize(res3, 2, final)
    put(final, y_t)
    for copy in outs:
        copy.wait()
    for k in range(max(0, pieces - 2), pieces):
        h_copy(k).wait()
        g_copy(k).wait()
        g_push(k).wait_send()
    for k in range(pieces):
        g_push(k).wait_recv()
    for push in pushes:
        push.wait()


def run_forward(x, w_qkv, w_out, w_up, w_down, segs, gains, cosine, sine):
    tokens, width = x.shape
    hidden = w_up.shape[1]
    hdim = width // HEADS
    hbm = pl.BlockSpec(memory_space=pl.ANY)
    vmem = pl.BlockSpec(memory_space=pltpu.VMEM)
    flat = (width, tokens)
    shapes = [
        jax.ShapeDtypeStruct(shape, dtype)
        for shape, dtype in (
            (flat, BF16),
            ((hidden, tokens), BF16),
            (flat, BF16),
            (flat, BF16),
            (flat, BF16),
            ((hidden, tokens), BF16),
            (flat, BF16),
            (flat, BF16),
            (flat, BF16),
            (flat, F32),
            ((width, 128), F32),
            (flat, F32),
            (flat, BF16),
            ((hidden, tokens), BF16),
            ((3 * width, tokens), BF16),
            ((HEADS, 1, tokens), F32),
        )
    ]
    dma = pltpu.SemaphoreType.DMA
    return pl.pallas_call(
        forward_kernel,
        out_shape=shapes,
        in_specs=[hbm] * 5 + [vmem] * 6,
        out_specs=[hbm] * 15 + [vmem],
        scratch_shapes=[
            pltpu.VMEM((SLOTS, width, width), BF16),
            pltpu.VMEM((tokens, width), BF16),
            pltpu.VMEM(flat, BF16),
            pltpu.VMEM(flat, BF16),
            pltpu.VMEM(flat, BF16),
            pltpu.VMEM(flat, BF16),
            pltpu.VMEM(flat, BF16),
            pltpu.VMEM((3 * width, tokens), BF16),
            pltpu.VMEM(flat, F32),
            pltpu.VMEM(flat, F32),
            pltpu.VMEM((2,) + flat, BF16),
            pltpu.VMEM((2,) + flat, BF16),
            pltpu.VMEM((tokens, tokens), F32),
            pltpu.VMEM((width, 128), F32),
            pltpu.VMEM((8, width), F32),
            dma((SLOTS,)),
            dma(()),
            dma((9,)),
            dma((2,)),
            dma((2,)),
            dma((3,)),
            dma((3,)),
            dma((2,)),
            dma((hidden // width,)),
        ],
        compiler_params=pltpu.CompilerParams(
            collective_id=1, has_side_effects=True, vmem_limit_bytes=60 << 20
        ),
        name="forward",
    )(x, w_qkv, w_out, w_up, w_down, segs, *gains, cosine, sine)


LEAD = 3


def backward_kernel(
    table,
    size,
    y_t,
    g_t,
    a2_t,
    o_t,
    a1_t,
    g_o,
    a2_o,
    o_o,
    a1_o,
    y_flat,
    cot,
    w_head,
    x3_t,
    x2_t,
    x_t,
    h_t,
    qkv_t,
    gain_columns,
    w_down,
    w_up,
    w_out,
    w_qkv,
    lse,
    seg_row,
    head_bias,
    cosine,
    sine,
    out_head,
    out_down,
    out_up,
    out_out,
    out_qkv,
    out_small,
    out_entry,
    out_levels,
    e3_o,
    eh_o,
    e2_o,
    ep_o,
    eh_mine,
    lbuf,
    rbuf,
    cbuf,
    grad,
    recv1,
    pair,
    recv2,
    line,
    recv_up,
    recv_down,
    side,
    side_up,
    side_down,
    side1,
    side2,
    total,
    sums,
    sums_in,
    dx,
    work,
    acc,
    ebuf,
    bias,
    gains,
    wrows,
    wcols,
    hbuf,
    ehbuf,
    ep,
    eo,
    heads,
    obuf,
    push_send,
    push_recv,
    left_sem,
    right_sem,
    send1_sem,
    recv1_sem,
    send2_sem,
    recv2_sem,
    up_send,
    up_recv,
    down_send,
    down_recv,
    side_up_send,
    side_up_recv,
    side_down_send,
    side_down_recv,
    side1_send,
    side1_recv,
    side2_send,
    side2_recv,
    local_sem,
    swap_send,
    swap_recv,
    small_send,
    small_recv,
    row_sem,
    col_sem,
    h_sem,
    eh_out_sem,
    eh_in_sem,
    head_sem,
    fetch_sem,
    entry_sem,
):
    n = len(table)
    length = size // 4
    me = lax.axis_index("dp")
    core = lax.axis_index("head")
    other = 1 - core
    xi = lax.rem(me, 2)
    yi = lax.rem(me // 2, 2)
    zi = me // 4
    width, tokens = dx.shape
    hidden = h_t.shape[0]
    cols = width // 2
    block = width // size
    count, hdim = eo.shape[:2]
    scale = 1.0 / math.sqrt(hdim)
    flip_x = me + 1 - 2 * xi
    flip_y = me + 2 * (1 - 2 * yi)
    first_bit = jnp.where(core == 0, xi, yi)
    second_bit = jnp.where(core == 0, yi, xi)
    first_peer = jnp.where(core == 0, flip_x, flip_y)
    second_peer = jnp.where(core == 0, flip_y, flip_x)
    far = lax.rem(me + size // 2, size)
    near = me + 4 * (1 - 2 * lax.rem(zi, 2))
    rings = recv1.shape[0]
    ring2 = recv2.shape[0]
    ring_line = line.shape[0]
    ring_side, ring_in = side.shape[0], side1.shape[0]
    main = grad.shape[-1]

    fetch_head_weight = pltpu.make_async_copy(w_head, wcols.at[0], fetch_sem.at[0])
    fetch_x3 = pltpu.make_async_copy(x3_t, work, fetch_sem.at[1])
    fetch_gains = pltpu.make_async_copy(gain_columns, gains, fetch_sem.at[4])
    fetch_x2 = pltpu.make_async_copy(x2_t, work, fetch_sem.at[1])
    fetch_x = pltpu.make_async_copy(x_t, ebuf, fetch_sem.at[0])

    def local_c(half, which):
        start = pl.multiple_of(which * tokens, 16)
        return pltpu.make_async_copy(
            cot.at[pl.ds(start, tokens)], cbuf.at[half], fetch_sem.at[2 + half]
        )

    lefts = (y_t, g_t, a2_t, o_t, a1_t)
    left_others = (None, g_o, a2_o, o_o, a1_o)
    pieces = hidden // width

    def start_left(c):
        i, j = table[c]
        lower = pl.ds(j * block, block) if i == 1 else slice(None)
        for half, source in ((0, lefts[i]), (1, left_others[i])):
            pltpu.make_async_copy(
                source.at[:, lower, :], lbuf.at[c % 2, half], left_sem.at[c % 2, half]
            ).start()

    fetch_y = pltpu.make_async_copy(y_t, lbuf.at[0, 0], left_sem.at[0, 0])
    fetch_y.start()
    local_c(1, other).start()
    fetch_head_weight.start()
    local_c(0, core).start()
    fetch_x3.start()
    fetch_gains.start()
    start_left(1)

    barrier = pltpu.get_barrier_semaphore()
    for index, which in ((me, other), (flip_x, core), (flip_y, core), (far, core)):
        pl.semaphore_signal(barrier, inc=1, device_id=(index, which), device_id_type=MESH)

    @pl.when(zi > 0)
    def _():
        pl.semaphore_signal(barrier, inc=1, device_id=(me - 4, core), device_id_type=MESH)

    @pl.when(zi < length - 1)
    def _():
        pl.semaphore_signal(barrier, inc=1, device_id=(me + 4, core), device_id_type=MESH)

    inner = jnp.where(zi > 0, 1, 0) + jnp.where(zi < length - 1, 1, 0)
    pl.semaphore_wait(barrier, 4 + inner)

    def remote(src, dst, send, recv, index, which):
        return pltpu.make_async_remote_copy(
            src_ref=src,
            dst_ref=dst,
            send_sem=send,
            recv_sem=recv,
            device_id=(index, which),
            device_id_type=MESH,
        )

    PE3, PE2, PEP, PY, PDY, PLEVEL = range(6)

    def push(k):
        if k == PY:
            src, dst = lbuf.at[0, 0], lbuf.at[0, 1]
        elif k in (PDY, PLEVEL):
            src, dst = ehbuf, hbuf
        elif k == PEP:
            wide = 3 * cols
            src, dst = ep.at[pl.ds(pl.multiple_of(other * wide, 16), wide)], ep_o
        else:
            src, dst = ebuf, (e3_o, e2_o)[k]
            src = src.at[pl.ds(pl.multiple_of(other * cols, 16), cols)]
        return remote(src, dst, push_send.at[k], push_recv.at[k], me, other)

    fetch_y.wait()
    push(PY).start()
    fetch_head_weight.wait()
    local_c(1, other).wait()
    for i in range(2):
        ehbuf[i] = nt(wcols[0, i * cols : (i + 1) * cols], cbuf[1]).astype(BF16)
    push(PDY).start()
    local_c(0, core).wait()

    def start_right(c):
        i, j = table[c]
        slot = c % 2
        mine = pl.ds(pl.multiple_of(core * cols, 16), cols)
        rows = pl.ds(j * cols, cols)
        if i == 1:
            own, its = ebuf.at[mine], e3_o
            if j == 0:
                push(PE3).wait_recv()
        elif i == 2:
            own, its = eh_mine.at[rows], eh_o.at[rows]
            eh_push(j).wait_recv()
        elif i == 3:
            own, its = ebuf.at[mine], e2_o
            push(PE2).wait_recv()
        else:
            start = pl.multiple_of(core * 3 * cols + j * cols, 16)
            own, its = ep.at[pl.ds(start, cols)], ep_o.at[rows]
            if j == 0:
                push(PEP).wait_recv()
        pltpu.make_async_copy(own, rbuf.at[slot, 0], right_sem.at[slot, 0]).start()
        pltpu.make_async_copy(its, rbuf.at[slot, 1], right_sem.at[slot, 1]).start()

    def eh_push(piece):
        return remote(
            ehbuf.at[0],
            eh_o.at[pl.ds(pl.multiple_of(piece * cols, 16), cols)],
            eh_out_sem.at[0],
            eh_in_sem.at[piece],
            me,
            other,
        )

    def eh_keep(piece):
        return pltpu.make_async_copy(
            ehbuf.at[1],
            eh_mine.at[pl.ds(pl.multiple_of(piece * cols, 16), cols)],
            eh_out_sem.at[1],
        )

    def wait_left(slot):
        for half in range(2):
            pltpu.make_async_copy(
                lbuf.at[slot, half], lbuf.at[slot, half], left_sem.at[slot, half]
            ).wait()

    def wait_right(slot):
        for half in range(2):
            pltpu.make_async_copy(
                rbuf.at[slot, half], rbuf.at[slot, half], right_sem.at[slot, half]
            ).wait()

    def form(c, right, multiply):
        slot, ring, to = lax.rem(c, 2), lax.rem(c, LEAD), lax.rem(c, ring_side)

        for z in range(length):
            value = None
            for half in range(2):
                left = lbuf[slot, half, 4 * z : 4 * z + 4].reshape(4 * block, tokens)
                part = multiply(left, right[half])
                value = part if value is None else value + part
            value = value.astype(BF16)
            for q in range(4):
                x, y = q % 2, q // 2
                one = jnp.where(core == 0, x, y)
                two = jnp.where(core == 0, y, x)
                part = value[q * block : (q + 1) * block]
                grad[ring, one, two, z] = part[:, :main]
                side[to, z, one, two] = part[:, main:]
        send1(c).start()
        start_side(c, 1)

    def send1(c):
        ring, spot = lax.rem(c, LEAD), lax.rem(c, rings)
        return remote(
            grad.at[ring, 1 - first_bit],
            recv1.at[spot],
            send1_sem.at[ring],
            recv1_sem.at[spot],
            first_peer,
            core,
        )

    def send2(c):
        ring, spot = lax.rem(c, 2), lax.rem(c, ring2)
        return remote(
            pair.at[ring, 1 - second_bit],
            recv2.at[spot],
            send2_sem.at[ring],
            recv2_sem.at[spot],
            second_peer,
            core,
        )

    def send_up(c, step):
        ring, spot = lax.rem(c, ring_line), lax.rem(c, rings)
        return remote(
            line.at[ring, jnp.minimum(zi + (length - step), length - 1)],
            recv_up.at[spot, step - 1],
            up_send.at[ring, step - 1],
            up_recv.at[spot, step - 1],
            jnp.minimum(me + 4, size - 1),
            core,
        )

    def send_down(c, step):
        ring, spot = lax.rem(c, ring_line), lax.rem(c, rings)
        return remote(
            line.at[ring, jnp.maximum(zi - (length - step), 0)],
            recv_down.at[spot, step - 1],
            down_send.at[ring, step - 1],
            down_recv.at[spot, step - 1],
            jnp.maximum(me - 4, 0),
            core,
        )

    def side_send_up(c, step):
        ring, spot = lax.rem(c, ring_side), lax.rem(c, ring_in)
        return remote(
            side.at[ring, jnp.minimum(zi + (length - step), length - 1)],
            side_up.at[spot, step - 1],
            side_up_send.at[ring, step - 1],
            side_up_recv.at[spot, step - 1],
            jnp.minimum(me + 4, size - 1),
            core,
        )

    def side_send_down(c, step):
        ring, spot = lax.rem(c, ring_side), lax.rem(c, ring_in)
        return remote(
            side.at[ring, jnp.maximum(zi - (length - step), 0)],
            side_down.at[spot, step - 1],
            side_down_send.at[ring, step - 1],
            side_down_recv.at[spot, step - 1],
            jnp.maximum(me - 4, 0),
            core,
        )

    def side_send1(c):
        ring, spot = lax.rem(c, ring_side), lax.rem(c, ring_in)
        return remote(
            side.at[ring, zi, 1 - first_bit],
            side1.at[spot],
            side1_send.at[ring],
            side1_recv.at[spot],
            first_peer,
            core,
        )

    def side_send2(c):
        ring, spot = lax.rem(c, ring_side), lax.rem(c, ring_in)
        return remote(
            side.at[ring, zi, first_bit, 1 - second_bit],
            side2.at[spot],
            side2_send.at[ring],
            side2_recv.at[spot],
            second_peer,
            core,
        )

    def start_side(c, step):
        @pl.when(zi < step)
        def _():
            side_send_up(c, step).start()

        @pl.when(zi >= length - step)
        def _():
            side_send_down(c, step).start()

    def exchange_side(t):
        for step in range(1, length):

            @pl.when((t >= step - 1) & (t <= n + step - 2))
            def _():
                c = t - step + 1
                ring, at = lax.rem(c, ring_side), lax.rem(c, ring_in)
                up_in = (zi >= 1) & (zi <= step)
                down_in = (zi <= length - 2) & (zi >= length - 1 - step)

                @pl.when(up_in)
                def _():
                    side_send_up(c, step).wait_recv()
                    spot = jnp.minimum(zi + (length - 1 - step), length - 1)
                    side[ring, spot] = side[ring, spot] + side_up[at, step - 1]

                @pl.when(down_in)
                def _():
                    side_send_down(c, step).wait_recv()
                    spot = jnp.maximum(zi - (length - 1 - step), 0)
                    side[ring, spot] = side[ring, spot] + side_down[at, step - 1]

                if step < length - 1:
                    start_side(c, step + 1)
                else:
                    side_send1(c).start()

        @pl.when((t >= length - 1) & (t <= n + length - 2))
        def _():
            c = t - length + 1
            ring, at = lax.rem(c, ring_side), lax.rem(c, ring_in)
            side_send1(c).wait_recv()
            side[ring, zi, first_bit] = side[ring, zi, first_bit] + side1[at]
            side_send2(c).start()

        @pl.when((t >= length) & (t <= n + length - 1))
        def _():
            c = t - length
            ring, at = lax.rem(c, ring_side), lax.rem(c, ring_in)
            side_send2(c).wait_recv()
            total[c, :, main:] = side[ring, zi, first_bit, second_bit].astype(F32) + side2[
                at
            ].astype(F32)
            for back in range(1, length):

                @pl.when(zi < back)
                def _():
                    side_send_up(c, back).wait_send()

                @pl.when(zi >= length - back)
                def _():
                    side_send_down(c, back).wait_send()

            side_send1(c).wait_send()
            side_send2(c).wait_send()

    def start_line(c, step):
        @pl.when(zi < step)
        def _():
            send_up(c, step).start()

        @pl.when(zi >= length - step)
        def _():
            send_down(c, step).start()

    def wait_line_sent(c, step):
        @pl.when(zi < step)
        def _():
            send_up(c, step).wait_send()

        @pl.when(zi >= length - step)
        def _():
            send_down(c, step).wait_send()

    def results(c):
        i, j = table[c]
        if i == 0:
            return [pltpu.make_async_copy(total.at[c], out_head, local_sem.at[c])]
        if i == 1:
            target = out_down.at[
                pl.ds((j % 2) * block, block), pl.ds(pl.multiple_of(core * cols, 128), cols)
            ]
            return [
                pltpu.make_async_copy(total.at[c], target, local_sem.at[c]),
                remote(total.at[c], target, swap_send.at[c], swap_recv.at[c], me, other),
            ]
        target = (None, None, out_up, out_out, out_qkv)[i]
        wide = target.shape[1] // 2
        place = target.at[:, pl.ds(pl.multiple_of(core * wide + j * cols, 128), cols)]
        half = block // 2
        mine = pl.ds(pl.multiple_of(core * half, 8), half)
        its = pl.ds(pl.multiple_of(other * half, 8), half)
        return [
            pltpu.make_async_copy(total.at[c, mine], place, local_sem.at[c]),
            remote(total.at[c, its], place, swap_send.at[c], swap_recv.at[c], me, other),
        ]

    def start_results(c):
        i, j = table[c]
        copies = results(c)
        if i == 1:
            owner = j // (pieces // 2)
            pl.when(core == owner)(copies[0].start)
            pl.when(core != owner)(copies[1].start)
        else:
            for copy in copies:
                copy.start()

    def end_results(c):
        i, j = table[c]
        copies = results(c)
        if i == 1:
            owner = j // (pieces // 2)
            pl.when(core == owner)(copies[0].wait)
            pl.when(core == owner)(copies[1].wait_recv)
            pl.when(core != owner)(copies[1].wait_send)
        else:
            for copy in copies:
                copy.wait()

    def exchange(t):
        exchange_side(t)

        @pl.when(t < n)
        def _():
            c = t
            send1(c).wait_recv()
            ring, spot, to = lax.rem(c, LEAD), lax.rem(c, rings), lax.rem(c, 2)

            @pl.when(c >= 2)
            def _():
                send2(c - 2).wait_send()

            for two in range(2):

                @pl.loop(0, length)
                def _(z):
                    pair[to, two, z] = grad[ring, first_bit, two, z] + recv1[spot, two, z]

            send2(c).start()

        @pl.when((t >= 1) & (t <= n))
        def _():
            c = t - 1
            send2(c).wait_recv()
            ring, spot, to = lax.rem(c, 2), lax.rem(c, ring2), lax.rem(c, ring_line)

            @pl.loop(0, length)
            def _(z):
                line[to, z] = pair[ring, second_bit, z] + recv2[spot, z]

            start_line(c, 1)


        for step in range(1, length):

            @pl.when((t >= 1 + step) & (t <= n + step))
            def _():
                c = t - 1 - step
                ring, at = lax.rem(c, ring_line), lax.rem(c, rings)
                last = step == length - 1
                up_in = (zi >= 1) & (zi <= step)
                down_in = (zi <= length - 2) & (zi >= length - 1 - step)

                @pl.when(up_in)
                def _():
                    send_up(c, step).wait_recv()
                    spot = jnp.minimum(zi + (length - 1 - step), length - 1)
                    if not last:
                        line[ring, spot] = line[ring, spot] + recv_up[at, step - 1]

                @pl.when(down_in)
                def _():
                    send_down(c, step).wait_recv()
                    spot = jnp.maximum(zi - (length - 1 - step), 0)
                    if not last:
                        line[ring, spot] = line[ring, spot] + recv_down[at, step - 1]

                if not last:
                    start_line(c, step + 1)
                else:
                    total[c, :, :main] = line[ring, zi].astype(F32)

                    @pl.when(up_in)
                    def _():
                        total[c, :, :main] += recv_up[at, step - 1].astype(F32)

                    @pl.when(down_in)
                    def _():
                        total[c, :, :main] += recv_down[at, step - 1].astype(F32)

                    for back in range(1, length):
                        wait_line_sent(c, back)

                    for d in range(n):

                        @pl.when(c == d)
                        def _():
                            start_results(d)

    push(PY).wait_recv()
    form(0, [cbuf[0], cbuf[1]], nn)
    push(PY).wait_send()
    start_left(2)

    def emit_final(k, rows, value):
        dx[rows] = value
        ebuf[rows] = value.astype(BF16)

    push(PDY).wait_recv()
    for i in range(2):
        rows = slice(i * cols, (i + 1) * cols)
        dx[rows] = nt(wcols[0, rows], cbuf[0]) + hbuf[i].astype(F32)
    fetch_x3.wait()
    fetch_gains.wait()
    norm_backward(work, dx, gains, 2, emit_final)
    push(PE3).start()
    fetch_x2.start()
    sums[0] = jnp.zeros_like(sums[0])
    for i in range(2):
        share = jnp.sum(cbuf[i].astype(F32), axis=0, keepdims=True)
        at = pl.ds(pl.multiple_of(core * cols, 128), cols)
        sums[0, 3:4, at] = sums[0, 3:4, at] + share
    push(PDY).wait_send()
    for c in range(1, LEAD):
        start_right(c)
        wait_left(c % 2)
        wait_right(c % 2)
        form(c, [rbuf[c % 2, 0], rbuf[c % 2, 1]], nt)
        start_left(c + 2)
    def row_tile(k, slot, source):
        return pltpu.make_async_copy(
            source.at[pl.ds(pl.multiple_of(k * cols, 16), cols)], wrows.at[slot], row_sem.at[slot]
        )

    def col_tile(k, slot, source):
        return pltpu.make_async_copy(
            source.at[:, pl.ds(pl.multiple_of(k * cols, 128), cols)],
            wcols.at[slot],
            col_sem.at[slot],
        )

    def h_tile(k, slot):
        return pltpu.make_async_copy(
            h_t.at[pl.ds(pl.multiple_of(k * cols, 16), cols)], hbuf.at[slot], h_sem.at[slot]
        )

    def mlp_tiles(k):
        return jnp.where(lax.rem(k, 2) == 0, other, core) * pieces + k // 2

    def fetch_mlp(k):
        slot = lax.rem(k, 2)
        tile = mlp_tiles(k)
        row_tile(tile, slot, w_down).start()
        col_tile(tile, slot, w_up).start()
        h_tile(tile, slot).start()

    def mlp_step(k):
        slot = lax.rem(k, 2)
        tile = mlp_tiles(k)
        row_tile(tile, slot, w_down).wait()
        h_tile(tile, slot).wait()

        @pl.when((k >= 2) & (slot == 0))
        def _():
            eh_push(0).wait_send()

        @pl.when((k >= 2) & (slot == 1))
        def _():
            eh_keep(0).wait()

        part = cols // 2
        for i in range(2):
            rows = slice(i * part, (i + 1) * part)
            value = nn(wrows[slot, rows], ebuf[...])
            pre = hbuf[slot, rows].astype(F32)
            sig = 0.5 * jnp.tanh(0.5 * pre) + 0.5
            ehbuf[slot, rows] = (value * sig * (1.0 + pre * (1.0 - sig))).astype(BF16)

        @pl.when(slot == 0)
        def _():
            eh_push(k // 2).start()

        @pl.when(slot == 1)
        def _():
            eh_keep(k // 2).start()

        col_tile(tile, slot, w_up).wait()
        accumulate(wcols.at[slot], ehbuf.at[slot], k == 0)

        @pl.when(k + 2 < 2 * pieces)
        def _():
            fetch_mlp(k + 2)

    def accumulate(left, right, first):
        @pl.when(first)
        def _():
            acc[...] = jnp.zeros_like(acc)

        part = width // 4
        for i in range(4):
            rows = slice(i * part, (i + 1) * part)
            acc[rows] += nn(left[rows], right[...])

    fetch_mlp(0)
    fetch_mlp(1)

    def emit_mlp(k, rows, value):
        value = dx[rows] + value
        dx[rows] = value
        ebuf[rows] = value.astype(BF16)

    def middle():
        eh_push(0).wait_send()
        eh_keep(0).wait()
        row_tile(0, 0, w_out).start()
        row_tile(1, 1, w_out).start()
        push(PE3).wait_send()
        fetch_x2.wait()
        norm_backward(work, acc, gains, 1, emit_mlp)
        push(PE2).start()

        @pl.loop(0, 2)
        def _(k):
            row_tile(k, k, w_out).wait()

            group = cols // hdim
            value = nn(wrows[k], ebuf[...]).astype(BF16)
            eo[pl.ds(k * group, group)] = value.reshape(group, hdim, tokens)

        mask_of(seg_row, bias)

    def level_copy(k, which, slot):
        return pltpu.make_async_copy(
            obuf.at[slot],
            out_levels.at[
                pl.ds(pl.multiple_of(which * tokens, 8), tokens), k * STRIP : (k + 1) * STRIP
            ],
            entry_sem.at[slot],
        )

    def levels(source, which):
        last = cols // STRIP
        for k in range(last):
            if k >= 2:
                level_copy(k - 2, which, k % 2).wait()
            part = slice(k * STRIP, (k + 1) * STRIP)
            obuf[k % 2] = (
                tt(source[0], wcols[0, :cols, part])
                + tt(source[1], wcols[0, cols:, part])
                + head_bias[...].reshape(1, cols)[:, part]
            )
            level_copy(k, which, k % 2).start()
        for k in range(last - 2, last):
            level_copy(k, which, k % 2).wait()

    pairs = count // TOGETHER
    per_turn = -(-pairs // 3)

    def head_copy(head, slot, u, part):
        return pltpu.make_async_copy(
            qkv_t.at[pl.ds(pl.multiple_of(part * width + head * hdim, 16), hdim)],
            heads.at[slot, u, part],
            head_sem.at[slot, u, part],
        )

    def fetch_heads(i):
        for u in range(TOGETHER):
            for part in range(3):
                head_copy(i * TOGETHER + u, lax.rem(i, 2), u, part).start()

    def attend_head(head, slot, u):
        q_t, k_t, v_t = (heads[slot, u, part] for part in range(3))
        e_t = eo[head]
        q, k, v, e = q_t.T, k_t.T, v_t.T, e_t.T
        blocks = list(query_blocks(tokens))
        weight = lse[head]
        ek, ev, eqs = [[] for _ in blocks], [[] for _ in blocks], []
        for low, high, asked in blocks:
            scores = nn(k[low:high], q_t[:, asked]) * scale + bias[low:high, asked]
            p = jnp.exp(scores - weight[:, asked])
            ep_t = nn(v[low:high], e_t[:, asked])
            share = jnp.sum(p * ep_t, axis=0, keepdims=True)
            es = (p * (ep_t - share)).astype(BF16)
            eqs.append(nn(k_t[:, low:high], es))
            one, two = nn(es, q[asked]), nn(p.astype(BF16), e[asked])
            for number, (_, _, own) in enumerate(blocks):
                if low <= own.start < high:
                    ek[number].append(one[own.start - low : own.stop - low])
                    ev[number].append(two[own.start - low : own.stop - low])
        ek_t = jnp.concatenate([sum(terms[1:], terms[0]) for terms in ek], axis=0).T
        ev_t = jnp.concatenate([sum(terms[1:], terms[0]) for terms in ev], axis=0).T
        half = hdim // 2
        for part, value in ((0, jnp.concatenate(eqs, axis=1)), (1, ek_t)):
            one, two = value[:half] * scale, value[half:] * scale
            turned = jnp.concatenate(
                [one * cosine[...] + two * sine[...], two * cosine[...] - one * sine[...]],
                axis=0,
            )
            to = pl.ds(pl.multiple_of(part * width + head * hdim, 16), hdim)
            ep[to] = turned.astype(BF16)
        to = pl.ds(pl.multiple_of(2 * width + head * hdim, 16), hdim)
        ep[to] = ev_t.astype(BF16)

    def attend(turn):
        @pl.when(turn == 0)
        def _():
            fetch_heads(0)

        @pl.loop(turn * per_turn, jnp.minimum((turn + 1) * per_turn, pairs))
        def _(i):
            slot = lax.rem(i, 2)
            for u in range(TOGETHER):
                for part in range(3):
                    head_copy(i * TOGETHER + u, slot, u, part).wait()

            @pl.when((i + 1) * TOGETHER < count)
            def _():
                fetch_heads(i + 1)

            for u in range(TOGETHER):
                attend_head(i * TOGETHER + u, slot, u)

        @pl.when(turn == 2)
        def _():
            push(PEP).start()

    def fetch_qkv(k):
        col_tile(k, lax.rem(k, 2), w_qkv).start()

    def qkv_step(k):
        slot = lax.rem(k, 2)
        col_tile(k, slot, w_qkv).wait()
        rows = pl.ds(pl.multiple_of(k * cols, 16), cols)
        accumulate(wcols.at[slot], ep.at[rows], k == 0)

        @pl.when(k + 2 < 6)
        def _():
            fetch_qkv(k + 2)

    def entry_copy(k, slot):
        return pltpu.make_async_copy(
            obuf.at[slot],
            out_entry.at[:, pl.ds(pl.multiple_of(k * STRIP, STRIP), STRIP)],
            entry_sem.at[slot],
        )

    def emit_entry(k, rows, value):
        slot = lax.rem(k, 2)

        @pl.when(k >= 2)
        def _():
            entry_copy(k, slot).wait()

        obuf[slot] = (dx[rows] + value).T
        entry_copy(k, slot).start()

    peers = ((me, other), (flip_x, core), (flip_y, core), (near, core), (far, core))
    steps = len(peers)

    def small_copy(i):
        return remote(
            sums.at[i], sums_in.at[i], small_send.at[i], small_recv.at[i], peers[i][0], peers[i][1]
        )

    def last():
        fetch_x.wait()
        norm_backward(ebuf, acc, gains, 0, emit_entry)
        for slot in range(2):
            entry_copy(0, slot).wait()
        sums[0] = sums[0] + gains[...].T[8:16]
        small_copy(0).start()

    @pl.loop(0, n + length)
    def _(t):
        for c in range(LEAD, n):
            if table[c] != (4, 0):

                @pl.when(t == c - LEAD)
                def _():
                    start_right(c)

        exchange(t)

        for c in range(LEAD, n):
            if table[c] == (4, 0):

                @pl.when(t == c - LEAD)
                def _():
                    start_right(c)

        @pl.when(t + LEAD < n)
        def _():
            c = t + LEAD
            slot = lax.rem(c, 2)
            wait_left(slot)
            wait_right(slot)
            send1(t).wait_send()
            form(c, [rbuf[slot, 0], rbuf[slot, 1]], nt)
            for d in range(LEAD + 2, n):

                @pl.when(c == d - 2)
                def _():
                    start_left(d)

        @pl.when(t < 3)
        def _():
            @pl.loop(t * 3, jnp.minimum(t * 3 + 3, 2 * pieces))
            def _(k):
                mlp_step(k)

        @pl.when(t == 3)
        def _():
            middle()

        @pl.when((t >= 4) & (t < 7))
        def _():
            attend(t - 4)

        @pl.when(t == 6)
        def _():
            fetch_qkv(0)
            fetch_qkv(1)

        @pl.when((t == 7) | (t == 8))
        def _():
            @pl.loop(0, 3)
            def _(i):
                qkv_step((t - 7) * 3 + i)

        @pl.when(t == 9)
        def _():
            pltpu.make_async_copy(w_head, wcols.at[0], col_sem.at[0]).start()
            fetch_level = pltpu.make_async_copy(y_flat, ehbuf, h_sem.at[0])
            fetch_level.start()
            last()
            fetch_level.wait()
            push(PLEVEL).start()

        @pl.when(t == 10)
        def _():
            pltpu.make_async_copy(w_head, wcols.at[0], col_sem.at[0]).wait()
            levels(ehbuf, core)

        @pl.when(t == 11)
        def _():
            push(PLEVEL).wait()
            levels(hbuf, other)

        for i in range(steps):

            @pl.when(t == 10 + i)
            def _():
                small_copy(i).wait()
                value = sums[i] + sums_in[i]
                if i == steps - 1:
                    out_small[...] = value
                else:
                    sums[i + 1] = value
                    small_copy(i + 1).start()

        @pl.when(t == 8)
        def _():
            push(PE2).wait_send()
            fetch_x.start()

    for c in range(n):
        end_results(c)
    for c in range(n - LEAD, n):
        send1(c).wait_send()
    for c in range(n - 2, n):
        send2(c).wait_send()
    push(PEP).wait_send()


def run_backward(lefts, left_others, others, weights, tables):
    size = lax.axis_size("dp")
    width, tokens = lefts[0].shape
    hidden = lefts[1].shape[0]
    block = width // size
    cols = width // 2
    table = chunk_table(width, hidden)
    n = len(table)
    length = size // 4
    share = block // 2
    hdim = width // HEADS
    hbm = pl.BlockSpec(memory_space=pl.ANY)
    vmem = pl.BlockSpec(memory_space=pltpu.VMEM)
    y_flat = lefts[0].reshape(2, cols, tokens)
    lefts = [left.reshape(size, left.shape[0] // size, tokens) for left in lefts + left_others]
    shapes = [
        jax.ShapeDtypeStruct((block, cols), F32),
        jax.ShapeDtypeStruct((hidden // size // 2, width), F32),
        jax.ShapeDtypeStruct((share, hidden), F32),
        jax.ShapeDtypeStruct((share, width), F32),
        jax.ShapeDtypeStruct((share, 3 * width), F32),
        jax.ShapeDtypeStruct((8, width), F32),
        jax.ShapeDtypeStruct((tokens, width), F32),
        jax.ShapeDtypeStruct((2 * tokens, cols), F32),
    ]
    shapes += [
        jax.ShapeDtypeStruct((rows, tokens), BF16)
        for rows in (cols, hidden // 2, cols, 3 * cols, hidden // 2)
    ]
    dma = pltpu.SemaphoreType.DMA
    ring1, ring2, ring_line = 6, 4, length + 1
    main = cols - 128
    results = pl.pallas_call(
        functools.partial(backward_kernel, table, size),
        out_shape=shapes,
        in_specs=[hbm] * 22 + [vmem] * 5,
        out_specs=[hbm] * 5 + [vmem] + [hbm] * 7,
        scratch_shapes=[
            pltpu.VMEM((2, 2, size, block, tokens), BF16),
            pltpu.VMEM((2, 2, cols, tokens), BF16),
            pltpu.VMEM((2, tokens, cols), BF16),
            pltpu.VMEM((LEAD, 2, 2, length, block, main), BF16),
            pltpu.VMEM((ring1, 2, length, block, main), BF16),
            pltpu.VMEM((2, 2, length, block, main), BF16),
            pltpu.VMEM((ring2, length, block, main), BF16),
            pltpu.VMEM((ring_line, length, block, main), BF16),
            pltpu.VMEM((ring1, length - 1, block, main), BF16),
            pltpu.VMEM((ring1, length - 1, block, main), BF16),
            pltpu.VMEM((length + 4, length, 2, 2, block, cols - main), BF16),
            pltpu.VMEM((length + 3, length - 1, 2, 2, block, cols - main), BF16),
            pltpu.VMEM((length + 3, length - 1, 2, 2, block, cols - main), BF16),
            pltpu.VMEM((length + 3, 2, block, cols - main), BF16),
            pltpu.VMEM((length + 3, block, cols - main), BF16),
            pltpu.VMEM((n, block, cols), F32),
            pltpu.VMEM((5, 8, width), F32),
            pltpu.VMEM((5, 8, width), F32),
            pltpu.VMEM((width, tokens), F32),
            pltpu.VMEM((width, tokens), F32),
            pltpu.VMEM((width, tokens), F32),
            pltpu.VMEM((width, tokens), BF16),
            pltpu.VMEM((tokens, tokens), F32),
            pltpu.VMEM((width, 128), F32),
            pltpu.VMEM((2, cols, width), BF16),
            pltpu.VMEM((2, width, cols), BF16),
            pltpu.VMEM((2, cols, tokens), BF16),
            pltpu.VMEM((2, cols, tokens), BF16),
            pltpu.VMEM((3 * width, tokens), BF16),
            pltpu.VMEM((HEADS, hdim, tokens), BF16),
            pltpu.VMEM((2, TOGETHER, 3, hdim, tokens), BF16),
            pltpu.VMEM((2, tokens, 128), F32),
            dma((6,)),
            dma((6,)),
            dma((2, 2)),
            dma((2, 2)),
            dma((LEAD,)),
            dma((ring1,)),
            dma((2,)),
            dma((ring2,)),
            dma((ring_line, length - 1)),
            dma((ring1, length - 1)),
            dma((ring_line, length - 1)),
            dma((ring1, length - 1)),
            dma((length + 4, length - 1)),
            dma((length + 3, length - 1)),
            dma((length + 4, length - 1)),
            dma((length + 3, length - 1)),
            dma((length + 4,)),
            dma((length + 3,)),
            dma((length + 4,)),
            dma((length + 3,)),
            dma((n,)),
            dma((n,)),
            dma((n,)),
            dma((5,)),
            dma((5,)),
            dma((2,)),
            dma((2,)),
            dma((2,)),
            dma((2,)),
            dma((hidden // width,)),
            dma((2, TOGETHER, 3)),
            dma((5,)),
            dma((2,)),
        ],
        compiler_params=pltpu.CompilerParams(
            collective_id=0, has_side_effects=True, vmem_limit_bytes=62 << 20
        ),
        name="backward",
    )(*lefts, y_flat, *others, *weights, *tables)
    return results[:8]


def finish_kernel(copied, *refs):
    sources, sums = refs[:copied], refs[copied]
    targets = refs[copied + 1 : 2 * copied + 1]
    gain_attn, gain_mlp, gain_final, bias = refs[2 * copied + 1 : 2 * copied + 5]
    held = refs[2 * copied + 5 : 3 * copied + 5]
    fetch_sem, copy_sem = refs[3 * copied + 5 :]
    me = lax.axis_index("dp")
    core = lax.axis_index("head")
    width = sums.shape[1]
    share, half = gain_attn.shape[0], bias.shape[0]
    arrivals = [
        pltpu.make_async_copy(source, buffer, fetch_sem.at[i])
        for i, (source, buffer) in enumerate(zip(sources, held))
    ]
    copies = [
        pltpu.make_async_copy(buffer, target, copy_sem.at[i])
        for i, (buffer, target) in enumerate(zip(held, targets))
    ]
    for arrival in arrivals:
        arrival.start()
    start = (me * 2 + core) * share
    rolled = pltpu.roll(sums[...], lax.rem(width - start, width), 1)
    for i, target in enumerate((gain_attn, gain_mlp, gain_final)):
        target[...] = rolled[i, :share]
    bias[...] = sums[3, pl.ds(pl.multiple_of(core * half, 128), half)]
    for arrival, copy in zip(arrivals, copies):
        arrival.wait()
        copy.start()
    for copy in copies:
        copy.wait()


def run_finish(copied, sums):
    width = sums.shape[1]
    share = width // (2 * lax.axis_size("dp"))
    hbm = pl.BlockSpec(memory_space=pl.ANY)
    vmem = pl.BlockSpec(memory_space=pltpu.VMEM)
    dma = pltpu.SemaphoreType.DMA
    shapes = [jax.ShapeDtypeStruct(value.shape, F32) for value in copied]
    shapes += [jax.ShapeDtypeStruct((share,), F32)] * 3
    shapes += [jax.ShapeDtypeStruct((width // 2,), F32)]
    return pl.pallas_call(
        functools.partial(finish_kernel, len(copied)),
        out_shape=shapes,
        in_specs=[hbm] * len(copied) + [vmem],
        out_specs=[hbm] * len(copied) + [vmem] * 4,
        scratch_shapes=[pltpu.VMEM(value.shape, F32) for value in copied]
        + [dma((len(copied),)), dma((len(copied),))],
        compiler_params=pltpu.CompilerParams(vmem_limit_bytes=60 << 20),
        name="finish",
    )(*copied, sums)


def per_device(
    inputs,
    segment_ids,
    gain_attn,
    w_qkv,
    w_out,
    gain_mlp,
    w_up,
    w_down,
    gain_final,
    head_projection_weight,
    head_output_bias,
    cotangent,
):
    core = lax.axis_index("head")
    place = lax.axis_index("dp")
    size = lax.axis_size("dp")
    rows, sequence_span = segment_ids.shape
    count, width = inputs.shape
    hdim = width // HEADS
    scale = 1.0 / math.sqrt(hdim)
    share = width // (2 * size)
    fused = size == HEADS and lax.axis_size("head") == 2 and rows == 1

    if fused:
        half = width // 2
        turn = hdim // 2
        freq = np.float32(10000.0) ** (-np.arange(turn, dtype=np.float32) / np.float32(turn))
        angle = np.arange(sequence_span, dtype=np.float32)[None, :] * freq[:, None]
        cosine_t, sine_t = jnp.asarray(np.cos(angle)), jnp.asarray(np.sin(angle))
        (
            y_t,
            g_t,
            a2_t,
            o_t,
            a1_t,
            g_o,
            a2_o,
            o_o,
            a1_o,
            x3_t,
            gain_columns,
            x2_t,
            x_t,
            h_t,
            qkv_t,
            lse,
        ) = run_forward(
            inputs,
            w_qkv,
            w_out,
            w_up,
            w_down,
            segment_ids,
            [gain_attn, gain_mlp, gain_final],
            cosine_t,
            sine_t,
        )
        head, down, up, out, qkv, sums, entry, levels = run_backward(
            [y_t, g_t, a2_t, o_t, a1_t],
            [g_o, a2_o, o_o, a1_o],
            [
                cotangent,
                head_projection_weight,
                x3_t,
                x2_t,
                x_t,
                h_t,
                qkv_t,
                gain_columns,
            ],
            [w_down, w_up, w_out, w_qkv],
            [lse, segment_ids, head_output_bias, cosine_t, sine_t],
        )
        (
            predicted_levels,
            entry_sensitivity_matrix,
            grad_head,
            grad_down,
            grad_up,
            grad_out,
            grad_qkv,
            *gains,
            grad_bias,
        ) = run_finish([levels, entry, head, down, up, out, qkv], sums)
    else:
        other_rows = lax.dynamic_slice_in_dim(cotangent, (1 - core) * count, count, 0)
        own_rows = lax.dynamic_slice_in_dim(cotangent, core * count, count, 0)
        got = swap_cores(contract_cols(head_projection_weight, other_rows).astype(BF16))
        grad_final_t = contract_cols(head_projection_weight, own_rows) + got.astype(F32)
        bias_local = jnp.sum(cotangent, axis=0, dtype=F32)

        cosine, sine = rotary_tables(sequence_span, hdim)
        tokens = inputs.astype(jnp.float32)
        normed_one, inverse_one = rms_forward(tokens, gain_attn)
        act_one = normed_one.astype(jnp.bfloat16)
        projected = jnp.dot(act_one, w_qkv, preferred_element_type=jnp.float32).reshape(
            rows, sequence_span, 3, HEADS, hdim
        )
        query = rotate(projected[:, :, 0], cosine, sine).astype(jnp.bfloat16)
        key = rotate(projected[:, :, 1], cosine, sine).astype(jnp.bfloat16)
        value = projected[:, :, 2].astype(jnp.bfloat16)
        attended, log_total = lax.map(
            lambda items: attend_forward(items, scale), (query, key, value, segment_ids)
        )
        mixed = attended.reshape(rows * sequence_span, width)
        resid_two = tokens + jnp.dot(mixed, w_out, preferred_element_type=jnp.float32)
        normed_two, inverse_two = rms_forward(resid_two, gain_mlp)
        act_two = normed_two.astype(jnp.bfloat16)
        hidden_pre = jnp.dot(act_two, w_up, preferred_element_type=jnp.float32)
        hidden = jax.nn.silu(hidden_pre).astype(jnp.bfloat16)
        resid_three = resid_two + jnp.dot(hidden, w_down, preferred_element_type=jnp.float32)
        normed_three, inverse_three = rms_forward(resid_three, gain_final)
        final_hidden = normed_three.astype(jnp.bfloat16)
        other_hidden = swap_cores(final_hidden)
        collected_rows = jnp.concatenate(
            [
                jnp.where(core == 0, final_hidden, other_hidden),
                jnp.where(core == 0, other_hidden, final_hidden),
            ],
            axis=0,
        )
        predicted_levels = (
            jnp.dot(collected_rows, head_projection_weight, preferred_element_type=jnp.float32)
            + head_output_bias
        )
        grad_head = lax.psum_scatter(
            contract_rows(collected_rows, cotangent), "dp", scatter_dimension=0, tiled=True
        )
        grad_three, grad_gain_final = rms_backward(
            resid_three, inverse_three, gain_final, grad_final_t.T
        )
        grad_mlp_out = grad_three.astype(jnp.bfloat16)
        grad_hidden = contract_cols(grad_mlp_out, w_down)
        sigmoid = jax.nn.sigmoid(hidden_pre)
        grad_pre = (grad_hidden * sigmoid * (1.0 + hidden_pre * (1.0 - sigmoid))).astype(BF16)
        grad_norm_two, grad_gain_mlp = rms_backward(
            resid_two, inverse_two, gain_mlp, contract_cols(grad_pre, w_up)
        )
        grad_two = grad_three + grad_norm_two
        grad_branch = grad_two.astype(jnp.bfloat16)
        grad_mixed = (
            contract_cols(grad_branch, w_out)
            .astype(jnp.bfloat16)
            .reshape(rows, sequence_span, HEADS, hdim)
        )
        grad_query, grad_key, grad_value = lax.map(
            lambda items: attend_backward(items, scale),
            (query, key, value, segment_ids, log_total, grad_mixed),
        )
        grad_query = unrotate(grad_query, cosine, sine)
        grad_key = unrotate(grad_key, cosine, sine)
        grad_proj = (
            jnp.stack([grad_query, grad_key, grad_value], axis=2)
            .reshape(rows * sequence_span, 3 * width)
            .astype(jnp.bfloat16)
        )
        grad_norm_one, grad_gain_attn = rms_backward(
            tokens, inverse_one, gain_attn, contract_cols(grad_proj, w_qkv)
        )
        entry_sensitivity_matrix = grad_two + grad_norm_one
        grad_down = scatter_rows(hidden, grad_mlp_out)
        grad_up = scatter_rows(act_two, grad_pre)
        grad_out = scatter_rows(mixed, grad_branch)
        grad_qkv = scatter_rows(act_one, grad_proj)
        gains = sum_everywhere(jnp.stack([grad_gain_attn, grad_gain_mlp, grad_gain_final]), True)
        gains = lax.dynamic_slice_in_dim(gains, (place * 2 + core) * share, share, 1)
        grad_bias = sum_everywhere(bias_local, False)
    return (
        predicted_levels,
        entry_sensitivity_matrix,
        gains[0],
        grad_qkv,
        grad_out,
        gains[1],
        grad_up,
        grad_down,
        gains[2],
        grad_head,
        grad_bias,
    )


def solution(mesh):
    return jax.shard_map(
        per_device,
        mesh=mesh,
        in_specs=(
            P(("dp", "head"), None),
            P(("dp", "head"), None),
            P(),
            P(),
            P(),
            P(),
            P(),
            P(),
            P(),
            P(None, "head"),
            P("head"),
            P("dp", "head"),
        ),
        out_specs=(
            P("dp", "head"),
            P(("dp", "head"), None),
            P(("dp", "head")),
            P(("dp", "head"), None),
            P(("dp", "head"), None),
            P(("dp", "head")),
            P(("dp", "head"), None),
            P(("dp", "head"), None),
            P(("dp", "head")),
            P("dp", "head"),
            P("head"),
        ),
        check_vma=False,
    )
```

```python
import functools
import math

import jax
import jax.numpy as jnp
import numpy as np
from jax import lax
from jax.experimental import pallas as pl
from jax.experimental.pallas import tpu as pltpu
from jax.sharding import PartitionSpec as P

HEADS = 16
F32 = jnp.float32
BF16 = jnp.bfloat16

epsilon = 1e-06


def rms_forward(values, gain):
    inverse = lax.rsqrt(jnp.mean(values * values, axis=-1, keepdims=True) + epsilon)
    return (values * inverse * gain, inverse)


def rms_backward(values, inverse, gain, grad):
    normed = values * inverse
    scaled = grad * gain
    grad_gain = jnp.sum(grad * normed, axis=0)
    grad_values = inverse * (scaled - normed * jnp.mean(scaled * normed, axis=-1, keepdims=True))
    return (grad_values, grad_gain)


def rotary_tables(sequence_span, hdim):
    half = hdim // 2
    freq = 10000.0 ** (-jnp.arange(half, dtype=jnp.float32) / half)
    angle = jnp.arange(sequence_span, dtype=jnp.float32)[:, None] * freq[None, :]
    return (jnp.cos(angle)[:, None, :], jnp.sin(angle)[:, None, :])


def rotate(values, cosine, sine):
    half = values.shape[-1] // 2
    first = values[..., :half]
    second = values[..., half:]
    return jnp.concatenate(
        [first * cosine - second * sine, second * cosine + first * sine], axis=-1
    )


def unrotate(grads, cosine, sine):
    half = grads.shape[-1] // 2
    first = grads[..., :half]
    second = grads[..., half:]
    return jnp.concatenate(
        [first * cosine + second * sine, second * cosine - first * sine], axis=-1
    )


def allowed_mask(segs):
    place = jnp.arange(segs.shape[0])
    return (segs[:, None] == segs[None, :]) & (place[:, None] >= place[None, :])


def row_scores(query, key, segs, scale):
    scores = jnp.einsum("qhd,khd->hqk", query, key, preferred_element_type=jnp.float32) * scale
    allowed = allowed_mask(segs)[None]
    return (jnp.where(allowed, scores, -1e30), allowed)


def attend_forward(items, scale):
    query, key, value, segs = items
    scores, allowed = row_scores(query, key, segs, scale)
    peak = jnp.max(scores, axis=-1, keepdims=True)
    expo = jnp.exp(scores - peak)
    overall_number = jnp.sum(expo, axis=-1, keepdims=True)
    probs = (expo / overall_number).astype(jnp.bfloat16)
    attended = jnp.einsum("hqk,khd->qhd", probs, value, preferred_element_type=jnp.float32)
    return (attended.astype(jnp.bfloat16), peak + jnp.log(overall_number))


def attend_backward(items, scale):
    query, key, value, segs, log_total, grad_attended = items
    scores, allowed = row_scores(query, key, segs, scale)
    probs = jnp.where(allowed, jnp.exp(scores - log_total), 0.0)
    grad_value = jnp.einsum(
        "hqk,qhd->khd",
        probs.astype(jnp.bfloat16),
        grad_attended,
        preferred_element_type=jnp.float32,
    )
    grad_probs = jnp.einsum(
        "qhd,khd->hqk", grad_attended, value, preferred_element_type=jnp.float32
    )
    grad_scores = (
        probs * (grad_probs - jnp.sum(grad_probs * probs, axis=-1, keepdims=True))
    ).astype(jnp.bfloat16)
    grad_query = (
        jnp.einsum("hqk,khd->qhd", grad_scores, key, preferred_element_type=jnp.float32) * scale
    )
    grad_key = (
        jnp.einsum("hqk,qhd->khd", grad_scores, query, preferred_element_type=jnp.float32) * scale
    )
    return (grad_query, grad_key, grad_value)


def contract_rows(left, right):
    return lax.dot_general(
        left, right, (((0,), (0,)), ((), ())), preferred_element_type=jnp.float32
    )


def contract_cols(left, right):
    return lax.dot_general(
        left, right, (((1,), (1,)), ((), ())), preferred_element_type=jnp.float32
    )


def swap_cores(values):
    return lax.ppermute(values, "head", [(0, 1), (1, 0)])


def flip(values, bit):
    size = lax.axis_size("dp")
    return lax.ppermute(values, "dp", [(i, i ^ bit) for i in range(size)])


def scatter_rows(left, right):
    return lax.psum_scatter(
        contract_rows(left, right), ("dp", "head"), scatter_dimension=0, tiled=True
    )


def sum_everywhere(values, over_head):
    size = lax.axis_size("dp")
    if over_head:
        values = values + swap_cores(values)
    bit = 1
    while bit < size:
        values = values + flip(values, bit)
        bit *= 2
    return values


MESH = pl.DeviceIdType.MESH


def chunk_table(width, hidden):
    table = [(0, 0)]
    table += [(1, j) for j in range(hidden // width)]
    table += [(2, j) for j in range(hidden // width)]
    table += [(3, 0)]
    table += [(4, j) for j in range(3)]
    return table


def nt(left, right):
    return lax.dot_general(
        left, right, (((1,), (1,)), ((), ())), preferred_element_type=jnp.float32
    )


def nn(left, right):
    return jnp.dot(left, right, preferred_element_type=jnp.float32)


def tt(left, right):
    return lax.dot_general(
        left, right, (((0,), (0,)), ((), ())), preferred_element_type=jnp.float32
    )


def columns_of(rows, scratch):
    scratch[...] = jnp.zeros_like(scratch)
    for i, row in enumerate(rows):
        scratch[i : i + 1] = row[...].reshape(1, row.shape[0])
    return scratch[...].T


def mask_of(seg_row, bias):
    tokens = bias.shape[0]
    ids = seg_row[...].astype(F32)
    wide = jnp.broadcast_to(ids, (8, tokens)).T[:, :1]
    own = lax.broadcasted_iota(jnp.int32, (tokens, tokens), 0)
    asked = lax.broadcasted_iota(jnp.int32, (tokens, tokens), 1)
    bias[...] = jnp.where((wide == ids) & (own <= asked), 0.0, -1e30)


STRIP = 128
SLOTS = 4
REACH = 256
TOGETHER = 2


def query_blocks(tokens):
    for start in range(0, tokens, REACH):
        stop = min(start + REACH, tokens)
        yield max(0, start - REACH), stop, slice(start, stop)


def norm_backward(vref, eref, gains, index, emit):
    width, tokens = vref.shape

    def sums_of(k, carry):
        squares, products = carry
        rows = pl.ds(pl.multiple_of(k * STRIP, STRIP), STRIP)
        v = vref[rows].astype(F32)
        e = eref[rows]
        gain = gains[rows, index : index + 1]
        squares = squares + jnp.sum(v * v, axis=0, keepdims=True)
        products = products + jnp.sum(e * gain * v, axis=0, keepdims=True)
        return squares, products

    blank = jnp.zeros((1, tokens), F32)
    squares, products = lax.fori_loop(0, width // STRIP, sums_of, (blank, blank))
    inverse = lax.rsqrt(squares / width + epsilon)
    mean = products * inverse / width

    @pl.loop(0, width // STRIP)
    def _(k):
        rows = pl.ds(pl.multiple_of(k * STRIP, STRIP), STRIP)
        normed = vref[rows].astype(F32) * inverse
        e = eref[rows]
        gain = gains[rows, index : index + 1]
        gains[rows, 8 + index : 9 + index] = jnp.sum(e * normed, axis=1, keepdims=True)
        emit(k, rows, inverse * (e * gain - normed * mean))


def forward_kernel(
    x,
    w_qkv,
    w_out,
    w_up,
    w_down,
    seg_row,
    gain_attn,
    gain_mlp,
    gain_final,
    cosine,
    sine,
    y_t,
    g_t,
    a2_t,
    o_t,
    a1_t,
    g_o,
    a2_o,
    o_o,
    a1_o,
    x3_t,
    gain_columns,
    x2_t,
    x_t,
    h_t,
    qkv_t,
    lse,
    weights,
    xin,
    xt,
    act1,
    act2,
    final,
    mixed,
    qkv,
    res2,
    res3,
    hbuf,
    gbuf,
    bias,
    gains,
    gain_rows,
    weight_sem,
    in_sem,
    out_sem,
    h_sem,
    g_sem,
    push_send,
    push_recv,
    g_send,
    g_recv,
):
    width, tokens = res2.shape
    hidden = h_t.shape[0]
    pieces = hidden // width
    half = width // 2
    count = HEADS
    hdim = width // count
    scale = 1.0 / math.sqrt(hdim)
    first_tiles = [w_qkv.at[:, k * width : (k + 1) * width] for k in range(3)] + [w_out]

    def fetch(k):
        return pltpu.make_async_copy(first_tiles[k], weights.at[k], weight_sem.at[k])

    def fetch_up(k):
        slot = lax.rem(2 * k, SLOTS)
        source = w_up.at[:, pl.ds(pl.multiple_of(k * width, 128), width)]
        return pltpu.make_async_copy(source, weights.at[slot], weight_sem.at[slot])

    def fetch_down(k):
        slot = lax.rem(2 * k + 1, SLOTS)
        source = w_down.at[pl.ds(pl.multiple_of(k * width, 16), width)]
        return pltpu.make_async_copy(source, weights.at[slot], weight_sem.at[slot])

    me = lax.axis_index("dp")
    core = lax.axis_index("head")
    other = 1 - core

    def remote(src, dst, send, recv):
        return pltpu.make_async_remote_copy(
            src_ref=src,
            dst_ref=dst,
            send_sem=send,
            recv_sem=recv,
            device_id=(me, other),
            device_id_type=MESH,
        )

    fetch_x = pltpu.make_async_copy(x, xin, in_sem)
    fetch_x.start()
    for k in range(SLOTS):
        fetch(k).start()

    barrier = pltpu.get_barrier_semaphore()
    pl.semaphore_signal(barrier, inc=1, device_id=(me, other), device_id_type=MESH)
    gains[...] = jnp.zeros_like(gains)
    gains[:, :8] = columns_of((gain_attn, gain_mlp, gain_final), gain_rows)
    pl.semaphore_wait(barrier, 1)

    mask_of(seg_row, bias)
    fetch_x.wait()
    xt[...] = xin[...].T
    outs, pushes = [], []

    def put(source, target, also=None):
        copy = pltpu.make_async_copy(source, target, out_sem.at[len(outs)])
        outs.append(copy)
        copy.start()
        if also is not None:
            number = len(pushes)
            pushes.append(remote(source, also, push_send.at[number], push_recv.at[number]))
            pushes[-1].start()

    put(xt, x_t)
    put(gains, gain_columns)

    def squares_of(ref):
        def step(k, total):
            v = ref[pl.ds(pl.multiple_of(k * STRIP, STRIP), STRIP)].astype(F32)
            return total + jnp.sum(v * v, axis=0, keepdims=True)

        return lax.fori_loop(0, width // STRIP, step, jnp.zeros((1, tokens), F32))

    def normalize(ref, index, to):
        inverse = lax.rsqrt(squares_of(ref) / width + epsilon)

        @pl.loop(0, width // STRIP)
        def _(k):
            rows = pl.ds(pl.multiple_of(k * STRIP, STRIP), STRIP)
            to[rows] = (ref[rows].astype(F32) * inverse * gains[rows, index : index + 1]).astype(
                BF16
            )

    normalize(xt, 0, act1)
    put(act1, a1_t, a1_o)

    turn = hdim // 2
    for part in range(3):
        fetch(part).wait()

    @pl.loop(0, 2)
    def _(part):
        for lower in range(2):
            value = tt(weights[part, :, lower * half : (lower + 1) * half], act1[...])
            for head in range(count // 2):
                one = value[head * hdim : head * hdim + turn]
                two = value[head * hdim + turn : (head + 1) * hdim]
                turned = jnp.concatenate(
                    [one * cosine[...] - two * sine[...], two * cosine[...] + one * sine[...]],
                    axis=0,
                )
                base = pl.multiple_of(part * width + lower * half + head * hdim, 16)
                qkv[pl.ds(base, hdim)] = turned.astype(BF16)

    fetch_up(0).start()
    fetch_down(0).start()
    for lower in range(2):
        rows = slice(lower * half, (lower + 1) * half)
        value = tt(weights[2, :, rows], act1[...])
        qkv[2 * width + lower * half : 2 * width + (lower + 1) * half] = value.astype(BF16)
    fetch_up(1).start()
    put(qkv, qkv_t)

    def attend(head):
        def rows_of(part):
            return pl.ds(pl.multiple_of(part * width + head * hdim, 16), hdim)

        q_t = qkv[rows_of(0)]
        v_t = qkv[rows_of(2)]
        k = qkv[rows_of(1)].T
        for low, high, asked in query_blocks(tokens):
            scores = nn(k[low:high], q_t[:, asked]) * scale + bias[low:high, asked]
            peak = jnp.max(scores, axis=0, keepdims=True)
            expo = jnp.exp(scores - peak)
            amount = jnp.sum(expo, axis=0, keepdims=True)
            probs = (expo * (1.0 / amount)).astype(BF16)
            mixed[rows_of(0), asked] = nn(v_t[:, low:high], probs).astype(BF16)
            lse[head, :, asked] = peak + jnp.log(amount)

    @pl.loop(0, count // 4)
    def _(i):
        for u in range(4):
            attend(i * 4 + u)

    put(mixed, o_t, o_o)

    fetch(3).wait()
    for lower in range(2):
        rows = slice(lower * half, (lower + 1) * half)
        res2[rows] = xt[rows].astype(F32) + tt(weights[3, :, rows], mixed[...])
        res3[rows] = res2[rows]
    fetch_down(1).start()
    put(res2, x2_t)
    normalize(res2, 1, act2)
    put(act2, a2_t, a2_o)

    def piece(k):
        return pl.ds(pl.multiple_of(k * width, 16), width)

    def h_copy(k):
        slot = lax.rem(k, 2)
        return pltpu.make_async_copy(hbuf.at[slot], h_t.at[piece(k)], h_sem.at[slot])

    def g_copy(k):
        slot = lax.rem(k, 2)
        return pltpu.make_async_copy(gbuf.at[slot], g_t.at[piece(k)], g_sem.at[slot])

    def g_push(k):
        slot = lax.rem(k, 2)
        return remote(gbuf.at[slot], g_o.at[piece(k)], g_send.at[slot], g_recv.at[k])

    @pl.loop(0, pieces)
    def _(k):
        slot, up, down = lax.rem(k, 2), lax.rem(2 * k, SLOTS), lax.rem(2 * k + 1, SLOTS)
        fetch_up(k).wait()

        @pl.when(k >= 2)
        def _():
            h_copy(k - 2).wait()
            g_copy(k - 2).wait()
            g_push(k - 2).wait_send()

        for lower in range(2):
            rows = slice(lower * half, (lower + 1) * half)
            value = tt(weights[up, :, rows], act2[...])
            hbuf[slot, rows] = value.astype(BF16)
            gbuf[slot, rows] = (value * (0.5 * jnp.tanh(0.5 * value) + 0.5)).astype(BF16)

        @pl.when(k + 2 < pieces)
        def _():
            fetch_up(k + 2).start()

        h_copy(k).start()
        g_copy(k).start()
        g_push(k).start()
        fetch_down(k).wait()
        for lower in range(2):
            rows = slice(lower * half, (lower + 1) * half)
            res3[rows] += tt(weights[down, :, rows], gbuf[slot])

        @pl.when(k + 2 < pieces)
        def _():
            fetch_down(k + 2).start()

    put(res3, x3_t)
    normalize(res3, 2, final)
    put(final, y_t)
    for copy in outs:
        copy.wait()
    for k in range(max(0, pieces - 2), pieces):
        h_copy(k).wait()
        g_copy(k).wait()
        g_push(k).wait_send()
    for k in range(pieces):
        g_push(k).wait_recv()
    for push in pushes:
        push.wait()


def run_forward(x, w_qkv, w_out, w_up, w_down, segs, gains, cosine, sine):
    tokens, width = x.shape
    hidden = w_up.shape[1]
    hdim = width // HEADS
    hbm = pl.BlockSpec(memory_space=pl.ANY)
    vmem = pl.BlockSpec(memory_space=pltpu.VMEM)
    flat = (width, tokens)
    shapes = [
        jax.ShapeDtypeStruct(shape, dtype)
        for shape, dtype in (
            (flat, BF16),
            ((hidden, tokens), BF16),
            (flat, BF16),
            (flat, BF16),
            (flat, BF16),
            ((hidden, tokens), BF16),
            (flat, BF16),
            (flat, BF16),
            (flat, BF16),
            (flat, F32),
            ((width, 128), F32),
            (flat, F32),
            (flat, BF16),
            ((hidden, tokens), BF16),
            ((3 * width, tokens), BF16),
            ((HEADS, 1, tokens), F32),
        )
    ]
    dma = pltpu.SemaphoreType.DMA
    return pl.pallas_call(
        forward_kernel,
        out_shape=shapes,
        in_specs=[hbm] * 5 + [vmem] * 6,
        out_specs=[hbm] * 15 + [vmem],
        scratch_shapes=[
            pltpu.VMEM((SLOTS, width, width), BF16),
            pltpu.VMEM((tokens, width), BF16),
            pltpu.VMEM(flat, BF16),
            pltpu.VMEM(flat, BF16),
            pltpu.VMEM(flat, BF16),
            pltpu.VMEM(flat, BF16),
            pltpu.VMEM(flat, BF16),
            pltpu.VMEM((3 * width, tokens), BF16),
            pltpu.VMEM(flat, F32),
            pltpu.VMEM(flat, F32),
            pltpu.VMEM((2,) + flat, BF16),
            pltpu.VMEM((2,) + flat, BF16),
            pltpu.VMEM((tokens, tokens), F32),
            pltpu.VMEM((width, 128), F32),
            pltpu.VMEM((8, width), F32),
            dma((SLOTS,)),
            dma(()),
            dma((9,)),
            dma((2,)),
            dma((2,)),
            dma((3,)),
            dma((3,)),
            dma((2,)),
            dma((hidden // width,)),
        ],
        compiler_params=pltpu.CompilerParams(
            collective_id=1, has_side_effects=True, vmem_limit_bytes=60 << 20
        ),
        name="forward",
    )(x, w_qkv, w_out, w_up, w_down, segs, *gains, cosine, sine)


LEAD = 3


def backward_kernel(
    table,
    size,
    y_t,
    g_t,
    a2_t,
    o_t,
    a1_t,
    g_o,
    a2_o,
    o_o,
    a1_o,
    y_flat,
    cot,
    w_head,
    x3_t,
    x2_t,
    x_t,
    h_t,
    qkv_t,
    gain_columns,
    w_down,
    w_up,
    w_out,
    w_qkv,
    lse,
    seg_row,
    head_bias,
    cosine,
    sine,
    out_head,
    out_down,
    out_up,
    out_out,
    out_qkv,
    out_small,
    out_entry,
    out_levels,
    e3_o,
    eh_o,
    e2_o,
    ep_o,
    eh_mine,
    lbuf,
    rbuf,
    cbuf,
    grad,
    recv1,
    pair,
    recv2,
    line,
    recv_up,
    recv_down,
    side,
    side_up,
    side_down,
    side1,
    side2,
    total,
    sums,
    sums_in,
    dx,
    work,
    acc,
    ebuf,
    bias,
    gains,
    wrows,
    wcols,
    hbuf,
    ehbuf,
    ep,
    eo,
    heads,
    obuf,
    push_send,
    push_recv,
    left_sem,
    right_sem,
    send1_sem,
    recv1_sem,
    send2_sem,
    recv2_sem,
    up_send,
    up_recv,
    down_send,
    down_recv,
    side_up_send,
    side_up_recv,
    side_down_send,
    side_down_recv,
    side1_send,
    side1_recv,
    side2_send,
    side2_recv,
    local_sem,
    swap_send,
    swap_recv,
    small_send,
    small_recv,
    row_sem,
    col_sem,
    h_sem,
    eh_out_sem,
    eh_in_sem,
    head_sem,
    fetch_sem,
    entry_sem,
):
    n = len(table)
    length = size // 4
    me = lax.axis_index("dp")
    core = lax.axis_index("head")
    other = 1 - core
    xi = lax.rem(me, 2)
    yi = lax.rem(me // 2, 2)
    zi = me // 4
    width, tokens = dx.shape
    hidden = h_t.shape[0]
    cols = width // 2
    block = width // size
    count, hdim = eo.shape[:2]
    scale = 1.0 / math.sqrt(hdim)
    flip_x = me + 1 - 2 * xi
    flip_y = me + 2 * (1 - 2 * yi)
    first_bit = jnp.where(core == 0, xi, yi)
    second_bit = jnp.where(core == 0, yi, xi)
    first_peer = jnp.where(core == 0, flip_x, flip_y)
    second_peer = jnp.where(core == 0, flip_y, flip_x)
    far = lax.rem(me + size // 2, size)
    near = me + 4 * (1 - 2 * lax.rem(zi, 2))
    rings = recv1.shape[0]
    ring2 = recv2.shape[0]
    ring_line = line.shape[0]
    ring_side, ring_in = side.shape[0], side1.shape[0]
    main = grad.shape[-1]

    fetch_head_weight = pltpu.make_async_copy(w_head, wcols.at[0], fetch_sem.at[0])
    fetch_x3 = pltpu.make_async_copy(x3_t, work, fetch_sem.at[1])
    fetch_gains = pltpu.make_async_copy(gain_columns, gains, fetch_sem.at[4])
    fetch_x2 = pltpu.make_async_copy(x2_t, work, fetch_sem.at[1])
    fetch_x = pltpu.make_async_copy(x_t, ebuf, fetch_sem.at[0])

    def local_c(half, which):
        start = pl.multiple_of(which * tokens, 16)
        return pltpu.make_async_copy(
            cot.at[pl.ds(start, tokens)], cbuf.at[half], fetch_sem.at[2 + half]
        )

    lefts = (y_t, g_t, a2_t, o_t, a1_t)
    left_others = (None, g_o, a2_o, o_o, a1_o)
    pieces = hidden // width

    def start_left(c):
        i, j = table[c]
        lower = pl.ds(j * block, block) if i == 1 else slice(None)
        for half, source in ((0, lefts[i]), (1, left_others[i])):
            pltpu.make_async_copy(
                source.at[:, lower, :], lbuf.at[c % 2, half], left_sem.at[c % 2, half]
            ).start()

    fetch_y = pltpu.make_async_copy(y_t, lbuf.at[0, 0], left_sem.at[0, 0])
    fetch_y.start()
    local_c(1, other).start()
    fetch_head_weight.start()
    local_c(0, core).start()
    fetch_x3.start()
    fetch_gains.start()
    start_left(1)

    barrier = pltpu.get_barrier_semaphore()
    for index, which in ((me, other), (flip_x, core), (flip_y, core), (far, core)):
        pl.semaphore_signal(barrier, inc=1, device_id=(index, which), device_id_type=MESH)

    @pl.when(zi > 0)
    def _():
        pl.semaphore_signal(barrier, inc=1, device_id=(me - 4, core), device_id_type=MESH)

    @pl.when(zi < length - 1)
    def _():
        pl.semaphore_signal(barrier, inc=1, device_id=(me + 4, core), device_id_type=MESH)

    inner = jnp.where(zi > 0, 1, 0) + jnp.where(zi < length - 1, 1, 0)
    pl.semaphore_wait(barrier, 4 + inner)

    def remote(src, dst, send, recv, index, which):
        return pltpu.make_async_remote_copy(
            src_ref=src,
            dst_ref=dst,
            send_sem=send,
            recv_sem=recv,
            device_id=(index, which),
            device_id_type=MESH,
        )

    PE3, PE2, PEP, PY, PDY, PLEVEL = range(6)

    def push(k):
        if k == PY:
            src, dst = lbuf.at[0, 0], lbuf.at[0, 1]
        elif k in (PDY, PLEVEL):
            src, dst = ehbuf, hbuf
        elif k == PEP:
            wide = 3 * cols
            src, dst = ep.at[pl.ds(pl.multiple_of(other * wide, 16), wide)], ep_o
        else:
            src, dst = ebuf, (e3_o, e2_o)[k]
            src = src.at[pl.ds(pl.multiple_of(other * cols, 16), cols)]
        return remote(src, dst, push_send.at[k], push_recv.at[k], me, other)

    fetch_y.wait()
    push(PY).start()
    fetch_head_weight.wait()
    local_c(1, other).wait()
    for i in range(2):
        ehbuf[i] = nt(wcols[0, i * cols : (i + 1) * cols], cbuf[1]).astype(BF16)
    push(PDY).start()
    local_c(0, core).wait()

    def start_right(c):
        i, j = table[c]
        slot = c % 2
        mine = pl.ds(pl.multiple_of(core * cols, 16), cols)
        rows = pl.ds(j * cols, cols)
        if i == 1:
            own, its = ebuf.at[mine], e3_o
            if j == 0:
                push(PE3).wait_recv()
        elif i == 2:
            own, its = eh_mine.at[rows], eh_o.at[rows]
            eh_push(j).wait_recv()
        elif i == 3:
            own, its = ebuf.at[mine], e2_o
            push(PE2).wait_recv()
        else:
            start = pl.multiple_of(core * 3 * cols + j * cols, 16)
            own, its = ep.at[pl.ds(start, cols)], ep_o.at[rows]
            if j == 0:
                push(PEP).wait_recv()
        pltpu.make_async_copy(own, rbuf.at[slot, 0], right_sem.at[slot, 0]).start()
        pltpu.make_async_copy(its, rbuf.at[slot, 1], right_sem.at[slot, 1]).start()

    def eh_push(piece):
        return remote(
            ehbuf.at[0],
            eh_o.at[pl.ds(pl.multiple_of(piece * cols, 16), cols)],
            eh_out_sem.at[0],
            eh_in_sem.at[piece],
            me,
            other,
        )

    def eh_keep(piece):
        return pltpu.make_async_copy(
            ehbuf.at[1],
            eh_mine.at[pl.ds(pl.multiple_of(piece * cols, 16), cols)],
            eh_out_sem.at[1],
        )

    def wait_left(slot):
        for half in range(2):
            pltpu.make_async_copy(
                lbuf.at[slot, half], lbuf.at[slot, half], left_sem.at[slot, half]
            ).wait()

    def wait_right(slot):
        for half in range(2):
            pltpu.make_async_copy(
                rbuf.at[slot, half], rbuf.at[slot, half], right_sem.at[slot, half]
            ).wait()

    def form(c, right, multiply):
        slot, ring, to = lax.rem(c, 2), lax.rem(c, LEAD), lax.rem(c, ring_side)

        for z in range(length):
            value = None
            for half in range(2):
                left = lbuf[slot, half, 4 * z : 4 * z + 4].reshape(4 * block, tokens)
                part = multiply(left, right[half])
                value = part if value is None else value + part
            value = value.astype(BF16)
            for q in range(4):
                x, y = q % 2, q // 2
                one = jnp.where(core == 0, x, y)
                two = jnp.where(core == 0, y, x)
                part = value[q * block : (q + 1) * block]
                grad[ring, one, two, z] = part[:, :main]
                side[to, z, one, two] = part[:, main:]
        send1(c).start()
        start_side(c, 1)

    def send1(c):
        ring, spot = lax.rem(c, LEAD), lax.rem(c, rings)
        return remote(
            grad.at[ring, 1 - first_bit],
            recv1.at[spot],
            send1_sem.at[ring],
            recv1_sem.at[spot],
            first_peer,
            core,
        )

    def send2(c):
        ring, spot = lax.rem(c, 2), lax.rem(c, ring2)
        return remote(
            pair.at[ring, 1 - second_bit],
            recv2.at[spot],
            send2_sem.at[ring],
            recv2_sem.at[spot],
            second_peer,
            core,
        )

    def send_up(c, step):
        ring, spot = lax.rem(c, ring_line), lax.rem(c, rings)
        return remote(
            line.at[ring, jnp.minimum(zi + (length - step), length - 1)],
            recv_up.at[spot, step - 1],
            up_send.at[ring, step - 1],
            up_recv.at[spot, step - 1],
            jnp.minimum(me + 4, size - 1),
            core,
        )

    def send_down(c, step):
        ring, spot = lax.rem(c, ring_line), lax.rem(c, rings)
        return remote(
            line.at[ring, jnp.maximum(zi - (length - step), 0)],
            recv_down.at[spot, step - 1],
            down_send.at[ring, step - 1],
            down_recv.at[spot, step - 1],
            jnp.maximum(me - 4, 0),
            core,
        )

    def side_send_up(c, step):
        ring, spot = lax.rem(c, ring_side), lax.rem(c, ring_in)
        return remote(
            side.at[ring, jnp.minimum(zi + (length - step), length - 1)],
            side_up.at[spot, step - 1],
            side_up_send.at[ring, step - 1],
            side_up_recv.at[spot, step - 1],
            jnp.minimum(me + 4, size - 1),
            core,
        )

    def side_send_down(c, step):
        ring, spot = lax.rem(c, ring_side), lax.rem(c, ring_in)
        return remote(
            side.at[ring, jnp.maximum(zi - (length - step), 0)],
            side_down.at[spot, step - 1],
            side_down_send.at[ring, step - 1],
            side_down_recv.at[spot, step - 1],
            jnp.maximum(me - 4, 0),
            core,
        )

    def side_send1(c):
        ring, spot = lax.rem(c, ring_side), lax.rem(c, ring_in)
        return remote(
            side.at[ring, zi, 1 - first_bit],
            side1.at[spot],
            side1_send.at[ring],
            side1_recv.at[spot],
            first_peer,
            core,
        )

    def side_send2(c):
        ring, spot = lax.rem(c, ring_side), lax.rem(c, ring_in)
        return remote(
            side.at[ring, zi, first_bit, 1 - second_bit],
            side2.at[spot],
            side2_send.at[ring],
            side2_recv.at[spot],
            second_peer,
            core,
        )

    def start_side(c, step):
        @pl.when(zi < step)
        def _():
            side_send_up(c, step).start()

        @pl.when(zi >= length - step)
        def _():
            side_send_down(c, step).start()

    def exchange_side(t):
        for step in range(1, length):

            @pl.when((t >= step - 1) & (t <= n + step - 2))
            def _():
                c = t - step + 1
                ring, at = lax.rem(c, ring_side), lax.rem(c, ring_in)
                up_in = (zi >= 1) & (zi <= step)
                down_in = (zi <= length - 2) & (zi >= length - 1 - step)

                @pl.when(up_in)
                def _():
                    side_send_up(c, step).wait_recv()
                    spot = jnp.minimum(zi + (length - 1 - step), length - 1)
                    side[ring, spot] = side[ring, spot] + side_up[at, step - 1]

                @pl.when(down_in)
                def _():
                    side_send_down(c, step).wait_recv()
                    spot = jnp.maximum(zi - (length - 1 - step), 0)
                    side[ring, spot] = side[ring, spot] + side_down[at, step - 1]

                if step < length - 1:
                    start_side(c, step + 1)
                else:
                    side_send1(c).start()

        @pl.when((t >= length - 1) & (t <= n + length - 2))
        def _():
            c = t - length + 1
            ring, at = lax.rem(c, ring_side), lax.rem(c, ring_in)
            side_send1(c).wait_recv()
            side[ring, zi, first_bit] = side[ring, zi, first_bit] + side1[at]
            side_send2(c).start()

        @pl.when((t >= length) & (t <= n + length - 1))
        def _():
            c = t - length
            ring, at = lax.rem(c, ring_side), lax.rem(c, ring_in)
            side_send2(c).wait_recv()
            total[c, :, main:] = side[ring, zi, first_bit, second_bit].astype(F32) + side2[
                at
            ].astype(F32)
            for back in range(1, length):

                @pl.when(zi < back)
                def _():
                    side_send_up(c, back).wait_send()

                @pl.when(zi >= length - back)
                def _():
                    side_send_down(c, back).wait_send()

            side_send1(c).wait_send()
            side_send2(c).wait_send()

    def start_line(c, step):
        @pl.when(zi < step)
        def _():
            send_up(c, step).start()

        @pl.when(zi >= length - step)
        def _():
            send_down(c, step).start()

    def wait_line_sent(c, step):
        @pl.when(zi < step)
        def _():
            send_up(c, step).wait_send()

        @pl.when(zi >= length - step)
        def _():
            send_down(c, step).wait_send()

    def results(c):
        i, j = table[c]
        if i == 0:
            return [pltpu.make_async_copy(total.at[c], out_head, local_sem.at[c])]
        if i == 1:
            target = out_down.at[
                pl.ds((j % 2) * block, block), pl.ds(pl.multiple_of(core * cols, 128), cols)
            ]
            return [
                pltpu.make_async_copy(total.at[c], target, local_sem.at[c]),
                remote(total.at[c], target, swap_send.at[c], swap_recv.at[c], me, other),
            ]
        target = (None, None, out_up, out_out, out_qkv)[i]
        wide = target.shape[1] // 2
        place = target.at[:, pl.ds(pl.multiple_of(core * wide + j * cols, 128), cols)]
        half = block // 2
        mine = pl.ds(pl.multiple_of(core * half, 8), half)
        its = pl.ds(pl.multiple_of(other * half, 8), half)
        return [
            pltpu.make_async_copy(total.at[c, mine], place, local_sem.at[c]),
            remote(total.at[c, its], place, swap_send.at[c], swap_recv.at[c], me, other),
        ]

    def start_results(c):
        i, j = table[c]
        copies = results(c)
        if i == 1:
            owner = j // (pieces // 2)
            pl.when(core == owner)(copies[0].start)
            pl.when(core != owner)(copies[1].start)
        else:
            for copy in copies:
                copy.start()

    def end_results(c):
        i, j = table[c]
        copies = results(c)
        if i == 1:
            owner = j // (pieces // 2)
            pl.when(core == owner)(copies[0].wait)
            pl.when(core == owner)(copies[1].wait_recv)
            pl.when(core != owner)(copies[1].wait_send)
        else:
            for copy in copies:
                copy.wait()

    def exchange(t):
        exchange_side(t)

        @pl.when(t < n)
        def _():
            c = t
            send1(c).wait_recv()
            ring, spot, to = lax.rem(c, LEAD), lax.rem(c, rings), lax.rem(c, 2)

            @pl.when(c >= 2)
            def _():
                send2(c - 2).wait_send()

            for two in range(2):

                @pl.loop(0, length)
                def _(z):
                    pair[to, two, z] = grad[ring, first_bit, two, z] + recv1[spot, two, z]

            send2(c).start()

        @pl.when((t >= 1) & (t <= n))
        def _():
            c = t - 1
            send2(c).wait_recv()
            ring, spot, to = lax.rem(c, 2), lax.rem(c, ring2), lax.rem(c, ring_line)

            @pl.loop(0, length)
            def _(z):
                line[to, z] = pair[ring, second_bit, z] + recv2[spot, z]

            start_line(c, 1)


        for step in range(1, length):

            @pl.when((t >= 1 + step) & (t <= n + step))
            def _():
                c = t - 1 - step
                ring, at = lax.rem(c, ring_line), lax.rem(c, rings)
                last = step == length - 1
                up_in = (zi >= 1) & (zi <= step)
                down_in = (zi <= length - 2) & (zi >= length - 1 - step)

                @pl.when(up_in)
                def _():
                    send_up(c, step).wait_recv()
                    spot = jnp.minimum(zi + (length - 1 - step), length - 1)
                    if not last:
                        line[ring, spot] = line[ring, spot] + recv_up[at, step - 1]

                @pl.when(down_in)
                def _():
                    send_down(c, step).wait_recv()
                    spot = jnp.maximum(zi - (length - 1 - step), 0)
                    if not last:
                        line[ring, spot] = line[ring, spot] + recv_down[at, step - 1]

                if not last:
                    start_line(c, step + 1)
                else:
                    total[c, :, :main] = line[ring, zi].astype(F32)

                    @pl.when(up_in)
                    def _():
                        total[c, :, :main] += recv_up[at, step - 1].astype(F32)

                    @pl.when(down_in)
                    def _():
                        total[c, :, :main] += recv_down[at, step - 1].astype(F32)

                    for back in range(1, length):
                        wait_line_sent(c, back)

                    for d in range(n):

                        @pl.when(c == d)
                        def _():
                            start_results(d)

    def row_tile(k, slot, source):
        return pltpu.make_async_copy(
            source.at[pl.ds(pl.multiple_of(k * cols, 16), cols)], wrows.at[slot], row_sem.at[slot]
        )

    def col_tile(k, slot, source):
        return pltpu.make_async_copy(
            source.at[:, pl.ds(pl.multiple_of(k * cols, 128), cols)],
            wcols.at[slot],
            col_sem.at[slot],
        )

    def h_tile(k, slot):
        return pltpu.make_async_copy(
            h_t.at[pl.ds(pl.multiple_of(k * cols, 16), cols)], hbuf.at[slot], h_sem.at[slot]
        )

    def mlp_tiles(k):
        return jnp.where(lax.rem(k, 2) == 0, other, core) * pieces + k // 2

    def fetch_mlp(k):
        slot = lax.rem(k, 2)
        tile = mlp_tiles(k)
        row_tile(tile, slot, w_down).start()
        col_tile(tile, slot, w_up).start()
        h_tile(tile, slot).start()

    push(PY).wait_recv()
    form(0, [cbuf[0], cbuf[1]], nn)
    push(PY).wait_send()
    start_left(2)

    def emit_final(k, rows, value):
        dx[rows] = value
        ebuf[rows] = value.astype(BF16)

    push(PDY).wait_recv()
    for i in range(2):
        rows = slice(i * cols, (i + 1) * cols)
        dx[rows] = nt(wcols[0, rows], cbuf[0]) + hbuf[i].astype(F32)
    fetch_mlp(0)
    fetch_mlp(1)
    fetch_x3.wait()
    fetch_gains.wait()
    norm_backward(work, dx, gains, 2, emit_final)
    push(PE3).start()
    fetch_x2.start()
    push(PDY).wait_send()
    for c in range(1, LEAD):
        start_right(c)
        wait_left(c % 2)
        wait_right(c % 2)
        form(c, [rbuf[c % 2, 0], rbuf[c % 2, 1]], nt)
        start_left(c + 2)
    def mlp_step(k):
        slot = lax.rem(k, 2)
        tile = mlp_tiles(k)
        row_tile(tile, slot, w_down).wait()
        h_tile(tile, slot).wait()

        @pl.when((k >= 2) & (slot == 0))
        def _():
            eh_push(0).wait_send()

        @pl.when((k >= 2) & (slot == 1))
        def _():
            eh_keep(0).wait()

        part = cols // 2
        for i in range(2):
            rows = slice(i * part, (i + 1) * part)
            value = nn(wrows[slot, rows], ebuf[...])
            pre = hbuf[slot, rows].astype(F32)
            sig = 0.5 * jnp.tanh(0.5 * pre) + 0.5
            ehbuf[slot, rows] = (value * sig * (1.0 + pre * (1.0 - sig))).astype(BF16)

        @pl.when(slot == 0)
        def _():
            eh_push(k // 2).start()

        @pl.when(slot == 1)
        def _():
            eh_keep(k // 2).start()

        col_tile(tile, slot, w_up).wait()
        accumulate(wcols.at[slot], ehbuf.at[slot], k == 0)

        @pl.when(k + 2 < 2 * pieces)
        def _():
            fetch_mlp(k + 2)

    def accumulate(left, right, first):
        @pl.when(first)
        def _():
            acc[...] = jnp.zeros_like(acc)

        part = width // 4
        for i in range(4):
            rows = slice(i * part, (i + 1) * part)
            acc[rows] += nn(left[rows], right[...])


    def emit_mlp(k, rows, value):
        value = dx[rows] + value
        dx[rows] = value
        ebuf[rows] = value.astype(BF16)

    def middle():
        eh_push(0).wait_send()
        eh_keep(0).wait()
        row_tile(0, 0, w_out).start()
        row_tile(1, 1, w_out).start()
        push(PE3).wait_send()
        fetch_x2.wait()
        norm_backward(work, acc, gains, 1, emit_mlp)
        push(PE2).start()

        @pl.loop(0, 2)
        def _(k):
            row_tile(k, k, w_out).wait()

            group = cols // hdim
            value = nn(wrows[k], ebuf[...]).astype(BF16)
            eo[pl.ds(k * group, group)] = value.reshape(group, hdim, tokens)

        mask_of(seg_row, bias)

    def level_copy(k, which, slot):
        return pltpu.make_async_copy(
            obuf.at[slot],
            out_levels.at[
                pl.ds(pl.multiple_of(which * tokens, 8), tokens), k * STRIP : (k + 1) * STRIP
            ],
            entry_sem.at[slot],
        )

    def levels(source, which):
        last = cols // STRIP
        for k in range(last):
            if k >= 2:
                level_copy(k - 2, which, k % 2).wait()
            part = slice(k * STRIP, (k + 1) * STRIP)
            obuf[k % 2] = (
                tt(source[0], wcols[0, :cols, part])
                + tt(source[1], wcols[0, cols:, part])
                + head_bias[...].reshape(1, cols)[:, part]
            )
            level_copy(k, which, k % 2).start()
        for k in range(last - 2, last):
            level_copy(k, which, k % 2).wait()

    pairs = count // TOGETHER
    per_turn = -(-pairs // 3)

    def head_copy(head, slot, u, part):
        return pltpu.make_async_copy(
            qkv_t.at[pl.ds(pl.multiple_of(part * width + head * hdim, 16), hdim)],
            heads.at[slot, u, part],
            head_sem.at[slot, u, part],
        )

    def fetch_heads(i):
        for u in range(TOGETHER):
            for part in range(3):
                head_copy(i * TOGETHER + u, lax.rem(i, 2), u, part).start()

    def attend_head(head, slot, u):
        q_t, k_t, v_t = (heads[slot, u, part] for part in range(3))
        e_t = eo[head]
        q, k, v, e = q_t.T, k_t.T, v_t.T, e_t.T
        blocks = list(query_blocks(tokens))
        weight = lse[head]
        ek, ev, eqs = [[] for _ in blocks], [[] for _ in blocks], []
        for low, high, asked in blocks:
            scores = nn(k[low:high], q_t[:, asked]) * scale + bias[low:high, asked]
            p = jnp.exp(scores - weight[:, asked])
            ep_t = nn(v[low:high], e_t[:, asked])
            share = jnp.sum(p * ep_t, axis=0, keepdims=True)
            es = (p * (ep_t - share)).astype(BF16)
            eqs.append(nn(k_t[:, low:high], es))
            one, two = nn(es, q[asked]), nn(p.astype(BF16), e[asked])
            for number, (_, _, own) in enumerate(blocks):
                if low <= own.start < high:
                    ek[number].append(one[own.start - low : own.stop - low])
                    ev[number].append(two[own.start - low : own.stop - low])
        ek_t = jnp.concatenate([sum(terms[1:], terms[0]) for terms in ek], axis=0).T
        ev_t = jnp.concatenate([sum(terms[1:], terms[0]) for terms in ev], axis=0).T
        half = hdim // 2
        for part, value in ((0, jnp.concatenate(eqs, axis=1)), (1, ek_t)):
            one, two = value[:half] * scale, value[half:] * scale
            turned = jnp.concatenate(
                [one * cosine[...] + two * sine[...], two * cosine[...] - one * sine[...]],
                axis=0,
            )
            to = pl.ds(pl.multiple_of(part * width + head * hdim, 16), hdim)
            ep[to] = turned.astype(BF16)
        to = pl.ds(pl.multiple_of(2 * width + head * hdim, 16), hdim)
        ep[to] = ev_t.astype(BF16)

    def attend(turn):
        @pl.when(turn == 0)
        def _():
            fetch_heads(0)

        @pl.loop(turn * per_turn, jnp.minimum((turn + 1) * per_turn, pairs))
        def _(i):
            slot = lax.rem(i, 2)
            for u in range(TOGETHER):
                for part in range(3):
                    head_copy(i * TOGETHER + u, slot, u, part).wait()

            @pl.when((i + 1) * TOGETHER < count)
            def _():
                fetch_heads(i + 1)

            for u in range(TOGETHER):
                attend_head(i * TOGETHER + u, slot, u)

        @pl.when(turn == 2)
        def _():
            push(PEP).start()

    def fetch_qkv(k):
        col_tile(k, lax.rem(k, 2), w_qkv).start()

    def qkv_step(k):
        slot = lax.rem(k, 2)
        col_tile(k, slot, w_qkv).wait()
        rows = pl.ds(pl.multiple_of(k * cols, 16), cols)
        accumulate(wcols.at[slot], ep.at[rows], k == 0)

        @pl.when(k + 2 < 6)
        def _():
            fetch_qkv(k + 2)

    def entry_copy(k, slot):
        return pltpu.make_async_copy(
            obuf.at[slot],
            out_entry.at[:, pl.ds(pl.multiple_of(k * STRIP, STRIP), STRIP)],
            entry_sem.at[slot],
        )

    def emit_entry(k, rows, value):
        slot = lax.rem(k, 2)

        @pl.when(k >= 2)
        def _():
            entry_copy(k, slot).wait()

        obuf[slot] = (dx[rows] + value).T
        entry_copy(k, slot).start()

    peers = ((me, other), (flip_x, core), (flip_y, core), (near, core), (far, core))
    steps = len(peers)

    def small_copy(i):
        return remote(
            sums.at[i], sums_in.at[i], small_send.at[i], small_recv.at[i], peers[i][0], peers[i][1]
        )

    def last():
        fetch_x.wait()
        norm_backward(ebuf, acc, gains, 0, emit_entry)
        for slot in range(2):
            entry_copy(0, slot).wait()
        sums[0] = sums[0] + gains[...].T[8:16]
        small_copy(0).start()

    @pl.loop(0, n + length)
    def _(t):
        for c in range(LEAD, n):
            if table[c] != (4, 0):

                @pl.when(t == c - LEAD)
                def _():
                    start_right(c)

        exchange(t)

        for c in range(LEAD, n):
            if table[c] == (4, 0):

                @pl.when(t == c - LEAD)
                def _():
                    start_right(c)

        @pl.when(t + LEAD < n)
        def _():
            c = t + LEAD
            slot = lax.rem(c, 2)
            wait_left(slot)
            wait_right(slot)
            send1(t).wait_send()
            form(c, [rbuf[slot, 0], rbuf[slot, 1]], nt)
            for d in range(LEAD + 2, n):

                @pl.when(c == d - 2)
                def _():
                    start_left(d)

        @pl.when(t < 3)
        def _():
            @pl.loop(t * 3, jnp.minimum(t * 3 + 3, 2 * pieces))
            def _(k):
                mlp_step(k)

        @pl.when(t == 3)
        def _():
            middle()

        @pl.when((t >= 4) & (t < 7))
        def _():
            attend(t - 4)

        @pl.when(t == 6)
        def _():
            fetch_qkv(0)
            fetch_qkv(1)
            sums[0] = jnp.zeros_like(sums[0])
            for i in range(2):
                share = jnp.sum(cbuf[i].astype(F32), axis=0, keepdims=True)
                at = pl.ds(pl.multiple_of(core * cols, 128), cols)
                sums[0, 3:4, at] = sums[0, 3:4, at] + share

        @pl.when((t == 7) | (t == 8))
        def _():
            @pl.loop(0, 3)
            def _(i):
                qkv_step((t - 7) * 3 + i)

        @pl.when(t == 9)
        def _():
            pltpu.make_async_copy(w_head, wcols.at[0], col_sem.at[0]).start()
            fetch_level = pltpu.make_async_copy(y_flat, ehbuf, h_sem.at[0])
            fetch_level.start()
            last()
            fetch_level.wait()
            push(PLEVEL).start()

        @pl.when(t == 10)
        def _():
            pltpu.make_async_copy(w_head, wcols.at[0], col_sem.at[0]).wait()
            levels(ehbuf, core)

        @pl.when(t == 11)
        def _():
            push(PLEVEL).wait()
            levels(hbuf, other)

        for i in range(steps):

            @pl.when(t == 10 + i)
            def _():
                small_copy(i).wait()
                value = sums[i] + sums_in[i]
                if i == steps - 1:
                    out_small[...] = value
                else:
                    sums[i + 1] = value
                    small_copy(i + 1).start()

        @pl.when(t == 8)
        def _():
            push(PE2).wait_send()
            fetch_x.start()

    for c in range(n):
        end_results(c)
    for c in range(n - LEAD, n):
        send1(c).wait_send()
    for c in range(n - 2, n):
        send2(c).wait_send()
    push(PEP).wait_send()


def run_backward(lefts, left_others, others, weights, tables):
    size = lax.axis_size("dp")
    width, tokens = lefts[0].shape
    hidden = lefts[1].shape[0]
    block = width // size
    cols = width // 2
    table = chunk_table(width, hidden)
    n = len(table)
    length = size // 4
    share = block // 2
    hdim = width // HEADS
    hbm = pl.BlockSpec(memory_space=pl.ANY)
    vmem = pl.BlockSpec(memory_space=pltpu.VMEM)
    y_flat = lefts[0].reshape(2, cols, tokens)
    lefts = [left.reshape(size, left.shape[0] // size, tokens) for left in lefts + left_others]
    shapes = [
        jax.ShapeDtypeStruct((block, cols), F32),
        jax.ShapeDtypeStruct((hidden // size // 2, width), F32),
        jax.ShapeDtypeStruct((share, hidden), F32),
        jax.ShapeDtypeStruct((share, width), F32),
        jax.ShapeDtypeStruct((share, 3 * width), F32),
        jax.ShapeDtypeStruct((8, width), F32),
        jax.ShapeDtypeStruct((tokens, width), F32),
        jax.ShapeDtypeStruct((2 * tokens, cols), F32),
    ]
    shapes += [
        jax.ShapeDtypeStruct((rows, tokens), BF16)
        for rows in (cols, hidden // 2, cols, 3 * cols, hidden // 2)
    ]
    dma = pltpu.SemaphoreType.DMA
    ring1, ring2, ring_line = 6, 4, length + 1
    main = cols - 128
    results = pl.pallas_call(
        functools.partial(backward_kernel, table, size),
        out_shape=shapes,
        in_specs=[hbm] * 22 + [vmem] * 5,
        out_specs=[hbm] * 5 + [vmem] + [hbm] * 7,
        scratch_shapes=[
            pltpu.VMEM((2, 2, size, block, tokens), BF16),
            pltpu.VMEM((2, 2, cols, tokens), BF16),
            pltpu.VMEM((2, tokens, cols), BF16),
            pltpu.VMEM((LEAD, 2, 2, length, block, main), BF16),
            pltpu.VMEM((ring1, 2, length, block, main), BF16),
            pltpu.VMEM((2, 2, length, block, main), BF16),
            pltpu.VMEM((ring2, length, block, main), BF16),
            pltpu.VMEM((ring_line, length, block, main), BF16),
            pltpu.VMEM((ring1, length - 1, block, main), BF16),
            pltpu.VMEM((ring1, length - 1, block, main), BF16),
            pltpu.VMEM((length + 4, length, 2, 2, block, cols - main), BF16),
            pltpu.VMEM((length + 3, length - 1, 2, 2, block, cols - main), BF16),
            pltpu.VMEM((length + 3, length - 1, 2, 2, block, cols - main), BF16),
            pltpu.VMEM((length + 3, 2, block, cols - main), BF16),
            pltpu.VMEM((length + 3, block, cols - main), BF16),
            pltpu.VMEM((n, block, cols), F32),
            pltpu.VMEM((5, 8, width), F32),
            pltpu.VMEM((5, 8, width), F32),
            pltpu.VMEM((width, tokens), F32),
            pltpu.VMEM((width, tokens), F32),
            pltpu.VMEM((width, tokens), F32),
            pltpu.VMEM((width, tokens), BF16),
            pltpu.VMEM((tokens, tokens), F32),
            pltpu.VMEM((width, 128), F32),
            pltpu.VMEM((2, cols, width), BF16),
            pltpu.VMEM((2, width, cols), BF16),
            pltpu.VMEM((2, cols, tokens), BF16),
            pltpu.VMEM((2, cols, tokens), BF16),
            pltpu.VMEM((3 * width, tokens), BF16),
            pltpu.VMEM((HEADS, hdim, tokens), BF16),
            pltpu.VMEM((2, TOGETHER, 3, hdim, tokens), BF16),
            pltpu.VMEM((2, tokens, 128), F32),
            dma((6,)),
            dma((6,)),
            dma((2, 2)),
            dma((2, 2)),
            dma((LEAD,)),
            dma((ring1,)),
            dma((2,)),
            dma((ring2,)),
            dma((ring_line, length - 1)),
            dma((ring1, length - 1)),
            dma((ring_line, length - 1)),
            dma((ring1, length - 1)),
            dma((length + 4, length - 1)),
            dma((length + 3, length - 1)),
            dma((length + 4, length - 1)),
            dma((length + 3, length - 1)),
            dma((length + 4,)),
            dma((length + 3,)),
            dma((length + 4,)),
            dma((length + 3,)),
            dma((n,)),
            dma((n,)),
            dma((n,)),
            dma((5,)),
            dma((5,)),
            dma((2,)),
            dma((2,)),
            dma((2,)),
            dma((2,)),
            dma((hidden // width,)),
            dma((2, TOGETHER, 3)),
            dma((5,)),
            dma((2,)),
        ],
        compiler_params=pltpu.CompilerParams(
            collective_id=0, has_side_effects=True, vmem_limit_bytes=62 << 20
        ),
        name="backward",
    )(*lefts, y_flat, *others, *weights, *tables)
    return results[:8]


def finish_kernel(copied, *refs):
    sources, sums = refs[:copied], refs[copied]
    targets = refs[copied + 1 : 2 * copied + 1]
    gain_attn, gain_mlp, gain_final, bias = refs[2 * copied + 1 : 2 * copied + 5]
    held = refs[2 * copied + 5 : 3 * copied + 5]
    fetch_sem, copy_sem = refs[3 * copied + 5 :]
    me = lax.axis_index("dp")
    core = lax.axis_index("head")
    width = sums.shape[1]
    share, half = gain_attn.shape[0], bias.shape[0]
    arrivals = [
        pltpu.make_async_copy(source, buffer, fetch_sem.at[i])
        for i, (source, buffer) in enumerate(zip(sources, held))
    ]
    copies = [
        pltpu.make_async_copy(buffer, target, copy_sem.at[i])
        for i, (buffer, target) in enumerate(zip(held, targets))
    ]
    for arrival in arrivals:
        arrival.start()
    start = (me * 2 + core) * share
    rolled = pltpu.roll(sums[...], lax.rem(width - start, width), 1)
    for i, target in enumerate((gain_attn, gain_mlp, gain_final)):
        target[...] = rolled[i, :share]
    bias[...] = sums[3, pl.ds(pl.multiple_of(core * half, 128), half)]
    for arrival, copy in zip(arrivals, copies):
        arrival.wait()
        copy.start()
    for copy in copies:
        copy.wait()


def run_finish(copied, sums):
    width = sums.shape[1]
    share = width // (2 * lax.axis_size("dp"))
    hbm = pl.BlockSpec(memory_space=pl.ANY)
    vmem = pl.BlockSpec(memory_space=pltpu.VMEM)
    dma = pltpu.SemaphoreType.DMA
    shapes = [jax.ShapeDtypeStruct(value.shape, F32) for value in copied]
    shapes += [jax.ShapeDtypeStruct((share,), F32)] * 3
    shapes += [jax.ShapeDtypeStruct((width // 2,), F32)]
    return pl.pallas_call(
        functools.partial(finish_kernel, len(copied)),
        out_shape=shapes,
        in_specs=[hbm] * len(copied) + [vmem],
        out_specs=[hbm] * len(copied) + [vmem] * 4,
        scratch_shapes=[pltpu.VMEM(value.shape, F32) for value in copied]
        + [dma((len(copied),)), dma((len(copied),))],
        compiler_params=pltpu.CompilerParams(vmem_limit_bytes=60 << 20),
        name="finish",
    )(*copied, sums)


def per_device(
    inputs,
    segment_ids,
    gain_attn,
    w_qkv,
    w_out,
    gain_mlp,
    w_up,
    w_down,
    gain_final,
    head_projection_weight,
    head_output_bias,
    cotangent,
):
    core = lax.axis_index("head")
    place = lax.axis_index("dp")
    size = lax.axis_size("dp")
    rows, sequence_span = segment_ids.shape
    count, width = inputs.shape
    hdim = width // HEADS
    scale = 1.0 / math.sqrt(hdim)
    share = width // (2 * size)
    fused = size == HEADS and lax.axis_size("head") == 2 and rows == 1

    if fused:
        half = width // 2
        turn = hdim // 2
        freq = np.float32(10000.0) ** (-np.arange(turn, dtype=np.float32) / np.float32(turn))
        angle = np.arange(sequence_span, dtype=np.float32)[None, :] * freq[:, None]
        cosine_t, sine_t = jnp.asarray(np.cos(angle)), jnp.asarray(np.sin(angle))
        (
            y_t,
            g_t,
            a2_t,
            o_t,
            a1_t,
            g_o,
            a2_o,
            o_o,
            a1_o,
            x3_t,
            gain_columns,
            x2_t,
            x_t,
            h_t,
            qkv_t,
            lse,
        ) = run_forward(
            inputs,
            w_qkv,
            w_out,
            w_up,
            w_down,
            segment_ids,
            [gain_attn, gain_mlp, gain_final],
            cosine_t,
            sine_t,
        )
        head, down, up, out, qkv, sums, entry, levels = run_backward(
            [y_t, g_t, a2_t, o_t, a1_t],
            [g_o, a2_o, o_o, a1_o],
            [
                cotangent,
                head_projection_weight,
                x3_t,
                x2_t,
                x_t,
                h_t,
                qkv_t,
                gain_columns,
            ],
            [w_down, w_up, w_out, w_qkv],
            [lse, segment_ids, head_output_bias, cosine_t, sine_t],
        )
        (
            predicted_levels,
            entry_sensitivity_matrix,
            grad_head,
            grad_down,
            grad_up,
            grad_out,
            grad_qkv,
            *gains,
            grad_bias,
        ) = run_finish([levels, entry, head, down, up, out, qkv], sums)
    else:
        other_rows = lax.dynamic_slice_in_dim(cotangent, (1 - core) * count, count, 0)
        own_rows = lax.dynamic_slice_in_dim(cotangent, core * count, count, 0)
        got = swap_cores(contract_cols(head_projection_weight, other_rows).astype(BF16))
        grad_final_t = contract_cols(head_projection_weight, own_rows) + got.astype(F32)
        bias_local = jnp.sum(cotangent, axis=0, dtype=F32)

        cosine, sine = rotary_tables(sequence_span, hdim)
        tokens = inputs.astype(jnp.float32)
        normed_one, inverse_one = rms_forward(tokens, gain_attn)
        act_one = normed_one.astype(jnp.bfloat16)
        projected = jnp.dot(act_one, w_qkv, preferred_element_type=jnp.float32).reshape(
            rows, sequence_span, 3, HEADS, hdim
        )
        query = rotate(projected[:, :, 0], cosine, sine).astype(jnp.bfloat16)
        key = rotate(projected[:, :, 1], cosine, sine).astype(jnp.bfloat16)
        value = projected[:, :, 2].astype(jnp.bfloat16)
        attended, log_total = lax.map(
            lambda items: attend_forward(items, scale), (query, key, value, segment_ids)
        )
        mixed = attended.reshape(rows * sequence_span, width)
        resid_two = tokens + jnp.dot(mixed, w_out, preferred_element_type=jnp.float32)
        normed_two, inverse_two = rms_forward(resid_two, gain_mlp)
        act_two = normed_two.astype(jnp.bfloat16)
        hidden_pre = jnp.dot(act_two, w_up, preferred_element_type=jnp.float32)
        hidden = jax.nn.silu(hidden_pre).astype(jnp.bfloat16)
        resid_three = resid_two + jnp.dot(hidden, w_down, preferred_element_type=jnp.float32)
        normed_three, inverse_three = rms_forward(resid_three, gain_final)
        final_hidden = normed_three.astype(jnp.bfloat16)
        other_hidden = swap_cores(final_hidden)
        collected_rows = jnp.concatenate(
            [
                jnp.where(core == 0, final_hidden, other_hidden),
                jnp.where(core == 0, other_hidden, final_hidden),
            ],
            axis=0,
        )
        predicted_levels = (
            jnp.dot(collected_rows, head_projection_weight, preferred_element_type=jnp.float32)
            + head_output_bias
        )
        grad_head = lax.psum_scatter(
            contract_rows(collected_rows, cotangent), "dp", scatter_dimension=0, tiled=True
        )
        grad_three, grad_gain_final = rms_backward(
            resid_three, inverse_three, gain_final, grad_final_t.T
        )
        grad_mlp_out = grad_three.astype(jnp.bfloat16)
        grad_hidden = contract_cols(grad_mlp_out, w_down)
        sigmoid = jax.nn.sigmoid(hidden_pre)
        grad_pre = (grad_hidden * sigmoid * (1.0 + hidden_pre * (1.0 - sigmoid))).astype(BF16)
        grad_norm_two, grad_gain_mlp = rms_backward(
            resid_two, inverse_two, gain_mlp, contract_cols(grad_pre, w_up)
        )
        grad_two = grad_three + grad_norm_two
        grad_branch = grad_two.astype(jnp.bfloat16)
        grad_mixed = (
            contract_cols(grad_branch, w_out)
            .astype(jnp.bfloat16)
            .reshape(rows, sequence_span, HEADS, hdim)
        )
        grad_query, grad_key, grad_value = lax.map(
            lambda items: attend_backward(items, scale),
            (query, key, value, segment_ids, log_total, grad_mixed),
        )
        grad_query = unrotate(grad_query, cosine, sine)
        grad_key = unrotate(grad_key, cosine, sine)
        grad_proj = (
            jnp.stack([grad_query, grad_key, grad_value], axis=2)
            .reshape(rows * sequence_span, 3 * width)
            .astype(jnp.bfloat16)
        )
        grad_norm_one, grad_gain_attn = rms_backward(
            tokens, inverse_one, gain_attn, contract_cols(grad_proj, w_qkv)
        )
        entry_sensitivity_matrix = grad_two + grad_norm_one
        grad_down = scatter_rows(hidden, grad_mlp_out)
        grad_up = scatter_rows(act_two, grad_pre)
        grad_out = scatter_rows(mixed, grad_branch)
        grad_qkv = scatter_rows(act_one, grad_proj)
        gains = sum_everywhere(jnp.stack([grad_gain_attn, grad_gain_mlp, grad_gain_final]), True)
        gains = lax.dynamic_slice_in_dim(gains, (place * 2 + core) * share, share, 1)
        grad_bias = sum_everywhere(bias_local, False)
    return (
        predicted_levels,
        entry_sensitivity_matrix,
        gains[0],
        grad_qkv,
        grad_out,
        gains[1],
        grad_up,
        grad_down,
        gains[2],
        grad_head,
        grad_bias,
    )


def solution(mesh):
    return jax.shard_map(
        per_device,
        mesh=mesh,
        in_specs=(
            P(("dp", "head"), None),
            P(("dp", "head"), None),
            P(),
            P(),
            P(),
            P(),
            P(),
            P(),
            P(),
            P(None, "head"),
            P("head"),
            P("dp", "head"),
        ),
        out_specs=(
            P("dp", "head"),
            P(("dp", "head"), None),
            P(("dp", "head")),
            P(("dp", "head"), None),
            P(("dp", "head"), None),
            P(("dp", "head")),
            P(("dp", "head"), None),
            P(("dp", "head"), None),
            P(("dp", "head")),
            P("dp", "head"),
            P("head"),
        ),
        check_vma=False,
    )
```
